32 devices in a mesh: fsdp: 2 (over x), ctx: 4 (over y, core), tp: 4 (over z).
Axes of the slice: x: 2, y: 2, z: 4, core: 2. Of those that a mesh axis runs over, the one named last changes fastest.
Arguments:
- hidden_in: bfloat16 [2, 2, 512, 1536], P(None, 'fsdp', 'ctx'), may hold values from -6 to 6
- parents: int32 [2, 2, 4], P(None, 'fsdp'), may hold values from 0 to 2, as said below
- routes: int32 [2, 2, 512, 8], P(None, 'fsdp', 'ctx'), may hold values from 0 to 39, all different within a row; in each aligned block of 128 rows (0 to 127, 128 to 255, ..., all dimensions but the last counted through in order) at most 32 rows name the same one
- attn_gain: bfloat16 [1536], P('fsdp'), may hold values from 0.5 to 1.5
- w_query: bfloat16 [1536, 1536], P('fsdp', 'tp'), may hold values from -0.625 to 0.625
- key_projection: bfloat16 [1536, 512], P('fsdp', 'tp'), may hold values from -0.625 to 0.625
- value_projection: bfloat16 [1536, 512], P('fsdp', 'tp'), may hold values from -0.15625 to 0.15625
- w_out: bfloat16 [1536, 1536], P('tp', 'fsdp'), may hold values from -2 to 2
- moe_gain: bfloat16 [1536], P('fsdp'), may hold values from 0.5 to 1.5
- w_router: bfloat16 [1536, 40], P('fsdp'), may hold values from -0.078125 to 0.078125
- w_gate_up: bfloat16 [40, 1536, 2, 512], P(None, 'fsdp', None, 'tp'), may hold values from -0.15625 to 0.15625
- w_down: bfloat16 [40, 512, 1536], P(None, 'tp', 'fsdp'), may hold values from -4 to 4
- d_out: bfloat16 [2, 2, 512, 1536], P(None, 'fsdp', 'ctx'), may hold values from -6 to 6
Outputs:
- layer_out: float32 [2, 2, 512, 1536], P(None, 'fsdp', 'ctx')
- d_hidden: float32 [2, 2, 512, 1536], P(None, 'fsdp', 'ctx')
- d_attn_gain: float32 [1536], P('fsdp')
- d_w_query: float32 [1536, 1536], P('fsdp', 'tp')
- d_w_key: float32 [1536, 512], P('fsdp', 'tp')
- d_w_value: float32 [1536, 512], P('fsdp', 'tp')
- d_w_out: float32 [1536, 1536], P('tp', 'fsdp')
- d_moe_gain: float32 [1536], P('fsdp')
- d_w_router: float32 [1536, 40], P('fsdp')
- d_w_gate_up: float32 [40, 1536, 2, 512], P(None, 'fsdp', None, 'tp')
- d_w_down: float32 [40, 512, 1536], P(None, 'tp', 'fsdp')
The draws below stay inside these ranges and needn't reach their ends.
Inputs may be any that keep to these rules, and one draw needn't show every extreme that they name: `parents`: segment 0 of each tree is its root (its own parent); every other segment's parent is a lower segment; the last segment's parent is the segment before it. `routes`: each token names 8 different experts; within each aligned block of 128 rows (one device's tokens of one micro-batch) no expert is named by more than 32 rows, and in some blocks one is named by exactly 32.
All inputs are finite; a program needn't handle non-finite values.
Results may differ from the reference program's by a relative error of at most 0.025.
Values may be sent and summed in bfloat16 or wider, within the bound.
No kernel may reach another device: no remote copies, remote signals or barrier semaphores. Data moves between devices by JAX's collectives and lax.ppermute only.
A program may use at most 320 MiB of HBM per device.

```python
import math
import jax
import jax.numpy as jnp
import numpy as np
from jax import lax

MODEL_DIM = 1536
QUERY_HEADS = 24
KEY_VALUE_HEADS = 8
HEAD_DIM = 64
EXPERTS = 40
FF = 512
TOPK = 8
MB = 2
TOK_DEV = 128
TREE_TOKENS = 512
SEGS = 4
TREES = 2
CAP = 32
N_CTX = 4
N_TP = 4


def draw_parents(key, part):
    seg_ids = jnp.arange(SEGS, dtype=jnp.int32)
    upper_bound = jnp.maximum(seg_ids, 1)
    picked = jax.random.randint(key, (MB, TREES, SEGS), 0, upper_bound[None, None, :])
    picked = jnp.where(seg_ids[None, None, :] == 0, 0, picked)
    picked = jnp.where(seg_ids[None, None, :] == SEGS - 1, SEGS - 2, picked)
    return picked.astype(jnp.int32)


def block_levels(stream_key, extent, pieces, low, high):
    loudness, own = 1.0, jax.random.fold_in(stream_key, 6)
    for dim, parts in pieces:
        heights = jnp.exp(jax.random.uniform(jax.random.fold_in(own, dim), (parts,), jnp.float32, low / len(pieces), high / len(pieces)))
        loudness = loudness * jnp.repeat(heights, extent[dim] // parts).reshape([-1 if axis == dim else 1 for axis in range(len(extent))])
    return loudness


def shared_out(key, own, number, rows, amount, top, limit, slope):
    ranking = jax.random.permutation(key, amount)
    crowded, usual = load_shares(amount, rows * top, limit, slope, True), load_shares(amount, rows * top, limit, slope, False)
    places = jnp.arange(amount)

    def named(tallies, offset_by):
        used = int((tallies > 0).sum())
        fixed = max(1, used // 4)
        shifted = fixed + (places - fixed + offset_by * (used - fixed)) % max(1, amount - fixed)
        return jnp.zeros((amount,), jnp.int32).at[ranking[jnp.where(places < fixed, places, shifted)]].set(jnp.asarray(tallies, jnp.int32))

    tallies = jnp.where(number % 4 == 0, named(crowded, number // 4), named(usual, number - number // 4 - 1))
    mixed = jax.random.permutation(jax.random.fold_in(own, 3), amount)
    source_of, taker = mixed[0:amount // 2 * 2:2], mixed[1:amount // 2 * 2:2]
    slack = jnp.minimum(tallies[source_of] - 1, limit - tallies[taker]) // 2
    slack = jnp.where((source_of == ranking[0]) | (taker == ranking[0]) | (tallies[taker] == 0), 0, jnp.maximum(slack, 0))
    shifted = jax.random.randint(jax.random.fold_in(own, 4), (amount // 2,), 0, 1 << 20) % (slack + 1)
    tallies = tallies.at[source_of].add(-shifted).at[taker].add(shifted)
    members = jnp.searchsorted(jnp.cumsum(tallies), jnp.arange(rows * top), side="right").astype(jnp.int32)
    listing = members.reshape(top, rows).T
    listing = listing[jax.random.permutation(jax.random.fold_in(own, 1), rows)]
    offset_by = jax.random.randint(jax.random.fold_in(own, 2), (rows, 1), 0, top)
    return jnp.take_along_axis(listing, (jnp.arange(top)[None, :] + offset_by) % top, axis=1)


def load_shares(count, total, limit, skew, full):
    portions = [(1 << 20) // math.isqrt(grade ** skew) + 1 for grade in range(1, count + 1)]
    largest = limit if full else min(limit, max(-(-total // count), total * portions[0] // sum(portions)))
    least = 1 if total - largest >= count - 1 else 0
    given, rest = [largest] + [least] * (count - 1), total - largest - least * (count - 1)
    while rest > 0:
        free = [i for i in range(1, count) if given[i] < largest] or [i for i in range(1, count) if given[i] < limit]
        mass, left = sum([portions[i] for i in free]), rest
        for i in free:
            extra = min(limit - given[i], max(1, left * portions[i] // mass), rest)
            given[i] = given[i] + extra
            rest = rest - extra
    return np.array(given)


def normal_values(key, dims, width, most, shards=(), kind=jnp.bfloat16):
    result = jax.random.normal(key, dims, jnp.float32) * width
    if len(shards) > 0:
        result = block_levels(key, dims, shards, -0.22, 0.18) * result
    return jnp.clip(result, min=-most, max=most).astype(kind)


def setup_inputs(seed: int = 0) -> dict:
    key_of = jax.random.split(jax.random.key(seed), 14)
    hidden_in = normal_values(key_of[0], (MB, TREES, TREE_TOKENS, MODEL_DIM), 1.0, 6.0, ((1, 2), (2, 4)))
    parents = draw_parents(jax.random.fold_in(key_of[13], 71), 0)
    routes_keys = jax.random.split(jax.random.fold_in(key_of[2], 1), MB * TREES * TREE_TOKENS // TOK_DEV)
    routes_turns = jax.random.permutation(jax.random.fold_in(key_of[2], 3), MB * TREES * TREE_TOKENS // TOK_DEV)
    routes = jax.vmap(lambda own, number: shared_out(jax.random.fold_in(key_of[2], 2), own, number, TOK_DEV, EXPERTS, TOPK, CAP, 1))(routes_keys, routes_turns).reshape((MB, TREES, TREE_TOKENS, TOPK))
    attn_gain = jnp.clip(1.0 + 0.1 * jax.random.normal(key_of[3], (MODEL_DIM,), jnp.float32), 0.5, 1.5).astype(jnp.bfloat16)
    w_query = normal_values(key_of[4], (MODEL_DIM, QUERY_HEADS * HEAD_DIM), (MODEL_DIM // 16) ** -0.5, 0.625, ((0, 2), (1, 4)))
    key_projection = normal_values(key_of[5], (MODEL_DIM, KEY_VALUE_HEADS * HEAD_DIM), (MODEL_DIM // 16) ** -0.5, 0.625, ((0, 2), (1, 4)))
    value_projection = normal_values(key_of[6], (MODEL_DIM, KEY_VALUE_HEADS * HEAD_DIM), MODEL_DIM ** -0.5, 0.15625, ((0, 2), (1, 4)))
    w_out = normal_values(key_of[7], (QUERY_HEADS * HEAD_DIM, MODEL_DIM), (max(HEAD_DIM // 8, 1)) ** -0.5, 2.0, ((0, 4), (1, 2)))
    moe_gain = jnp.clip(1.0 + 0.1 * jax.random.normal(key_of[8], (MODEL_DIM,), jnp.float32), 0.5, 1.5).astype(jnp.bfloat16)
    w_router = normal_values(key_of[9], (MODEL_DIM, EXPERTS), (4 * MODEL_DIM) ** -0.5, 0.078125, ((0, 2),))
    w_gate_up = normal_values(key_of[10], (EXPERTS, MODEL_DIM, 2, FF), MODEL_DIM ** -0.5, 0.15625, ((1, 2), (3, 4)))
    w_down = normal_values(key_of[11], (EXPERTS, FF, MODEL_DIM), (max(FF // 256, 1)) ** -0.5, 4.0, ((1, 4), (2, 2)))
    d_out = normal_values(key_of[12], (MB, TREES, TREE_TOKENS, MODEL_DIM), 1.0, 6.0, ((1, 2), (2, 4)))
    return dict(hidden_in=hidden_in, parents=parents, routes=routes, attn_gain=attn_gain, w_query=w_query, key_projection=key_projection, value_projection=value_projection, w_out=w_out, moe_gain=moe_gain, w_router=w_router, w_gate_up=w_gate_up, w_down=w_down, d_out=d_out)


@jax.custom_vjp
def reduced_precision(v):
    return lax.optimization_barrier(v.astype(jnp.bfloat16)).astype(jnp.float32)

@jax.custom_vjp
def reduced_backward(v):
    return v

def low_keep(v):
    return (reduced_precision(v), None)

def low_pass(kept, grad):
    return (grad,)

def back_keep(v):
    return (v, None)

def back_low(kept, grad):
    return (reduced_precision(grad),)
reduced_precision.defvjp(low_keep, low_pass)
reduced_backward.defvjp(back_keep, back_low)
EPSILON = 1e-06
RESIDUAL_SCALE = 0.22
SCORE_SCALE = 1.0 / 64.0
ROPE_BASE = 10000.0
TOP_PRECISION = lax.Precision.HIGHEST

def tree_tables(parent_row, tree_len):
    seg_total = parent_row.shape[0]
    seg_len = tree_len // seg_total
    seg_ids = jnp.arange(seg_total, dtype=jnp.int32)
    parent_links = (parent_row[:, None] == seg_ids[None, :]).astype(jnp.float32)
    reach_table = jnp.maximum(parent_links, jnp.eye(seg_total, dtype=jnp.float32))
    for squaring in range(max(seg_total - 1, 1).bit_length()):
        reach_table = jnp.minimum(jnp.dot(reach_table, reach_table, precision=TOP_PRECISION), 1.0)
    seg_depth = lax.optimization_barrier(jnp.sum(reach_table, axis=1)) - 1.0
    token_ids = jnp.arange(tree_len, dtype=jnp.int32)
    tok_owner = ((token_ids // seg_len)[:, None] == seg_ids[None, :]).astype(jnp.float32)
    tok_offset = (token_ids % seg_len).astype(jnp.float32)
    places = jnp.dot(tok_owner, seg_depth, precision=TOP_PRECISION) * seg_len + tok_offset
    return (places, jnp.dot(tok_owner, reach_table, precision=TOP_PRECISION), tok_owner)

def rope_tables(places):
    half_dim = HEAD_DIM // 2
    inverse = ROPE_BASE ** (-jnp.arange(half_dim, dtype=jnp.float32) * 2.0 / HEAD_DIM)
    angles = places[:, None] * inverse[None, :]
    cosine_table = jnp.concatenate([jnp.cos(angles), jnp.cos(angles)], axis=1)
    sine_values = jnp.concatenate([jnp.sin(angles), jnp.sin(angles)], axis=1)
    return (cosine_table, sine_values)

def apply_rotary(values, cosine_table, sine_values):
    half_dim = values.shape[-1] // 2
    turned = jnp.concatenate([-values[..., half_dim:], values[..., :half_dim]], axis=-1)
    return values * cosine_table[:, None, :] + turned * sine_values[:, None, :]

def norm_scale(values):
    return lax.rsqrt(lax.optimization_barrier(jnp.mean(values * values, axis=-1, keepdims=True)) + EPSILON)

def tree_layer(tree_in, parent_row, route_row, gain_one, query_w, key_matrix, value_matrix, out_w, gain_two, router_w, gate_up_w, down_w):
    places, reach_rows, tok_owner = tree_tables(parent_row, TREE_TOKENS)
    allowed = (jnp.dot(reach_rows, tok_owner.T, precision=TOP_PRECISION) > 0.5) & (places[None, :] <= places[:, None])
    cosine_table, sine_values = rope_tables(places)
    first_normed = reduced_precision(tree_in * norm_scale(tree_in) * gain_one)
    query_unrotated = reduced_backward(jnp.dot(first_normed, query_w, precision=TOP_PRECISION)).reshape(TREE_TOKENS, QUERY_HEADS, HEAD_DIM)
    key_unrotated = reduced_backward(jnp.dot(first_normed, key_matrix, precision=TOP_PRECISION)).reshape(TREE_TOKENS, KEY_VALUE_HEADS, HEAD_DIM)
    value_reduced = reduced_precision(reduced_backward(jnp.dot(first_normed, value_matrix, precision=TOP_PRECISION))).reshape(TREE_TOKENS, KEY_VALUE_HEADS, HEAD_DIM)
    query_reduced = reduced_precision(apply_rotary(query_unrotated, cosine_table, sine_values)).reshape(TREE_TOKENS, KEY_VALUE_HEADS, QUERY_HEADS // KEY_VALUE_HEADS, HEAD_DIM).transpose(1, 2, 0, 3)
    key_low = reduced_precision(apply_rotary(key_unrotated, cosine_table, sine_values)).transpose(1, 0, 2)
    value_heads = value_reduced.transpose(1, 0, 2)

    def head_block(items):
        query_head, key_head, value_head = items
        raw_scores = reduced_backward(jnp.einsum('jqd,kd->jqk', query_head, key_head, precision=TOP_PRECISION))
        scores = jnp.where(allowed[None], raw_scores * SCORE_SCALE, -1e+30)
        probs = jax.nn.softmax(scores, axis=-1)
        return jnp.einsum('jqk,kd->jqd', reduced_precision(probs), value_head, precision=TOP_PRECISION)
    head_out = lax.map(jax.checkpoint(head_block), (query_reduced, key_low, value_heads))
    head_low = reduced_precision(reduced_backward(head_out.transpose(2, 0, 1, 3).reshape(TREE_TOKENS, QUERY_HEADS * HEAD_DIM)))
    per_share = QUERY_HEADS * HEAD_DIM // N_TP
    attn_parts = jnp.einsum('tgc,gcd->gtd', head_low.reshape(TREE_TOKENS, N_TP, per_share), out_w.reshape(N_TP, per_share, MODEL_DIM), precision=TOP_PRECISION)
    mixed = tree_in + RESIDUAL_SCALE * reduced_backward(lax.optimization_barrier(jnp.sum(reduced_precision(attn_parts), axis=0)))
    normed_two = reduced_precision(mixed * norm_scale(mixed) * gain_two)
    logits = reduced_backward(jnp.dot(normed_two, router_w, precision=TOP_PRECISION))
    expert_ids = jnp.arange(EXPERTS, dtype=jnp.int32)
    picked = (route_row[:, :, None] == expert_ids[None, None, :]).astype(jnp.float32)
    gates = jax.nn.softmax(lax.optimization_barrier(jnp.sum(picked * logits[:, None, :], axis=2)), axis=1)
    capacity = N_CTX * CAP
    flat_ids = route_row.reshape(-1).astype(jnp.int32)
    flat_hot = (flat_ids[:, None] == expert_ids[None, :]).astype(jnp.int32)
    slots = lax.optimization_barrier(jnp.sum((jnp.cumsum(flat_hot, axis=0) - flat_hot) * flat_hot, axis=1)).astype(jnp.int32)
    targets = flat_ids * capacity + slots
    sources = jnp.zeros((EXPERTS * capacity,), jnp.int32).at[targets].set(jnp.arange(TREE_TOKENS * TOPK, dtype=jnp.int32) // TOPK)
    filled = jnp.zeros((EXPERTS * capacity, 1), jnp.float32).at[targets].set(1.0)
    dispatched = (normed_two[sources] * filled).reshape(EXPERTS, capacity, MODEL_DIM)
    gate_up = reduced_backward(jnp.einsum('ecd,edsf->ecsf', dispatched, gate_up_w, precision=TOP_PRECISION))
    activ_low = reduced_precision(jax.nn.silu(gate_up[:, :, 0]) * gate_up[:, :, 1])
    share_width = FF // N_TP
    activ_groups = activ_low.reshape(EXPERTS, capacity, N_TP, share_width).transpose(2, 0, 1, 3)
    down_groups = down_w.reshape(EXPERTS, N_TP, share_width, MODEL_DIM).transpose(1, 0, 2, 3)

    def share_block(items):
        activ_share, down_share = items
        expert_out = reduced_backward(jnp.einsum('ecf,efd->ecd', activ_share, down_share, precision=TOP_PRECISION)).reshape(EXPERTS * capacity, MODEL_DIM)
        entry_out = expert_out[targets].reshape(TREE_TOKENS, TOPK, MODEL_DIM)
        return reduced_precision(lax.optimization_barrier(jnp.sum(gates[:, :, None] * entry_out, axis=1)))
    moe_sum = lax.optimization_barrier(jnp.sum(lax.map(jax.checkpoint(share_block), (activ_groups, down_groups)), axis=0))
    return mixed + RESIDUAL_SCALE * moe_sum

def reference(hidden_in, parents, routes, attn_gain, w_query, key_projection, value_projection, w_out, moe_gain, w_router, w_gate_up, w_down, d_out):
    tree_count = MB * TREES
    flat_hidden = hidden_in.astype(jnp.float32).reshape(tree_count, TREE_TOKENS, MODEL_DIM)
    flat_parents = parents.reshape(tree_count, SEGS).astype(jnp.int32)
    flat_routes = routes.reshape(tree_count, TREE_TOKENS, TOPK).astype(jnp.int32)

    def forward(flat_in, gain_one, query_w, key_matrix, value_matrix, out_w, gain_two, router_w, gate_up_w, down_w):

        def one_tree(items):
            tree_in, parent_row, route_row = items
            return tree_layer(tree_in, parent_row, route_row, gain_one, query_w, key_matrix, value_matrix, out_w, gain_two, router_w, gate_up_w, down_w)
        return lax.map(jax.checkpoint(one_tree), (flat_in, flat_parents, flat_routes))
    layer_out, pull_back = jax.vjp(forward, flat_hidden, attn_gain.astype(jnp.float32), w_query.astype(jnp.float32), key_projection.astype(jnp.float32), value_projection.astype(jnp.float32), w_out.astype(jnp.float32), moe_gain.astype(jnp.float32), w_router.astype(jnp.float32), w_gate_up.astype(jnp.float32), w_down.astype(jnp.float32))
    all_grads = pull_back(d_out.astype(jnp.float32).reshape(tree_count, TREE_TOKENS, MODEL_DIM))
    return (layer_out.reshape(MB, TREES, TREE_TOKENS, MODEL_DIM), all_grads[0].reshape(MB, TREES, TREE_TOKENS, MODEL_DIM), all_grads[1], all_grads[2], all_grads[3], all_grads[4], all_grads[5], all_grads[6], all_grads[7], all_grads[8], all_grads[9])
```

```python
import jax
import jax.numpy as jnp
from jax import lax
from jax.experimental import pallas as pl
from jax.experimental.pallas import tpu as pltpu
from jax.sharding import PartitionSpec as P

HEAD_DIM = 64
CAP = 32


EPSILON = 1e-06
RESIDUAL_SCALE = 0.22
SCORE_SCALE = 1.0 / 64.0
ROPE_BASE = 10000.0
TOP_PRECISION = lax.Precision.HIGHEST


def tree_tables(parent_row, tree_len):
    seg_total = parent_row.shape[0]
    seg_len = tree_len // seg_total
    seg_ids = jnp.arange(seg_total, dtype=jnp.int32)
    parent_links = (parent_row[:, None] == seg_ids[None, :]).astype(jnp.float32)
    reach_table = jnp.maximum(parent_links, jnp.eye(seg_total, dtype=jnp.float32))
    for squaring in range(max(seg_total - 1, 1).bit_length()):
        reach_table = jnp.minimum(jnp.dot(reach_table, reach_table, precision=TOP_PRECISION), 1.0)
    seg_depth = jnp.sum(reach_table, axis=1) - 1.0
    token_ids = jnp.arange(tree_len, dtype=jnp.int32)
    tok_owner = ((token_ids // seg_len)[:, None] == seg_ids[None, :]).astype(jnp.float32)
    tok_offset = (token_ids % seg_len).astype(jnp.float32)
    places = jnp.dot(tok_owner, seg_depth, precision=TOP_PRECISION) * seg_len + tok_offset
    return (places, jnp.dot(tok_owner, reach_table, precision=TOP_PRECISION), tok_owner)


def rope_tables(places):
    half_dim = HEAD_DIM // 2
    inverse = ROPE_BASE ** (-jnp.arange(half_dim, dtype=jnp.float32) * 2.0 / HEAD_DIM)
    angles = places[:, None] * inverse[None, :]
    cosine_table = jnp.concatenate([jnp.cos(angles), jnp.cos(angles)], axis=1)
    sine_values = jnp.concatenate([jnp.sin(angles), jnp.sin(angles)], axis=1)
    return (cosine_table, sine_values)


def apply_rotary(values, cosine_table, sine_values):
    half_dim = values.shape[-1] // 2
    turned = jnp.concatenate([-values[..., half_dim:], values[..., :half_dim]], axis=-1)
    return values * cosine_table[:, None, :] + turned * sine_values[:, None, :]


def norm_scale(values):
    return lax.rsqrt(jnp.mean(values * values, axis=-1, keepdims=True) + EPSILON)


def add_tuples(first_tuple, second_tuple):
    return tuple(
        (left_part + right_part for left_part, right_part in zip(first_tuple, second_tuple))
    )


def expert_work(rows, row_grads, gate_up_w, down_w, down_form):
    gate_up = jnp.einsum("ecd,edsf->ecsf", rows, gate_up_w, preferred_element_type=jnp.float32)
    gate_pre = gate_up[:, :, 0]
    up_pre = gate_up[:, :, 1]
    sigmoid = jax.nn.sigmoid(gate_pre)
    activ_low = (gate_pre * sigmoid * up_pre).astype(jnp.bfloat16)
    expert_out = jnp.einsum(
        "ecf," + down_form + "->ecd", activ_low, down_w, preferred_element_type=jnp.float32
    )
    activ_grad = jnp.einsum(
        "ecd," + down_form + "->ecf", row_grads, down_w, preferred_element_type=jnp.float32
    )
    gate_grad = activ_grad * up_pre * sigmoid * (1.0 + gate_pre * (1.0 - sigmoid))
    up_grad = activ_grad * gate_pre * sigmoid
    gate_up_grad = jnp.stack([gate_grad, up_grad], axis=2).astype(jnp.bfloat16)
    row_input_grad = jnp.einsum(
        "ecsf,edsf->ecd", gate_up_grad, gate_up_w, preferred_element_type=jnp.float32
    )
    grad_gate_up = jnp.einsum(
        "ecd,ecsf->edsf", rows, gate_up_grad, preferred_element_type=jnp.float32
    )
    grad_down = jnp.einsum(
        "ecf,ecd->" + down_form, activ_low, row_grads, preferred_element_type=jnp.float32
    )
    return (expert_out, row_input_grad, grad_gate_up, grad_down)


def body(
    hidden_in,
    parents,
    routes,
    attn_gain,
    w_query,
    key_projection,
    value_projection,
    w_out,
    moe_gain,
    w_router,
    w_gate_up,
    w_down,
    d_out,
):
    experts = w_gate_up.shape[0]
    gathered = (
        lax.all_gather(attn_gain, "fsdp", axis=0, tiled=True),
        lax.all_gather(w_query, "fsdp", axis=0, tiled=True),
        lax.all_gather(key_projection, "fsdp", axis=0, tiled=True),
        lax.all_gather(value_projection, "fsdp", axis=0, tiled=True),
        lax.all_gather(w_out, "fsdp", axis=1, tiled=True),
        lax.all_gather(moe_gain, "fsdp", axis=0, tiled=True),
        lax.all_gather(w_router, "fsdp", axis=0, tiled=True),
        lax.all_gather(w_gate_up, "fsdp", axis=1, tiled=True),
        lax.all_gather(w_down, "fsdp", axis=2, tiled=True),
    )
    gate_up_full = gathered[7]
    down_full = gathered[8]
    down_form = "efd"
    gain_one = gathered[0].astype(jnp.float32)
    query_full = gathered[1]
    key_full = gathered[2]
    value_full = gathered[3]
    out_full = gathered[4]
    gain_two = gathered[5].astype(jnp.float32)
    router_full = gathered[6]
    micro_count = hidden_in.shape[0]
    local_rows = hidden_in.shape[2]
    model_width = hidden_in.shape[3]
    top_count = routes.shape[3]
    kv_heads = key_projection.shape[1] // HEAD_DIM
    q_heads = w_query.shape[1] // HEAD_DIM
    group_size = q_heads // kv_heads
    tree_len = local_rows * lax.axis_size("ctx")
    row_start = lax.axis_index("ctx") * local_rows
    capacity = CAP
    expert_ids = jnp.arange(experts, dtype=jnp.int32)
    outputs = []
    input_grads = []
    totals = None
    for batch_index in range(micro_count):
        tree_places, reach_rows, tok_owner = tree_tables(parents[batch_index, 0], tree_len)
        local_places = lax.dynamic_slice_in_dim(tree_places, row_start, local_rows, 0)
        local_reach = lax.dynamic_slice_in_dim(reach_rows, row_start, local_rows, 0)
        allowed = (jnp.dot(local_reach, tok_owner.T, precision=TOP_PRECISION) > 0.5) & (
            tree_places[None, :] <= local_places[:, None]
        )
        cosine_table, sine_values = rope_tables(local_places)
        inputs = hidden_in[batch_index, 0].astype(jnp.float32)
        scale_one = norm_scale(inputs)
        first_normed = (inputs * scale_one * gain_one).astype(jnp.bfloat16)
        query_unrotated = jnp.dot(
            first_normed, query_full, preferred_element_type=jnp.float32
        ).reshape(local_rows, q_heads, HEAD_DIM)
        key_unrotated = jnp.dot(first_normed, key_full, preferred_element_type=jnp.float32).reshape(
            local_rows, kv_heads, HEAD_DIM
        )
        value_reduced = jnp.dot(
            first_normed, value_full, preferred_element_type=jnp.float32
        ).astype(jnp.bfloat16)
        query_reduced = (
            apply_rotary(query_unrotated, cosine_table, sine_values)
            .astype(jnp.bfloat16)
            .reshape(local_rows, kv_heads, group_size, HEAD_DIM)
        )
        key_low = (
            apply_rotary(key_unrotated, cosine_table, sine_values)
            .astype(jnp.bfloat16)
            .reshape(local_rows, kv_heads * HEAD_DIM)
        )
        tree_keys, tree_values = (
            lax.all_gather(key_low, "ctx", axis=0, tiled=True),
            lax.all_gather(value_reduced, "ctx", axis=0, tiled=True),
        )
        tree_keys = tree_keys.reshape(tree_len, kv_heads, HEAD_DIM)
        tree_values = tree_values.reshape(tree_len, kv_heads, HEAD_DIM)

        def masked_scores():
            raw_scores = jnp.einsum(
                "qhjd,khd->hjqk", query_reduced, tree_keys, preferred_element_type=jnp.float32
            )
            return jnp.where(allowed[None, None], raw_scores * SCORE_SCALE, -1e30)

        scores = masked_scores()
        top_score = jnp.max(scores, axis=-1, keepdims=True)
        log_total = top_score + jnp.log(
            jnp.sum(jnp.exp(scores - top_score), axis=-1, keepdims=True)
        )
        probs_low = jnp.exp(scores - log_total).astype(jnp.bfloat16)
        head_out = jnp.einsum(
            "hjqk,khd->qhjd", probs_low, tree_values, preferred_element_type=jnp.float32
        )
        head_low = head_out.reshape(local_rows, q_heads * HEAD_DIM).astype(jnp.bfloat16)
        attn_part = jnp.dot(head_low, out_full, preferred_element_type=jnp.float32)
        attended = lax.psum(attn_part.astype(jnp.bfloat16), "tp").astype(jnp.float32)
        mixed = inputs + RESIDUAL_SCALE * attended
        scale_two = norm_scale(mixed)
        normed_two = (mixed * scale_two * gain_two).astype(jnp.bfloat16)
        logits = jnp.dot(normed_two, router_full, preferred_element_type=jnp.float32)
        chosen_ids = routes[batch_index, 0]
        picked = (chosen_ids[:, :, None] == expert_ids[None, None, :]).astype(jnp.float32)
        chosen = jnp.sum(picked * logits[:, None, :], axis=2)
        gates = jax.nn.softmax(chosen, axis=1)
        flat_ids = chosen_ids.reshape(-1)
        flat_hot = (flat_ids[:, None] == expert_ids[None, :]).astype(jnp.int32)
        slots = jnp.sum((jnp.cumsum(flat_hot, axis=0) - flat_hot) * flat_hot, axis=1)
        targets = flat_ids * capacity + slots
        sources = (
            jnp.zeros((experts * capacity,), jnp.int32)
            .at[targets]
            .set(jnp.arange(local_rows * top_count, dtype=jnp.int32) // top_count)
        )
        filled = jnp.zeros((experts * capacity, 1), jnp.bfloat16).at[targets].set(1)
        dispatched = (normed_two[sources] * filled).reshape(experts, capacity, model_width)
        grad_out = d_out[batch_index, 0].astype(jnp.float32)
        grad_moe = RESIDUAL_SCALE * grad_out
        entry_grad = (
            (gates[:, :, None] * grad_moe[:, None, :])
            .astype(jnp.bfloat16)
            .reshape(local_rows * top_count, model_width)
        )
        slot_grad = (
            jnp.zeros((experts * capacity, model_width), jnp.bfloat16)
            .at[targets]
            .set(entry_grad)
            .reshape(experts, capacity, model_width)
        )
        expert_out, slot_input_grad, grad_gate_up, grad_down = expert_work(
            dispatched, slot_grad, gate_up_full, down_full, down_form
        )
        entry_out = expert_out.reshape(experts * capacity, model_width)[targets].reshape(
            local_rows, top_count, model_width
        )
        moe_part = jnp.sum(gates[:, :, None] * entry_out, axis=1)
        moe_sum = lax.psum(moe_part.astype(jnp.bfloat16), "tp").astype(jnp.float32)
        outputs.append(mixed + RESIDUAL_SCALE * moe_sum)
        gate_grad_part = jnp.sum(grad_moe[:, None, :] * entry_out, axis=2)
        expert_input_grad = jnp.sum(
            slot_input_grad.reshape(experts * capacity, model_width)[targets].reshape(
                local_rows, top_count, model_width
            ),
            axis=1,
        )
        expert_input_grad, gate_grads = (
            lax.psum(expert_input_grad.astype(jnp.bfloat16), "tp").astype(jnp.float32),
            lax.psum(gate_grad_part.astype(jnp.bfloat16), "tp").astype(jnp.float32),
        )
        chosen_grad = gates * (gate_grads - jnp.sum(gates * gate_grads, axis=1, keepdims=True))
        logit_grad = jnp.sum(picked * chosen_grad[:, :, None], axis=1).astype(jnp.bfloat16)
        normed_two_grad = expert_input_grad + jnp.einsum(
            "te,de->td", logit_grad, router_full, preferred_element_type=jnp.float32
        )
        grad_router = jnp.einsum(
            "td,te->de", normed_two, logit_grad, preferred_element_type=jnp.float32
        )
        unit_two = mixed * scale_two
        grad_gain_two = jnp.sum(normed_two_grad * unit_two, axis=0)
        scaled_two = normed_two_grad * gain_two
        mixed_grad = grad_out + scale_two * (
            scaled_two - unit_two * jnp.mean(scaled_two * unit_two, axis=-1, keepdims=True)
        )
        attn_grad = (RESIDUAL_SCALE * mixed_grad).astype(jnp.bfloat16)
        grad_out_proj = jnp.einsum(
            "tc,td->cd", head_low, attn_grad, preferred_element_type=jnp.float32
        )
        head_grad = (
            jnp.einsum("td,cd->tc", attn_grad, out_full, preferred_element_type=jnp.float32)
            .astype(jnp.bfloat16)
            .reshape(local_rows, kv_heads, group_size, HEAD_DIM)
        )
        scores = masked_scores()
        probs = jnp.exp(scores - log_total)
        probs_low = probs.astype(jnp.bfloat16)
        prob_grad = jnp.einsum(
            "qhjd,khd->hjqk", head_grad, tree_values, preferred_element_type=jnp.float32
        )
        value_grad = jnp.einsum(
            "hjqk,qhjd->khd", probs_low, head_grad, preferred_element_type=jnp.float32
        )
        score_grad = (
            SCORE_SCALE * probs * (prob_grad - jnp.sum(probs * prob_grad, axis=-1, keepdims=True))
        ).astype(jnp.bfloat16)
        query_grad = jnp.einsum(
            "hjqk,khd->qhjd", score_grad, tree_keys, preferred_element_type=jnp.float32
        ).reshape(local_rows, q_heads, HEAD_DIM)
        key_grad = jnp.einsum(
            "hjqk,qhjd->khd", score_grad, query_reduced, preferred_element_type=jnp.float32
        )
        key_grad, value_grad = (
            lax.psum_scatter(
                key_grad.reshape(tree_len, kv_heads * HEAD_DIM).astype(jnp.bfloat16),
                "ctx",
                scatter_dimension=0,
                tiled=True,
            ).astype(jnp.float32),
            lax.psum_scatter(
                value_grad.reshape(tree_len, kv_heads * HEAD_DIM).astype(jnp.bfloat16),
                "ctx",
                scatter_dimension=0,
                tiled=True,
            ).astype(jnp.float32),
        )
        query_pre_grad = (
            apply_rotary(query_grad, cosine_table, -sine_values)
            .astype(jnp.bfloat16)
            .reshape(local_rows, q_heads * HEAD_DIM)
        )
        key_pre_grad = (
            apply_rotary(
                key_grad.reshape(local_rows, kv_heads, HEAD_DIM), cosine_table, -sine_values
            )
            .astype(jnp.bfloat16)
            .reshape(local_rows, kv_heads * HEAD_DIM)
        )
        value_pre_grad = value_grad.astype(jnp.bfloat16)
        normed_one_grad = jnp.einsum(
            "tc,dc->td", query_pre_grad, query_full, preferred_element_type=jnp.float32
        )
        normed_one_grad = normed_one_grad + jnp.einsum(
            "tc,dc->td", key_pre_grad, key_full, preferred_element_type=jnp.float32
        )
        normed_one_grad = normed_one_grad + jnp.einsum(
            "tc,dc->td", value_pre_grad, value_full, preferred_element_type=jnp.float32
        )
        grad_query = jnp.einsum(
            "td,tc->dc", first_normed, query_pre_grad, preferred_element_type=jnp.float32
        )
        grad_key = jnp.einsum(
            "td,tc->dc", first_normed, key_pre_grad, preferred_element_type=jnp.float32
        )
        grad_value = jnp.einsum(
            "td,tc->dc", first_normed, value_pre_grad, preferred_element_type=jnp.float32
        )
        normed_one_grad = lax.psum(normed_one_grad.astype(jnp.bfloat16), "tp").astype(jnp.float32)
        unit_one = inputs * scale_one
        grad_gain_one = jnp.sum(normed_one_grad * unit_one, axis=0)
        scaled_one = normed_one_grad * gain_one
        input_grads.append(
            mixed_grad
            + scale_one
            * (scaled_one - unit_one * jnp.mean(scaled_one * unit_one, axis=-1, keepdims=True))
        )
        piece = (
            grad_gain_one,
            grad_query,
            grad_key,
            grad_value,
            grad_out_proj,
            grad_gain_two,
            grad_router,
            grad_gate_up,
            grad_down,
        )
        totals = piece if batch_index == 0 else add_tuples(totals, piece)
    summed = (
        lax.psum_scatter(totals[0], ("fsdp", "ctx"), scatter_dimension=0, tiled=True),
        lax.psum_scatter(totals[1], ("fsdp", "ctx"), scatter_dimension=0, tiled=True),
        lax.psum_scatter(totals[2], ("fsdp", "ctx"), scatter_dimension=0, tiled=True),
        lax.psum_scatter(totals[3], ("fsdp", "ctx"), scatter_dimension=0, tiled=True),
        lax.psum_scatter(totals[4], ("fsdp", "ctx"), scatter_dimension=1, tiled=True),
        lax.psum_scatter(totals[5], ("fsdp", "ctx"), scatter_dimension=0, tiled=True),
        lax.psum_scatter(totals[6], ("fsdp", "ctx"), scatter_dimension=0, tiled=True),
        lax.psum_scatter(totals[7], ("fsdp", "ctx"), scatter_dimension=1, tiled=True),
        lax.psum_scatter(totals[8], ("fsdp", "ctx"), scatter_dimension=2, tiled=True),
    )
    shares = (
        lax.all_gather(summed[0].astype(jnp.bfloat16), "ctx", axis=0, tiled=True).astype(
            jnp.float32
        ),
        lax.all_gather(summed[1].astype(jnp.bfloat16), "ctx", axis=0, tiled=True).astype(
            jnp.float32
        ),
        lax.all_gather(summed[2].astype(jnp.bfloat16), "ctx", axis=0, tiled=True).astype(
            jnp.float32
        ),
        lax.all_gather(summed[3].astype(jnp.bfloat16), "ctx", axis=0, tiled=True).astype(
            jnp.float32
        ),
        lax.all_gather(summed[4].astype(jnp.bfloat16), "ctx", axis=1, tiled=True).astype(
            jnp.float32
        ),
        lax.all_gather(summed[5].astype(jnp.bfloat16), "ctx", axis=0, tiled=True).astype(
            jnp.float32
        ),
        lax.all_gather(summed[6].astype(jnp.bfloat16), "ctx", axis=0, tiled=True).astype(
            jnp.float32
        ),
        lax.all_gather(summed[7].astype(jnp.bfloat16), "ctx", axis=1, tiled=True).astype(
            jnp.float32
        ),
        lax.all_gather(summed[8].astype(jnp.bfloat16), "ctx", axis=2, tiled=True).astype(
            jnp.float32
        ),
    )
    layer_out = jnp.stack(outputs, axis=0)[:, None]
    d_hidden = jnp.stack(input_grads, axis=0)[:, None]
    return (
        layer_out,
        d_hidden,
        shares[0],
        shares[1],
        shares[2],
        shares[3],
        shares[4],
        shares[5],
        shares[6],
        shares[7],
        shares[8],
    )


def dot(left, right, left_dim=1, right_dim=0):
    return lax.dot_general(
        left, right, (((left_dim,), (right_dim,)), ((), ())), preferred_element_type=jnp.float32
    )


def vmem_params(count=1):
    return pltpu.CompilerParams(
        dimension_semantics=("arbitrary",) * count, vmem_limit_bytes=60 * 1024 * 1024
    )


def attend_kernel(seen_ref, query_ref, kv0, kv1, kv2, kv3, out_ref, probs_ref):
    blocks = (kv0, kv1, kv2, kv3)
    micro = seen_ref.shape[0]
    rows = query_ref.shape[0] // micro
    kv_heads = kv0.shape[1] // (2 * HEAD_DIM)
    group = query_ref.shape[1] // HEAD_DIM // kv_heads
    shape = (group * rows, rows)
    causal = (
        lax.broadcasted_iota(jnp.int32, shape, 1)
        <= lax.broadcasted_iota(jnp.int32, shape, 0) % rows
    )
    for m in range(micro):
        span = pl.ds(m * rows, rows)
        whole = query_ref[span, :]
        pieces = []
        for g in range(kv_heads):
            lanes = slice(g * HEAD_DIM, (g + 1) * HEAD_DIM)
            query = jnp.concatenate(
                [
                    whole[:, (g * group + h) * HEAD_DIM : (g * group + h + 1) * HEAD_DIM]
                    for h in range(group)
                ],
                axis=0,
            )
            parts = []
            for r in range(4):
                part = dot(query, blocks[r][span, :][:, lanes], 1, 1) * SCORE_SCALE
                if r == 0:
                    part = jnp.where(causal, part, -1e30)
                else:
                    part = jnp.where(seen_ref[m, r] > 0, part, -1e30)
                parts.append(part)
            scores = jnp.concatenate(parts, axis=1)
            powers = jnp.exp(scores - jnp.max(scores, axis=1, keepdims=True))
            probs = powers / jnp.sum(powers, axis=1, keepdims=True)
            probs_ref[m * kv_heads + g] = probs
            low = probs.astype(jnp.bfloat16)
            values = jnp.concatenate(
                [
                    blocks[r][span, :][:, (kv_heads + g) * HEAD_DIM : (kv_heads + g + 1) * HEAD_DIM]
                    for r in range(4)
                ],
                axis=0,
            )
            mixed = dot(low, values)
            pieces += [mixed[h * rows : (h + 1) * rows] for h in range(group)]
        out_ref[span, :] = jnp.concatenate(pieces, axis=1).astype(jnp.bfloat16)


def attend_back_kernel(
    query_ref, grad_ref, kv0, kv1, kv2, kv3, probs_ref, query_grad_ref, kv_grad_ref
):
    blocks = (kv0, kv1, kv2, kv3)
    kv_heads = kv0.shape[1] // (2 * HEAD_DIM)
    micro = probs_ref.shape[0] // kv_heads
    rows = query_ref.shape[0] // micro
    group = query_ref.shape[1] // HEAD_DIM // kv_heads
    for m in range(micro):
        span = pl.ds(m * rows, rows)
        whole = query_ref[span, :]
        whole_grad = grad_ref[span, :]
        pieces = []
        key_grads = []
        value_grads = []
        for g in range(kv_heads):

            def heads(source):
                return jnp.concatenate(
                    [
                        source[:, (g * group + h) * HEAD_DIM : (g * group + h + 1) * HEAD_DIM]
                        for h in range(group)
                    ],
                    axis=0,
                )

            query = heads(whole)
            head_grad = heads(whole_grad)
            keys = jnp.concatenate(
                [blocks[r][span, :][:, g * HEAD_DIM : (g + 1) * HEAD_DIM] for r in range(4)], axis=0
            )
            values = jnp.concatenate(
                [
                    blocks[r][span, :][:, (kv_heads + g) * HEAD_DIM : (kv_heads + g + 1) * HEAD_DIM]
                    for r in range(4)
                ],
                axis=0,
            )
            probs = probs_ref[m * kv_heads + g]
            prob_grad = dot(head_grad, values, 1, 1)
            inner = jnp.sum(probs * prob_grad, axis=1, keepdims=True)
            score_grad = (SCORE_SCALE * probs * (prob_grad - inner)).astype(jnp.bfloat16)
            value_grads.append(dot(probs.astype(jnp.bfloat16), head_grad, 0, 0))
            key_grads.append(dot(score_grad, query, 0, 0))
            query_grad = dot(score_grad, keys)
            pieces += [query_grad[h * rows : (h + 1) * rows] for h in range(group)]
        query_grad_ref[span, :] = jnp.concatenate(pieces, axis=1)
        joined = jnp.concatenate(key_grads + value_grads, axis=1).astype(jnp.bfloat16)
        for r in range(4):
            kv_grad_ref[r, span, :] = joined[r * rows : (r + 1) * rows]


def expert_kernel(
    place_ref,
    near_ref,
    far_ref,
    near_out_ref,
    far_out_ref,
    rank_ref,
    gate_ref,
    gate_up_ref,
    down_ref,
    other0,
    other1,
    other2,
    other3,
    *rest,
):
    if len(rest) == 12:
        held_out, held_grad = rest[:2]
        rest = rest[2:]
    else:
        held_out = held_grad = None
    out_ref, grad_ref, slots_ref, gate_grad_ref, rows_buf, grads_buf, moe_buf, back_buf, hot_buf, gate_buf = rest
    others = (other0, other1, other2, other3)
    half = down_ref.shape[-1]
    width = down_ref.shape[-2]
    quarter = [place_ref[1] ^ r for r in range(4)]
    iota = lax.broadcasted_iota(jnp.int32, (CAP, 128), 0)

    @pl.when(pl.program_id(0) == 0)
    def _():
        if held_out is None:
            out_ref[...] = jnp.zeros_like(out_ref)
            grad_ref[...] = jnp.zeros_like(grad_ref)
        else:
            out_ref[...] = held_out[...]
            grad_ref[...] = held_grad[...]

    for b in range(4):
        hot = jnp.concatenate(
            [
                jnp.where(iota == rank_ref[quarter[r], 0, pl.ds(b, 1), :], 1.0, 0.0)
                for r in range(4)
            ],
            axis=0,
        )
        gates = jnp.concatenate(
            [
                jnp.broadcast_to(gate_ref[quarter[r], 0, pl.ds(b, 1), :], (CAP, 128))
                for r in range(4)
            ],
            axis=0,
        )
        gate_buf[b] = jnp.broadcast_to(jnp.sum(hot * gates, axis=1, keepdims=True), (4 * CAP, 128))
        low = hot.astype(jnp.bfloat16)
        hot_buf[b] = low
        span = pl.ds((b % 2) * 128, 128)
        for part in range(2):
            keep = pl.ds(part * half, half)
            if b < 2:
                rows, grads = near_ref[span, keep], near_out_ref[span, keep]
            else:
                swap = pl.ds((1 - part) * half, half)
                rows, grads = far_ref[span, swap], far_out_ref[span, swap]
            rows_buf[b, :, keep] = dot(low, rows).astype(jnp.bfloat16)
            grads_buf[b, :, keep] = dot(low, grads).astype(jnp.bfloat16)
    for r in range(4):
        q = quarter[r]
        slot = slice(r * CAP, (r + 1) * CAP)
        rows = jnp.concatenate([rows_buf[b, slot, :] for b in range(4)], axis=0)
        grads = jnp.concatenate([grads_buf[b, slot, :] for b in range(4)], axis=0)
        gate = jnp.concatenate([gate_buf[b, slot, :] for b in range(4)], axis=0)
        near_w = jnp.concatenate([gate_up_ref[q, 0, 0], gate_up_ref[q, 0, 1]], axis=1)
        far_w = jnp.concatenate([others[r][0, :half, :], others[r][0, half : 2 * half, :]], axis=1)
        near_down = down_ref[0, q, 0]
        far_down = jnp.concatenate(
            [
                others[r][0, 2 * half + j * width : 2 * half + (j + 1) * width, :]
                for j in range(half // 128)
            ],
            axis=1,
        )
        gate_up = dot(rows[:, :half], near_w) + dot(rows[:, half:], far_w)
        gate_pre = gate_up[:, :width]
        up_pre = gate_up[:, width:]
        sigmoid = 1.0 / (1.0 + jnp.exp(-gate_pre))
        activ = (gate_pre * sigmoid * up_pre).astype(jnp.bfloat16)
        pulled = RESIDUAL_SCALE * (
            dot(grads[:, :half], near_down, 1, 1) + dot(grads[:, half:], far_down, 1, 1)
        )
        activ_wide = activ.astype(jnp.float32)
        gate_grad = jnp.sum(activ_wide * pulled, axis=1, keepdims=True)
        activ_grad = pulled * gate
        gate_pre_grad = activ_grad * up_pre * sigmoid * (1.0 + gate_pre * (1.0 - sigmoid))
        up_pre_grad = activ_grad * gate_pre * sigmoid
        both = jnp.concatenate([gate_pre_grad, up_pre_grad], axis=1).astype(jnp.bfloat16)
        slots_ref[q, 0, :, : 2 * width] = both
        slots_ref[q, 0, :, 2 * width :] = (activ_wide * gate * RESIDUAL_SCALE).astype(jnp.bfloat16)
        for part, (wide, low_w) in enumerate(((near_w, near_down), (far_w, far_down))):
            keep = pl.ds(part * half, half)
            made = dot(activ, low_w)
            back = dot(both, wide, 1, 1)
            for b in range(4):
                piece = slice(b * CAP, (b + 1) * CAP)
                scale = jnp.concatenate([gate[piece]] * (half // 128), axis=1)
                moe_buf[b, slot, keep] = (made[piece] * scale).astype(jnp.bfloat16)
                back_buf[b, slot, keep] = back[piece].astype(jnp.bfloat16)
        for b in range(4):
            hot = hot_buf[b, slot, :].astype(jnp.float32)
            gate_grad_ref[q, 0, pl.ds(b, 1), :] = jnp.sum(
                hot * gate_grad[b * CAP : (b + 1) * CAP], axis=0, keepdims=True
            )
    for b in range(4):
        span = pl.ds(b * 128, 128)
        out_ref[span, :] += dot(hot_buf[b], moe_buf[b], 0, 0)
        grad_ref[span, :] += dot(hot_buf[b], back_buf[b], 0, 0)


def run_experts(place, near, far, near_out, far_out, rank, gate, gate_up, down, others, held, first):
    steps, packed, lanes = others[0].shape
    quarters, each, sides, half, width = gate_up.shape
    tokens = 2 * near_out.shape[0]
    full = 2 * half

    def fixed(array):
        return pl.BlockSpec(array.shape, lambda j, sp: (0,) * array.ndim)

    table = pl.BlockSpec((quarters, 1, 4, 128), lambda j, sp: (0, first + j, 0, 0))
    in_specs = [
        fixed(near),
        fixed(far),
        fixed(near_out),
        fixed(far_out),
        table,
        table,
        pl.BlockSpec((quarters, 1, sides, half, width), lambda j, sp: (0, first + j, 0, 0, 0)),
        pl.BlockSpec((1, quarters, 1, width, half), lambda j, sp: (sp[0], 0, first + j, 0, 0)),
    ] + [pl.BlockSpec((1, packed, lanes), lambda j, sp: (j, 0, 0))] * 4
    operands = [place, near, far, near_out, far_out, rank, gate, gate_up, down, *others]
    aliases = {}
    total = jax.ShapeDtypeStruct((tokens, full), jnp.float32)
    if held is not None:
        in_specs += [fixed(held[0]), fixed(held[1])]
        aliases = {len(operands): 0, len(operands) + 1: 1}
        operands += list(held)
    slots = jax.ShapeDtypeStruct((quarters, steps, 4 * CAP, 3 * width), jnp.bfloat16)
    gate_grads = jax.ShapeDtypeStruct((quarters, steps, 4, 128), jnp.float32)
    return pl.pallas_call(
        expert_kernel,
        out_shape=(total, total, slots, gate_grads),
        grid_spec=pltpu.PrefetchScalarGridSpec(
            num_scalar_prefetch=1,
            grid=(steps,),
            in_specs=in_specs,
            out_specs=(
                pl.BlockSpec(total.shape, lambda j, sp: (0, 0)),
                pl.BlockSpec(total.shape, lambda j, sp: (0, 0)),
                pl.BlockSpec((quarters, 1, 4 * CAP, 3 * width), lambda j, sp: (0, j, 0, 0)),
                pl.BlockSpec((quarters, 1, 4, 128), lambda j, sp: (0, j, 0, 0)),
            ),
            scratch_shapes=[pltpu.VMEM((4, 4 * CAP, full), jnp.bfloat16)] * 4
            + [
                pltpu.VMEM((4, 4 * CAP, 128), jnp.bfloat16),
                pltpu.VMEM((4, 4 * CAP, 128), jnp.float32),
            ],
        ),
        input_output_aliases=aliases,
        compiler_params=vmem_params(),
        name="experts",
    )(*operands)


def weight_grad_kernel(place_ref, *refs):
    rows_in, grads_in, slots_in = refs[:4], refs[4:8], refs[8:12]
    rank_ref = refs[12]
    gate_up_ref, down_ref, rows_buf, grads_buf = refs[-4:]
    half = down_ref.shape[-1]
    width = down_ref.shape[-2]
    side = pl.program_id(1)
    iota = lax.broadcasted_iota(jnp.int32, (CAP, 128), 0)
    for k in range(4):
        for b in range(4):
            hot = jnp.concatenate(
                [
                    jnp.where(iota == rank_ref[0, q, 0, pl.ds(4 * k + b, 1), :], 1.0, 0.0)
                    for q in range(4)
                ],
                axis=0,
            ).astype(jnp.bfloat16)
            span = pl.ds(b * 128, 128)
            spot = 4 * k + (b ^ (2 * side))
            rows_buf[spot] = dot(hot, rows_in[k][span, :]).astype(jnp.bfloat16)
            grads_buf[spot] = dot(hot, grads_in[k][span, :]).astype(jnp.bfloat16)
    for q in range(4):
        slot = slice(q * CAP, (q + 1) * CAP)
        rows = jnp.concatenate([rows_buf[n, slot, :] for n in range(16)], axis=0)
        grads = jnp.concatenate([grads_buf[n, slot, :] for n in range(16)], axis=0)
        taken = jnp.concatenate([slots_in[k][0, q, 0] for k in range(4)], axis=0)
        made = dot(rows, taken[:, : 2 * width], 0, 0)
        gate_up_ref[0, q, 0, pl.ds(0, half, stride=2), :] = made[:, :width]
        gate_up_ref[0, q, 0, pl.ds(1, half, stride=2), :] = made[:, width:]
        down_ref[0, q, 0] = dot(taken[:, 2 * width :], grads, 0, 0)


def run_weight_grads(place, rows, grads, slots, rank, held, first, each):
    sides, quarters, steps, slot_count, lanes = slots[0].shape
    width = lanes // 3
    tokens = rows[0].shape[0]
    half = rank_half(rows, grads)
    in_specs = (
        [pl.BlockSpec((tokens, half), lambda j, a, sp: (0, 0))] * 8
        + [
            pl.BlockSpec(
                (1, quarters, 1, slot_count, lanes), lambda j, a, sp: (a, 0, j, 0, 0)
            )
        ]
        * 4
        + [pl.BlockSpec((1, quarters, 1, 16, 128), lambda j, a, sp: (a, 0, first + j, 0, 0))]
    )
    operands = [place, *rows, *grads, *slots, rank]
    aliases = {}
    if held is not None:
        in_specs += [pl.BlockSpec(memory_space=pl.ANY)] * 2
        aliases = {len(operands): 0, len(operands) + 1: 1}
        operands += list(held)
    return pl.pallas_call(
        weight_grad_kernel,
        out_shape=(
            jax.ShapeDtypeStruct((sides, quarters, each, 2 * half, width), jnp.float32),
            jax.ShapeDtypeStruct((sides, quarters, each, width, half), jnp.float32),
        ),
        grid_spec=pltpu.PrefetchScalarGridSpec(
            num_scalar_prefetch=1,
            grid=(steps, sides),
            in_specs=in_specs,
            out_specs=(
                pl.BlockSpec(
                    (1, quarters, 1, 2 * half, width),
                    lambda j, a, sp: (sp[0] ^ a, 0, first + j, 0, 0),
                ),
                pl.BlockSpec(
                    (1, quarters, 1, width, half),
                    lambda j, a, sp: (sp[0] ^ a, 0, first + j, 0, 0),
                ),
            ),
            scratch_shapes=[pltpu.VMEM((16, 4 * CAP, half), jnp.bfloat16)] * 2,
        ),
        input_output_aliases=aliases,
        compiler_params=vmem_params(2),
        name="weight_grads",
    )(*operands)


def rank_half(rows, grads):
    return min(array.shape[1] for array in (*rows, *grads))


def swap_halves(values):
    half = values.shape[-1] // 2
    return jnp.concatenate([values[..., half:], values[..., :half]], axis=-1)


def turn_heads(values):
    half_dim = HEAD_DIM // 2
    lane = lax.broadcasted_iota(jnp.int32, values.shape, 1) % HEAD_DIM
    return jnp.where(
        lane < half_dim,
        -jnp.roll(values, -half_dim, axis=1),
        jnp.roll(values, half_dim, axis=1),
    )


def fast_body(
    hidden_in,
    parents,
    routes,
    attn_gain,
    w_query,
    key_projection,
    value_projection,
    w_out,
    moe_gain,
    w_router,
    w_gate_up,
    w_down,
    d_out,
):
    low, wide = jnp.bfloat16, jnp.float32
    x_pos = lax.axis_index("fsdp")
    c_pos = lax.axis_index("ctx")
    z_pos = lax.axis_index("tp")
    tp_size = lax.axis_size("tp")
    micro, _, rows, model = hidden_in.shape
    half = model // 2
    tokens = micro * rows
    experts = w_gate_up.shape[0]
    mine = experts // 2
    each = mine // 4
    width = w_down.shape[1]
    q_cols = w_query.shape[1]
    k_cols = key_projection.shape[1]
    chunks = ((0, 2), (2, 2), (4, 1))

    def across(value):
        return lax.ppermute(value, "fsdp", [(0, 1), (1, 0)])

    def beside(value):
        return lax.ppermute(value, "ctx", [(i, i ^ 1) for i in range(4)])

    def along(value):
        return lax.ppermute(value, "ctx", [(i, i ^ 2) for i in range(4)])

    def from_tp(value, step):
        return lax.ppermute(
            value, "tp", [((i + step) % tp_size, i) for i in range(tp_size)]
        )

    def all_ctx(value):
        nearby = beside(value)
        distant = along(value)
        return [value, nearby, distant, beside(distant)]

    def own_first(value):
        return jnp.where(x_pos == 0, value, swap_halves(value))

    def ctx_join(first, second, axis):
        return jnp.where(
            c_pos % 2 == 0,
            jnp.concatenate([first, second], axis=axis),
            jnp.concatenate([second, first], axis=axis),
        )

    def sum_tp(value):
        part = value.shape[0] // tp_size

        def piece(step):
            return lax.dynamic_slice_in_dim(value, ((z_pos + step) % tp_size) * part, part, 0)

        total = piece(0).astype(wide)
        for step in range(1, tp_size):
            total = total + from_tp(piece(tp_size - step), step).astype(wide)
        total = total.astype(low)
        found = [total] + [from_tp(total, step) for step in range(1, tp_size)]
        return lax.dynamic_slice_in_dim(
            jnp.concatenate(found + found, axis=0), ((tp_size - z_pos) % tp_size) * part, tokens, 0
        )

    small = jnp.concatenate(
        [
            w_query,
            key_projection,
            value_projection,
            jnp.pad(
                jnp.concatenate([w_router, attn_gain[:, None], moe_gain[:, None]], axis=1),
                ((0, 0), (0, 128 - experts - 2)),
            ),
        ],
        axis=1,
    )
    core = c_pos % 2
    sent = across(lax.dynamic_slice_in_dim(small, core * (half // 2), half // 2, 0))
    small_far = ctx_join(sent, beside(sent), 0)
    qkv_cols = q_cols + 2 * k_cols
    qkv_full = jnp.concatenate([small[:, :qkv_cols], small_far[:, :qkv_cols]], axis=0)
    rest_full = jnp.concatenate([small[:, qkv_cols:], small_far[:, qkv_cols:]], axis=0)
    gain_one = rest_full[:, experts].astype(wide)
    gain_two = rest_full[:, experts + 1].astype(wide)
    router = jnp.where(
        x_pos == 0,
        rest_full[:, :experts],
        jnp.concatenate([rest_full[:, mine:experts], rest_full[:, :mine]], axis=1),
    )

    routes_low = jnp.pad(
        routes.reshape(tokens, -1).astype(low), ((0, 0), (0, 128 - routes.shape[-1]))
    )
    near_out = jnp.concatenate([own_first(d_out.reshape(tokens, model)), routes_low], axis=1)
    far_out = across(near_out)

    gate_up_mine = (
        lax.dynamic_slice_in_dim(w_gate_up, x_pos * mine, mine, 0)
        .transpose(0, 2, 1, 3)
        .reshape(4, each, 2, half, width)
    )
    away = (1 - x_pos) * mine + c_pos * each
    far_weights = []
    for first, count in chunks:
        gate_up_sent = (
            lax.dynamic_slice_in_dim(w_gate_up, away + first, count, 0)
            .transpose(0, 2, 1, 3)
            .reshape(count, 2 * half, width)
        )
        down_sent = (
            lax.dynamic_slice_in_dim(w_down, away + first, count, 0)
            .reshape(count, width, half // 128, 128)
            .transpose(0, 2, 1, 3)
            .reshape(count, half, 128)
        )
        far_weights.append(all_ctx(across(jnp.concatenate([gate_up_sent, down_sent], axis=1))))
    down_all = w_down.reshape(2, 4, each, width, half)

    heads_sent = lax.dynamic_slice_in_dim(w_out, core * (q_cols // 2), q_cols // 2, 0)
    heads_both = jnp.concatenate([heads_sent, across(heads_sent)], axis=1)
    heads_rest = jnp.stack([from_tp(heads_both, step) for step in range(1, tp_size)], axis=0)
    heads_rest = jnp.concatenate([heads_both[None], heads_rest], axis=0)
    out_full = ctx_join(heads_rest, beside(heads_rest), 1)

    seg_ids = jnp.arange(4, dtype=jnp.int32)
    seen_rows = []
    angle_rows = []
    half_dim = HEAD_DIM // 2
    inverse = ROPE_BASE ** (-jnp.arange(half_dim, dtype=wide) * 2.0 / HEAD_DIM)
    for m in range(micro):
        current = c_pos
        reach = seg_ids == current
        for _ in range(3):
            current = jnp.sum(jnp.where(seg_ids == current, parents[m, 0], 0))
            reach = reach | (seg_ids == current)
        reach = reach.astype(jnp.int32)
        depth = jnp.sum(reach) - 1
        seen_rows.append(
            jnp.stack([jnp.sum(jnp.where(seg_ids == (c_pos ^ r), reach, 0)) for r in range(4)])
        )
        places = (depth * rows + jnp.arange(rows, dtype=jnp.int32)).astype(wide)
        angle_rows.append(places[:, None] * inverse[None, :])
    seen = jnp.stack(seen_rows)
    angles = jnp.concatenate(angle_rows, axis=0)
    turns = (q_cols + k_cols) // half_dim
    cosines = jnp.tile(jnp.cos(angles), (1, turns))
    sines = jnp.tile(jnp.sin(angles), (1, turns))

    inputs = own_first(hidden_in.reshape(tokens, model)).astype(wide)
    scale_one = norm_scale(inputs)
    unit_one = inputs * scale_one
    first_normed = (unit_one * gain_one).astype(low)
    unrotated = dot(first_normed, qkv_full)
    turned_part = unrotated[:, : q_cols + k_cols]
    rotated = (turned_part * cosines + turn_heads(turned_part) * sines).astype(low)
    query = rotated[:, :q_cols]
    key_value = jnp.concatenate(
        [rotated[:, q_cols:], unrotated[:, q_cols + k_cols :].astype(low)], axis=1
    )
    blocks = all_ctx(key_value)
    smem = pl.BlockSpec(memory_space=pltpu.SMEM)
    vmem = pl.BlockSpec(memory_space=pltpu.VMEM)
    kv_heads = k_cols // HEAD_DIM
    group = q_cols // k_cols
    head_low, probs = pl.pallas_call(
        attend_kernel,
        out_shape=(
            jax.ShapeDtypeStruct((tokens, q_cols), low),
            jax.ShapeDtypeStruct((micro * kv_heads, group * rows, 4 * rows), wide),
        ),
        in_specs=[smem] + [vmem] * 5,
        out_specs=(vmem, vmem),
        compiler_params=pltpu.CompilerParams(vmem_limit_bytes=60 * 1024 * 1024),
        name="attend",
    )(seen, query, *blocks)
    heads = [head_low] + [from_tp(head_low, step) for step in range(1, tp_size)]
    attended = dot(jnp.concatenate(heads, axis=1), out_full.reshape(tp_size * q_cols, model))
    mixed = inputs + RESIDUAL_SCALE * attended
    scale_two = norm_scale(mixed)
    unit_two = mixed * scale_two
    normed_two = (unit_two * gain_two).astype(low)

    expert_ids = (jnp.arange(experts, dtype=jnp.int32) + x_pos * mine) % experts
    flat_routes = routes.reshape(tokens, -1)
    named = jnp.any(flat_routes[:, :, None] == expert_ids[None, None, :], axis=1)
    logits = jnp.where(named, dot(normed_two, router), -1e30)
    powers = jnp.where(named, jnp.exp(logits - jnp.max(logits, axis=1, keepdims=True)), 0.0)
    gates = powers / jnp.sum(powers, axis=1, keepdims=True)

    gates_sent = gates[:, mine:]
    gates_high = gates_sent.astype(low)
    gates_rest = (gates_sent - gates_high.astype(wide)).astype(low)
    near = jnp.concatenate(
        [
            normed_two,
            jnp.pad(
                jnp.concatenate([gates_high, gates_rest], axis=1), ((0, 0), (0, 128 - 2 * mine))
            ),
        ],
        axis=1,
    )
    far = across(near)
    far_gates = far[:, model : model + mine].astype(wide) + far[
        :, model + mine : model + 2 * mine
    ].astype(wide)
    upper = (
        lax.broadcasted_iota(jnp.int32, (rows, rows), 0)
        < lax.broadcasted_iota(jnp.int32, (rows, rows), 1)
    ).astype(low)

    def ranks(route_table, ids):
        flat = route_table.astype(jnp.int32).T
        hit = jnp.zeros((ids.shape[0], flat.shape[1]), jnp.bool_)
        for k in range(flat.shape[0]):
            hit = hit | (flat[k][None, :] == ids[:, None])
        hot = hit.astype(low).reshape(-1, rows)
        before = dot(hot, upper)
        found = jnp.where(hot > 0, before, -1.0).astype(jnp.int32)
        return found.reshape(ids.shape[0], -1, rows)

    top = routes.shape[-1]
    pair_routes = jnp.concatenate([routes_low, far_out[:, model:]], axis=0)[:, :top]
    rank_pair = ranks(pair_routes, expert_ids[:mine]).reshape(4, each, 4, rows)
    gate_pair = (
        jnp.concatenate([gates[:, :mine], far_gates], axis=0).T.reshape(4, each, 4, rows)
    )
    place = jnp.stack([x_pos, c_pos]).astype(jnp.int32)

    held = None
    slots = []
    gate_grad_parts = []
    for (first, count), others in zip(chunks, far_weights):
        moe_all, back_all, slot_part, gate_part = run_experts(
            place,
            near,
            far,
            near_out,
            far_out,
            rank_pair,
            gate_pair,
            gate_up_mine,
            down_all,
            others,
            held,
            first,
        )
        held = (moe_all, back_all)
        slots.append(slot_part)
        gate_grad_parts.append(gate_part)
    gate_grad_all = jnp.concatenate(gate_grad_parts, axis=1).reshape(mine, 2 * tokens).T

    back_sent = jnp.concatenate(
        [
            back_all[tokens:].astype(low),
            jnp.pad(gate_grad_all[tokens:].astype(low), ((0, 0), (0, 128 - mine))),
        ],
        axis=1,
    )
    back_got = across(back_sent)
    back_sum = (back_all[:tokens] + swap_halves(back_got[:, :model]).astype(wide)).astype(low)
    gathered = sum_tp(
        jnp.concatenate(
            [
                back_sum,
                jnp.pad(
                    jnp.concatenate(
                        [gate_grad_all[:tokens].astype(low), back_got[:, model : model + mine]],
                        axis=1,
                    ),
                    ((0, 0), (0, 128 - experts)),
                ),
            ],
            axis=1,
        )
    )
    gate_grads = gathered[:, model : model + experts].astype(wide)
    logit_grad = (gates * (gate_grads - jnp.sum(gates * gate_grads, axis=1, keepdims=True))).astype(
        low
    )
    normed_two_grad = gathered[:, :model].astype(wide) + dot(logit_grad, router, 1, 1)
    grad_out = near_out[:, :model].astype(wide)
    gain_two_part = jnp.sum(normed_two_grad * unit_two, axis=0)
    scaled_two = normed_two_grad * gain_two
    mixed_grad = grad_out + scale_two * (
        scaled_two - unit_two * jnp.mean(scaled_two * unit_two, axis=-1, keepdims=True)
    )
    attn_grad = (RESIDUAL_SCALE * mixed_grad).astype(low)

    moe_got = across(moe_all[tokens:].astype(low))
    moe_part = (moe_all[:tokens] + swap_halves(moe_got).astype(wide)).astype(low)
    moe_sum = lax.psum(moe_part, "tp").astype(wide)
    layer_out = own_first(mixed + RESIDUAL_SCALE * moe_sum)

    head_grad = dot(attn_grad, out_full[0], 1, 1).astype(low)
    query_grad, kv_grads = pl.pallas_call(
        attend_back_kernel,
        out_shape=(
            jax.ShapeDtypeStruct((tokens, q_cols), wide),
            jax.ShapeDtypeStruct((4, tokens, 2 * k_cols), low),
        ),
        in_specs=[vmem] * 7,
        out_specs=(vmem, vmem),
        compiler_params=pltpu.CompilerParams(vmem_limit_bytes=60 * 1024 * 1024),
        name="attend_back",
    )(query, head_grad, *blocks, probs)
    near_pair = beside(jnp.stack([kv_grads[1], kv_grads[3]]))
    far_part = (kv_grads[2].astype(wide) + near_pair[1].astype(wide)).astype(low)
    kv_grad = (
        kv_grads[0].astype(wide) + near_pair[0].astype(wide) + along(far_part).astype(wide)
    )
    turned_grad = jnp.concatenate([query_grad, kv_grad[:, :k_cols]], axis=1)
    qkv_grad = jnp.concatenate(
        [turned_grad * cosines - turn_heads(turned_grad) * sines, kv_grad[:, k_cols:]], axis=1
    ).astype(low)
    normed_one_grad = sum_tp(dot(qkv_grad, qkv_full, 1, 1).astype(low)).astype(wide)
    gain_one_part = jnp.sum(normed_one_grad * unit_one, axis=0)
    scaled_one = normed_one_grad * gain_one
    d_hidden = own_first(
        mixed_grad
        + scale_one
        * (scaled_one - unit_one * jnp.mean(scaled_one * unit_one, axis=-1, keepdims=True))
    )

    first_far = across(first_normed[:, half:])
    early = all_ctx(
        jnp.concatenate(
            [
                jnp.concatenate([near_out[:, :half], first_normed[:, :half], routes_low], axis=1),
                jnp.concatenate(
                    [far_out[:, half:model], first_far, far_out[:, model:]], axis=1
                ),
            ],
            axis=0,
        )
    )
    rows_two = all_ctx(jnp.concatenate([normed_two[:, :half], far[:, half:model]], axis=0))
    heads_all = all_ctx(jnp.concatenate([head_low, across(head_low)], axis=0))
    logit_pad = jnp.pad(logit_grad, ((0, 0), (0, 128 - experts)))
    late_far = across(jnp.concatenate([attn_grad[:, half:], logit_pad], axis=1))
    late_far = jnp.concatenate(
        [
            late_far[:, :half],
            late_far[:, half + mine : half + experts],
            late_far[:, half : half + mine],
            late_far[:, half + experts :],
        ],
        axis=1,
    )
    late = all_ctx(
        jnp.concatenate(
            [jnp.concatenate([attn_grad[:, :half], logit_pad], axis=1), late_far], axis=0
        )
    )
    qkv_all = all_ctx(jnp.concatenate([qkv_grad, across(qkv_grad)], axis=0))

    all_routes = jnp.concatenate([part[:, 2 * half : 2 * half + top] for part in early], axis=0)
    rank_all = ranks(all_routes, expert_ids).reshape(2, 4, each, 16, rows)
    grads = None
    for (first, count), part in zip(chunks, slots):
        pair = all_ctx(jnp.stack([part, across(part)]))
        grads = run_weight_grads(place, rows_two, early, pair, rank_all, grads, first, each)
    d_gate_up = grads[0].reshape(experts, half, 2, width)
    d_down = grads[1].reshape(experts, width, half)

    def over_tokens(left, right):
        return sum(dot(a, b, 0, 0) for a, b in zip(left, right))

    d_qkv = over_tokens([part[:, half : 2 * half] for part in early], qkv_all)
    d_w_out = over_tokens(heads_all, [part[:, :half] for part in late])
    d_router = over_tokens(rows_two, [part[:, half : half + experts] for part in late])
    d_router = jnp.where(
        x_pos == 0, d_router, jnp.concatenate([d_router[:, mine:], d_router[:, :mine]], axis=1)
    )

    def sum_gain(part):
        part = part + beside(part)
        part = part + along(part)
        return part[:half] + across(part[half:])

    return (
        layer_out.reshape(micro, 1, rows, model),
        d_hidden.reshape(micro, 1, rows, model),
        sum_gain(gain_one_part),
        d_qkv[:, :q_cols],
        d_qkv[:, q_cols : q_cols + k_cols],
        d_qkv[:, q_cols + k_cols :],
        d_w_out,
        sum_gain(gain_two_part),
        d_router,
        d_gate_up,
        d_down,
    )


def solution(mesh):
    placed = (
        P(None, "fsdp", "ctx", None),
        P(None, "fsdp", None),
        P(None, "fsdp", "ctx", None),
        P("fsdp"),
        P("fsdp", "tp"),
        P("fsdp", "tp"),
        P("fsdp", "tp"),
        P("tp", "fsdp"),
        P("fsdp"),
        P("fsdp", None),
        P(None, "fsdp", None, "tp"),
        P(None, "tp", "fsdp"),
        P(None, "fsdp", "ctx", None),
    )
    fits = mesh.shape["fsdp"] == 2 and mesh.shape["ctx"] == 4
    return jax.shard_map(
        fast_body if fits else body,
        mesh=mesh,
        in_specs=placed,
        out_specs=(
            P(None, "fsdp", "ctx", None),
            P(None, "fsdp", "ctx", None),
            P("fsdp"),
            P("fsdp", "tp"),
            P("fsdp", "tp"),
            P("fsdp", "tp"),
            P("tp", "fsdp"),
            P("fsdp"),
            P("fsdp", None),
            P(None, "fsdp", None, "tp"),
            P(None, "tp", "fsdp"),
        ),
        check_vma=False,
    )
```

```python
import jax
import jax.numpy as jnp
from jax import lax
from jax.experimental import pallas as pl
from jax.experimental.pallas import tpu as pltpu
from jax.sharding import PartitionSpec as P

HEAD_DIM = 64
CAP = 32


EPSILON = 1e-06
RESIDUAL_SCALE = 0.22
SCORE_SCALE = 1.0 / 64.0
ROPE_BASE = 10000.0
TOP_PRECISION = lax.Precision.HIGHEST


def tree_tables(parent_row, tree_len):
    seg_total = parent_row.shape[0]
    seg_len = tree_len // seg_total
    seg_ids = jnp.arange(seg_total, dtype=jnp.int32)
    parent_links = (parent_row[:, None] == seg_ids[None, :]).astype(jnp.float32)
    reach_table = jnp.maximum(parent_links, jnp.eye(seg_total, dtype=jnp.float32))
    for squaring in range(max(seg_total - 1, 1).bit_length()):
        reach_table = jnp.minimum(jnp.dot(reach_table, reach_table, precision=TOP_PRECISION), 1.0)
    seg_depth = jnp.sum(reach_table, axis=1) - 1.0
    token_ids = jnp.arange(tree_len, dtype=jnp.int32)
    tok_owner = ((token_ids // seg_len)[:, None] == seg_ids[None, :]).astype(jnp.float32)
    tok_offset = (token_ids % seg_len).astype(jnp.float32)
    places = jnp.dot(tok_owner, seg_depth, precision=TOP_PRECISION) * seg_len + tok_offset
    return (places, jnp.dot(tok_owner, reach_table, precision=TOP_PRECISION), tok_owner)


def rope_tables(places):
    half_dim = HEAD_DIM // 2
    inverse = ROPE_BASE ** (-jnp.arange(half_dim, dtype=jnp.float32) * 2.0 / HEAD_DIM)
    angles = places[:, None] * inverse[None, :]
    cosine_table = jnp.concatenate([jnp.cos(angles), jnp.cos(angles)], axis=1)
    sine_values = jnp.concatenate([jnp.sin(angles), jnp.sin(angles)], axis=1)
    return (cosine_table, sine_values)


def apply_rotary(values, cosine_table, sine_values):
    half_dim = values.shape[-1] // 2
    turned = jnp.concatenate([-values[..., half_dim:], values[..., :half_dim]], axis=-1)
    return values * cosine_table[:, None, :] + turned * sine_values[:, None, :]


def norm_scale(values):
    return lax.rsqrt(jnp.mean(values * values, axis=-1, keepdims=True) + EPSILON)


def add_tuples(first_tuple, second_tuple):
    return tuple(
        (left_part + right_part for left_part, right_part in zip(first_tuple, second_tuple))
    )


def expert_work(rows, row_grads, gate_up_w, down_w, down_form):
    gate_up = jnp.einsum("ecd,edsf->ecsf", rows, gate_up_w, preferred_element_type=jnp.float32)
    gate_pre = gate_up[:, :, 0]
    up_pre = gate_up[:, :, 1]
    sigmoid = jax.nn.sigmoid(gate_pre)
    activ_low = (gate_pre * sigmoid * up_pre).astype(jnp.bfloat16)
    expert_out = jnp.einsum(
        "ecf," + down_form + "->ecd", activ_low, down_w, preferred_element_type=jnp.float32
    )
    activ_grad = jnp.einsum(
        "ecd," + down_form + "->ecf", row_grads, down_w, preferred_element_type=jnp.float32
    )
    gate_grad = activ_grad * up_pre * sigmoid * (1.0 + gate_pre * (1.0 - sigmoid))
    up_grad = activ_grad * gate_pre * sigmoid
    gate_up_grad = jnp.stack([gate_grad, up_grad], axis=2).astype(jnp.bfloat16)
    row_input_grad = jnp.einsum(
        "ecsf,edsf->ecd", gate_up_grad, gate_up_w, preferred_element_type=jnp.float32
    )
    grad_gate_up = jnp.einsum(
        "ecd,ecsf->edsf", rows, gate_up_grad, preferred_element_type=jnp.float32
    )
    grad_down = jnp.einsum(
        "ecf,ecd->" + down_form, activ_low, row_grads, preferred_element_type=jnp.float32
    )
    return (expert_out, row_input_grad, grad_gate_up, grad_down)


def body(
    hidden_in,
    parents,
    routes,
    attn_gain,
    w_query,
    key_projection,
    value_projection,
    w_out,
    moe_gain,
    w_router,
    w_gate_up,
    w_down,
    d_out,
):
    experts = w_gate_up.shape[0]
    gathered = (
        lax.all_gather(attn_gain, "fsdp", axis=0, tiled=True),
        lax.all_gather(w_query, "fsdp", axis=0, tiled=True),
        lax.all_gather(key_projection, "fsdp", axis=0, tiled=True),
        lax.all_gather(value_projection, "fsdp", axis=0, tiled=True),
        lax.all_gather(w_out, "fsdp", axis=1, tiled=True),
        lax.all_gather(moe_gain, "fsdp", axis=0, tiled=True),
        lax.all_gather(w_router, "fsdp", axis=0, tiled=True),
        lax.all_gather(w_gate_up, "fsdp", axis=1, tiled=True),
        lax.all_gather(w_down, "fsdp", axis=2, tiled=True),
    )
    gate_up_full = gathered[7]
    down_full = gathered[8]
    down_form = "efd"
    gain_one = gathered[0].astype(jnp.float32)
    query_full = gathered[1]
    key_full = gathered[2]
    value_full = gathered[3]
    out_full = gathered[4]
    gain_two = gathered[5].astype(jnp.float32)
    router_full = gathered[6]
    micro_count = hidden_in.shape[0]
    local_rows = hidden_in.shape[2]
    model_width = hidden_in.shape[3]
    top_count = routes.shape[3]
    kv_heads = key_projection.shape[1] // HEAD_DIM
    q_heads = w_query.shape[1] // HEAD_DIM
    group_size = q_heads // kv_heads
    tree_len = local_rows * lax.axis_size("ctx")
    row_start = lax.axis_index("ctx") * local_rows
    capacity = CAP
    expert_ids = jnp.arange(experts, dtype=jnp.int32)
    outputs = []
    input_grads = []
    totals = None
    for batch_index in range(micro_count):
        tree_places, reach_rows, tok_owner = tree_tables(parents[batch_index, 0], tree_len)
        local_places = lax.dynamic_slice_in_dim(tree_places, row_start, local_rows, 0)
        local_reach = lax.dynamic_slice_in_dim(reach_rows, row_start, local_rows, 0)
        allowed = (jnp.dot(local_reach, tok_owner.T, precision=TOP_PRECISION) > 0.5) & (
            tree_places[None, :] <= local_places[:, None]
        )
        cosine_table, sine_values = rope_tables(local_places)
        inputs = hidden_in[batch_index, 0].astype(jnp.float32)
        scale_one = norm_scale(inputs)
        first_normed = (inputs * scale_one * gain_one).astype(jnp.bfloat16)
        query_unrotated = jnp.dot(
            first_normed, query_full, preferred_element_type=jnp.float32
        ).reshape(local_rows, q_heads, HEAD_DIM)
        key_unrotated = jnp.dot(first_normed, key_full, preferred_element_type=jnp.float32).reshape(
            local_rows, kv_heads, HEAD_DIM
        )
        value_reduced = jnp.dot(
            first_normed, value_full, preferred_element_type=jnp.float32
        ).astype(jnp.bfloat16)
        query_reduced = (
            apply_rotary(query_unrotated, cosine_table, sine_values)
            .astype(jnp.bfloat16)
            .reshape(local_rows, kv_heads, group_size, HEAD_DIM)
        )
        key_low = (
            apply_rotary(key_unrotated, cosine_table, sine_values)
            .astype(jnp.bfloat16)
            .reshape(local_rows, kv_heads * HEAD_DIM)
        )
        tree_keys, tree_values = (
            lax.all_gather(key_low, "ctx", axis=0, tiled=True),
            lax.all_gather(value_reduced, "ctx", axis=0, tiled=True),
        )
        tree_keys = tree_keys.reshape(tree_len, kv_heads, HEAD_DIM)
        tree_values = tree_values.reshape(tree_len, kv_heads, HEAD_DIM)

        def masked_scores():
            raw_scores = jnp.einsum(
                "qhjd,khd->hjqk", query_reduced, tree_keys, preferred_element_type=jnp.float32
            )
            return jnp.where(allowed[None, None], raw_scores * SCORE_SCALE, -1e30)

        scores = masked_scores()
        top_score = jnp.max(scores, axis=-1, keepdims=True)
        log_total = top_score + jnp.log(
            jnp.sum(jnp.exp(scores - top_score), axis=-1, keepdims=True)
        )
        probs_low = jnp.exp(scores - log_total).astype(jnp.bfloat16)
        head_out = jnp.einsum(
            "hjqk,khd->qhjd", probs_low, tree_values, preferred_element_type=jnp.float32
        )
        head_low = head_out.reshape(local_rows, q_heads * HEAD_DIM).astype(jnp.bfloat16)
        attn_part = jnp.dot(head_low, out_full, preferred_element_type=jnp.float32)
        attended = lax.psum(attn_part.astype(jnp.bfloat16), "tp").astype(jnp.float32)
        mixed = inputs + RESIDUAL_SCALE * attended
        scale_two = norm_scale(mixed)
        normed_two = (mixed * scale_two * gain_two).astype(jnp.bfloat16)
        logits = jnp.dot(normed_two, router_full, preferred_element_type=jnp.float32)
        chosen_ids = routes[batch_index, 0]
        picked = (chosen_ids[:, :, None] == expert_ids[None, None, :]).astype(jnp.float32)
        chosen = jnp.sum(picked * logits[:, None, :], axis=2)
        gates = jax.nn.softmax(chosen, axis=1)
        flat_ids = chosen_ids.reshape(-1)
        flat_hot = (flat_ids[:, None] == expert_ids[None, :]).astype(jnp.int32)
        slots = jnp.sum((jnp.cumsum(flat_hot, axis=0) - flat_hot) * flat_hot, axis=1)
        targets = flat_ids * capacity + slots
        sources = (
            jnp.zeros((experts * capacity,), jnp.int32)
            .at[targets]
            .set(jnp.arange(local_rows * top_count, dtype=jnp.int32) // top_count)
        )
        filled = jnp.zeros((experts * capacity, 1), jnp.bfloat16).at[targets].set(1)
        dispatched = (normed_two[sources] * filled).reshape(experts, capacity, model_width)
        grad_out = d_out[batch_index, 0].astype(jnp.float32)
        grad_moe = RESIDUAL_SCALE * grad_out
        entry_grad = (
            (gates[:, :, None] * grad_moe[:, None, :])
            .astype(jnp.bfloat16)
            .reshape(local_rows * top_count, model_width)
        )
        slot_grad = (
            jnp.zeros((experts * capacity, model_width), jnp.bfloat16)
            .at[targets]
            .set(entry_grad)
            .reshape(experts, capacity, model_width)
        )
        expert_out, slot_input_grad, grad_gate_up, grad_down = expert_work(
            dispatched, slot_grad, gate_up_full, down_full, down_form
        )
        entry_out = expert_out.reshape(experts * capacity, model_width)[targets].reshape(
            local_rows, top_count, model_width
        )
        moe_part = jnp.sum(gates[:, :, None] * entry_out, axis=1)
        moe_sum = lax.psum(moe_part.astype(jnp.bfloat16), "tp").astype(jnp.float32)
        outputs.append(mixed + RESIDUAL_SCALE * moe_sum)
        gate_grad_part = jnp.sum(grad_moe[:, None, :] * entry_out, axis=2)
        expert_input_grad = jnp.sum(
            slot_input_grad.reshape(experts * capacity, model_width)[targets].reshape(
                local_rows, top_count, model_width
            ),
            axis=1,
        )
        expert_input_grad, gate_grads = (
            lax.psum(expert_input_grad.astype(jnp.bfloat16), "tp").astype(jnp.float32),
            lax.psum(gate_grad_part.astype(jnp.bfloat16), "tp").astype(jnp.float32),
        )
        chosen_grad = gates * (gate_grads - jnp.sum(gates * gate_grads, axis=1, keepdims=True))
        logit_grad = jnp.sum(picked * chosen_grad[:, :, None], axis=1).astype(jnp.bfloat16)
        normed_two_grad = expert_input_grad + jnp.einsum(
            "te,de->td", logit_grad, router_full, preferred_element_type=jnp.float32
        )
        grad_router = jnp.einsum(
            "td,te->de", normed_two, logit_grad, preferred_element_type=jnp.float32
        )
        unit_two = mixed * scale_two
        grad_gain_two = jnp.sum(normed_two_grad * unit_two, axis=0)
        scaled_two = normed_two_grad * gain_two
        mixed_grad = grad_out + scale_two * (
            scaled_two - unit_two * jnp.mean(scaled_two * unit_two, axis=-1, keepdims=True)
        )
        attn_grad = (RESIDUAL_SCALE * mixed_grad).astype(jnp.bfloat16)
        grad_out_proj = jnp.einsum(
            "tc,td->cd", head_low, attn_grad, preferred_element_type=jnp.float32
        )
        head_grad = (
            jnp.einsum("td,cd->tc", attn_grad, out_full, preferred_element_type=jnp.float32)
            .astype(jnp.bfloat16)
            .reshape(local_rows, kv_heads, group_size, HEAD_DIM)
        )
        scores = masked_scores()
        probs = jnp.exp(scores - log_total)
        probs_low = probs.astype(jnp.bfloat16)
        prob_grad = jnp.einsum(
            "qhjd,khd->hjqk", head_grad, tree_values, preferred_element_type=jnp.float32
        )
        value_grad = jnp.einsum(
            "hjqk,qhjd->khd", probs_low, head_grad, preferred_element_type=jnp.float32
        )
        score_grad = (
            SCORE_SCALE * probs * (prob_grad - jnp.sum(probs * prob_grad, axis=-1, keepdims=True))
        ).astype(jnp.bfloat16)
        query_grad = jnp.einsum(
            "hjqk,khd->qhjd", score_grad, tree_keys, preferred_element_type=jnp.float32
        ).reshape(local_rows, q_heads, HEAD_DIM)
        key_grad = jnp.einsum(
            "hjqk,qhjd->khd", score_grad, query_reduced, preferred_element_type=jnp.float32
        )
        key_grad, value_grad = (
            lax.psum_scatter(
                key_grad.reshape(tree_len, kv_heads * HEAD_DIM).astype(jnp.bfloat16),
                "ctx",
                scatter_dimension=0,
                tiled=True,
            ).astype(jnp.float32),
            lax.psum_scatter(
                value_grad.reshape(tree_len, kv_heads * HEAD_DIM).astype(jnp.bfloat16),
                "ctx",
                scatter_dimension=0,
                tiled=True,
            ).astype(jnp.float32),
        )
        query_pre_grad = (
            apply_rotary(query_grad, cosine_table, -sine_values)
            .astype(jnp.bfloat16)
            .reshape(local_rows, q_heads * HEAD_DIM)
        )
        key_pre_grad = (
            apply_rotary(
                key_grad.reshape(local_rows, kv_heads, HEAD_DIM), cosine_table, -sine_values
            )
            .astype(jnp.bfloat16)
            .reshape(local_rows, kv_heads * HEAD_DIM)
        )
        value_pre_grad = value_grad.astype(jnp.bfloat16)
        normed_one_grad = jnp.einsum(
            "tc,dc->td", query_pre_grad, query_full, preferred_element_type=jnp.float32
        )
        normed_one_grad = normed_one_grad + jnp.einsum(
            "tc,dc->td", key_pre_grad, key_full, preferred_element_type=jnp.float32
        )
        normed_one_grad = normed_one_grad + jnp.einsum(
            "tc,dc->td", value_pre_grad, value_full, preferred_element_type=jnp.float32
        )
        grad_query = jnp.einsum(
            "td,tc->dc", first_normed, query_pre_grad, preferred_element_type=jnp.float32
        )
        grad_key = jnp.einsum(
            "td,tc->dc", first_normed, key_pre_grad, preferred_element_type=jnp.float32
        )
        grad_value = jnp.einsum(
            "td,tc->dc", first_normed, value_pre_grad, preferred_element_type=jnp.float32
        )
        normed_one_grad = lax.psum(normed_one_grad.astype(jnp.bfloat16), "tp").astype(jnp.float32)
        unit_one = inputs * scale_one
        grad_gain_one = jnp.sum(normed_one_grad * unit_one, axis=0)
        scaled_one = normed_one_grad * gain_one
        input_grads.append(
            mixed_grad
            + scale_one
            * (scaled_one - unit_one * jnp.mean(scaled_one * unit_one, axis=-1, keepdims=True))
        )
        piece = (
            grad_gain_one,
            grad_query,
            grad_key,
            grad_value,
            grad_out_proj,
            grad_gain_two,
            grad_router,
            grad_gate_up,
            grad_down,
        )
        totals = piece if batch_index == 0 else add_tuples(totals, piece)
    summed = (
        lax.psum_scatter(totals[0], ("fsdp", "ctx"), scatter_dimension=0, tiled=True),
        lax.psum_scatter(totals[1], ("fsdp", "ctx"), scatter_dimension=0, tiled=True),
        lax.psum_scatter(totals[2], ("fsdp", "ctx"), scatter_dimension=0, tiled=True),
        lax.psum_scatter(totals[3], ("fsdp", "ctx"), scatter_dimension=0, tiled=True),
        lax.psum_scatter(totals[4], ("fsdp", "ctx"), scatter_dimension=1, tiled=True),
        lax.psum_scatter(totals[5], ("fsdp", "ctx"), scatter_dimension=0, tiled=True),
        lax.psum_scatter(totals[6], ("fsdp", "ctx"), scatter_dimension=0, tiled=True),
        lax.psum_scatter(totals[7], ("fsdp", "ctx"), scatter_dimension=1, tiled=True),
        lax.psum_scatter(totals[8], ("fsdp", "ctx"), scatter_dimension=2, tiled=True),
    )
    shares = (
        lax.all_gather(summed[0].astype(jnp.bfloat16), "ctx", axis=0, tiled=True).astype(
            jnp.float32
        ),
        lax.all_gather(summed[1].astype(jnp.bfloat16), "ctx", axis=0, tiled=True).astype(
            jnp.float32
        ),
        lax.all_gather(summed[2].astype(jnp.bfloat16), "ctx", axis=0, tiled=True).astype(
            jnp.float32
        ),
        lax.all_gather(summed[3].astype(jnp.bfloat16), "ctx", axis=0, tiled=True).astype(
            jnp.float32
        ),
        lax.all_gather(summed[4].astype(jnp.bfloat16), "ctx", axis=1, tiled=True).astype(
            jnp.float32
        ),
        lax.all_gather(summed[5].astype(jnp.bfloat16), "ctx", axis=0, tiled=True).astype(
            jnp.float32
        ),
        lax.all_gather(summed[6].astype(jnp.bfloat16), "ctx", axis=0, tiled=True).astype(
            jnp.float32
        ),
        lax.all_gather(summed[7].astype(jnp.bfloat16), "ctx", axis=1, tiled=True).astype(
            jnp.float32
        ),
        lax.all_gather(summed[8].astype(jnp.bfloat16), "ctx", axis=2, tiled=True).astype(
            jnp.float32
        ),
    )
    layer_out = jnp.stack(outputs, axis=0)[:, None]
    d_hidden = jnp.stack(input_grads, axis=0)[:, None]
    return (
        layer_out,
        d_hidden,
        shares[0],
        shares[1],
        shares[2],
        shares[3],
        shares[4],
        shares[5],
        shares[6],
        shares[7],
        shares[8],
    )


def dot(left, right, left_dim=1, right_dim=0):
    return lax.dot_general(
        left, right, (((left_dim,), (right_dim,)), ((), ())), preferred_element_type=jnp.float32
    )


def vmem_params(count=1):
    return pltpu.CompilerParams(
        dimension_semantics=("arbitrary",) * count, vmem_limit_bytes=60 * 1024 * 1024
    )


def attend_kernel(seen_ref, query_ref, kv0, kv1, kv2, kv3, out_ref, probs_ref):
    blocks = (kv0, kv1, kv2, kv3)
    micro = seen_ref.shape[0]
    rows = query_ref.shape[0] // micro
    kv_heads = kv0.shape[1] // (2 * HEAD_DIM)
    group = query_ref.shape[1] // HEAD_DIM // kv_heads
    shape = (group * rows, rows)
    causal = (
        lax.broadcasted_iota(jnp.int32, shape, 1)
        <= lax.broadcasted_iota(jnp.int32, shape, 0) % rows
    )
    for m in range(micro):
        span = pl.ds(m * rows, rows)
        whole = query_ref[span, :]
        pieces = []
        for g in range(kv_heads):
            lanes = slice(g * HEAD_DIM, (g + 1) * HEAD_DIM)
            query = jnp.concatenate(
                [
                    whole[:, (g * group + h) * HEAD_DIM : (g * group + h + 1) * HEAD_DIM]
                    for h in range(group)
                ],
                axis=0,
            )
            parts = []
            for r in range(4):
                part = dot(query, blocks[r][span, :][:, lanes], 1, 1) * SCORE_SCALE
                if r == 0:
                    part = jnp.where(causal, part, -1e30)
                else:
                    part = jnp.where(seen_ref[m, r] > 0, part, -1e30)
                parts.append(part)
            scores = jnp.concatenate(parts, axis=1)
            powers = jnp.exp(scores - jnp.max(scores, axis=1, keepdims=True))
            probs = powers / jnp.sum(powers, axis=1, keepdims=True)
            probs_ref[m * kv_heads + g] = probs
            low = probs.astype(jnp.bfloat16)
            values = jnp.concatenate(
                [
                    blocks[r][span, :][:, (kv_heads + g) * HEAD_DIM : (kv_heads + g + 1) * HEAD_DIM]
                    for r in range(4)
                ],
                axis=0,
            )
            mixed = dot(low, values)
            pieces += [mixed[h * rows : (h + 1) * rows] for h in range(group)]
        out_ref[span, :] = jnp.concatenate(pieces, axis=1).astype(jnp.bfloat16)


def attend_back_kernel(
    query_ref, grad_ref, kv0, kv1, kv2, kv3, probs_ref, query_grad_ref, kv_grad_ref
):
    blocks = (kv0, kv1, kv2, kv3)
    kv_heads = kv0.shape[1] // (2 * HEAD_DIM)
    micro = probs_ref.shape[0] // kv_heads
    rows = query_ref.shape[0] // micro
    group = query_ref.shape[1] // HEAD_DIM // kv_heads
    for m in range(micro):
        span = pl.ds(m * rows, rows)
        whole = query_ref[span, :]
        whole_grad = grad_ref[span, :]
        pieces = []
        key_grads = []
        value_grads = []
        for g in range(kv_heads):

            def heads(source):
                return jnp.concatenate(
                    [
                        source[:, (g * group + h) * HEAD_DIM : (g * group + h + 1) * HEAD_DIM]
                        for h in range(group)
                    ],
                    axis=0,
                )

            query = heads(whole)
            head_grad = heads(whole_grad)
            keys = jnp.concatenate(
                [blocks[r][span, :][:, g * HEAD_DIM : (g + 1) * HEAD_DIM] for r in range(4)], axis=0
            )
            values = jnp.concatenate(
                [
                    blocks[r][span, :][:, (kv_heads + g) * HEAD_DIM : (kv_heads + g + 1) * HEAD_DIM]
                    for r in range(4)
                ],
                axis=0,
            )
            probs = probs_ref[m * kv_heads + g]
            prob_grad = dot(head_grad, values, 1, 1)
            inner = jnp.sum(probs * prob_grad, axis=1, keepdims=True)
            score_grad = (SCORE_SCALE * probs * (prob_grad - inner)).astype(jnp.bfloat16)
            value_grads.append(dot(probs.astype(jnp.bfloat16), head_grad, 0, 0))
            key_grads.append(dot(score_grad, query, 0, 0))
            query_grad = dot(score_grad, keys)
            pieces += [query_grad[h * rows : (h + 1) * rows] for h in range(group)]
        query_grad_ref[span, :] = jnp.concatenate(pieces, axis=1)
        joined = jnp.concatenate(key_grads + value_grads, axis=1).astype(jnp.bfloat16)
        for r in range(4):
            kv_grad_ref[r, span, :] = joined[r * rows : (r + 1) * rows]


def expert_kernel(
    place_ref,
    near_ref,
    far_ref,
    near_out_ref,
    far_out_ref,
    rank_ref,
    gate_ref,
    gate_up_ref,
    down_ref,
    other0,
    other1,
    other2,
    other3,
    *rest,
):
    if len(rest) == 12:
        held_out, held_grad = rest[:2]
        rest = rest[2:]
    else:
        held_out = held_grad = None
    out_ref, grad_ref, slots_ref, gate_grad_ref, rows_buf, grads_buf, moe_buf, back_buf, hot_buf, gate_buf = rest
    others = (other0, other1, other2, other3)
    half = down_ref.shape[-1]
    width = down_ref.shape[-2]
    quarter = [place_ref[1] ^ r for r in range(4)]
    iota = lax.broadcasted_iota(jnp.int32, (CAP, 128), 0)

    @pl.when(pl.program_id(0) == 0)
    def _():
        if held_out is None:
            out_ref[...] = jnp.zeros_like(out_ref)
            grad_ref[...] = jnp.zeros_like(grad_ref)
        else:
            out_ref[...] = held_out[...]
            grad_ref[...] = held_grad[...]

    for b in range(4):
        hot = jnp.concatenate(
            [
                jnp.where(iota == rank_ref[quarter[r], 0, pl.ds(b, 1), :], 1.0, 0.0)
                for r in range(4)
            ],
            axis=0,
        )
        gates = jnp.concatenate(
            [
                jnp.broadcast_to(gate_ref[quarter[r], 0, pl.ds(b, 1), :], (CAP, 128))
                for r in range(4)
            ],
            axis=0,
        )
        gate_buf[b] = jnp.broadcast_to(jnp.sum(hot * gates, axis=1, keepdims=True), (4 * CAP, 128))
        low = hot.astype(jnp.bfloat16)
        hot_buf[b] = low
        span = pl.ds((b % 2) * 128, 128)
        for part in range(2):
            keep = pl.ds(part * half, half)
            if b < 2:
                rows, grads = near_ref[span, keep], near_out_ref[span, keep]
            else:
                swap = pl.ds((1 - part) * half, half)
                rows, grads = far_ref[span, swap], far_out_ref[span, swap]
            rows_buf[b, :, keep] = dot(low, rows).astype(jnp.bfloat16)
            grads_buf[b, :, keep] = dot(low, grads).astype(jnp.bfloat16)
    for r in range(4):
        q = quarter[r]
        slot = slice(r * CAP, (r + 1) * CAP)
        rows = jnp.concatenate([rows_buf[b, slot, :] for b in range(4)], axis=0)
        grads = jnp.concatenate([grads_buf[b, slot, :] for b in range(4)], axis=0)
        gate = jnp.concatenate([gate_buf[b, slot, :] for b in range(4)], axis=0)
        near_w = jnp.concatenate([gate_up_ref[q, 0, 0], gate_up_ref[q, 0, 1]], axis=1)
        far_w = jnp.concatenate([others[r][0, :half, :], others[r][0, half : 2 * half, :]], axis=1)
        near_down = down_ref[0, q, 0]
        far_down = jnp.concatenate(
            [
                others[r][0, 2 * half + j * width : 2 * half + (j + 1) * width, :]
                for j in range(half // 128)
            ],
            axis=1,
        )
        gate_up = dot(rows[:, :half], near_w) + dot(rows[:, half:], far_w)
        gate_pre = gate_up[:, :width]
        up_pre = gate_up[:, width:]
        sigmoid = 1.0 / (1.0 + jnp.exp(-gate_pre))
        activ = (gate_pre * sigmoid * up_pre).astype(jnp.bfloat16)
        pulled = RESIDUAL_SCALE * (
            dot(grads[:, :half], near_down, 1, 1) + dot(grads[:, half:], far_down, 1, 1)
        )
        activ_wide = activ.astype(jnp.float32)
        gate_grad = jnp.sum(activ_wide * pulled, axis=1, keepdims=True)
        activ_grad = pulled * gate
        gate_pre_grad = activ_grad * up_pre * sigmoid * (1.0 + gate_pre * (1.0 - sigmoid))
        up_pre_grad = activ_grad * gate_pre * sigmoid
        both = jnp.concatenate([gate_pre_grad, up_pre_grad], axis=1).astype(jnp.bfloat16)
        slots_ref[q, 0, :, : 2 * width] = both
        slots_ref[q, 0, :, 2 * width :] = (activ_wide * gate * RESIDUAL_SCALE).astype(jnp.bfloat16)
        for part, (wide, low_w) in enumerate(((near_w, near_down), (far_w, far_down))):
            keep = pl.ds(part * half, half)
            made = dot(activ, low_w)
            back = dot(both, wide, 1, 1)
            for b in range(4):
                piece = slice(b * CAP, (b + 1) * CAP)
                scale = jnp.concatenate([gate[piece]] * (half // 128), axis=1)
                moe_buf[b, slot, keep] = (made[piece] * scale).astype(jnp.bfloat16)
                back_buf[b, slot, keep] = back[piece].astype(jnp.bfloat16)
        for b in range(4):
            hot = hot_buf[b, slot, :].astype(jnp.float32)
            gate_grad_ref[q, 0, pl.ds(b, 1), :] = jnp.sum(
                hot * gate_grad[b * CAP : (b + 1) * CAP], axis=0, keepdims=True
            )
    for b in range(4):
        span = pl.ds(b * 128, 128)
        out_ref[span, :] += dot(hot_buf[b], moe_buf[b], 0, 0)
        grad_ref[span, :] += dot(hot_buf[b], back_buf[b], 0, 0)


def run_experts(place, near, far, near_out, far_out, rank, gate, gate_up, down, others, held, first):
    steps, packed, lanes = others[0].shape
    quarters, each, sides, half, width = gate_up.shape
    tokens = 2 * near_out.shape[0]
    full = 2 * half

    def fixed(array):
        return pl.BlockSpec(array.shape, lambda j, sp: (0,) * array.ndim)

    table = pl.BlockSpec((quarters, 1, 4, 128), lambda j, sp: (0, first + j, 0, 0))
    in_specs = [
        fixed(near),
        fixed(far),
        fixed(near_out),
        fixed(far_out),
        table,
        table,
        pl.BlockSpec((quarters, 1, sides, half, width), lambda j, sp: (0, first + j, 0, 0, 0)),
        pl.BlockSpec((1, quarters, 1, width, half), lambda j, sp: (sp[0], 0, first + j, 0, 0)),
    ] + [pl.BlockSpec((1, packed, lanes), lambda j, sp: (j, 0, 0))] * 4
    operands = [place, near, far, near_out, far_out, rank, gate, gate_up, down, *others]
    aliases = {}
    total = jax.ShapeDtypeStruct((tokens, full), jnp.float32)
    if held is not None:
        in_specs += [fixed(held[0]), fixed(held[1])]
        aliases = {len(operands): 0, len(operands) + 1: 1}
        operands += list(held)
    slots = jax.ShapeDtypeStruct((quarters, steps, 4 * CAP, 3 * width), jnp.bfloat16)
    gate_grads = jax.ShapeDtypeStruct((quarters, steps, 4, 128), jnp.float32)
    return pl.pallas_call(
        expert_kernel,
        out_shape=(total, total, slots, gate_grads),
        grid_spec=pltpu.PrefetchScalarGridSpec(
            num_scalar_prefetch=1,
            grid=(steps,),
            in_specs=in_specs,
            out_specs=(
                pl.BlockSpec(total.shape, lambda j, sp: (0, 0)),
                pl.BlockSpec(total.shape, lambda j, sp: (0, 0)),
                pl.BlockSpec((quarters, 1, 4 * CAP, 3 * width), lambda j, sp: (0, j, 0, 0)),
                pl.BlockSpec((quarters, 1, 4, 128), lambda j, sp: (0, j, 0, 0)),
            ),
            scratch_shapes=[pltpu.VMEM((4, 4 * CAP, full), jnp.bfloat16)] * 4
            + [
                pltpu.VMEM((4, 4 * CAP, 128), jnp.bfloat16),
                pltpu.VMEM((4, 4 * CAP, 128), jnp.float32),
            ],
        ),
        input_output_aliases=aliases,
        compiler_params=vmem_params(),
        name="experts",
    )(*operands)


def weight_grad_kernel(place_ref, *refs):
    rows_ref, grads_ref, slots_ref, rank_ref = refs[:4]
    gate_up_ref, down_ref, rows_buf, grads_buf = refs[-4:]
    half = down_ref.shape[-1]
    width = down_ref.shape[-2]
    side = pl.program_id(1)
    iota = lax.broadcasted_iota(jnp.int32, (CAP, 128), 0)
    for k in range(4):
        for b in range(4):
            hot = jnp.concatenate(
                [
                    jnp.where(iota == rank_ref[0, q, 0, pl.ds(4 * k + b, 1), :], 1.0, 0.0)
                    for q in range(4)
                ],
                axis=0,
            ).astype(jnp.bfloat16)
            span = pl.ds(b * 128, 128)
            spot = 4 * k + (b ^ (2 * side))
            rows_buf[spot] = dot(hot, rows_ref[k, span, :]).astype(jnp.bfloat16)
            grads_buf[spot] = dot(hot, grads_ref[k, span, :]).astype(jnp.bfloat16)
    for q in range(4):
        slot = slice(q * CAP, (q + 1) * CAP)
        rows = jnp.concatenate([rows_buf[n, slot, :] for n in range(16)], axis=0)
        grads = jnp.concatenate([grads_buf[n, slot, :] for n in range(16)], axis=0)
        taken = jnp.concatenate([slots_ref[0, k, q, 0] for k in range(4)], axis=0)
        made = dot(rows, taken[:, : 2 * width], 0, 0)
        gate_up_ref[0, q, 0, pl.ds(0, half, stride=2), :] = made[:, :width]
        gate_up_ref[0, q, 0, pl.ds(1, half, stride=2), :] = made[:, width:]
        down_ref[0, q, 0] = dot(taken[:, 2 * width :], grads, 0, 0)


def run_weight_grads(place, rows, grads, slots, rank, held, first, each):
    sides, _, quarters, steps, slot_count, lanes = slots.shape
    width = lanes // 3
    half = rows.shape[-1]
    in_specs = [
        pl.BlockSpec(rows.shape, lambda j, a, sp: (0, 0, 0)),
        pl.BlockSpec(rows.shape, lambda j, a, sp: (0, 0, 0)),
        pl.BlockSpec(
            (1, 4, quarters, 1, slot_count, lanes),
            lambda j, a, sp: (sp[0] ^ a, 0, 0, j, 0, 0),
        ),
        pl.BlockSpec((1, quarters, 1, 16, 128), lambda j, a, sp: (a, 0, first + j, 0, 0)),
    ]
    operands = [place, rows, grads, slots, rank]
    aliases = {}
    if held is not None:
        in_specs += [pl.BlockSpec(memory_space=pl.ANY)] * 2
        aliases = {len(operands): 0, len(operands) + 1: 1}
        operands += list(held)
    return pl.pallas_call(
        weight_grad_kernel,
        out_shape=(
            jax.ShapeDtypeStruct((sides, quarters, each, 2 * half, width), jnp.float32),
            jax.ShapeDtypeStruct((sides, quarters, each, width, half), jnp.float32),
        ),
        grid_spec=pltpu.PrefetchScalarGridSpec(
            num_scalar_prefetch=1,
            grid=(steps, sides),
            in_specs=in_specs,
            out_specs=(
                pl.BlockSpec(
                    (1, quarters, 1, 2 * half, width),
                    lambda j, a, sp: (sp[0] ^ a, 0, first + j, 0, 0),
                ),
                pl.BlockSpec(
                    (1, quarters, 1, width, half),
                    lambda j, a, sp: (sp[0] ^ a, 0, first + j, 0, 0),
                ),
            ),
            scratch_shapes=[pltpu.VMEM((16, 4 * CAP, half), jnp.bfloat16)] * 2,
        ),
        input_output_aliases=aliases,
        compiler_params=vmem_params(2),
        name="weight_grads",
    )(*operands)


def swap_halves(values):
    half = values.shape[-1] // 2
    return jnp.concatenate([values[..., half:], values[..., :half]], axis=-1)


def turn_heads(values):
    half_dim = HEAD_DIM // 2
    lane = lax.broadcasted_iota(jnp.int32, values.shape, 1) % HEAD_DIM
    return jnp.where(
        lane < half_dim,
        -jnp.roll(values, -half_dim, axis=1),
        jnp.roll(values, half_dim, axis=1),
    )


def fast_body(
    hidden_in,
    parents,
    routes,
    attn_gain,
    w_query,
    key_projection,
    value_projection,
    w_out,
    moe_gain,
    w_router,
    w_gate_up,
    w_down,
    d_out,
):
    low, wide = jnp.bfloat16, jnp.float32
    x_pos = lax.axis_index("fsdp")
    c_pos = lax.axis_index("ctx")
    z_pos = lax.axis_index("tp")
    tp_size = lax.axis_size("tp")
    micro, _, rows, model = hidden_in.shape
    half = model // 2
    tokens = micro * rows
    experts = w_gate_up.shape[0]
    mine = experts // 2
    each = mine // 4
    width = w_down.shape[1]
    q_cols = w_query.shape[1]
    k_cols = key_projection.shape[1]
    chunks = ((0, 2), (2, 2), (4, 1))

    def across(value):
        return lax.ppermute(value, "fsdp", [(0, 1), (1, 0)])

    def beside(value):
        return lax.ppermute(value, "ctx", [(i, i ^ 1) for i in range(4)])

    def along(value):
        return lax.ppermute(value, "ctx", [(i, i ^ 2) for i in range(4)])

    def from_tp(value, step):
        return lax.ppermute(
            value, "tp", [((i + step) % tp_size, i) for i in range(tp_size)]
        )

    def all_ctx(value):
        nearby = beside(value)
        distant = along(value)
        return [value, nearby, distant, beside(distant)]

    def after(value, *earlier):
        return lax.optimization_barrier((value, *earlier))[0]

    def own_first(value):
        return jnp.where(x_pos == 0, value, swap_halves(value))

    def ctx_join(first, second, axis):
        return jnp.where(
            c_pos % 2 == 0,
            jnp.concatenate([first, second], axis=axis),
            jnp.concatenate([second, first], axis=axis),
        )

    def sum_tp(value):
        part = value.shape[0] // tp_size

        def piece(step):
            return lax.dynamic_slice_in_dim(value, ((z_pos + step) % tp_size) * part, part, 0)

        total = piece(0).astype(wide)
        for step in range(1, tp_size):
            total = total + from_tp(piece(tp_size - step), step).astype(wide)
        total = total.astype(low)
        found = [total] + [from_tp(total, step) for step in range(1, tp_size)]
        return lax.dynamic_slice_in_dim(
            jnp.concatenate(found + found, axis=0), ((tp_size - z_pos) % tp_size) * part, tokens, 0
        )

    small = jnp.concatenate(
        [
            w_query,
            key_projection,
            value_projection,
            jnp.pad(
                jnp.concatenate([w_router, attn_gain[:, None], moe_gain[:, None]], axis=1),
                ((0, 0), (0, 128 - experts - 2)),
            ),
        ],
        axis=1,
    )
    core = c_pos % 2
    sent = across(lax.dynamic_slice_in_dim(small, core * (half // 2), half // 2, 0))
    small_far = ctx_join(sent, beside(sent), 0)
    qkv_cols = q_cols + 2 * k_cols
    qkv_full = jnp.concatenate([small[:, :qkv_cols], small_far[:, :qkv_cols]], axis=0)
    rest_full = jnp.concatenate([small[:, qkv_cols:], small_far[:, qkv_cols:]], axis=0)
    gain_one = rest_full[:, experts].astype(wide)
    gain_two = rest_full[:, experts + 1].astype(wide)
    router = jnp.where(
        x_pos == 0,
        rest_full[:, :experts],
        jnp.concatenate([rest_full[:, mine:experts], rest_full[:, :mine]], axis=1),
    )

    routes_low = jnp.pad(
        routes.reshape(tokens, -1).astype(low), ((0, 0), (0, 128 - routes.shape[-1]))
    )
    near_out = jnp.concatenate([own_first(d_out.reshape(tokens, model)), routes_low], axis=1)
    away = (1 - x_pos) * mine + c_pos * each
    far_weights = []
    last_x = sent
    last_y = sent
    for number, (first, count) in enumerate(chunks):
        gate_up_sent = (
            lax.dynamic_slice_in_dim(w_gate_up, away + first, count, 0)
            .transpose(0, 2, 1, 3)
            .reshape(count, 2 * half, width)
        )
        down_sent = (
            lax.dynamic_slice_in_dim(w_down, away + first, count, 0)
            .reshape(count, width, half // 128, 128)
            .transpose(0, 2, 1, 3)
            .reshape(count, half, 128)
        )
        packed = jnp.concatenate([gate_up_sent, down_sent], axis=1)
        got = across(after(packed, last_x))
        last_x = got
        nearby = beside(got)
        distant = along(after(got, last_y))
        last_y = distant
        far_weights.append([got, nearby, distant, beside(distant)])
        if number == 1:
            far_out = across(after(near_out, got))
            last_x = far_out
    down_all = w_down.reshape(2, 4, each, width, half)

    seg_ids = jnp.arange(4, dtype=jnp.int32)
    seen_rows = []
    angle_rows = []
    half_dim = HEAD_DIM // 2
    inverse = ROPE_BASE ** (-jnp.arange(half_dim, dtype=wide) * 2.0 / HEAD_DIM)
    for m in range(micro):
        current = c_pos
        reach = seg_ids == current
        for _ in range(3):
            current = jnp.sum(jnp.where(seg_ids == current, parents[m, 0], 0))
            reach = reach | (seg_ids == current)
        reach = reach.astype(jnp.int32)
        depth = jnp.sum(reach) - 1
        seen_rows.append(
            jnp.stack([jnp.sum(jnp.where(seg_ids == (c_pos ^ r), reach, 0)) for r in range(4)])
        )
        places = (depth * rows + jnp.arange(rows, dtype=jnp.int32)).astype(wide)
        angle_rows.append(places[:, None] * inverse[None, :])
    seen = jnp.stack(seen_rows)
    angles = jnp.concatenate(angle_rows, axis=0)
    turns = (q_cols + k_cols) // half_dim
    cosines = jnp.tile(jnp.cos(angles), (1, turns))
    sines = jnp.tile(jnp.sin(angles), (1, turns))

    inputs = own_first(hidden_in.reshape(tokens, model)).astype(wide)
    scale_one = norm_scale(inputs)
    unit_one = inputs * scale_one
    first_normed = (unit_one * gain_one).astype(low)
    unrotated = dot(first_normed, qkv_full)
    turned_part = unrotated[:, : q_cols + k_cols]
    rotated = (turned_part * cosines + turn_heads(turned_part) * sines).astype(low)
    query = rotated[:, :q_cols]
    gate_up_mine = (
        lax.dynamic_slice_in_dim(after(w_gate_up, query), x_pos * mine, mine, 0)
        .transpose(0, 2, 1, 3)
        .reshape(4, each, 2, half, width)
    )
    key_value = jnp.concatenate(
        [rotated[:, q_cols:], unrotated[:, q_cols + k_cols :].astype(low)], axis=1
    )
    blocks = all_ctx(key_value)
    smem = pl.BlockSpec(memory_space=pltpu.SMEM)
    vmem = pl.BlockSpec(memory_space=pltpu.VMEM)
    kv_heads = k_cols // HEAD_DIM
    group = q_cols // k_cols
    head_low, probs = pl.pallas_call(
        attend_kernel,
        out_shape=(
            jax.ShapeDtypeStruct((tokens, q_cols), low),
            jax.ShapeDtypeStruct((micro * kv_heads, group * rows, 4 * rows), wide),
        ),
        in_specs=[smem] + [vmem] * 5,
        out_specs=(vmem, vmem),
        compiler_params=pltpu.CompilerParams(vmem_limit_bytes=60 * 1024 * 1024),
        name="attend",
    )(seen, query, *blocks)
    out_near = after(w_out, sent)
    out_core = lax.dynamic_slice_in_dim(out_near, core * (q_cols // 2), q_cols // 2, 0)
    out_got = across(out_core)
    out_far = ctx_join(out_got, beside(out_got), 0)
    attn_part = jnp.concatenate([dot(head_low, w_out), dot(head_low, out_far)], axis=1).astype(low)
    attended = lax.psum(attn_part, "tp").astype(wide)
    attended = after(attended, far_weights[1][0], far_weights[0][2])
    mixed = inputs + RESIDUAL_SCALE * attended
    scale_two = norm_scale(mixed)
    unit_two = mixed * scale_two
    normed_two = (unit_two * gain_two).astype(low)

    expert_ids = (jnp.arange(experts, dtype=jnp.int32) + x_pos * mine) % experts
    flat_routes = routes.reshape(tokens, -1)
    named = jnp.any(flat_routes[:, :, None] == expert_ids[None, None, :], axis=1)
    logits = jnp.where(named, dot(normed_two, router), -1e30)
    powers = jnp.where(named, jnp.exp(logits - jnp.max(logits, axis=1, keepdims=True)), 0.0)
    gates = powers / jnp.sum(powers, axis=1, keepdims=True)

    gates_sent = gates[:, mine:]
    gates_high = gates_sent.astype(low)
    gates_rest = (gates_sent - gates_high.astype(wide)).astype(low)
    near = jnp.concatenate(
        [
            normed_two,
            jnp.pad(
                jnp.concatenate([gates_high, gates_rest], axis=1), ((0, 0), (0, 128 - 2 * mine))
            ),
        ],
        axis=1,
    )
    far = across(near)
    far_gates = far[:, model : model + mine].astype(wide) + far[
        :, model + mine : model + 2 * mine
    ].astype(wide)
    upper = (
        lax.broadcasted_iota(jnp.int32, (rows, rows), 0)
        < lax.broadcasted_iota(jnp.int32, (rows, rows), 1)
    ).astype(low)

    def ranks(route_table, ids):
        flat = route_table.astype(jnp.int32).T
        hit = jnp.zeros((ids.shape[0], flat.shape[1]), jnp.bool_)
        for k in range(flat.shape[0]):
            hit = hit | (flat[k][None, :] == ids[:, None])
        hot = hit.astype(low).reshape(-1, rows)
        before = dot(hot, upper)
        found = jnp.where(hot > 0, before, -1.0).astype(jnp.int32)
        return found.reshape(ids.shape[0], -1, rows)

    top = routes.shape[-1]
    pair_routes = jnp.concatenate([routes_low, far_out[:, model:]], axis=0)[:, :top]
    rank_pair = ranks(pair_routes, expert_ids[:mine]).reshape(4, each, 4, rows)
    gate_pair = (
        jnp.concatenate([gates[:, :mine], far_gates], axis=0).T.reshape(4, each, 4, rows)
    )
    place = jnp.stack([x_pos, c_pos]).astype(jnp.int32)

    held = None
    slots = []
    gate_grad_parts = []
    for (first, count), others in zip(chunks, far_weights):
        moe_all, back_all, slot_part, gate_part = run_experts(
            place,
            near,
            far,
            near_out,
            far_out,
            rank_pair,
            gate_pair,
            gate_up_mine,
            down_all,
            others,
            held,
            first,
        )
        held = (moe_all, back_all)
        slots.append(slot_part)
        gate_grad_parts.append(gate_part)
    gate_grad_all = jnp.concatenate(gate_grad_parts, axis=1).reshape(mine, 2 * tokens).T

    back_sent = jnp.concatenate(
        [
            back_all[tokens:].astype(low),
            jnp.pad(gate_grad_all[tokens:].astype(low), ((0, 0), (0, 128 - mine))),
        ],
        axis=1,
    )
    back_got = across(back_sent)
    back_sum = (back_all[:tokens] + swap_halves(back_got[:, :model]).astype(wide)).astype(low)
    gathered = sum_tp(
        jnp.concatenate(
            [
                back_sum,
                jnp.pad(
                    jnp.concatenate(
                        [gate_grad_all[:tokens].astype(low), back_got[:, model : model + mine]],
                        axis=1,
                    ),
                    ((0, 0), (0, 128 - experts)),
                ),
            ],
            axis=1,
        )
    )
    gate_grads = gathered[:, model : model + experts].astype(wide)
    logit_grad = (gates * (gate_grads - jnp.sum(gates * gate_grads, axis=1, keepdims=True))).astype(
        low
    )
    normed_two_grad = gathered[:, :model].astype(wide) + dot(logit_grad, router, 1, 1)
    grad_out = near_out[:, :model].astype(wide)
    gain_two_part = jnp.sum(normed_two_grad * unit_two, axis=0)
    scaled_two = normed_two_grad * gain_two
    mixed_grad = grad_out + scale_two * (
        scaled_two - unit_two * jnp.mean(scaled_two * unit_two, axis=-1, keepdims=True)
    )
    attn_grad = (RESIDUAL_SCALE * mixed_grad).astype(low)

    moe_got = across(moe_all[tokens:].astype(low))
    moe_part = (moe_all[:tokens] + swap_halves(moe_got).astype(wide)).astype(low)
    moe_sum = sum_tp(after(moe_part, gathered)).astype(wide)
    layer_out = own_first(mixed + RESIDUAL_SCALE * moe_sum)

    head_grad = (
        dot(attn_grad[:, :half], w_out, 1, 1) + dot(attn_grad[:, half:], out_far, 1, 1)
    ).astype(low)
    query_grad, kv_grads = pl.pallas_call(
        attend_back_kernel,
        out_shape=(
            jax.ShapeDtypeStruct((tokens, q_cols), wide),
            jax.ShapeDtypeStruct((4, tokens, 2 * k_cols), low),
        ),
        in_specs=[vmem] * 7,
        out_specs=(vmem, vmem),
        compiler_params=pltpu.CompilerParams(vmem_limit_bytes=60 * 1024 * 1024),
        name="attend_back",
    )(query, head_grad, *blocks, probs)
    near_pair = beside(jnp.stack([kv_grads[1], kv_grads[3]]))
    far_part = (kv_grads[2].astype(wide) + near_pair[1].astype(wide)).astype(low)
    kv_grad = (
        kv_grads[0].astype(wide) + near_pair[0].astype(wide) + along(far_part).astype(wide)
    )
    turned_grad = jnp.concatenate([query_grad, kv_grad[:, :k_cols]], axis=1)
    qkv_grad = jnp.concatenate(
        [turned_grad * cosines - turn_heads(turned_grad) * sines, kv_grad[:, k_cols:]], axis=1
    ).astype(low)
    normed_one_part = dot(qkv_grad, qkv_full, 1, 1).astype(low)
    normed_one_grad = sum_tp(normed_one_part).astype(wide)
    gain_one_part = jnp.sum(normed_one_part.astype(wide) * unit_one, axis=0)
    gain_one_part = sum([from_tp(gain_one_part, step) for step in range(1, tp_size)], gain_one_part)
    scaled_one = normed_one_grad * gain_one
    d_hidden = own_first(
        mixed_grad
        + scale_one
        * (scaled_one - unit_one * jnp.mean(scaled_one * unit_one, axis=-1, keepdims=True))
    )

    early = lax.all_gather(
        jnp.concatenate(
            [
                jnp.concatenate([near_out[:, :half], routes_low], axis=1),
                far_out[:, half:],
            ],
            axis=0,
        ),
        "ctx",
    )
    rows_two = lax.all_gather(
        jnp.concatenate([normed_two[:, :half], far[:, half:model]], axis=0), "ctx"
    )
    all_routes = early[:, :, half : half + top].reshape(4 * 2 * tokens, top)
    rank_all = ranks(all_routes, expert_ids).reshape(2, 4, each, 16, rows)
    grads = None
    for (first, count), part in zip(chunks, slots):
        pair = lax.all_gather(part, ("fsdp", "ctx")).reshape(2, 4, *part.shape)
        grads = run_weight_grads(place, rows_two, early, pair, rank_all, grads, first, each)
    d_gate_up = grads[0].reshape(experts, half, 2, width)
    d_down = grads[1].reshape(experts, width, half)

    def sum_plane(part):
        share = part.shape[1] // 2
        kept = lax.dynamic_slice_in_dim(part, core * share, share, 1)
        given = lax.dynamic_slice_in_dim(part, (1 - core) * share, share, 1)
        kept = kept + beside(given.astype(low)).astype(wide)
        total = kept[0] + across(kept[1].astype(low)).astype(wide)
        total = (total + along(total.astype(low)).astype(wide)).astype(low)
        return ctx_join(total, beside(total), 0).astype(wide)

    logit_cols = jnp.where(
        x_pos == 0,
        logit_grad,
        jnp.concatenate([logit_grad[:, mine:], logit_grad[:, :mine]], axis=1),
    )

    def both(left, right):
        return jnp.stack(
            [dot(left, right[:, :half], 0, 0), dot(left, right[:, half:], 0, 0)], axis=0
        )

    side_grads = sum_plane(
        jnp.concatenate(
            [
                both(head_low, attn_grad),
                both(logit_cols, normed_two),
                jnp.pad(gain_two_part.reshape(2, 1, half), ((0, 0), (0, 23), (0, 0))),
            ],
            axis=1,
        )
    )
    d_w_out = side_grads[:q_cols]
    d_router = side_grads[q_cols : q_cols + experts].T
    d_qkv = sum_plane(dot(first_normed, qkv_grad, 0, 0).reshape(2, half, qkv_cols))

    def sum_gain(part):
        part = part + beside(part)
        part = part + along(part)
        return part[:half] + across(part[half:])

    return (
        layer_out.reshape(micro, 1, rows, model),
        d_hidden.reshape(micro, 1, rows, model),
        sum_gain(gain_one_part),
        d_qkv[:, :q_cols],
        d_qkv[:, q_cols : q_cols + k_cols],
        d_qkv[:, q_cols + k_cols :],
        d_w_out,
        side_grads[q_cols + experts],
        d_router,
        d_gate_up,
        d_down,
    )


def solution(mesh):
    placed = (
        P(None, "fsdp", "ctx", None),
        P(None, "fsdp", None),
        P(None, "fsdp", "ctx", None),
        P("fsdp"),
        P("fsdp", "tp"),
        P("fsdp", "tp"),
        P("fsdp", "tp"),
        P("tp", "fsdp"),
        P("fsdp"),
        P("fsdp", None),
        P(None, "fsdp", None, "tp"),
        P(None, "tp", "fsdp"),
        P(None, "fsdp", "ctx", None),
    )
    fits = mesh.shape["fsdp"] == 2 and mesh.shape["ctx"] == 4
    return jax.shard_map(
        fast_body if fits else body,
        mesh=mesh,
        in_specs=placed,
        out_specs=(
            P(None, "fsdp", "ctx", None),
            P(None, "fsdp", "ctx", None),
            P("fsdp"),
            P("fsdp", "tp"),
            P("fsdp", "tp"),
            P("fsdp", "tp"),
            P("tp", "fsdp"),
            P("fsdp"),
            P("fsdp", None),
            P(None, "fsdp", None, "tp"),
            P(None, "tp", "fsdp"),
        ),
        check_vma=False,
    )
```

```python
import jax
import jax.numpy as jnp
from jax import lax
from jax.experimental import pallas as pl
from jax.experimental.pallas import tpu as pltpu
from jax.sharding import PartitionSpec as P

HEAD_DIM = 64
CAP = 32


EPSILON = 1e-06
RESIDUAL_SCALE = 0.22
SCORE_SCALE = 1.0 / 64.0
ROPE_BASE = 10000.0
TOP_PRECISION = lax.Precision.HIGHEST


def tree_tables(parent_row, tree_len):
    seg_total = parent_row.shape[0]
    seg_len = tree_len // seg_total
    seg_ids = jnp.arange(seg_total, dtype=jnp.int32)
    parent_links = (parent_row[:, None] == seg_ids[None, :]).astype(jnp.float32)
    reach_table = jnp.maximum(parent_links, jnp.eye(seg_total, dtype=jnp.float32))
    for squaring in range(max(seg_total - 1, 1).bit_length()):
        reach_table = jnp.minimum(jnp.dot(reach_table, reach_table, precision=TOP_PRECISION), 1.0)
    seg_depth = jnp.sum(reach_table, axis=1) - 1.0
    token_ids = jnp.arange(tree_len, dtype=jnp.int32)
    tok_owner = ((token_ids // seg_len)[:, None] == seg_ids[None, :]).astype(jnp.float32)
    tok_offset = (token_ids % seg_len).astype(jnp.float32)
    places = jnp.dot(tok_owner, seg_depth, precision=TOP_PRECISION) * seg_len + tok_offset
    return (places, jnp.dot(tok_owner, reach_table, precision=TOP_PRECISION), tok_owner)


def rope_tables(places):
    half_dim = HEAD_DIM // 2
    inverse = ROPE_BASE ** (-jnp.arange(half_dim, dtype=jnp.float32) * 2.0 / HEAD_DIM)
    angles = places[:, None] * inverse[None, :]
    cosine_table = jnp.concatenate([jnp.cos(angles), jnp.cos(angles)], axis=1)
    sine_values = jnp.concatenate([jnp.sin(angles), jnp.sin(angles)], axis=1)
    return (cosine_table, sine_values)


def apply_rotary(values, cosine_table, sine_values):
    half_dim = values.shape[-1] // 2
    turned = jnp.concatenate([-values[..., half_dim:], values[..., :half_dim]], axis=-1)
    return values * cosine_table[:, None, :] + turned * sine_values[:, None, :]


def norm_scale(values):
    return lax.rsqrt(jnp.mean(values * values, axis=-1, keepdims=True) + EPSILON)


def add_tuples(first_tuple, second_tuple):
    return tuple(
        (left_part + right_part for left_part, right_part in zip(first_tuple, second_tuple))
    )


def expert_work(rows, row_grads, gate_up_w, down_w, down_form):
    gate_up = jnp.einsum("ecd,edsf->ecsf", rows, gate_up_w, preferred_element_type=jnp.float32)
    gate_pre = gate_up[:, :, 0]
    up_pre = gate_up[:, :, 1]
    sigmoid = jax.nn.sigmoid(gate_pre)
    activ_low = (gate_pre * sigmoid * up_pre).astype(jnp.bfloat16)
    expert_out = jnp.einsum(
        "ecf," + down_form + "->ecd", activ_low, down_w, preferred_element_type=jnp.float32
    )
    activ_grad = jnp.einsum(
        "ecd," + down_form + "->ecf", row_grads, down_w, preferred_element_type=jnp.float32
    )
    gate_grad = activ_grad * up_pre * sigmoid * (1.0 + gate_pre * (1.0 - sigmoid))
    up_grad = activ_grad * gate_pre * sigmoid
    gate_up_grad = jnp.stack([gate_grad, up_grad], axis=2).astype(jnp.bfloat16)
    row_input_grad = jnp.einsum(
        "ecsf,edsf->ecd", gate_up_grad, gate_up_w, preferred_element_type=jnp.float32
    )
    grad_gate_up = jnp.einsum(
        "ecd,ecsf->edsf", rows, gate_up_grad, preferred_element_type=jnp.float32
    )
    grad_down = jnp.einsum(
        "ecf,ecd->" + down_form, activ_low, row_grads, preferred_element_type=jnp.float32
    )
    return (expert_out, row_input_grad, grad_gate_up, grad_down)


def body(
    hidden_in,
    parents,
    routes,
    attn_gain,
    w_query,
    key_projection,
    value_projection,
    w_out,
    moe_gain,
    w_router,
    w_gate_up,
    w_down,
    d_out,
):
    experts = w_gate_up.shape[0]
    gathered = (
        lax.all_gather(attn_gain, "fsdp", axis=0, tiled=True),
        lax.all_gather(w_query, "fsdp", axis=0, tiled=True),
        lax.all_gather(key_projection, "fsdp", axis=0, tiled=True),
        lax.all_gather(value_projection, "fsdp", axis=0, tiled=True),
        lax.all_gather(w_out, "fsdp", axis=1, tiled=True),
        lax.all_gather(moe_gain, "fsdp", axis=0, tiled=True),
        lax.all_gather(w_router, "fsdp", axis=0, tiled=True),
        lax.all_gather(w_gate_up, "fsdp", axis=1, tiled=True),
        lax.all_gather(w_down, "fsdp", axis=2, tiled=True),
    )
    gate_up_full = gathered[7]
    down_full = gathered[8]
    down_form = "efd"
    gain_one = gathered[0].astype(jnp.float32)
    query_full = gathered[1]
    key_full = gathered[2]
    value_full = gathered[3]
    out_full = gathered[4]
    gain_two = gathered[5].astype(jnp.float32)
    router_full = gathered[6]
    micro_count = hidden_in.shape[0]
    local_rows = hidden_in.shape[2]
    model_width = hidden_in.shape[3]
    top_count = routes.shape[3]
    kv_heads = key_projection.shape[1] // HEAD_DIM
    q_heads = w_query.shape[1] // HEAD_DIM
    group_size = q_heads // kv_heads
    tree_len = local_rows * lax.axis_size("ctx")
    row_start = lax.axis_index("ctx") * local_rows
    capacity = CAP
    expert_ids = jnp.arange(experts, dtype=jnp.int32)
    outputs = []
    input_grads = []
    totals = None
    for batch_index in range(micro_count):
        tree_places, reach_rows, tok_owner = tree_tables(parents[batch_index, 0], tree_len)
        local_places = lax.dynamic_slice_in_dim(tree_places, row_start, local_rows, 0)
        local_reach = lax.dynamic_slice_in_dim(reach_rows, row_start, local_rows, 0)
        allowed = (jnp.dot(local_reach, tok_owner.T, precision=TOP_PRECISION) > 0.5) & (
            tree_places[None, :] <= local_places[:, None]
        )
        cosine_table, sine_values = rope_tables(local_places)
        inputs = hidden_in[batch_index, 0].astype(jnp.float32)
        scale_one = norm_scale(inputs)
        first_normed = (inputs * scale_one * gain_one).astype(jnp.bfloat16)
        query_unrotated = jnp.dot(
            first_normed, query_full, preferred_element_type=jnp.float32
        ).reshape(local_rows, q_heads, HEAD_DIM)
        key_unrotated = jnp.dot(first_normed, key_full, preferred_element_type=jnp.float32).reshape(
            local_rows, kv_heads, HEAD_DIM
        )
        value_reduced = jnp.dot(
            first_normed, value_full, preferred_element_type=jnp.float32
        ).astype(jnp.bfloat16)
        query_reduced = (
            apply_rotary(query_unrotated, cosine_table, sine_values)
            .astype(jnp.bfloat16)
            .reshape(local_rows, kv_heads, group_size, HEAD_DIM)
        )
        key_low = (
            apply_rotary(key_unrotated, cosine_table, sine_values)
            .astype(jnp.bfloat16)
            .reshape(local_rows, kv_heads * HEAD_DIM)
        )
        tree_keys, tree_values = (
            lax.all_gather(key_low, "ctx", axis=0, tiled=True),
            lax.all_gather(value_reduced, "ctx", axis=0, tiled=True),
        )
        tree_keys = tree_keys.reshape(tree_len, kv_heads, HEAD_DIM)
        tree_values = tree_values.reshape(tree_len, kv_heads, HEAD_DIM)

        def masked_scores():
            raw_scores = jnp.einsum(
                "qhjd,khd->hjqk", query_reduced, tree_keys, preferred_element_type=jnp.float32
            )
            return jnp.where(allowed[None, None], raw_scores * SCORE_SCALE, -1e30)

        scores = masked_scores()
        top_score = jnp.max(scores, axis=-1, keepdims=True)
        log_total = top_score + jnp.log(
            jnp.sum(jnp.exp(scores - top_score), axis=-1, keepdims=True)
        )
        probs_low = jnp.exp(scores - log_total).astype(jnp.bfloat16)
        head_out = jnp.einsum(
            "hjqk,khd->qhjd", probs_low, tree_values, preferred_element_type=jnp.float32
        )
        head_low = head_out.reshape(local_rows, q_heads * HEAD_DIM).astype(jnp.bfloat16)
        attn_part = jnp.dot(head_low, out_full, preferred_element_type=jnp.float32)
        attended = lax.psum(attn_part.astype(jnp.bfloat16), "tp").astype(jnp.float32)
        mixed = inputs + RESIDUAL_SCALE * attended
        scale_two = norm_scale(mixed)
        normed_two = (mixed * scale_two * gain_two).astype(jnp.bfloat16)
        logits = jnp.dot(normed_two, router_full, preferred_element_type=jnp.float32)
        chosen_ids = routes[batch_index, 0]
        picked = (chosen_ids[:, :, None] == expert_ids[None, None, :]).astype(jnp.float32)
        chosen = jnp.sum(picked * logits[:, None, :], axis=2)
        gates = jax.nn.softmax(chosen, axis=1)
        flat_ids = chosen_ids.reshape(-1)
        flat_hot = (flat_ids[:, None] == expert_ids[None, :]).astype(jnp.int32)
        slots = jnp.sum((jnp.cumsum(flat_hot, axis=0) - flat_hot) * flat_hot, axis=1)
        targets = flat_ids * capacity + slots
        sources = (
            jnp.zeros((experts * capacity,), jnp.int32)
            .at[targets]
            .set(jnp.arange(local_rows * top_count, dtype=jnp.int32) // top_count)
        )
        filled = jnp.zeros((experts * capacity, 1), jnp.bfloat16).at[targets].set(1)
        dispatched = (normed_two[sources] * filled).reshape(experts, capacity, model_width)
        grad_out = d_out[batch_index, 0].astype(jnp.float32)
        grad_moe = RESIDUAL_SCALE * grad_out
        entry_grad = (
            (gates[:, :, None] * grad_moe[:, None, :])
            .astype(jnp.bfloat16)
            .reshape(local_rows * top_count, model_width)
        )
        slot_grad = (
            jnp.zeros((experts * capacity, model_width), jnp.bfloat16)
            .at[targets]
            .set(entry_grad)
            .reshape(experts, capacity, model_width)
        )
        expert_out, slot_input_grad, grad_gate_up, grad_down = expert_work(
            dispatched, slot_grad, gate_up_full, down_full, down_form
        )
        entry_out = expert_out.reshape(experts * capacity, model_width)[targets].reshape(
            local_rows, top_count, model_width
        )
        moe_part = jnp.sum(gates[:, :, None] * entry_out, axis=1)
        moe_sum = lax.psum(moe_part.astype(jnp.bfloat16), "tp").astype(jnp.float32)
        outputs.append(mixed + RESIDUAL_SCALE * moe_sum)
        gate_grad_part = jnp.sum(grad_moe[:, None, :] * entry_out, axis=2)
        expert_input_grad = jnp.sum(
            slot_input_grad.reshape(experts * capacity, model_width)[targets].reshape(
                local_rows, top_count, model_width
            ),
            axis=1,
        )
        expert_input_grad, gate_grads = (
            lax.psum(expert_input_grad.astype(jnp.bfloat16), "tp").astype(jnp.float32),
            lax.psum(gate_grad_part.astype(jnp.bfloat16), "tp").astype(jnp.float32),
        )
        chosen_grad = gates * (gate_grads - jnp.sum(gates * gate_grads, axis=1, keepdims=True))
        logit_grad = jnp.sum(picked * chosen_grad[:, :, None], axis=1).astype(jnp.bfloat16)
        normed_two_grad = expert_input_grad + jnp.einsum(
            "te,de->td", logit_grad, router_full, preferred_element_type=jnp.float32
        )
        grad_router = jnp.einsum(
            "td,te->de", normed_two, logit_grad, preferred_element_type=jnp.float32
        )
        unit_two = mixed * scale_two
        grad_gain_two = jnp.sum(normed_two_grad * unit_two, axis=0)
        scaled_two = normed_two_grad * gain_two
        mixed_grad = grad_out + scale_two * (
            scaled_two - unit_two * jnp.mean(scaled_two * unit_two, axis=-1, keepdims=True)
        )
        attn_grad = (RESIDUAL_SCALE * mixed_grad).astype(jnp.bfloat16)
        grad_out_proj = jnp.einsum(
            "tc,td->cd", head_low, attn_grad, preferred_element_type=jnp.float32
        )
        head_grad = (
            jnp.einsum("td,cd->tc", attn_grad, out_full, preferred_element_type=jnp.float32)
            .astype(jnp.bfloat16)
            .reshape(local_rows, kv_heads, group_size, HEAD_DIM)
        )
        scores = masked_scores()
        probs = jnp.exp(scores - log_total)
        probs_low = probs.astype(jnp.bfloat16)
        prob_grad = jnp.einsum(
            "qhjd,khd->hjqk", head_grad, tree_values, preferred_element_type=jnp.float32
        )
        value_grad = jnp.einsum(
            "hjqk,qhjd->khd", probs_low, head_grad, preferred_element_type=jnp.float32
        )
        score_grad = (
            SCORE_SCALE * probs * (prob_grad - jnp.sum(probs * prob_grad, axis=-1, keepdims=True))
        ).astype(jnp.bfloat16)
        query_grad = jnp.einsum(
            "hjqk,khd->qhjd", score_grad, tree_keys, preferred_element_type=jnp.float32
        ).reshape(local_rows, q_heads, HEAD_DIM)
        key_grad = jnp.einsum(
            "hjqk,qhjd->khd", score_grad, query_reduced, preferred_element_type=jnp.float32
        )
        key_grad, value_grad = (
            lax.psum_scatter(
                key_grad.reshape(tree_len, kv_heads * HEAD_DIM).astype(jnp.bfloat16),
                "ctx",
                scatter_dimension=0,
                tiled=True,
            ).astype(jnp.float32),
            lax.psum_scatter(
                value_grad.reshape(tree_len, kv_heads * HEAD_DIM).astype(jnp.bfloat16),
                "ctx",
                scatter_dimension=0,
                tiled=True,
            ).astype(jnp.float32),
        )
        query_pre_grad = (
            apply_rotary(query_grad, cosine_table, -sine_values)
            .astype(jnp.bfloat16)
            .reshape(local_rows, q_heads * HEAD_DIM)
        )
        key_pre_grad = (
            apply_rotary(
                key_grad.reshape(local_rows, kv_heads, HEAD_DIM), cosine_table, -sine_values
            )
            .astype(jnp.bfloat16)
            .reshape(local_rows, kv_heads * HEAD_DIM)
        )
        value_pre_grad = value_grad.astype(jnp.bfloat16)
        normed_one_grad = jnp.einsum(
            "tc,dc->td", query_pre_grad, query_full, preferred_element_type=jnp.float32
        )
        normed_one_grad = normed_one_grad + jnp.einsum(
            "tc,dc->td", key_pre_grad, key_full, preferred_element_type=jnp.float32
        )
        normed_one_grad = normed_one_grad + jnp.einsum(
            "tc,dc->td", value_pre_grad, value_full, preferred_element_type=jnp.float32
        )
        grad_query = jnp.einsum(
            "td,tc->dc", first_normed, query_pre_grad, preferred_element_type=jnp.float32
        )
        grad_key = jnp.einsum(
            "td,tc->dc", first_normed, key_pre_grad, preferred_element_type=jnp.float32
        )
        grad_value = jnp.einsum(
            "td,tc->dc", first_normed, value_pre_grad, preferred_element_type=jnp.float32
        )
        normed_one_grad = lax.psum(normed_one_grad.astype(jnp.bfloat16), "tp").astype(jnp.float32)
        unit_one = inputs * scale_one
        grad_gain_one = jnp.sum(normed_one_grad * unit_one, axis=0)
        scaled_one = normed_one_grad * gain_one
        input_grads.append(
            mixed_grad
            + scale_one
            * (scaled_one - unit_one * jnp.mean(scaled_one * unit_one, axis=-1, keepdims=True))
        )
        piece = (
            grad_gain_one,
            grad_query,
            grad_key,
            grad_value,
            grad_out_proj,
            grad_gain_two,
            grad_router,
            grad_gate_up,
            grad_down,
        )
        totals = piece if batch_index == 0 else add_tuples(totals, piece)
    summed = (
        lax.psum_scatter(totals[0], ("fsdp", "ctx"), scatter_dimension=0, tiled=True),
        lax.psum_scatter(totals[1], ("fsdp", "ctx"), scatter_dimension=0, tiled=True),
        lax.psum_scatter(totals[2], ("fsdp", "ctx"), scatter_dimension=0, tiled=True),
        lax.psum_scatter(totals[3], ("fsdp", "ctx"), scatter_dimension=0, tiled=True),
        lax.psum_scatter(totals[4], ("fsdp", "ctx"), scatter_dimension=1, tiled=True),
        lax.psum_scatter(totals[5], ("fsdp", "ctx"), scatter_dimension=0, tiled=True),
        lax.psum_scatter(totals[6], ("fsdp", "ctx"), scatter_dimension=0, tiled=True),
        lax.psum_scatter(totals[7], ("fsdp", "ctx"), scatter_dimension=1, tiled=True),
        lax.psum_scatter(totals[8], ("fsdp", "ctx"), scatter_dimension=2, tiled=True),
    )
    shares = (
        lax.all_gather(summed[0].astype(jnp.bfloat16), "ctx", axis=0, tiled=True).astype(
            jnp.float32
        ),
        lax.all_gather(summed[1].astype(jnp.bfloat16), "ctx", axis=0, tiled=True).astype(
            jnp.float32
        ),
        lax.all_gather(summed[2].astype(jnp.bfloat16), "ctx", axis=0, tiled=True).astype(
            jnp.float32
        ),
        lax.all_gather(summed[3].astype(jnp.bfloat16), "ctx", axis=0, tiled=True).astype(
            jnp.float32
        ),
        lax.all_gather(summed[4].astype(jnp.bfloat16), "ctx", axis=1, tiled=True).astype(
            jnp.float32
        ),
        lax.all_gather(summed[5].astype(jnp.bfloat16), "ctx", axis=0, tiled=True).astype(
            jnp.float32
        ),
        lax.all_gather(summed[6].astype(jnp.bfloat16), "ctx", axis=0, tiled=True).astype(
            jnp.float32
        ),
        lax.all_gather(summed[7].astype(jnp.bfloat16), "ctx", axis=1, tiled=True).astype(
            jnp.float32
        ),
        lax.all_gather(summed[8].astype(jnp.bfloat16), "ctx", axis=2, tiled=True).astype(
            jnp.float32
        ),
    )
    layer_out = jnp.stack(outputs, axis=0)[:, None]
    d_hidden = jnp.stack(input_grads, axis=0)[:, None]
    return (
        layer_out,
        d_hidden,
        shares[0],
        shares[1],
        shares[2],
        shares[3],
        shares[4],
        shares[5],
        shares[6],
        shares[7],
        shares[8],
    )


def dot(left, right, left_dim=1, right_dim=0):
    return lax.dot_general(
        left, right, (((left_dim,), (right_dim,)), ((), ())), preferred_element_type=jnp.float32
    )


def vmem_params(count=1):
    return pltpu.CompilerParams(
        dimension_semantics=("arbitrary",) * count, vmem_limit_bytes=60 * 1024 * 1024
    )


def attend_kernel(seen_ref, query_ref, kv0, kv1, kv2, kv3, out_ref, probs_ref):
    blocks = (kv0, kv1, kv2, kv3)
    micro = seen_ref.shape[0]
    rows = query_ref.shape[0] // micro
    kv_heads = kv0.shape[1] // (2 * HEAD_DIM)
    group = query_ref.shape[1] // HEAD_DIM // kv_heads
    shape = (group * rows, rows)
    causal = (
        lax.broadcasted_iota(jnp.int32, shape, 1)
        <= lax.broadcasted_iota(jnp.int32, shape, 0) % rows
    )
    for m in range(micro):
        span = pl.ds(m * rows, rows)
        whole = query_ref[span, :]
        pieces = []
        for g in range(kv_heads):
            lanes = slice(g * HEAD_DIM, (g + 1) * HEAD_DIM)
            query = jnp.concatenate(
                [
                    whole[:, (g * group + h) * HEAD_DIM : (g * group + h + 1) * HEAD_DIM]
                    for h in range(group)
                ],
                axis=0,
            )
            parts = []
            for r in range(4):
                part = dot(query, blocks[r][span, :][:, lanes], 1, 1) * SCORE_SCALE
                if r == 0:
                    part = jnp.where(causal, part, -1e30)
                else:
                    part = jnp.where(seen_ref[m, r] > 0, part, -1e30)
                parts.append(part)
            scores = jnp.concatenate(parts, axis=1)
            powers = jnp.exp(scores - jnp.max(scores, axis=1, keepdims=True))
            probs = powers / jnp.sum(powers, axis=1, keepdims=True)
            probs_ref[m * kv_heads + g] = probs
            low = probs.astype(jnp.bfloat16)
            values = jnp.concatenate(
                [
                    blocks[r][span, :][:, (kv_heads + g) * HEAD_DIM : (kv_heads + g + 1) * HEAD_DIM]
                    for r in range(4)
                ],
                axis=0,
            )
            mixed = dot(low, values)
            pieces += [mixed[h * rows : (h + 1) * rows] for h in range(group)]
        out_ref[span, :] = jnp.concatenate(pieces, axis=1).astype(jnp.bfloat16)


def attend_back_kernel(
    query_ref, grad_ref, kv0, kv1, kv2, kv3, probs_ref, query_grad_ref, kv_grad_ref
):
    blocks = (kv0, kv1, kv2, kv3)
    kv_heads = kv0.shape[1] // (2 * HEAD_DIM)
    micro = probs_ref.shape[0] // kv_heads
    rows = query_ref.shape[0] // micro
    group = query_ref.shape[1] // HEAD_DIM // kv_heads
    for m in range(micro):
        span = pl.ds(m * rows, rows)
        whole = query_ref[span, :]
        whole_grad = grad_ref[span, :]
        pieces = []
        key_grads = []
        value_grads = []
        for g in range(kv_heads):

            def heads(source):
                return jnp.concatenate(
                    [
                        source[:, (g * group + h) * HEAD_DIM : (g * group + h + 1) * HEAD_DIM]
                        for h in range(group)
                    ],
                    axis=0,
                )

            query = heads(whole)
            head_grad = heads(whole_grad)
            keys = jnp.concatenate(
                [blocks[r][span, :][:, g * HEAD_DIM : (g + 1) * HEAD_DIM] for r in range(4)], axis=0
            )
            values = jnp.concatenate(
                [
                    blocks[r][span, :][:, (kv_heads + g) * HEAD_DIM : (kv_heads + g + 1) * HEAD_DIM]
                    for r in range(4)
                ],
                axis=0,
            )
            probs = probs_ref[m * kv_heads + g]
            prob_grad = dot(head_grad, values, 1, 1)
            inner = jnp.sum(probs * prob_grad, axis=1, keepdims=True)
            score_grad = (SCORE_SCALE * probs * (prob_grad - inner)).astype(jnp.bfloat16)
            value_grads.append(dot(probs.astype(jnp.bfloat16), head_grad, 0, 0))
            key_grads.append(dot(score_grad, query, 0, 0))
            query_grad = dot(score_grad, keys)
            pieces += [query_grad[h * rows : (h + 1) * rows] for h in range(group)]
        query_grad_ref[span, :] = jnp.concatenate(pieces, axis=1)
        joined = jnp.concatenate(key_grads + value_grads, axis=1).astype(jnp.bfloat16)
        for r in range(4):
            kv_grad_ref[r, span, :] = joined[r * rows : (r + 1) * rows]


def expert_kernel(
    place_ref,
    near_ref,
    far_ref,
    near_out_ref,
    far_out_ref,
    rank_ref,
    gate_ref,
    gate_up_ref,
    down_ref,
    other_ref,
    *rest,
):
    if len(rest) == 12:
        held_out, held_grad = rest[:2]
        rest = rest[2:]
    else:
        held_out = held_grad = None
    out_ref, grad_ref, slots_ref, gate_grad_ref, rows_buf, grads_buf, moe_buf, back_buf, hot_buf, gate_buf = rest
    half = down_ref.shape[-1]
    width = down_ref.shape[-2]
    quarter = [place_ref[1] ^ r for r in range(4)]
    iota = lax.broadcasted_iota(jnp.int32, (CAP, 128), 0)

    @pl.when(pl.program_id(0) == 0)
    def _():
        if held_out is None:
            out_ref[...] = jnp.zeros_like(out_ref)
            grad_ref[...] = jnp.zeros_like(grad_ref)
        else:
            out_ref[...] = held_out[...]
            grad_ref[...] = held_grad[...]

    for b in range(4):
        hot = jnp.concatenate(
            [
                jnp.where(iota == rank_ref[quarter[r], 0, pl.ds(b, 1), :], 1.0, 0.0)
                for r in range(4)
            ],
            axis=0,
        )
        gates = jnp.concatenate(
            [
                jnp.broadcast_to(gate_ref[quarter[r], 0, pl.ds(b, 1), :], (CAP, 128))
                for r in range(4)
            ],
            axis=0,
        )
        gate_buf[b] = jnp.broadcast_to(jnp.sum(hot * gates, axis=1, keepdims=True), (4 * CAP, 128))
        low = hot.astype(jnp.bfloat16)
        hot_buf[b] = low
        span = pl.ds((b % 2) * 128, 128)
        for part in range(2):
            keep = pl.ds(part * half, half)
            if b < 2:
                rows, grads = near_ref[span, keep], near_out_ref[span, keep]
            else:
                swap = pl.ds((1 - part) * half, half)
                rows, grads = far_ref[span, swap], far_out_ref[span, swap]
            rows_buf[b, :, keep] = dot(low, rows).astype(jnp.bfloat16)
            grads_buf[b, :, keep] = dot(low, grads).astype(jnp.bfloat16)
    for r in range(4):
        q = quarter[r]
        slot = slice(r * CAP, (r + 1) * CAP)
        rows = jnp.concatenate([rows_buf[b, slot, :] for b in range(4)], axis=0)
        grads = jnp.concatenate([grads_buf[b, slot, :] for b in range(4)], axis=0)
        gate = jnp.concatenate([gate_buf[b, slot, :] for b in range(4)], axis=0)
        near_w = jnp.concatenate([gate_up_ref[q, 0, 0], gate_up_ref[q, 0, 1]], axis=1)
        far_w = jnp.concatenate([other_ref[q, 0, :half, :], other_ref[q, 0, half : 2 * half, :]], axis=1)
        near_down = down_ref[0, q, 0]
        far_down = jnp.concatenate(
            [
                other_ref[q, 0, 2 * half + j * width : 2 * half + (j + 1) * width, :]
                for j in range(half // 128)
            ],
            axis=1,
        )
        gate_up = dot(rows[:, :half], near_w) + dot(rows[:, half:], far_w)
        gate_pre = gate_up[:, :width]
        up_pre = gate_up[:, width:]
        sigmoid = 1.0 / (1.0 + jnp.exp(-gate_pre))
        activ = (gate_pre * sigmoid * up_pre).astype(jnp.bfloat16)
        pulled = RESIDUAL_SCALE * (
            dot(grads[:, :half], near_down, 1, 1) + dot(grads[:, half:], far_down, 1, 1)
        )
        activ_wide = activ.astype(jnp.float32)
        gate_grad = jnp.sum(activ_wide * pulled, axis=1, keepdims=True)
        activ_grad = pulled * gate
        gate_pre_grad = activ_grad * up_pre * sigmoid * (1.0 + gate_pre * (1.0 - sigmoid))
        up_pre_grad = activ_grad * gate_pre * sigmoid
        both = jnp.concatenate([gate_pre_grad, up_pre_grad], axis=1).astype(jnp.bfloat16)
        slots_ref[q, 0, :, : 2 * width] = both
        slots_ref[q, 0, :, 2 * width :] = (activ_wide * gate * RESIDUAL_SCALE).astype(jnp.bfloat16)
        for part, (wide, low_w) in enumerate(((near_w, near_down), (far_w, far_down))):
            keep = pl.ds(part * half, half)
            made = dot(activ, low_w)
            back = dot(both, wide, 1, 1)
            for b in range(4):
                piece = slice(b * CAP, (b + 1) * CAP)
                scale = jnp.concatenate([gate[piece]] * (half // 128), axis=1)
                moe_buf[b, slot, keep] = (made[piece] * scale).astype(jnp.bfloat16)
                back_buf[b, slot, keep] = back[piece].astype(jnp.bfloat16)
        for b in range(4):
            hot = hot_buf[b, slot, :].astype(jnp.float32)
            gate_grad_ref[q, 0, pl.ds(b, 1), :] = jnp.sum(
                hot * gate_grad[b * CAP : (b + 1) * CAP], axis=0, keepdims=True
            )
    for b in range(4):
        span = pl.ds(b * 128, 128)
        out_ref[span, :] += dot(hot_buf[b], moe_buf[b], 0, 0)
        grad_ref[span, :] += dot(hot_buf[b], back_buf[b], 0, 0)


def run_experts(place, near, far, near_out, far_out, rank, gate, gate_up, down, others, held, first):
    _, steps, packed, lanes = others.shape
    quarters, each, sides, half, width = gate_up.shape
    tokens = 2 * near_out.shape[0]
    full = 2 * half

    def fixed(array):
        return pl.BlockSpec(array.shape, lambda j, sp: (0,) * array.ndim)

    table = pl.BlockSpec((quarters, 1, 4, 128), lambda j, sp: (0, first + j, 0, 0))
    in_specs = [
        fixed(near),
        fixed(far),
        fixed(near_out),
        fixed(far_out),
        table,
        table,
        pl.BlockSpec((quarters, 1, sides, half, width), lambda j, sp: (0, first + j, 0, 0, 0)),
        pl.BlockSpec((1, quarters, 1, width, half), lambda j, sp: (sp[0], 0, first + j, 0, 0)),
        pl.BlockSpec((quarters, 1, packed, lanes), lambda j, sp: (0, j, 0, 0)),
    ]
    operands = [place, near, far, near_out, far_out, rank, gate, gate_up, down, others]
    aliases = {}
    total = jax.ShapeDtypeStruct((tokens, full), jnp.float32)
    if held is not None:
        in_specs += [fixed(held[0]), fixed(held[1])]
        aliases = {len(operands): 0, len(operands) + 1: 1}
        operands += list(held)
    slots = jax.ShapeDtypeStruct((quarters, steps, 4 * CAP, 3 * width), jnp.bfloat16)
    gate_grads = jax.ShapeDtypeStruct((quarters, steps, 4, 128), jnp.float32)
    return pl.pallas_call(
        expert_kernel,
        out_shape=(total, total, slots, gate_grads),
        grid_spec=pltpu.PrefetchScalarGridSpec(
            num_scalar_prefetch=1,
            grid=(steps,),
            in_specs=in_specs,
            out_specs=(
                pl.BlockSpec(total.shape, lambda j, sp: (0, 0)),
                pl.BlockSpec(total.shape, lambda j, sp: (0, 0)),
                pl.BlockSpec((quarters, 1, 4 * CAP, 3 * width), lambda j, sp: (0, j, 0, 0)),
                pl.BlockSpec((quarters, 1, 4, 128), lambda j, sp: (0, j, 0, 0)),
            ),
            scratch_shapes=[pltpu.VMEM((4, 4 * CAP, full), jnp.bfloat16)] * 4
            + [
                pltpu.VMEM((4, 4 * CAP, 128), jnp.bfloat16),
                pltpu.VMEM((4, 4 * CAP, 128), jnp.float32),
            ],
        ),
        input_output_aliases=aliases,
        compiler_params=vmem_params(),
        name="experts",
    )(*operands)


def weight_grad_kernel(place_ref, *refs):
    rows_ref, grads_ref, slots_ref, rank_ref = refs[:4]
    gate_up_ref, down_ref, mark_ref, rows_buf, grads_buf = refs[-5:]
    mark_ref[...] = jnp.zeros_like(mark_ref)
    half = down_ref.shape[-1]
    width = down_ref.shape[-2]
    side = pl.program_id(1)
    iota = lax.broadcasted_iota(jnp.int32, (CAP, 128), 0)
    for k in range(4):
        for b in range(4):
            hot = jnp.concatenate(
                [
                    jnp.where(iota == rank_ref[0, q, 0, pl.ds(4 * k + b, 1), :], 1.0, 0.0)
                    for q in range(4)
                ],
                axis=0,
            ).astype(jnp.bfloat16)
            span = pl.ds(b * 128, 128)
            spot = 4 * k + (b ^ (2 * side))
            rows_buf[spot] = dot(hot, rows_ref[k, span, :]).astype(jnp.bfloat16)
            grads_buf[spot] = dot(hot, grads_ref[k, span, :]).astype(jnp.bfloat16)
    for q in range(4):
        slot = slice(q * CAP, (q + 1) * CAP)
        rows = jnp.concatenate([rows_buf[n, slot, :] for n in range(16)], axis=0)
        grads = jnp.concatenate([grads_buf[n, slot, :] for n in range(16)], axis=0)
        taken = jnp.concatenate([slots_ref[0, k, q, 0] for k in range(4)], axis=0)
        made = dot(rows, taken[:, : 2 * width], 0, 0)
        gate_up_ref[0, q, 0, pl.ds(0, half, stride=2), :] = made[:, :width]
        gate_up_ref[0, q, 0, pl.ds(1, half, stride=2), :] = made[:, width:]
        down_ref[0, q, 0] = dot(taken[:, 2 * width :], grads, 0, 0)


def run_weight_grads(place, rows, grads, slots, rank, held, first, each, mark):
    sides, _, quarters, steps, slot_count, lanes = slots.shape
    width = lanes // 3
    half = rows.shape[-1]
    in_specs = [
        pl.BlockSpec(rows.shape, lambda j, a, sp: (0, 0, 0)),
        pl.BlockSpec(rows.shape, lambda j, a, sp: (0, 0, 0)),
        pl.BlockSpec(
            (1, 4, quarters, 1, slot_count, lanes),
            lambda j, a, sp: (sp[0] ^ a, 0, 0, j, 0, 0),
        ),
        pl.BlockSpec((1, quarters, 1, 16, 128), lambda j, a, sp: (a, 0, first + j, 0, 0)),
        pl.BlockSpec(memory_space=pl.ANY),
    ]
    operands = [place, rows, grads, slots, rank, mark]
    aliases = {}
    if held is not None:
        in_specs += [pl.BlockSpec(memory_space=pl.ANY)] * 2
        aliases = {len(operands): 0, len(operands) + 1: 1}
        operands += list(held[:2])
    return pl.pallas_call(
        weight_grad_kernel,
        out_shape=(
            jax.ShapeDtypeStruct((sides, quarters, each, 2 * half, width), jnp.float32),
            jax.ShapeDtypeStruct((sides, quarters, each, width, half), jnp.float32),
            jax.ShapeDtypeStruct((8, 128), jnp.float32),
        ),
        grid_spec=pltpu.PrefetchScalarGridSpec(
            num_scalar_prefetch=1,
            grid=(steps, sides),
            in_specs=in_specs,
            out_specs=(
                pl.BlockSpec(
                    (1, quarters, 1, 2 * half, width),
                    lambda j, a, sp: (sp[0] ^ a, 0, first + j, 0, 0),
                ),
                pl.BlockSpec(
                    (1, quarters, 1, width, half),
                    lambda j, a, sp: (sp[0] ^ a, 0, first + j, 0, 0),
                ),
                pl.BlockSpec((8, 128), lambda j, a, sp: (0, 0)),
            ),
            scratch_shapes=[pltpu.VMEM((16, 4 * CAP, half), jnp.bfloat16)] * 2,
        ),
        input_output_aliases=aliases,
        compiler_params=vmem_params(2),
        name="weight_grads",
    )(*operands)


def swap_halves(values):
    half = values.shape[-1] // 2
    return jnp.concatenate([values[..., half:], values[..., :half]], axis=-1)


def turn_heads(values):
    half_dim = HEAD_DIM // 2
    lane = lax.broadcasted_iota(jnp.int32, values.shape, 1) % HEAD_DIM
    return jnp.where(
        lane < half_dim,
        -jnp.roll(values, -half_dim, axis=1),
        jnp.roll(values, half_dim, axis=1),
    )


def fast_body(
    hidden_in,
    parents,
    routes,
    attn_gain,
    w_query,
    key_projection,
    value_projection,
    w_out,
    moe_gain,
    w_router,
    w_gate_up,
    w_down,
    d_out,
):
    low, wide = jnp.bfloat16, jnp.float32
    x_pos = lax.axis_index("fsdp")
    c_pos = lax.axis_index("ctx")
    z_pos = lax.axis_index("tp")
    tp_size = lax.axis_size("tp")
    micro, _, rows, model = hidden_in.shape
    half = model // 2
    tokens = micro * rows
    experts = w_gate_up.shape[0]
    mine = experts // 2
    each = mine // 4
    width = w_down.shape[1]
    q_cols = w_query.shape[1]
    k_cols = key_projection.shape[1]
    chunks = ((0, 2), (2, 2), (4, 1))

    def across(value):
        return lax.ppermute(value, "fsdp", [(0, 1), (1, 0)])

    def beside(value):
        return lax.ppermute(value, "ctx", [(i, i ^ 1) for i in range(4)])

    def along(value):
        return lax.ppermute(value, "ctx", [(i, i ^ 2) for i in range(4)])

    def from_tp(value, step):
        return lax.ppermute(
            value, "tp", [((i + step) % tp_size, i) for i in range(tp_size)]
        )

    def all_ctx(value):
        nearby = beside(value)
        distant = along(value)
        return [value, nearby, distant, beside(distant)]

    def after(value, *earlier):
        return lax.optimization_barrier((value, *earlier))[0]

    def own_first(value):
        return jnp.where(x_pos == 0, value, swap_halves(value))

    def ctx_join(first, second, axis):
        return jnp.where(
            c_pos % 2 == 0,
            jnp.concatenate([first, second], axis=axis),
            jnp.concatenate([second, first], axis=axis),
        )

    def sum_tp(value, between=None):
        part = value.shape[0] // tp_size

        def piece(step):
            return lax.dynamic_slice_in_dim(value, ((z_pos + step) % tp_size) * part, part, 0)

        total = piece(0).astype(wide)
        for step in range(1, tp_size):
            total = total + from_tp(piece(tp_size - step), step).astype(wide)
        total = total.astype(low)
        if between is not None:
            total, *kept = between(total)
        found = [total] + [from_tp(total, step) for step in range(1, tp_size)]
        result = lax.dynamic_slice_in_dim(
            jnp.concatenate(found + found, axis=0), ((tp_size - z_pos) % tp_size) * part, tokens, 0
        )
        return result if between is None else (result, kept)

    small = jnp.concatenate(
        [
            w_query,
            key_projection,
            value_projection,
            jnp.pad(
                jnp.concatenate([w_router, attn_gain[:, None], moe_gain[:, None]], axis=1),
                ((0, 0), (0, 128 - experts - 2)),
            ),
        ],
        axis=1,
    )
    core = c_pos % 2
    sent = across(lax.dynamic_slice_in_dim(small, core * (half // 2), half // 2, 0))
    small_far = ctx_join(sent, beside(sent), 0)
    qkv_cols = q_cols + 2 * k_cols
    qkv_full = jnp.concatenate([small[:, :qkv_cols], small_far[:, :qkv_cols]], axis=0)
    rest_full = jnp.concatenate([small[:, qkv_cols:], small_far[:, qkv_cols:]], axis=0)
    gain_one = rest_full[:, experts].astype(wide)
    gain_two = rest_full[:, experts + 1].astype(wide)
    router = jnp.where(
        x_pos == 0,
        rest_full[:, :experts],
        jnp.concatenate([rest_full[:, mine:experts], rest_full[:, :mine]], axis=1),
    )

    routes_low = jnp.pad(
        routes.reshape(tokens, -1).astype(low), ((0, 0), (0, 128 - routes.shape[-1]))
    )
    near_out = jnp.concatenate([own_first(d_out.reshape(tokens, model)), routes_low], axis=1)
    away = (1 - x_pos) * mine + c_pos * each

    def pack(first, count, base):
        gate_up_sent = (
            lax.dynamic_slice_in_dim(w_gate_up, base + first, count, 0)
            .transpose(0, 2, 1, 3)
            .reshape(count, 2 * half, width)
        )
        down_sent = (
            lax.dynamic_slice_in_dim(w_down, base + first, count, 0)
            .reshape(count, width, half // 128, 128)
            .transpose(0, 2, 1, 3)
            .reshape(count, half, 128)
        )
        return jnp.concatenate([gate_up_sent, down_sent], axis=1)

    far_zero = across(after(pack(*chunks[0], away), sent))
    down_all = w_down.reshape(2, 4, each, width, half)

    seg_ids = jnp.arange(4, dtype=jnp.int32)
    seen_rows = []
    angle_rows = []
    half_dim = HEAD_DIM // 2
    inverse = ROPE_BASE ** (-jnp.arange(half_dim, dtype=wide) * 2.0 / HEAD_DIM)
    for m in range(micro):
        current = c_pos
        reach = seg_ids == current
        for _ in range(3):
            current = jnp.sum(jnp.where(seg_ids == current, parents[m, 0], 0))
            reach = reach | (seg_ids == current)
        reach = reach.astype(jnp.int32)
        depth = jnp.sum(reach) - 1
        seen_rows.append(
            jnp.stack([jnp.sum(jnp.where(seg_ids == (c_pos ^ r), reach, 0)) for r in range(4)])
        )
        places = (depth * rows + jnp.arange(rows, dtype=jnp.int32)).astype(wide)
        angle_rows.append(places[:, None] * inverse[None, :])
    seen = jnp.stack(seen_rows)
    angles = jnp.concatenate(angle_rows, axis=0)
    turns = (q_cols + k_cols) // half_dim
    cosines = jnp.tile(jnp.cos(angles), (1, turns))
    sines = jnp.tile(jnp.sin(angles), (1, turns))

    inputs = own_first(hidden_in.reshape(tokens, model)).astype(wide)
    scale_one = norm_scale(inputs)
    unit_one = inputs * scale_one
    first_normed = (unit_one * gain_one).astype(low)
    unrotated = dot(first_normed, qkv_full)
    turned_part = unrotated[:, : q_cols + k_cols]
    rotated = (turned_part * cosines + turn_heads(turned_part) * sines).astype(low)
    query = rotated[:, :q_cols]
    key_value = jnp.concatenate(
        [rotated[:, q_cols:], unrotated[:, q_cols + k_cols :].astype(low)], axis=1
    )
    away_next, key_value = lax.optimization_barrier((away, key_value))
    blocks = all_ctx(key_value)
    pack_one = pack(*chunks[1], away_next)
    *blocks, pack_one, far_zero = lax.optimization_barrier((*blocks, pack_one, far_zero))
    far_one = across(pack_one)
    smem = pl.BlockSpec(memory_space=pltpu.SMEM)
    vmem = pl.BlockSpec(memory_space=pltpu.VMEM)
    kv_heads = k_cols // HEAD_DIM
    group = q_cols // k_cols
    head_low, probs = pl.pallas_call(
        attend_kernel,
        out_shape=(
            jax.ShapeDtypeStruct((tokens, q_cols), low),
            jax.ShapeDtypeStruct((micro * kv_heads, group * rows, 4 * rows), wide),
        ),
        in_specs=[smem] + [vmem] * 5,
        out_specs=(vmem, vmem),
        compiler_params=pltpu.CompilerParams(vmem_limit_bytes=60 * 1024 * 1024),
        name="attend",
    )(seen, query, *blocks)
    out_near = after(w_out, sent)
    out_core = lax.dynamic_slice_in_dim(out_near, core * (q_cols // 2), q_cols // 2, 0)
    out_got = across(out_core)
    out_far = ctx_join(out_got, beside(out_got), 0)
    attn_part = jnp.concatenate([dot(head_low, w_out), dot(head_low, out_far)], axis=1).astype(low)
    base_mine, away_last, attn_part = lax.optimization_barrier((x_pos * mine, away, attn_part))
    gate_up_mine = (
        lax.dynamic_slice_in_dim(w_gate_up, base_mine, mine, 0)
        .transpose(0, 2, 1, 3)
        .reshape(4, each, 2, half, width)
    )
    pack_two = pack(*chunks[2], away_last)

    def between(total):
        return lax.optimization_barrier((total, near_out, far_one))

    attended, (near_out, far_one) = sum_tp(attn_part, between)
    far_out = across(near_out)
    attended, gate_up_mine, pack_two, far_out = lax.optimization_barrier(
        (attended.astype(wide), gate_up_mine, pack_two, far_out)
    )
    mixed = inputs + RESIDUAL_SCALE * attended
    scale_two = norm_scale(mixed)
    unit_two = mixed * scale_two
    normed_two = (unit_two * gain_two).astype(low)

    expert_ids = (jnp.arange(experts, dtype=jnp.int32) + x_pos * mine) % experts
    flat_routes = routes.reshape(tokens, -1)
    named = jnp.any(flat_routes[:, :, None] == expert_ids[None, None, :], axis=1)
    logits = jnp.where(named, dot(normed_two, router), -1e30)
    powers = jnp.where(named, jnp.exp(logits - jnp.max(logits, axis=1, keepdims=True)), 0.0)
    gates = powers / jnp.sum(powers, axis=1, keepdims=True)

    gates_sent = gates[:, mine:]
    gates_high = gates_sent.astype(low)
    gates_rest = (gates_sent - gates_high.astype(wide)).astype(low)
    near = jnp.concatenate(
        [
            normed_two,
            jnp.pad(
                jnp.concatenate([gates_high, gates_rest], axis=1), ((0, 0), (0, 128 - 2 * mine))
            ),
        ],
        axis=1,
    )
    far = across(near)
    far, pack_two = lax.optimization_barrier((far, pack_two))
    far_two = across(pack_two)
    far_weights = [lax.all_gather(got, "ctx") for got in (far_zero, far_one, far_two)]
    early = lax.all_gather(
        jnp.concatenate(
            [
                jnp.concatenate([near_out[:, :half], routes_low], axis=1),
                far_out[:, half:],
            ],
            axis=0,
        ),
        "ctx",
    )
    rows_two = lax.all_gather(
        jnp.concatenate([normed_two[:, :half], far[:, half:model]], axis=0), "ctx"
    )
    far_gates = far[:, model : model + mine].astype(wide) + far[
        :, model + mine : model + 2 * mine
    ].astype(wide)
    upper = (
        lax.broadcasted_iota(jnp.int32, (rows, rows), 0)
        < lax.broadcasted_iota(jnp.int32, (rows, rows), 1)
    ).astype(low)

    def ranks(route_table, ids):
        flat = route_table.astype(jnp.int32).T
        hit = jnp.zeros((ids.shape[0], flat.shape[1]), jnp.bool_)
        for k in range(flat.shape[0]):
            hit = hit | (flat[k][None, :] == ids[:, None])
        hot = hit.astype(low).reshape(-1, rows)
        before = dot(hot, upper)
        found = jnp.where(hot > 0, before, -1.0).astype(jnp.int32)
        return found.reshape(ids.shape[0], -1, rows)

    top = routes.shape[-1]
    pair_routes = jnp.concatenate([routes_low, far_out[:, model:]], axis=0)[:, :top]
    rank_pair = ranks(pair_routes, expert_ids[:mine]).reshape(4, each, 4, rows)
    gate_pair = (
        jnp.concatenate([gates[:, :mine], far_gates], axis=0).T.reshape(4, each, 4, rows)
    )
    place = jnp.stack([x_pos, c_pos]).astype(jnp.int32)

    held = None
    slots = []
    gate_grad_parts = []
    for (first, count), others in zip(chunks, far_weights):
        moe_all, back_all, slot_part, gate_part = run_experts(
            place,
            near,
            far,
            near_out,
            far_out,
            rank_pair,
            gate_pair,
            gate_up_mine,
            down_all,
            others,
            held,
            first,
        )
        held = (moe_all, back_all)
        if first == 2:
            place, early = lax.optimization_barrier((place, early))
        slots.append(slot_part)
        gate_grad_parts.append(gate_part)
    gate_grad_all = jnp.concatenate(gate_grad_parts, axis=1).reshape(mine, 2 * tokens).T

    back_sent = jnp.concatenate(
        [
            back_all[tokens:].astype(low),
            jnp.pad(gate_grad_all[tokens:].astype(low), ((0, 0), (0, 128 - mine))),
        ],
        axis=1,
    )
    moe_far = moe_all[tokens:].astype(low)
    back_got = across(back_sent)
    back_got, moe_far, rows_two = lax.optimization_barrier((back_got, moe_far, rows_two))
    pairs = [lax.all_gather(part, ("fsdp", "ctx")).reshape(2, 4, *part.shape) for part in slots]
    back_sum = (back_all[:tokens] + swap_halves(back_got[:, :model]).astype(wide)).astype(low)
    gathered = sum_tp(
        jnp.concatenate(
            [
                back_sum,
                jnp.pad(
                    jnp.concatenate(
                        [gate_grad_all[:tokens].astype(low), back_got[:, model : model + mine]],
                        axis=1,
                    ),
                    ((0, 0), (0, 128 - experts)),
                ),
            ],
            axis=1,
        )
    )
    gathered, pairs[0] = lax.optimization_barrier((gathered, pairs[0]))
    gate_grads = gathered[:, model : model + experts].astype(wide)
    logit_grad = (gates * (gate_grads - jnp.sum(gates * gate_grads, axis=1, keepdims=True))).astype(
        low
    )
    normed_two_grad = gathered[:, :model].astype(wide) + dot(logit_grad, router, 1, 1)
    grad_out = near_out[:, :model].astype(wide)
    gain_two_part = jnp.sum(normed_two_grad * unit_two, axis=0)
    scaled_two = normed_two_grad * gain_two
    mixed_grad = grad_out + scale_two * (
        scaled_two - unit_two * jnp.mean(scaled_two * unit_two, axis=-1, keepdims=True)
    )
    attn_grad = (RESIDUAL_SCALE * mixed_grad).astype(low)

    moe_got = across(moe_far)
    moe_part = (moe_all[:tokens] + swap_halves(moe_got).astype(wide)).astype(low)
    moe_part, attn_grad = lax.optimization_barrier((moe_part, attn_grad))
    moe_part, pairs[2] = lax.optimization_barrier((moe_part, pairs[2]))
    moe_sum = lax.psum(moe_part, "tp").astype(wide)
    layer_out = own_first(mixed + RESIDUAL_SCALE * moe_sum)

    all_routes = early[:, :, half : half + top].reshape(4 * 2 * tokens, top)
    rank_all = ranks(all_routes, expert_ids).reshape(2, 4, each, 16, rows)
    def grads_of(number, held, mark):
        return run_weight_grads(
            place, rows_two, early, pairs[number], rank_all, held, chunks[number][0], each, mark
        )

    head_grad = (
        dot(attn_grad[:, :half], w_out, 1, 1) + dot(attn_grad[:, half:], out_far, 1, 1)
    ).astype(low)
    query_grad, kv_grads = pl.pallas_call(
        attend_back_kernel,
        out_shape=(
            jax.ShapeDtypeStruct((tokens, q_cols), wide),
            jax.ShapeDtypeStruct((4, tokens, 2 * k_cols), low),
        ),
        in_specs=[vmem] * 7,
        out_specs=(vmem, vmem),
        compiler_params=pltpu.CompilerParams(vmem_limit_bytes=60 * 1024 * 1024),
        name="attend_back",
    )(query, head_grad, *blocks, probs)
    near_pair = beside(jnp.stack([kv_grads[1], kv_grads[3]]))
    far_part = (kv_grads[2].astype(wide) + near_pair[1].astype(wide)).astype(low)
    kv_grad = (
        kv_grads[0].astype(wide) + near_pair[0].astype(wide) + along(far_part).astype(wide)
    )
    turned_grad = jnp.concatenate([query_grad, kv_grad[:, :k_cols]], axis=1)
    qkv_grad = jnp.concatenate(
        [turned_grad * cosines - turn_heads(turned_grad) * sines, kv_grad[:, k_cols:]], axis=1
    ).astype(low)
    normed_one_part = dot(qkv_grad, qkv_full, 1, 1).astype(low)
    grads = grads_of(0, None, jnp.zeros((8, 128), wide))

    def with_grads(total):
        return lax.optimization_barrier((total, grads[2]))

    normed_one_grad, (mark,) = sum_tp(normed_one_part, with_grads)
    grads = grads_of(1, grads, mark)
    normed_one_grad, mark = lax.optimization_barrier((normed_one_grad, grads[2]))
    grads = grads_of(2, grads, mark)
    normed_one_grad = normed_one_grad.astype(wide)
    gain_one_part = jnp.sum(normed_one_part.astype(wide) * unit_one, axis=0)
    gain_one_part = sum([from_tp(gain_one_part, step) for step in range(1, tp_size)], gain_one_part)
    scaled_one = normed_one_grad * gain_one
    d_hidden = own_first(
        mixed_grad
        + scale_one
        * (scaled_one - unit_one * jnp.mean(scaled_one * unit_one, axis=-1, keepdims=True))
    )

    d_gate_up = grads[0].reshape(experts, half, 2, width)
    d_down = grads[1].reshape(experts, width, half)

    def sum_plane(part):
        share = part.shape[1] // 2
        kept = lax.dynamic_slice_in_dim(part, core * share, share, 1)
        given = lax.dynamic_slice_in_dim(part, (1 - core) * share, share, 1)
        kept = kept + beside(given.astype(low)).astype(wide)
        total = kept[0] + across(kept[1].astype(low)).astype(wide)
        total = (total + along(total.astype(low)).astype(wide)).astype(low)
        return ctx_join(total, beside(total), 0).astype(wide)

    logit_cols = jnp.where(
        x_pos == 0,
        logit_grad,
        jnp.concatenate([logit_grad[:, mine:], logit_grad[:, :mine]], axis=1),
    )

    def both(left, right):
        return jnp.stack(
            [dot(left, right[:, :half], 0, 0), dot(left, right[:, half:], 0, 0)], axis=0
        )

    side_grads = sum_plane(
        jnp.concatenate(
            [
                both(head_low, attn_grad),
                both(logit_cols, normed_two),
                jnp.pad(gain_two_part.reshape(2, 1, half), ((0, 0), (0, 23), (0, 0))),
            ],
            axis=1,
        )
    )
    d_w_out = side_grads[:q_cols]
    d_router = side_grads[q_cols : q_cols + experts].T
    d_qkv = sum_plane(dot(first_normed, qkv_grad, 0, 0).reshape(2, half, qkv_cols))

    def sum_gain(part):
        part = part + beside(part)
        part = part + along(part)
        return part[:half] + across(part[half:])

    return (
        layer_out.reshape(micro, 1, rows, model),
        d_hidden.reshape(micro, 1, rows, model),
        sum_gain(gain_one_part),
        d_qkv[:, :q_cols],
        d_qkv[:, q_cols : q_cols + k_cols],
        d_qkv[:, q_cols + k_cols :],
        d_w_out,
        side_grads[q_cols + experts],
        d_router,
        d_gate_up,
        d_down,
    )


def solution(mesh):
    placed = (
        P(None, "fsdp", "ctx", None),
        P(None, "fsdp", None),
        P(None, "fsdp", "ctx", None),
        P("fsdp"),
        P("fsdp", "tp"),
        P("fsdp", "tp"),
        P("fsdp", "tp"),
        P("tp", "fsdp"),
        P("fsdp"),
        P("fsdp", None),
        P(None, "fsdp", None, "tp"),
        P(None, "tp", "fsdp"),
        P(None, "fsdp", "ctx", None),
    )
    fits = mesh.shape["fsdp"] == 2 and mesh.shape["ctx"] == 4
    return jax.shard_map(
        fast_body if fits else body,
        mesh=mesh,
        in_specs=placed,
        out_specs=(
            P(None, "fsdp", "ctx", None),
            P(None, "fsdp", "ctx", None),
            P("fsdp"),
            P("fsdp", "tp"),
            P("fsdp", "tp"),
            P("fsdp", "tp"),
            P("tp", "fsdp"),
            P("fsdp"),
            P("fsdp", None),
            P(None, "fsdp", None, "tp"),
            P(None, "tp", "fsdp"),
        ),
        check_vma=False,
    )
```

```python
import functools

import jax
import jax.numpy as jnp
from jax import lax
from jax.experimental import pallas as pl
from jax.experimental.pallas import tpu as pltpu
from jax.sharding import PartitionSpec as P

HEAD_DIM = 64
CAP = 32


EPSILON = 1e-06
RESIDUAL_SCALE = 0.22
SCORE_SCALE = 1.0 / 64.0
ROPE_BASE = 10000.0
TOP_PRECISION = lax.Precision.HIGHEST


def tree_tables(parent_row, tree_len):
    seg_total = parent_row.shape[0]
    seg_len = tree_len // seg_total
    seg_ids = jnp.arange(seg_total, dtype=jnp.int32)
    parent_links = (parent_row[:, None] == seg_ids[None, :]).astype(jnp.float32)
    reach_table = jnp.maximum(parent_links, jnp.eye(seg_total, dtype=jnp.float32))
    for squaring in range(max(seg_total - 1, 1).bit_length()):
        reach_table = jnp.minimum(jnp.dot(reach_table, reach_table, precision=TOP_PRECISION), 1.0)
    seg_depth = jnp.sum(reach_table, axis=1) - 1.0
    token_ids = jnp.arange(tree_len, dtype=jnp.int32)
    tok_owner = ((token_ids // seg_len)[:, None] == seg_ids[None, :]).astype(jnp.float32)
    tok_offset = (token_ids % seg_len).astype(jnp.float32)
    places = jnp.dot(tok_owner, seg_depth, precision=TOP_PRECISION) * seg_len + tok_offset
    return (places, jnp.dot(tok_owner, reach_table, precision=TOP_PRECISION), tok_owner)


def rope_tables(places):
    half_dim = HEAD_DIM // 2
    inverse = ROPE_BASE ** (-jnp.arange(half_dim, dtype=jnp.float32) * 2.0 / HEAD_DIM)
    angles = places[:, None] * inverse[None, :]
    cosine_table = jnp.concatenate([jnp.cos(angles), jnp.cos(angles)], axis=1)
    sine_values = jnp.concatenate([jnp.sin(angles), jnp.sin(angles)], axis=1)
    return (cosine_table, sine_values)


def apply_rotary(values, cosine_table, sine_values):
    half_dim = values.shape[-1] // 2
    turned = jnp.concatenate([-values[..., half_dim:], values[..., :half_dim]], axis=-1)
    return values * cosine_table[:, None, :] + turned * sine_values[:, None, :]


def norm_scale(values):
    return lax.rsqrt(jnp.mean(values * values, axis=-1, keepdims=True) + EPSILON)


def add_tuples(first_tuple, second_tuple):
    return tuple(
        (left_part + right_part for left_part, right_part in zip(first_tuple, second_tuple))
    )


def expert_work(rows, row_grads, gate_up_w, down_w, down_form):
    gate_up = jnp.einsum("ecd,edsf->ecsf", rows, gate_up_w, preferred_element_type=jnp.float32)
    gate_pre = gate_up[:, :, 0]
    up_pre = gate_up[:, :, 1]
    sigmoid = jax.nn.sigmoid(gate_pre)
    activ_low = (gate_pre * sigmoid * up_pre).astype(jnp.bfloat16)
    expert_out = jnp.einsum(
        "ecf," + down_form + "->ecd", activ_low, down_w, preferred_element_type=jnp.float32
    )
    activ_grad = jnp.einsum(
        "ecd," + down_form + "->ecf", row_grads, down_w, preferred_element_type=jnp.float32
    )
    gate_grad = activ_grad * up_pre * sigmoid * (1.0 + gate_pre * (1.0 - sigmoid))
    up_grad = activ_grad * gate_pre * sigmoid
    gate_up_grad = jnp.stack([gate_grad, up_grad], axis=2).astype(jnp.bfloat16)
    row_input_grad = jnp.einsum(
        "ecsf,edsf->ecd", gate_up_grad, gate_up_w, preferred_element_type=jnp.float32
    )
    grad_gate_up = jnp.einsum(
        "ecd,ecsf->edsf", rows, gate_up_grad, preferred_element_type=jnp.float32
    )
    grad_down = jnp.einsum(
        "ecf,ecd->" + down_form, activ_low, row_grads, preferred_element_type=jnp.float32
    )
    return (expert_out, row_input_grad, grad_gate_up, grad_down)


def body(
    hidden_in,
    parents,
    routes,
    attn_gain,
    w_query,
    key_projection,
    value_projection,
    w_out,
    moe_gain,
    w_router,
    w_gate_up,
    w_down,
    d_out,
):
    experts = w_gate_up.shape[0]
    gathered = (
        lax.all_gather(attn_gain, "fsdp", axis=0, tiled=True),
        lax.all_gather(w_query, "fsdp", axis=0, tiled=True),
        lax.all_gather(key_projection, "fsdp", axis=0, tiled=True),
        lax.all_gather(value_projection, "fsdp", axis=0, tiled=True),
        lax.all_gather(w_out, "fsdp", axis=1, tiled=True),
        lax.all_gather(moe_gain, "fsdp", axis=0, tiled=True),
        lax.all_gather(w_router, "fsdp", axis=0, tiled=True),
        lax.all_gather(w_gate_up, "fsdp", axis=1, tiled=True),
        lax.all_gather(w_down, "fsdp", axis=2, tiled=True),
    )
    gate_up_full = gathered[7]
    down_full = gathered[8]
    down_form = "efd"
    gain_one = gathered[0].astype(jnp.float32)
    query_full = gathered[1]
    key_full = gathered[2]
    value_full = gathered[3]
    out_full = gathered[4]
    gain_two = gathered[5].astype(jnp.float32)
    router_full = gathered[6]
    micro_count = hidden_in.shape[0]
    local_rows = hidden_in.shape[2]
    model_width = hidden_in.shape[3]
    top_count = routes.shape[3]
    kv_heads = key_projection.shape[1] // HEAD_DIM
    q_heads = w_query.shape[1] // HEAD_DIM
    group_size = q_heads // kv_heads
    tree_len = local_rows * lax.axis_size("ctx")
    row_start = lax.axis_index("ctx") * local_rows
    capacity = CAP
    expert_ids = jnp.arange(experts, dtype=jnp.int32)
    outputs = []
    input_grads = []
    totals = None
    for batch_index in range(micro_count):
        tree_places, reach_rows, tok_owner = tree_tables(parents[batch_index, 0], tree_len)
        local_places = lax.dynamic_slice_in_dim(tree_places, row_start, local_rows, 0)
        local_reach = lax.dynamic_slice_in_dim(reach_rows, row_start, local_rows, 0)
        allowed = (jnp.dot(local_reach, tok_owner.T, precision=TOP_PRECISION) > 0.5) & (
            tree_places[None, :] <= local_places[:, None]
        )
        cosine_table, sine_values = rope_tables(local_places)
        inputs = hidden_in[batch_index, 0].astype(jnp.float32)
        scale_one = norm_scale(inputs)
        first_normed = (inputs * scale_one * gain_one).astype(jnp.bfloat16)
        query_unrotated = jnp.dot(
            first_normed, query_full, preferred_element_type=jnp.float32
        ).reshape(local_rows, q_heads, HEAD_DIM)
        key_unrotated = jnp.dot(first_normed, key_full, preferred_element_type=jnp.float32).reshape(
            local_rows, kv_heads, HEAD_DIM
        )
        value_reduced = jnp.dot(
            first_normed, value_full, preferred_element_type=jnp.float32
        ).astype(jnp.bfloat16)
        query_reduced = (
            apply_rotary(query_unrotated, cosine_table, sine_values)
            .astype(jnp.bfloat16)
            .reshape(local_rows, kv_heads, group_size, HEAD_DIM)
        )
        key_low = (
            apply_rotary(key_unrotated, cosine_table, sine_values)
            .astype(jnp.bfloat16)
            .reshape(local_rows, kv_heads * HEAD_DIM)
        )
        tree_keys, tree_values = (
            lax.all_gather(key_low, "ctx", axis=0, tiled=True),
            lax.all_gather(value_reduced, "ctx", axis=0, tiled=True),
        )
        tree_keys = tree_keys.reshape(tree_len, kv_heads, HEAD_DIM)
        tree_values = tree_values.reshape(tree_len, kv_heads, HEAD_DIM)

        def masked_scores():
            raw_scores = jnp.einsum(
                "qhjd,khd->hjqk", query_reduced, tree_keys, preferred_element_type=jnp.float32
            )
            return jnp.where(allowed[None, None], raw_scores * SCORE_SCALE, -1e30)

        scores = masked_scores()
        top_score = jnp.max(scores, axis=-1, keepdims=True)
        log_total = top_score + jnp.log(
            jnp.sum(jnp.exp(scores - top_score), axis=-1, keepdims=True)
        )
        probs_low = jnp.exp(scores - log_total).astype(jnp.bfloat16)
        head_out = jnp.einsum(
            "hjqk,khd->qhjd", probs_low, tree_values, preferred_element_type=jnp.float32
        )
        head_low = head_out.reshape(local_rows, q_heads * HEAD_DIM).astype(jnp.bfloat16)
        attn_part = jnp.dot(head_low, out_full, preferred_element_type=jnp.float32)
        attended = lax.psum(attn_part.astype(jnp.bfloat16), "tp").astype(jnp.float32)
        mixed = inputs + RESIDUAL_SCALE * attended
        scale_two = norm_scale(mixed)
        normed_two = (mixed * scale_two * gain_two).astype(jnp.bfloat16)
        logits = jnp.dot(normed_two, router_full, preferred_element_type=jnp.float32)
        chosen_ids = routes[batch_index, 0]
        picked = (chosen_ids[:, :, None] == expert_ids[None, None, :]).astype(jnp.float32)
        chosen = jnp.sum(picked * logits[:, None, :], axis=2)
        gates = jax.nn.softmax(chosen, axis=1)
        flat_ids = chosen_ids.reshape(-1)
        flat_hot = (flat_ids[:, None] == expert_ids[None, :]).astype(jnp.int32)
        slots = jnp.sum((jnp.cumsum(flat_hot, axis=0) - flat_hot) * flat_hot, axis=1)
        targets = flat_ids * capacity + slots
        sources = (
            jnp.zeros((experts * capacity,), jnp.int32)
            .at[targets]
            .set(jnp.arange(local_rows * top_count, dtype=jnp.int32) // top_count)
        )
        filled = jnp.zeros((experts * capacity, 1), jnp.bfloat16).at[targets].set(1)
        dispatched = (normed_two[sources] * filled).reshape(experts, capacity, model_width)
        grad_out = d_out[batch_index, 0].astype(jnp.float32)
        grad_moe = RESIDUAL_SCALE * grad_out
        entry_grad = (
            (gates[:, :, None] * grad_moe[:, None, :])
            .astype(jnp.bfloat16)
            .reshape(local_rows * top_count, model_width)
        )
        slot_grad = (
            jnp.zeros((experts * capacity, model_width), jnp.bfloat16)
            .at[targets]
            .set(entry_grad)
            .reshape(experts, capacity, model_width)
        )
        expert_out, slot_input_grad, grad_gate_up, grad_down = expert_work(
            dispatched, slot_grad, gate_up_full, down_full, down_form
        )
        entry_out = expert_out.reshape(experts * capacity, model_width)[targets].reshape(
            local_rows, top_count, model_width
        )
        moe_part = jnp.sum(gates[:, :, None] * entry_out, axis=1)
        moe_sum = lax.psum(moe_part.astype(jnp.bfloat16), "tp").astype(jnp.float32)
        outputs.append(mixed + RESIDUAL_SCALE * moe_sum)
        gate_grad_part = jnp.sum(grad_moe[:, None, :] * entry_out, axis=2)
        expert_input_grad = jnp.sum(
            slot_input_grad.reshape(experts * capacity, model_width)[targets].reshape(
                local_rows, top_count, model_width
            ),
            axis=1,
        )
        expert_input_grad, gate_grads = (
            lax.psum(expert_input_grad.astype(jnp.bfloat16), "tp").astype(jnp.float32),
            lax.psum(gate_grad_part.astype(jnp.bfloat16), "tp").astype(jnp.float32),
        )
        chosen_grad = gates * (gate_grads - jnp.sum(gates * gate_grads, axis=1, keepdims=True))
        logit_grad = jnp.sum(picked * chosen_grad[:, :, None], axis=1).astype(jnp.bfloat16)
        normed_two_grad = expert_input_grad + jnp.einsum(
            "te,de->td", logit_grad, router_full, preferred_element_type=jnp.float32
        )
        grad_router = jnp.einsum(
            "td,te->de", normed_two, logit_grad, preferred_element_type=jnp.float32
        )
        unit_two = mixed * scale_two
        grad_gain_two = jnp.sum(normed_two_grad * unit_two, axis=0)
        scaled_two = normed_two_grad * gain_two
        mixed_grad = grad_out + scale_two * (
            scaled_two - unit_two * jnp.mean(scaled_two * unit_two, axis=-1, keepdims=True)
        )
        attn_grad = (RESIDUAL_SCALE * mixed_grad).astype(jnp.bfloat16)
        grad_out_proj = jnp.einsum(
            "tc,td->cd", head_low, attn_grad, preferred_element_type=jnp.float32
        )
        head_grad = (
            jnp.einsum("td,cd->tc", attn_grad, out_full, preferred_element_type=jnp.float32)
            .astype(jnp.bfloat16)
            .reshape(local_rows, kv_heads, group_size, HEAD_DIM)
        )
        scores = masked_scores()
        probs = jnp.exp(scores - log_total)
        probs_low = probs.astype(jnp.bfloat16)
        prob_grad = jnp.einsum(
            "qhjd,khd->hjqk", head_grad, tree_values, preferred_element_type=jnp.float32
        )
        value_grad = jnp.einsum(
            "hjqk,qhjd->khd", probs_low, head_grad, preferred_element_type=jnp.float32
        )
        score_grad = (
            SCORE_SCALE * probs * (prob_grad - jnp.sum(probs * prob_grad, axis=-1, keepdims=True))
        ).astype(jnp.bfloat16)
        query_grad = jnp.einsum(
            "hjqk,khd->qhjd", score_grad, tree_keys, preferred_element_type=jnp.float32
        ).reshape(local_rows, q_heads, HEAD_DIM)
        key_grad = jnp.einsum(
            "hjqk,qhjd->khd", score_grad, query_reduced, preferred_element_type=jnp.float32
        )
        key_grad, value_grad = (
            lax.psum_scatter(
                key_grad.reshape(tree_len, kv_heads * HEAD_DIM).astype(jnp.bfloat16),
                "ctx",
                scatter_dimension=0,
                tiled=True,
            ).astype(jnp.float32),
            lax.psum_scatter(
                value_grad.reshape(tree_len, kv_heads * HEAD_DIM).astype(jnp.bfloat16),
                "ctx",
                scatter_dimension=0,
                tiled=True,
            ).astype(jnp.float32),
        )
        query_pre_grad = (
            apply_rotary(query_grad, cosine_table, -sine_values)
            .astype(jnp.bfloat16)
            .reshape(local_rows, q_heads * HEAD_DIM)
        )
        key_pre_grad = (
            apply_rotary(
                key_grad.reshape(local_rows, kv_heads, HEAD_DIM), cosine_table, -sine_values
            )
            .astype(jnp.bfloat16)
            .reshape(local_rows, kv_heads * HEAD_DIM)
        )
        value_pre_grad = value_grad.astype(jnp.bfloat16)
        normed_one_grad = jnp.einsum(
            "tc,dc->td", query_pre_grad, query_full, preferred_element_type=jnp.float32
        )
        normed_one_grad = normed_one_grad + jnp.einsum(
            "tc,dc->td", key_pre_grad, key_full, preferred_element_type=jnp.float32
        )
        normed_one_grad = normed_one_grad + jnp.einsum(
            "tc,dc->td", value_pre_grad, value_full, preferred_element_type=jnp.float32
        )
        grad_query = jnp.einsum(
            "td,tc->dc", first_normed, query_pre_grad, preferred_element_type=jnp.float32
        )
        grad_key = jnp.einsum(
            "td,tc->dc", first_normed, key_pre_grad, preferred_element_type=jnp.float32
        )
        grad_value = jnp.einsum(
            "td,tc->dc", first_normed, value_pre_grad, preferred_element_type=jnp.float32
        )
        normed_one_grad = lax.psum(normed_one_grad.astype(jnp.bfloat16), "tp").astype(jnp.float32)
        unit_one = inputs * scale_one
        grad_gain_one = jnp.sum(normed_one_grad * unit_one, axis=0)
        scaled_one = normed_one_grad * gain_one
        input_grads.append(
            mixed_grad
            + scale_one
            * (scaled_one - unit_one * jnp.mean(scaled_one * unit_one, axis=-1, keepdims=True))
        )
        piece = (
            grad_gain_one,
            grad_query,
            grad_key,
            grad_value,
            grad_out_proj,
            grad_gain_two,
            grad_router,
            grad_gate_up,
            grad_down,
        )
        totals = piece if batch_index == 0 else add_tuples(totals, piece)
    summed = (
        lax.psum_scatter(totals[0], ("fsdp", "ctx"), scatter_dimension=0, tiled=True),
        lax.psum_scatter(totals[1], ("fsdp", "ctx"), scatter_dimension=0, tiled=True),
        lax.psum_scatter(totals[2], ("fsdp", "ctx"), scatter_dimension=0, tiled=True),
        lax.psum_scatter(totals[3], ("fsdp", "ctx"), scatter_dimension=0, tiled=True),
        lax.psum_scatter(totals[4], ("fsdp", "ctx"), scatter_dimension=1, tiled=True),
        lax.psum_scatter(totals[5], ("fsdp", "ctx"), scatter_dimension=0, tiled=True),
        lax.psum_scatter(totals[6], ("fsdp", "ctx"), scatter_dimension=0, tiled=True),
        lax.psum_scatter(totals[7], ("fsdp", "ctx"), scatter_dimension=1, tiled=True),
        lax.psum_scatter(totals[8], ("fsdp", "ctx"), scatter_dimension=2, tiled=True),
    )
    shares = (
        lax.all_gather(summed[0].astype(jnp.bfloat16), "ctx", axis=0, tiled=True).astype(
            jnp.float32
        ),
        lax.all_gather(summed[1].astype(jnp.bfloat16), "ctx", axis=0, tiled=True).astype(
            jnp.float32
        ),
        lax.all_gather(summed[2].astype(jnp.bfloat16), "ctx", axis=0, tiled=True).astype(
            jnp.float32
        ),
        lax.all_gather(summed[3].astype(jnp.bfloat16), "ctx", axis=0, tiled=True).astype(
            jnp.float32
        ),
        lax.all_gather(summed[4].astype(jnp.bfloat16), "ctx", axis=1, tiled=True).astype(
            jnp.float32
        ),
        lax.all_gather(summed[5].astype(jnp.bfloat16), "ctx", axis=0, tiled=True).astype(
            jnp.float32
        ),
        lax.all_gather(summed[6].astype(jnp.bfloat16), "ctx", axis=0, tiled=True).astype(
            jnp.float32
        ),
        lax.all_gather(summed[7].astype(jnp.bfloat16), "ctx", axis=1, tiled=True).astype(
            jnp.float32
        ),
        lax.all_gather(summed[8].astype(jnp.bfloat16), "ctx", axis=2, tiled=True).astype(
            jnp.float32
        ),
    )
    layer_out = jnp.stack(outputs, axis=0)[:, None]
    d_hidden = jnp.stack(input_grads, axis=0)[:, None]
    return (
        layer_out,
        d_hidden,
        shares[0],
        shares[1],
        shares[2],
        shares[3],
        shares[4],
        shares[5],
        shares[6],
        shares[7],
        shares[8],
    )


def dot(left, right, left_dim=1, right_dim=0):
    return lax.dot_general(
        left, right, (((left_dim,), (right_dim,)), ((), ())), preferred_element_type=jnp.float32
    )


def kernel_params(count=0):
    return pltpu.CompilerParams(
        dimension_semantics=("arbitrary",) * count if count else None,
        vmem_limit_bytes=60 * 1024 * 1024,
    )


def single(kernel, name, out_shape, scratch, scalars, *arrays):
    smem = pl.BlockSpec(memory_space=pltpu.SMEM)
    vmem = pl.BlockSpec(memory_space=pltpu.VMEM)
    return pl.pallas_call(
        kernel,
        out_shape=tuple(jax.ShapeDtypeStruct(shape, kind) for shape, kind in out_shape),
        in_specs=[smem] * len(scalars) + [vmem] * len(arrays),
        out_specs=(vmem,) * len(out_shape),
        scratch_shapes=[pltpu.VMEM(shape, kind) for shape, kind in scratch],
        compiler_params=kernel_params(),
        name=name,
    )(*scalars, *arrays)


def tree_path(parents_ref, m, start):
    path = [start]
    for _ in range(3):
        path.append(parents_ref[m, path[-1]])
    return path


def own_then_other(x_pos, array):
    half = array.shape[-1] // 2
    first, second = array[..., :half], array[..., half:]
    return jnp.where(x_pos == 0, first, second), jnp.where(x_pos == 0, second, first)


def row_scale(near, far):
    total = jnp.sum(near * near, axis=1, keepdims=True) + jnp.sum(far * far, axis=1, keepdims=True)
    return lax.rsqrt(total / (2 * near.shape[1]) + EPSILON)


def turn_heads(values):
    half_dim = HEAD_DIM // 2
    lane = lax.broadcasted_iota(jnp.int32, values.shape, 1) % HEAD_DIM
    width = values.shape[1]
    return jnp.where(
        lane < half_dim,
        -pltpu.roll(values, width - half_dim, 1),
        pltpu.roll(values, half_dim, 1),
    )


def split_kernel(base_ref, both_ref, down_ref, out_ref, wide_buf):
    wide_buf[...] = both_ref[0].astype(jnp.float32)
    half = both_ref.shape[1] // 2
    out_ref[0, :half, :] = wide_buf[pl.ds(0, half, stride=2), :].astype(jnp.bfloat16)
    out_ref[0, half : 2 * half, :] = wide_buf[pl.ds(1, half, stride=2), :].astype(jnp.bfloat16)
    if down_ref is not None:
        width = down_ref.shape[1]
        for j in range(half // 128):
            out_ref[0, 2 * half + j * width : 2 * half + (j + 1) * width, :] = down_ref[
                0, :, j * 128 : (j + 1) * 128
            ]


def split_plain_kernel(base_ref, both_ref, out_ref, wide_buf):
    split_kernel(base_ref, both_ref, None, out_ref, wide_buf)


def split_weights(base, count, gate_up, down):
    _, rows, width = gate_up.shape
    packed = rows if down is None else rows + rows // 2
    in_specs = [pl.BlockSpec((1, rows, width), lambda i, base: (base[0] + i, 0, 0))]
    operands = [base, gate_up]
    if down is not None:
        in_specs.append(
            pl.BlockSpec((1, *down.shape[1:]), lambda i, base: (base[0] + i, 0, 0))
        )
        operands.append(down)
    return pl.pallas_call(
        split_plain_kernel if down is None else split_kernel,
        out_shape=jax.ShapeDtypeStruct((count, packed, width), jnp.bfloat16),
        grid_spec=pltpu.PrefetchScalarGridSpec(
            num_scalar_prefetch=1,
            grid=(count,),
            in_specs=in_specs,
            out_specs=pl.BlockSpec((1, packed, width), lambda i, base: (i, 0, 0)),
            scratch_shapes=[pltpu.VMEM((rows, width), jnp.float32)],
        ),
        compiler_params=kernel_params(1),
        name="split_weights",
    )(*operands)


def before_kernel(
    place_ref,
    parents_ref,
    hidden_ref,
    small_ref,
    sent_ref,
    next_ref,
    cosine_ref,
    sine_ref,
    normed_ref,
    query_ref,
    key_value_ref,
    far_ref,
    gains_ref,
    turn_ref,
):
    x_pos, c_pos = place_ref[0], place_ref[1]
    first_core = c_pos % 2 == 0
    half = small_ref.shape[1]
    part = half // 2
    q_cols = query_ref.shape[1]
    kv_cols = key_value_ref.shape[1]
    cols = q_cols + kv_cols
    turned_cols = q_cols + kv_cols // 2
    own_rows = small_ref[: 2 * part, :]
    sent, beside = sent_ref[:part, :], next_ref[:part, :]
    top = jnp.where(first_core, sent, beside)
    low_rows = jnp.where(first_core, beside, sent)
    far_ref[:part, :] = top
    far_ref[part:, :] = low_rows
    own_gain = small_ref[2 * part : 2 * part + 16, :].astype(jnp.float32)
    far_gain = sent_ref[part : part + 16, :].astype(jnp.float32)
    gains_ref[:, :half] = own_gain
    gains_ref[:, half:] = far_gain
    near, far = own_then_other(x_pos, hidden_ref[...].astype(jnp.float32))
    scale = row_scale(near, far)
    near_low = (near * scale * own_gain[:1]).astype(jnp.bfloat16)
    far_low = (far * scale * far_gain[:1]).astype(jnp.bfloat16)
    normed_ref[:, :half] = near_low
    normed_ref[:, half:] = far_low
    made = (
        dot(near_low, own_rows[:, :cols])
        + dot(far_low[:, :part], top[:, :cols])
        + dot(far_low[:, part:], low_rows[:, :cols])
    )
    micro = parents_ref.shape[0]
    rows = hidden_ref.shape[0] // micro
    turns = []
    for m in range(micro):
        path = tree_path(parents_ref, m, c_pos)
        depth = sum((path[i + 1] != path[i]).astype(jnp.int32) for i in range(3))
        span = pl.ds(depth * rows, rows)
        turns.append((cosine_ref[span, :], sine_ref[span, :]))
    cosines = jnp.concatenate([pair[0] for pair in turns], axis=0)
    sines = jnp.concatenate([pair[1] for pair in turns], axis=0)
    turn_ref[0] = cosines
    turn_ref[1] = sines
    count = turned_cols // 128
    values = made[:, :turned_cols]
    rotated = (
        values * jnp.concatenate([cosines] * count, axis=1)
        + turn_heads(values) * jnp.concatenate([sines] * count, axis=1)
    ).astype(jnp.bfloat16)
    query_ref[...] = rotated[:, :q_cols]
    key_value_ref[:, : kv_cols // 2] = rotated[:, q_cols:]
    key_value_ref[:, kv_cols // 2 :] = made[:, turned_cols:].astype(jnp.bfloat16)


def give_pieces(whole_ref, z_pos, piece_refs):
    count = len(piece_refs)
    part = whole_ref.shape[0] // count
    for s in range(count):
        start = pl.multiple_of(((z_pos + s) % count) * part, part)
        piece_refs[s][...] = whole_ref[pl.ds(start, part), :].astype(piece_refs[s].dtype)


def take_pieces(piece_refs, z_pos, whole_ref):
    count = len(piece_refs)
    part = whole_ref.shape[0] // count
    for s in range(count):
        start = pl.multiple_of(((z_pos + s) % count) * part, part)
        whole_ref[pl.ds(start, part), :] = piece_refs[s][...].astype(whole_ref.dtype)


def stack_heads(source, first, group):
    return jnp.concatenate(
        [source[:, (first + h) * HEAD_DIM : (first + h + 1) * HEAD_DIM] for h in range(group)],
        axis=0,
    )


def attend_kernel(
    place_ref,
    parents_ref,
    query_ref,
    kv0,
    kv1,
    kv2,
    kv3,
    out_near_ref,
    out_sent_ref,
    out_next_ref,
    head_ref,
    probs_ref,
    out_far_ref,
    *rest,
):
    piece_refs, whole_buf = rest[:-1], rest[-1]
    c_pos = place_ref[1]
    blocks = (kv0, kv1, kv2, kv3)
    micro = parents_ref.shape[0]
    rows = query_ref.shape[0] // micro
    kv_heads = kv0.shape[1] // (2 * HEAD_DIM)
    group = query_ref.shape[1] // HEAD_DIM // kv_heads
    shape = (group * rows, rows)
    causal = (
        lax.broadcasted_iota(jnp.int32, shape, 1)
        <= lax.broadcasted_iota(jnp.int32, shape, 0) % rows
    )
    for m in range(micro):
        span = pl.ds(m * rows, rows)
        whole = query_ref[span, :]
        path = tree_path(parents_ref, m, c_pos)
        pieces = []
        for g in range(kv_heads):
            query = stack_heads(whole, g * group, group)
            parts = []
            for r in range(4):
                keys = blocks[r][span, :][:, g * HEAD_DIM : (g + 1) * HEAD_DIM]
                part = dot(query, keys, 1, 1) * SCORE_SCALE
                if r == 0:
                    part = jnp.where(causal, part, -1e30)
                else:
                    seen = (path[1] == c_pos ^ r) | (path[2] == c_pos ^ r) | (path[3] == c_pos ^ r)
                    part = jnp.where(seen, part, -1e30)
                parts.append(part)
            scores = jnp.concatenate(parts, axis=1)
            powers = jnp.exp(scores - jnp.max(scores, axis=1, keepdims=True))
            probs = powers * (1.0 / jnp.sum(powers, axis=1, keepdims=True))
            probs_ref[m * kv_heads + g] = probs
            low = probs.astype(jnp.bfloat16)
            values = jnp.concatenate(
                [
                    blocks[r][span, :][:, (kv_heads + g) * HEAD_DIM : (kv_heads + g + 1) * HEAD_DIM]
                    for r in range(4)
                ],
                axis=0,
            )
            mixed = dot(low, values)
            pieces += [mixed[h * rows : (h + 1) * rows] for h in range(group)]
        head_ref[span, :] = jnp.concatenate(pieces, axis=1).astype(jnp.bfloat16)
    first_core = c_pos % 2 == 0
    sent, beside = out_sent_ref[...], out_next_ref[...]
    part = sent.shape[0]
    out_far_ref[:part, :] = jnp.where(first_core, sent, beside)
    out_far_ref[part:, :] = jnp.where(first_core, beside, sent)
    half = sent.shape[1]
    whole_buf[:, :half] = dot(head_ref[...], out_near_ref[...])
    whole_buf[:, half:] = dot(head_ref[...], out_far_ref[...])
    give_pieces(whole_buf, place_ref[2], piece_refs)


def after_kernel(place_ref, hidden_ref, gains_ref, small_ref, far_ref, routes_ref, *rest):
    mixed_ref, rows_ref, gates_ref, whole_buf = rest[-4:]
    take_pieces(rest[:-4], place_ref[2], whole_buf)
    half = small_ref.shape[1]
    near, far = own_then_other(place_ref[0], hidden_ref[...].astype(jnp.float32))
    near = near + RESIDUAL_SCALE * whole_buf[:, :half]
    far = far + RESIDUAL_SCALE * whole_buf[:, half:]
    mixed_ref[:, :half] = near
    mixed_ref[:, half:] = far
    scale = row_scale(near, far)
    near_low = (near * scale * gains_ref[1:2, :half]).astype(jnp.bfloat16)
    far_low = (far * scale * gains_ref[1:2, half:]).astype(jnp.bfloat16)
    rows_ref[:, :half] = near_low
    rows_ref[:, half : 2 * half] = far_low
    logits = dot(near_low, small_ref[:half, half - 128 :]) + dot(far_low, far_ref[:, half - 128 :])
    lane = lax.broadcasted_iota(jnp.int32, logits.shape, 1)
    named = lane == routes_ref[:, 0:1]
    for k in range(1, routes_ref.shape[1]):
        named = named | (lane == routes_ref[:, k : k + 1])
    logits = jnp.where(named, logits, -1e30)
    powers = jnp.where(named, jnp.exp(logits - jnp.max(logits, axis=1, keepdims=True)), 0.0)
    gates = powers / jnp.sum(powers, axis=1, keepdims=True)
    gates_ref[...] = gates
    high = gates.astype(jnp.bfloat16)
    rest_part = gates - high.astype(jnp.float32)
    rows_ref[:, 2 * half :] = jnp.where(
        lane < 64, high.astype(jnp.float32), pltpu.roll(rest_part, 64, 1)
    ).astype(jnp.bfloat16)


def expert_kernel(
    place_ref,
    near_ref,
    far_ref,
    near_out_ref,
    far_out_ref,
    rank_ref,
    gate_up_ref,
    down_ref,
    *rest,
    first,
    last,
    each,
    split,
):
    count = 4 if split else 1
    other_refs, rest = rest[:count], rest[count:]
    if first > 0:
        held_out, held_grad = rest[:2]
        rest = rest[2:]
    out_ref, grad_ref, slots_ref = rest[:3]
    rows_buf, grads_buf, moe_buf, back_buf, hot_buf, gate_buf = rest[-6:]
    half = down_ref.shape[-1]
    full = 2 * half
    width = down_ref.shape[-2]
    step = pl.program_id(0)
    quarter = [place_ref[1] ^ r for r in range(4)]
    expert = [(place_ref[0] * 4 + quarter[r]) * each + first + step for r in range(4)]
    iota = lax.broadcasted_iota(jnp.int32, (CAP, 128), 0)
    lane = lax.broadcasted_iota(jnp.int32, (CAP, 128), 1)

    @pl.when(step == 0)
    def _():
        if first == 0:
            out_ref[...] = jnp.zeros_like(out_ref)
            grad_ref[...] = jnp.zeros_like(grad_ref)
        else:
            out_ref[...] = held_out[...]
            grad_ref[...] = held_grad[...]

    marks = [((lane == expert[r]) | (lane == expert[r] + 64)) for r in range(4)]
    mark = jnp.concatenate(marks, axis=0)
    for b in range(4):
        low = jnp.concatenate(
            [
                jnp.where(iota == rank_ref[quarter[r], 0, pl.ds(b, 1), :], 1.0, 0.0)
                for r in range(4)
            ],
            axis=0,
        ).astype(jnp.bfloat16)
        hot_buf[b] = low
        span = pl.ds((b % 2) * 128, 128)
        source = near_ref if b < 2 else far_ref
        picked = jnp.where(mark, dot(low, source[span, pl.ds(full, 128)]), 0.0)
        gate_buf[b] = jnp.broadcast_to(jnp.sum(picked, axis=1, keepdims=True), (4 * CAP, 128))
        for part in range(2):
            keep = pl.ds(part * half, half)
            if b < 2:
                rows, grads = near_ref[span, keep], near_out_ref[span, keep]
            else:
                swap = pl.ds((1 - part) * half, half)
                rows, grads = far_ref[span, swap], far_out_ref[span, swap]
            rows_buf[b, :, keep] = dot(low, rows).astype(jnp.bfloat16)
            grads_buf[b, :, keep] = dot(low, grads).astype(jnp.bfloat16)
    for r in range(4):
        q = quarter[r]
        slot = slice(r * CAP, (r + 1) * CAP)
        rows = jnp.concatenate([rows_buf[b, slot, :] for b in range(4)], axis=0)
        grads = jnp.concatenate([grads_buf[b, slot, :] for b in range(4)], axis=0)
        gate = jnp.concatenate([gate_buf[b, slot, :] for b in range(4)], axis=0)
        near_w = jnp.concatenate(
            [gate_up_ref[q, 0, :half, :], gate_up_ref[q, 0, half:, :]], axis=1
        )
        def other(start, size):
            if split:
                return other_refs[r][0, start : start + size, :]
            return other_refs[0][q, 0, start : start + size, :]

        far_w = jnp.concatenate([other(0, half), other(half, half)], axis=1)
        near_down = down_ref[0, q, 0]
        far_down = jnp.concatenate(
            [other(2 * half + j * width, width) for j in range(half // 128)],
            axis=1,
        )
        gate_up = dot(rows[:, :half], near_w) + dot(rows[:, half:], far_w)
        gate_pre = gate_up[:, :width]
        up_pre = gate_up[:, width:]
        sigmoid = 1.0 / (1.0 + jnp.exp(-gate_pre))
        activ = (gate_pre * sigmoid * up_pre).astype(jnp.bfloat16)
        pulled = RESIDUAL_SCALE * (
            dot(grads[:, :half], near_down, 1, 1) + dot(grads[:, half:], far_down, 1, 1)
        )
        activ_wide = activ.astype(jnp.float32)
        gate_grad = jnp.sum(activ_wide * pulled, axis=1, keepdims=True)
        activ_grad = pulled * gate
        gate_pre_grad = activ_grad * up_pre * sigmoid * (1.0 + gate_pre * (1.0 - sigmoid))
        up_pre_grad = activ_grad * gate_pre * sigmoid
        both = jnp.concatenate([gate_pre_grad, up_pre_grad], axis=1).astype(jnp.bfloat16)
        slots_ref[q, 0, :, : 2 * width] = both
        slots_ref[q, 0, :, 2 * width :] = (activ_wide * gate * RESIDUAL_SCALE).astype(jnp.bfloat16)
        for part, (wide, low_w) in enumerate(((near_w, near_down), (far_w, far_down))):
            keep = pl.ds(part * half, half)
            made = dot(activ, low_w)
            back = dot(both, wide, 1, 1)
            for b in range(4):
                piece = slice(b * CAP, (b + 1) * CAP)
                scale = jnp.concatenate([gate[piece]] * (half // 128), axis=1)
                moe_buf[b, slot, keep] = (made[piece] * scale).astype(jnp.bfloat16)
                back_buf[b, slot, keep] = back[piece].astype(jnp.bfloat16)
        spot = lane == expert[r]
        for b in range(4):
            back_buf[b, slot, pl.ds(full, 128)] = jnp.where(
                spot, gate_grad[b * CAP : (b + 1) * CAP], 0.0
            ).astype(jnp.bfloat16)
    for b in range(4):
        span = pl.ds(b * 128, 128)
        out_ref[span, :] += dot(hot_buf[b], moe_buf[b], 0, 0)
        grad_ref[span, :] += dot(hot_buf[b], back_buf[b], 0, 0)

    if last:
        moe_far_ref, back_far_ref = rest[3:5]

        @pl.when(step == pl.num_programs(0) - 1)
        def _():
            span = pl.ds(256, 256)
            for part in range(2):
                keep, swap = pl.ds(part * half, half), pl.ds((1 - part) * half, half)
                moe_far_ref[:, keep] = out_ref[span, swap].astype(jnp.bfloat16)
                back_far_ref[:, keep] = grad_ref[span, swap].astype(jnp.bfloat16)
            back_far_ref[:, pl.ds(full, 128)] = grad_ref[span, pl.ds(full, 128)].astype(
                jnp.bfloat16
            )


def run_experts(place, near, far, near_out, far_out, rank, gate_up, down, other, held, first, each):
    split = isinstance(other, list)
    others = other if split else [other]
    steps, packed, lanes = others[0].shape[-3:]
    quarters, _, rows, width = gate_up.shape
    half = rows // 2
    full = 2 * half
    tokens = 2 * near.shape[0]
    last = first + steps == each

    def fixed(shape):
        return pl.BlockSpec(shape, lambda j, sp: (0,) * len(shape))

    in_specs = [
        fixed(near.shape),
        fixed(far.shape),
        fixed((tokens // 2, full)),
        fixed((tokens // 2, full)),
        pl.BlockSpec((quarters, 1, 4, 128), lambda j, sp: (0, first + j, 0, 0)),
        pl.BlockSpec((quarters, 1, rows, width), lambda j, sp: (0, first + j, 0, 0)),
        pl.BlockSpec((1, quarters, 1, width, half), lambda j, sp: (sp[0], 0, first + j, 0, 0)),
    ]
    if split:
        in_specs += [pl.BlockSpec((1, packed, lanes), lambda j, sp: (j, 0, 0))] * 4
    else:
        in_specs.append(pl.BlockSpec((quarters, 1, packed, lanes), lambda j, sp: (0, j, 0, 0)))
    operands = [place, near, far, near_out, far_out, rank, gate_up, down, *others]
    aliases = {}
    totals = [
        jax.ShapeDtypeStruct((tokens, full), jnp.float32),
        jax.ShapeDtypeStruct((tokens, full + 128), jnp.float32),
    ]
    if first > 0:
        in_specs += [fixed(held[0].shape), fixed(held[1].shape)]
        aliases = {len(operands): 0, len(operands) + 1: 1}
        operands += list(held[:2])
    out_shape = totals + [
        jax.ShapeDtypeStruct((quarters, steps, 4 * CAP, 3 * width), jnp.bfloat16)
    ]
    out_specs = [
        fixed(totals[0].shape),
        fixed(totals[1].shape),
        pl.BlockSpec((quarters, 1, 4 * CAP, 3 * width), lambda j, sp: (0, j, 0, 0)),
    ]
    if last:
        for lanes_out in (full, full + 128):
            out_shape.append(jax.ShapeDtypeStruct((tokens // 2, lanes_out), jnp.bfloat16))
            out_specs.append(fixed((tokens // 2, lanes_out)))
    return pl.pallas_call(
        functools.partial(expert_kernel, first=first, last=last, each=each, split=split),
        out_shape=tuple(out_shape),
        grid_spec=pltpu.PrefetchScalarGridSpec(
            num_scalar_prefetch=1,
            grid=(steps,),
            in_specs=in_specs,
            out_specs=tuple(out_specs),
            scratch_shapes=[pltpu.VMEM((4, 4 * CAP, full), jnp.bfloat16)] * 3
            + [
                pltpu.VMEM((4, 4 * CAP, full + 128), jnp.bfloat16),
                pltpu.VMEM((4, 4 * CAP, 128), jnp.bfloat16),
                pltpu.VMEM((4, 4 * CAP, 128), jnp.float32),
            ],
        ),
        input_output_aliases=aliases,
        compiler_params=kernel_params(1),
        name="experts",
    )(*operands)


def join_kernel(place_ref, total_ref, got_ref, *rest):
    piece_refs, whole_buf = rest[:-1], rest[-1]
    count = got_ref.shape[0]
    whole_buf[...] = total_ref[:count, :] + got_ref[...].astype(jnp.float32)
    give_pieces(whole_buf, place_ref[2], piece_refs)


def back_kernel(
    place_ref,
    mixed_ref,
    gates_ref,
    gains_ref,
    small_ref,
    far_ref,
    out_grad_ref,
    out_near_ref,
    out_far_ref,
    query_ref,
    turn_ref,
    kv0,
    kv1,
    kv2,
    kv3,
    probs_ref,
    *rest,
):
    (
        mixed_grad_ref,
        attn_grad_ref,
        logit_grad_ref,
        gain_grad_ref,
        query_grad_ref,
        kept_ref,
        given_ref,
        whole_buf,
        head_buf,
    ) = rest[-9:]
    take_pieces(rest[:-9], place_ref[2], whole_buf)
    half = small_ref.shape[1]
    full = 2 * half
    gates = gates_ref[...]
    gate_grads = whole_buf[:, full:]
    inner = jnp.sum(gates * gate_grads, axis=1, keepdims=True)
    logit_grad = (gates * (gate_grads - inner)).astype(jnp.bfloat16)
    logit_grad_ref[...] = logit_grad
    near, far = mixed_ref[:, :half], mixed_ref[:, half:]
    scale = row_scale(near, far)
    near_unit, far_unit = near * scale, far * scale
    near_grad = whole_buf[:, :half] + dot(logit_grad, small_ref[:half, half - 128 :], 1, 1)
    far_grad = whole_buf[:, half:full] + dot(logit_grad, far_ref[:, half - 128 :], 1, 1)
    gain_grad_ref[:, :half] = jnp.broadcast_to(
        jnp.sum(near_grad * near_unit, axis=0, keepdims=True), (8, half)
    )
    gain_grad_ref[:, half:] = jnp.broadcast_to(
        jnp.sum(far_grad * far_unit, axis=0, keepdims=True), (8, half)
    )
    near_scaled = near_grad * gains_ref[1:2, :half]
    far_scaled = far_grad * gains_ref[1:2, half:]
    mean = (
        jnp.sum(near_scaled * near_unit, axis=1, keepdims=True)
        + jnp.sum(far_scaled * far_unit, axis=1, keepdims=True)
    ) / full
    near_mixed = out_grad_ref[:, :half].astype(jnp.float32) + scale * (
        near_scaled - near_unit * mean
    )
    far_mixed = out_grad_ref[:, half:full].astype(jnp.float32) + scale * (
        far_scaled - far_unit * mean
    )
    mixed_grad_ref[:, :half] = near_mixed
    mixed_grad_ref[:, half:] = far_mixed
    near_attn = (RESIDUAL_SCALE * near_mixed).astype(jnp.bfloat16)
    far_attn = (RESIDUAL_SCALE * far_mixed).astype(jnp.bfloat16)
    attn_grad_ref[:, :half] = near_attn
    attn_grad_ref[:, half:] = far_attn
    head_buf[...] = (
        dot(near_attn, out_near_ref[...], 1, 1) + dot(far_attn, out_far_ref[...], 1, 1)
    ).astype(jnp.bfloat16)
    blocks = (kv0, kv1, kv2, kv3)
    kv_heads = kv0.shape[1] // (2 * HEAD_DIM)
    micro = probs_ref.shape[0] // kv_heads
    rows = query_ref.shape[0] // micro
    group = query_ref.shape[1] // HEAD_DIM // kv_heads
    count = query_ref.shape[1] // 128
    for m in range(micro):
        span = pl.ds(m * rows, rows)
        whole = query_ref[span, :]
        whole_grad = head_buf[span, :]
        pieces = []
        key_grads = []
        value_grads = []
        for g in range(kv_heads):
            query = stack_heads(whole, g * group, group)
            head_grad = stack_heads(whole_grad, g * group, group)
            keys = jnp.concatenate(
                [blocks[r][span, :][:, g * HEAD_DIM : (g + 1) * HEAD_DIM] for r in range(4)], axis=0
            )
            values = jnp.concatenate(
                [
                    blocks[r][span, :][:, (kv_heads + g) * HEAD_DIM : (kv_heads + g + 1) * HEAD_DIM]
                    for r in range(4)
                ],
                axis=0,
            )
            probs = probs_ref[m * kv_heads + g]
            prob_grad = dot(head_grad, values, 1, 1)
            inner = jnp.sum(probs * prob_grad, axis=1, keepdims=True)
            score_grad = (SCORE_SCALE * probs * (prob_grad - inner)).astype(jnp.bfloat16)
            value_grads.append(dot(probs.astype(jnp.bfloat16), head_grad, 0, 0))
            key_grads.append(dot(score_grad, query, 0, 0))
            query_grad = dot(score_grad, keys)
            pieces += [query_grad[h * rows : (h + 1) * rows] for h in range(group)]
        query_grad = jnp.concatenate(pieces, axis=1)
        query_grad_ref[span, :] = (
            query_grad * jnp.concatenate([turn_ref[0, span, :]] * count, axis=1)
            - turn_heads(query_grad) * jnp.concatenate([turn_ref[1, span, :]] * count, axis=1)
        ).astype(jnp.bfloat16)
        joined = jnp.concatenate(key_grads + value_grads, axis=1)
        kept_ref[0, span, :] = joined[:rows]
        kept_ref[1, span, :] = joined[2 * rows : 3 * rows]
        given_ref[0, span, :] = joined[rows : 2 * rows].astype(jnp.bfloat16)
        given_ref[1, span, :] = joined[3 * rows :].astype(jnp.bfloat16)


def last_kernel(
    place_ref,
    query_grad_ref,
    kept_ref,
    near_ref,
    along_ref,
    turn_ref,
    small_ref,
    far_ref,
    hidden_ref,
    *rest,
):
    grads_ref, gain_ref = rest[0], rest[1]
    piece_refs, whole_buf = rest[2:-1], rest[-1]
    q_cols = query_grad_ref.shape[1]
    k_cols = turn_ref.shape[2]
    cols = q_cols + 2 * k_cols
    half = small_ref.shape[1]
    total = (
        kept_ref[0] + near_ref[0].astype(jnp.float32) + along_ref[...].astype(jnp.float32)
    )
    keys = total[:, :k_cols]
    grads_ref[:, :q_cols] = query_grad_ref[...]
    grads_ref[:, q_cols : q_cols + k_cols] = (
        keys * turn_ref[0] - turn_heads(keys) * turn_ref[1]
    ).astype(jnp.bfloat16)
    grads_ref[:, q_cols + k_cols :] = total[:, k_cols:].astype(jnp.bfloat16)
    grads = grads_ref[...]
    near_part = dot(grads, small_ref[:half, :cols], 1, 1)
    far_part = dot(grads, far_ref[:, :cols], 1, 1)
    near, far = own_then_other(place_ref[0], hidden_ref[...].astype(jnp.float32))
    scale = row_scale(near, far)
    gain_ref[:, :half] = jnp.broadcast_to(
        jnp.sum(near_part * (near * scale), axis=0, keepdims=True), (8, half)
    )
    gain_ref[:, half:] = jnp.broadcast_to(
        jnp.sum(far_part * (far * scale), axis=0, keepdims=True), (8, half)
    )
    whole_buf[:, :half] = near_part
    whole_buf[:, half:] = far_part
    give_pieces(whole_buf, place_ref[2], piece_refs)


def output_kernel(place_ref, mixed_ref, *rest):
    out_ref, whole_buf = rest[-2:]
    take_pieces(rest[:-2], place_ref[2], whole_buf)
    half = out_ref.shape[1] // 2
    total = mixed_ref[...] + RESIDUAL_SCALE * whole_buf[...]
    first, second = own_then_other(place_ref[0], total)
    out_ref[:, :half] = first
    out_ref[:, half:] = second


def hidden_kernel(place_ref, hidden_ref, gains_ref, mixed_grad_ref, *rest):
    out_ref, whole_buf = rest[-2:]
    take_pieces(rest[:-2], place_ref[2], whole_buf)
    half = out_ref.shape[1] // 2
    near, far = own_then_other(place_ref[0], hidden_ref[...].astype(jnp.float32))
    scale = row_scale(near, far)
    near, far = near * scale, far * scale
    near_scaled = whole_buf[:, :half] * gains_ref[0:1, :half]
    far_scaled = whole_buf[:, half:] * gains_ref[0:1, half:]
    mean = (
        jnp.sum(near_scaled * near, axis=1, keepdims=True)
        + jnp.sum(far_scaled * far, axis=1, keepdims=True)
    ) / (2 * half)
    near_out = mixed_grad_ref[:, :half] + scale * (near_scaled - near * mean)
    far_out = mixed_grad_ref[:, half:] + scale * (far_scaled - far * mean)
    out_ref[:, :half] = jnp.where(place_ref[0] == 0, near_out, far_out)
    out_ref[:, half:] = jnp.where(place_ref[0] == 0, far_out, near_out)


def weight_grad_kernel(
    place_ref, rows_ref, grads_ref, slots_ref, rank_ref, *refs
):
    gate_up_ref, down_ref, mark_ref, rows_buf, grads_buf = refs[-5:]
    half = down_ref.shape[-1]
    width = down_ref.shape[-2]
    steps = rank_ref.shape[2]
    iota = lax.broadcasted_iota(jnp.int32, (CAP, 128), 0)
    step, side = pl.program_id(0), pl.program_id(1)
    mark_ref[...] = jnp.zeros_like(mark_ref)

    @pl.when((step == 0) & (side == 0))
    def _():
        for k in range(4):
            for b in range(4):
                span = pl.ds(b * 128, 128)
                for a in range(2):
                    hot = jnp.concatenate(
                        [
                            jnp.where(iota == rank_ref[a, q, j, pl.ds(4 * k + b, 1), :], 1.0, 0.0)
                            for j in range(steps)
                            for q in range(4)
                        ],
                        axis=0,
                    ).astype(jnp.bfloat16)
                    spot = 4 * k + (b ^ (2 * a))
                    rows = dot(hot, rows_ref[k, span, :]).astype(jnp.bfloat16)
                    grads = dot(hot, grads_ref[k, span, :]).astype(jnp.bfloat16)
                    for j in range(steps):
                        piece = slice(j * 4 * CAP, (j + 1) * 4 * CAP)
                        rows_buf[j * 2 + a, spot] = rows[piece]
                        grads_buf[j * 2 + a, spot] = grads[piece]

    place = step * 2 + side
    for q in range(4):
        slot = slice(q * CAP, (q + 1) * CAP)
        rows = jnp.concatenate([rows_buf[place, n, slot, :] for n in range(16)], axis=0)
        grads = jnp.concatenate([grads_buf[place, n, slot, :] for n in range(16)], axis=0)
        taken = jnp.concatenate([slots_ref[0, k, q, 0] for k in range(4)], axis=0)
        made = dot(rows, taken[:, : 2 * width], 0, 0)
        gate_up_ref[0, q, 0, pl.ds(0, half, stride=2), :] = made[:, :width]
        gate_up_ref[0, q, 0, pl.ds(1, half, stride=2), :] = made[:, width:]
        down_ref[0, q, 0] = dot(taken[:, 2 * width :], grads, 0, 0)


def run_weight_grads(place, plane, slots, rank, held, each, first, mark):
    sides, _, quarters, steps, slot_count, lanes = slots.shape
    width = lanes // 3
    half = (plane.shape[-1] - 128) // 2
    tokens = plane.shape[1]

    def place_of(j, a, sp):
        return (sp[0] ^ a, 0, first + j, 0, 0)

    in_specs = [
        pl.BlockSpec((4, tokens, half), lambda j, a, sp: (0, 0, 1)),
        pl.BlockSpec((4, tokens, half), lambda j, a, sp: (0, 0, 0)),
        pl.BlockSpec(
            (1, 4, quarters, 1, slot_count, lanes),
            lambda j, a, sp: (sp[0] ^ a, 0, 0, j, 0, 0),
        ),
        pl.BlockSpec(rank.shape, lambda j, a, sp: (0, 0, 0, 0, 0)),
        pl.BlockSpec(memory_space=pl.ANY),
    ]
    operands = [place, plane, plane, slots, rank, mark]
    aliases = {}
    if held is not None:
        in_specs += [pl.BlockSpec(memory_space=pl.ANY)] * 2
        aliases = {len(operands): 0, len(operands) + 1: 1}
        operands += list(held[:2])
    return pl.pallas_call(
        weight_grad_kernel,
        out_shape=(
            jax.ShapeDtypeStruct((sides, quarters, each, 2 * half, width), jnp.float32),
            jax.ShapeDtypeStruct((sides, quarters, each, width, half), jnp.float32),
            jax.ShapeDtypeStruct((8, 128), jnp.float32),
        ),
        grid_spec=pltpu.PrefetchScalarGridSpec(
            num_scalar_prefetch=1,
            grid=(steps, sides),
            in_specs=in_specs,
            out_specs=(
                pl.BlockSpec((1, quarters, 1, 2 * half, width), place_of),
                pl.BlockSpec((1, quarters, 1, width, half), place_of),
                pl.BlockSpec((8, 128), lambda j, a, sp: (0, 0)),
            ),
            scratch_shapes=[pltpu.VMEM((2 * steps, 16, 4 * CAP, half), jnp.bfloat16)] * 2,
        ),
        input_output_aliases=aliases,
        compiler_params=kernel_params(2),
        name="weight_grads",
    )(*operands)


def swap_halves(values):
    half = values.shape[-1] // 2
    return jnp.concatenate([values[..., half:], values[..., :half]], axis=-1)


def fast_body(
    hidden_in,
    parents,
    routes,
    attn_gain,
    w_query,
    key_projection,
    value_projection,
    w_out,
    moe_gain,
    w_router,
    w_gate_up,
    w_down,
    d_out,
):
    low, wide = jnp.bfloat16, jnp.float32
    x_pos = lax.axis_index("fsdp")
    c_pos = lax.axis_index("ctx")
    z_pos = lax.axis_index("tp")
    tp_size = lax.axis_size("tp")
    place = jnp.stack([x_pos, c_pos, z_pos]).astype(jnp.int32)
    micro, _, rows, model = hidden_in.shape
    half = model // 2
    tokens = micro * rows
    experts = w_gate_up.shape[0]
    mine = experts // 2
    each = mine // 4
    width = w_down.shape[1]
    q_cols = w_query.shape[1]
    k_cols = key_projection.shape[1]
    qkv_cols = q_cols + 2 * k_cols
    kv_heads = k_cols // HEAD_DIM
    group = q_cols // k_cols
    top = routes.shape[-1]
    chunks = ((0, 2), (2, 2), (4, 1))
    tie = lax.optimization_barrier

    def across(value):
        return lax.ppermute(value, "fsdp", [(0, 1), (1, 0)])

    def beside(value):
        return lax.ppermute(value, "ctx", [(i, i ^ 1) for i in range(4)])

    def along(value):
        return lax.ppermute(value, "ctx", [(i, i ^ 2) for i in range(4)])

    def from_tp(value, step):
        return lax.ppermute(value, "tp", [((i + step) % tp_size, i) for i in range(tp_size)])

    def all_ctx(value):
        nearby = beside(value)
        distant = along(value)
        return [value, nearby, distant, beside(distant)]

    def own_first(value):
        return jnp.where(x_pos == 0, value, swap_halves(value))

    def reduce_pieces(pieces):
        total = pieces[0].astype(wide)
        for step in range(1, tp_size):
            total = total + from_tp(pieces[tp_size - step], step).astype(wide)
        return total.astype(low)

    def spread_pieces(total):
        return [total] + [from_tp(total, step) for step in range(1, tp_size)]

    piece_shapes = [((tokens // tp_size, model), low)] * tp_size
    hidden = hidden_in.reshape(tokens, model)
    flat_routes = routes.reshape(tokens, top)

    core = c_pos % 2
    part = half // 2
    weights = jnp.concatenate(
        [
            w_query,
            key_projection,
            value_projection,
            jnp.pad(w_router, ((0, 0), (0, half - qkv_cols - experts))),
        ],
        axis=1,
    )
    gain_rows = jnp.pad(jnp.stack([attn_gain, moe_gain]), ((0, 14), (0, 0)))
    small = jnp.concatenate([weights, gain_rows], axis=0)
    sent = across(
        jnp.concatenate([lax.dynamic_slice_in_dim(weights, core * part, part, 0), gain_rows], axis=0)
    )

    both_view = w_gate_up.reshape(experts, 2 * half, width)
    base = (x_pos * mine).astype(jnp.int32)[None]
    away = ((1 - x_pos) * mine + c_pos * each).astype(jnp.int32)[None]
    packs = [split_weights(away + first, count, both_view, w_down) for first, count in chunks]
    down_all = w_down.reshape(2, 4, each, width, half)
    routes_low = jnp.pad(flat_routes.astype(low), ((0, 0), (0, 128 - top)))
    near_out = jnp.concatenate([own_first(d_out.reshape(tokens, model)), routes_low], axis=1)

    sent, packs[0], out_start = tie((sent, packs[0], core * (q_cols // 2)))
    out_sent = across(lax.dynamic_slice_in_dim(w_out, out_start, q_cols // 2, 0))

    half_dim = HEAD_DIM // 2
    inverse = ROPE_BASE ** (-jnp.arange(half_dim, dtype=wide) * 2.0 / HEAD_DIM)
    angles = jnp.arange(4 * rows, dtype=wide)[:, None] * inverse[None, :]
    cosines = jnp.tile(jnp.cos(angles), (1, 4))
    sines = jnp.tile(jnp.sin(angles), (1, 4))
    normed_one, query, key_value, small_far, gains, turns = single(
        before_kernel,
        "before",
        [
            ((tokens, model), low),
            ((tokens, q_cols), low),
            ((tokens, 2 * k_cols), low),
            ((half, half), low),
            ((16, model), wide),
            ((2, tokens, 128), wide),
        ],
        [],
        [place, parents.reshape(micro, 4)],
        hidden,
        small,
        sent,
        beside(sent),
        cosines,
        sines,
    )
    key_value, packs[0], near_out = tie((key_value, packs[0], near_out))
    blocks = all_ctx(key_value)
    far_out = across(near_out)
    far_zero = across(packs[0])
    head_low, probs, out_far, *pieces = single(
        attend_kernel,
        "attend",
        [
            ((tokens, q_cols), low),
            ((micro * kv_heads, group * rows, 4 * rows), wide),
            ((q_cols, half), low),
        ]
        + piece_shapes,
        [((tokens, model), wide)],
        [place, parents.reshape(micro, 4)],
        query,
        *blocks,
        w_out,
        out_sent,
        beside(out_sent),
    )
    total = reduce_pieces(pieces)
    total, far_zero, far_out, packs[1] = tie((total, far_zero, far_out, packs[1]))
    far_one = across(packs[1])
    mixed, near, gates = single(
        after_kernel,
        "after",
        [((tokens, model), wide), ((tokens, model + 128), low), ((tokens, 128), wide)],
        [((tokens, model), wide)],
        [place],
        hidden,
        gains,
        small,
        small_far,
        flat_routes,
        *spread_pieces(total),
    )
    near, packs[2], base = tie((near, packs[2], base))
    gate_up_mine = split_weights(base, mine, both_view, None).reshape(4, each, 2 * half, width)
    far = across(near)
    far, packs[2], far_one, gate_up_mine = tie((far, packs[2], far_one, gate_up_mine))
    far_two = across(packs[2])
    far_weights = [lax.all_gather(got, "ctx") for got in (far_zero, far_one)]
    plane_in = jnp.concatenate(
        [
            jnp.concatenate([near_out[:, :half], near[:, :half], routes_low], axis=1),
            jnp.concatenate([far_out[:, half:model], far[:, half:model], far_out[:, model:]], axis=1),
        ],
        axis=0,
    )

    upper = (
        lax.broadcasted_iota(jnp.int32, (rows, rows), 0)
        < lax.broadcasted_iota(jnp.int32, (rows, rows), 1)
    ).astype(low)

    def ranks(route_table, ids):
        flat = route_table.astype(jnp.int32).T
        hit = jnp.zeros((ids.shape[0], flat.shape[1]), jnp.bool_)
        for k in range(top):
            hit = hit | (flat[k][None, :] == ids[:, None])
        hot = hit.astype(low).reshape(-1, rows)
        found = jnp.where(hot > 0, dot(hot, upper), -1.0).astype(jnp.int32)
        return found.reshape(ids.shape[0], -1, rows)

    expert_ids = (jnp.arange(experts, dtype=jnp.int32) + x_pos * mine) % experts
    pair_routes = jnp.concatenate([routes_low, far_out[:, model:]], axis=0)[:, :top]
    rank_pair = ranks(pair_routes, expert_ids[:mine]).reshape(4, each, 4, rows)

    held = None
    slots = []
    for number, (first, count) in enumerate(chunks):
        if number == 1:
            slots[0], far_two, far_weights[1] = tie((slots[0], far_two, far_weights[1]))
            far_along = along(far_two)
            far_near = beside(far_two)
            plane_in, far_weights[1] = tie((plane_in, far_weights[1]))
            plane = lax.all_gather(plane_in, "ctx")
        if number == 2:
            slots[1], far_along, far_near = tie((slots[1], far_along, far_near))
            far_weights.append([far_two, far_near, far_along, beside(far_along)])
        held = run_experts(
            place,
            near,
            far,
            near_out,
            far_out,
            rank_pair,
            gate_up_mine,
            down_all,
            far_weights[number],
            held,
            first,
            each,
        )
        slots.append(held[2])
    moe_all, back_all, _, moe_far, back_far = held

    back_got = across(back_far)
    def gather_slots(part):
        return lax.all_gather(part, ("fsdp", "ctx")).reshape(2, 4, *part.shape)

    back_got, moe_far, plane, slots[0] = tie((back_got, moe_far, plane, slots[0]))
    moe_got = across(moe_far)
    pair_zero = gather_slots(slots[0])
    pieces = single(
        join_kernel,
        "join",
        [((tokens // tp_size, model + 128), low)] * tp_size,
        [((tokens, model + 128), wide)],
        [place],
        back_all,
        back_got,
    )
    found = spread_pieces(reduce_pieces(pieces))
    *found, pair_zero, moe_got, slots[1] = tie((*found, pair_zero, moe_got, slots[1]))
    pair_one = gather_slots(slots[1])
    moe_pieces = single(
        join_kernel, "join", piece_shapes, [((tokens, model), wide)], [place], moe_all, moe_got
    )
    moe_total = reduce_pieces(moe_pieces)
    (
        mixed_grad,
        attn_grad,
        logit_grad,
        gain_two_part,
        query_grad,
        kept,
        given,
    ) = single(
        back_kernel,
        "back",
        [
            ((tokens, model), wide),
            ((tokens, model), low),
            ((tokens, 128), low),
            ((8, model), wide),
            ((tokens, q_cols), low),
            ((2, tokens, 2 * k_cols), wide),
            ((2, tokens, 2 * k_cols), low),
        ],
        [((tokens, model + 128), wide), ((tokens, q_cols), low)],
        [place],
        mixed,
        gates,
        gains,
        small,
        small_far,
        near_out,
        w_out,
        out_far,
        query,
        turns,
        *blocks,
        probs,
        *found,
    )

    given, moe_total = tie((given, moe_total))
    near_pair = beside(given)
    moe_found = spread_pieces(moe_total)
    distant = along((kept[1] + near_pair[1].astype(wide)).astype(low))
    qkv_grad, gain_one_part, *pieces = single(
        last_kernel,
        "last",
        [((tokens, qkv_cols), low), ((8, model), wide)] + piece_shapes,
        [((tokens, model), wide)],
        [place],
        query_grad,
        kept,
        near_pair,
        distant,
        turns,
        small,
        small_far,
        hidden,
    )

    all_routes = plane[:, :, model : model + top].reshape(8 * tokens, top)
    rank_all = ranks(all_routes, expert_ids).reshape(2, 4, each, 16, rows)

    def grads_of(number, pair, held, mark):
        first, count = chunks[number]
        return run_weight_grads(
            place,
            plane,
            pair,
            rank_all[:, :, first : first + count],
            held,
            each,
            first,
            mark,
        )

    def hop_beside(value):
        share = value.shape[1] // 2
        kept = lax.dynamic_slice_in_dim(value, core * share, share, 1)
        given = lax.dynamic_slice_in_dim(value, (1 - core) * share, share, 1)
        return kept + beside(given.astype(low)).astype(wide)

    def hop_across(kept):
        return kept[0] + across(kept[1].astype(low)).astype(wide)

    def hop_along(total):
        return (total + along(total.astype(low)).astype(wide)).astype(low)

    def hop_join(total):
        other = beside(total)
        return jnp.where(
            core == 0,
            jnp.concatenate([total, other], axis=0),
            jnp.concatenate([other, total], axis=0),
        ).astype(wide)

    def both(left, right):
        return jnp.stack([dot(left, right[:, :half], 0, 0), dot(left, right[:, half:], 0, 0)])

    side = hop_beside(
        jnp.concatenate(
            [
                both(head_low, attn_grad),
                both(logit_grad[:, :experts], near[:, :model]),
                jnp.stack([gain_two_part[:, :half], gain_two_part[:, half:]]),
                jnp.zeros((2, 16, half), wide),
            ],
            axis=1,
        )
    )
    mark = jnp.zeros((8, 128), wide)
    tied = tie((*pieces, *moe_found, mark, side, qkv_grad, gain_one_part[0]))
    pieces, moe_found = tied[:tp_size], tied[tp_size : 2 * tp_size]
    mark, side, qkv_grad, gain_one = tied[2 * tp_size :]
    (layer_out,) = single(
        output_kernel,
        "output",
        [((tokens, model), wide)],
        [((tokens, model), wide)],
        [place],
        mixed,
        *moe_found,
    )
    total = reduce_pieces(pieces)
    grads = grads_of(0, pair_zero, None, mark)
    side = hop_across(side)
    d_qkv = hop_beside(dot(normed_one, qkv_grad, 0, 0).reshape(2, half, qkv_cols))
    total, mark, side, d_qkv, pair_one, slots[2] = tie(
        (total, grads[2], side, d_qkv, pair_one, slots[2])
    )
    pair_two = gather_slots(slots[2])
    found = spread_pieces(total)
    grads = grads_of(1, pair_one, grads, mark)
    side = hop_along(side)
    d_qkv = hop_across(d_qkv)
    gain_one = sum([from_tp(gain_one, step) for step in range(1, tp_size)], gain_one)
    *found, mark, side, d_qkv, gain_one = tie((*found, grads[2], side, d_qkv, gain_one))
    (d_hidden,) = single(
        hidden_kernel,
        "hidden",
        [((tokens, model), wide)],
        [((tokens, model), wide)],
        [place],
        hidden,
        gains,
        mixed_grad,
        *found,
    )
    grads = grads_of(2, pair_two, grads, mark)
    d_gate_up = grads[0].reshape(experts, half, 2, width)
    d_down = grads[1].reshape(experts, width, half)
    side_grads = hop_join(side)
    d_qkv = hop_join(hop_along(d_qkv))
    gain_one = gain_one + beside(gain_one)
    gain_one = gain_one + along(gain_one)
    gain_one = gain_one[:half] + across(gain_one[half:])
    return (
        layer_out.reshape(micro, 1, rows, model),
        d_hidden.reshape(micro, 1, rows, model),
        gain_one,
        d_qkv[:, :q_cols],
        d_qkv[:, q_cols : q_cols + k_cols],
        d_qkv[:, q_cols + k_cols :],
        side_grads[:q_cols],
        side_grads[q_cols + experts],
        side_grads[q_cols : q_cols + experts].T,
        d_gate_up,
        d_down,
    )


def solution(mesh):
    placed = (
        P(None, "fsdp", "ctx", None),
        P(None, "fsdp", None),
        P(None, "fsdp", "ctx", None),
        P("fsdp"),
        P("fsdp", "tp"),
        P("fsdp", "tp"),
        P("fsdp", "tp"),
        P("tp", "fsdp"),
        P("fsdp"),
        P("fsdp", None),
        P(None, "fsdp", None, "tp"),
        P(None, "tp", "fsdp"),
        P(None, "fsdp", "ctx", None),
    )
    fits = mesh.shape["fsdp"] == 2 and mesh.shape["ctx"] == 4
    return jax.shard_map(
        fast_body if fits else body,
        mesh=mesh,
        in_specs=placed,
        out_specs=(
            P(None, "fsdp", "ctx", None),
            P(None, "fsdp", "ctx", None),
            P("fsdp"),
            P("fsdp", "tp"),
            P("fsdp", "tp"),
            P("fsdp", "tp"),
            P("tp", "fsdp"),
            P("fsdp"),
            P("fsdp", None),
            P(None, "fsdp", None, "tp"),
            P(None, "tp", "fsdp"),
        ),
        check_vma=False,
    )
```

```python
import functools

import jax
import jax.numpy as jnp
from jax import lax
from jax.experimental import pallas as pl
from jax.experimental.pallas import tpu as pltpu
from jax.sharding import PartitionSpec as P

HEAD_DIM = 64
CAP = 32


EPSILON = 1e-06
RESIDUAL_SCALE = 0.22
SCORE_SCALE = 1.0 / 64.0
ROPE_BASE = 10000.0
TOP_PRECISION = lax.Precision.HIGHEST


def tree_tables(parent_row, tree_len):
    seg_total = parent_row.shape[0]
    seg_len = tree_len // seg_total
    seg_ids = jnp.arange(seg_total, dtype=jnp.int32)
    parent_links = (parent_row[:, None] == seg_ids[None, :]).astype(jnp.float32)
    reach_table = jnp.maximum(parent_links, jnp.eye(seg_total, dtype=jnp.float32))
    for squaring in range(max(seg_total - 1, 1).bit_length()):
        reach_table = jnp.minimum(jnp.dot(reach_table, reach_table, precision=TOP_PRECISION), 1.0)
    seg_depth = jnp.sum(reach_table, axis=1) - 1.0
    token_ids = jnp.arange(tree_len, dtype=jnp.int32)
    tok_owner = ((token_ids // seg_len)[:, None] == seg_ids[None, :]).astype(jnp.float32)
    tok_offset = (token_ids % seg_len).astype(jnp.float32)
    places = jnp.dot(tok_owner, seg_depth, precision=TOP_PRECISION) * seg_len + tok_offset
    return (places, jnp.dot(tok_owner, reach_table, precision=TOP_PRECISION), tok_owner)


def rope_tables(places):
    half_dim = HEAD_DIM // 2
    inverse = ROPE_BASE ** (-jnp.arange(half_dim, dtype=jnp.float32) * 2.0 / HEAD_DIM)
    angles = places[:, None] * inverse[None, :]
    cosine_table = jnp.concatenate([jnp.cos(angles), jnp.cos(angles)], axis=1)
    sine_values = jnp.concatenate([jnp.sin(angles), jnp.sin(angles)], axis=1)
    return (cosine_table, sine_values)


def apply_rotary(values, cosine_table, sine_values):
    half_dim = values.shape[-1] // 2
    turned = jnp.concatenate([-values[..., half_dim:], values[..., :half_dim]], axis=-1)
    return values * cosine_table[:, None, :] + turned * sine_values[:, None, :]


def norm_scale(values):
    return lax.rsqrt(jnp.mean(values * values, axis=-1, keepdims=True) + EPSILON)


def add_tuples(first_tuple, second_tuple):
    return tuple(
        (left_part + right_part for left_part, right_part in zip(first_tuple, second_tuple))
    )


def expert_work(rows, row_grads, gate_up_w, down_w, down_form):
    gate_up = jnp.einsum("ecd,edsf->ecsf", rows, gate_up_w, preferred_element_type=jnp.float32)
    gate_pre = gate_up[:, :, 0]
    up_pre = gate_up[:, :, 1]
    sigmoid = jax.nn.sigmoid(gate_pre)
    activ_low = (gate_pre * sigmoid * up_pre).astype(jnp.bfloat16)
    expert_out = jnp.einsum(
        "ecf," + down_form + "->ecd", activ_low, down_w, preferred_element_type=jnp.float32
    )
    activ_grad = jnp.einsum(
        "ecd," + down_form + "->ecf", row_grads, down_w, preferred_element_type=jnp.float32
    )
    gate_grad = activ_grad * up_pre * sigmoid * (1.0 + gate_pre * (1.0 - sigmoid))
    up_grad = activ_grad * gate_pre * sigmoid
    gate_up_grad = jnp.stack([gate_grad, up_grad], axis=2).astype(jnp.bfloat16)
    row_input_grad = jnp.einsum(
        "ecsf,edsf->ecd", gate_up_grad, gate_up_w, preferred_element_type=jnp.float32
    )
    grad_gate_up = jnp.einsum(
        "ecd,ecsf->edsf", rows, gate_up_grad, preferred_element_type=jnp.float32
    )
    grad_down = jnp.einsum(
        "ecf,ecd->" + down_form, activ_low, row_grads, preferred_element_type=jnp.float32
    )
    return (expert_out, row_input_grad, grad_gate_up, grad_down)


def body(
    hidden_in,
    parents,
    routes,
    attn_gain,
    w_query,
    key_projection,
    value_projection,
    w_out,
    moe_gain,
    w_router,
    w_gate_up,
    w_down,
    d_out,
):
    experts = w_gate_up.shape[0]
    gathered = (
        lax.all_gather(attn_gain, "fsdp", axis=0, tiled=True),
        lax.all_gather(w_query, "fsdp", axis=0, tiled=True),
        lax.all_gather(key_projection, "fsdp", axis=0, tiled=True),
        lax.all_gather(value_projection, "fsdp", axis=0, tiled=True),
        lax.all_gather(w_out, "fsdp", axis=1, tiled=True),
        lax.all_gather(moe_gain, "fsdp", axis=0, tiled=True),
        lax.all_gather(w_router, "fsdp", axis=0, tiled=True),
        lax.all_gather(w_gate_up, "fsdp", axis=1, tiled=True),
        lax.all_gather(w_down, "fsdp", axis=2, tiled=True),
    )
    gate_up_full = gathered[7]
    down_full = gathered[8]
    down_form = "efd"
    gain_one = gathered[0].astype(jnp.float32)
    query_full = gathered[1]
    key_full = gathered[2]
    value_full = gathered[3]
    out_full = gathered[4]
    gain_two = gathered[5].astype(jnp.float32)
    router_full = gathered[6]
    micro_count = hidden_in.shape[0]
    local_rows = hidden_in.shape[2]
    model_width = hidden_in.shape[3]
    top_count = routes.shape[3]
    kv_heads = key_projection.shape[1] // HEAD_DIM
    q_heads = w_query.shape[1] // HEAD_DIM
    group_size = q_heads // kv_heads
    tree_len = local_rows * lax.axis_size("ctx")
    row_start = lax.axis_index("ctx") * local_rows
    capacity = CAP
    expert_ids = jnp.arange(experts, dtype=jnp.int32)
    outputs = []
    input_grads = []
    totals = None
    for batch_index in range(micro_count):
        tree_places, reach_rows, tok_owner = tree_tables(parents[batch_index, 0], tree_len)
        local_places = lax.dynamic_slice_in_dim(tree_places, row_start, local_rows, 0)
        local_reach = lax.dynamic_slice_in_dim(reach_rows, row_start, local_rows, 0)
        allowed = (jnp.dot(local_reach, tok_owner.T, precision=TOP_PRECISION) > 0.5) & (
            tree_places[None, :] <= local_places[:, None]
        )
        cosine_table, sine_values = rope_tables(local_places)
        inputs = hidden_in[batch_index, 0].astype(jnp.float32)
        scale_one = norm_scale(inputs)
        first_normed = (inputs * scale_one * gain_one).astype(jnp.bfloat16)
        query_unrotated = jnp.dot(
            first_normed, query_full, preferred_element_type=jnp.float32
        ).reshape(local_rows, q_heads, HEAD_DIM)
        key_unrotated = jnp.dot(first_normed, key_full, preferred_element_type=jnp.float32).reshape(
            local_rows, kv_heads, HEAD_DIM
        )
        value_reduced = jnp.dot(
            first_normed, value_full, preferred_element_type=jnp.float32
        ).astype(jnp.bfloat16)
        query_reduced = (
            apply_rotary(query_unrotated, cosine_table, sine_values)
            .astype(jnp.bfloat16)
            .reshape(local_rows, kv_heads, group_size, HEAD_DIM)
        )
        key_low = (
            apply_rotary(key_unrotated, cosine_table, sine_values)
            .astype(jnp.bfloat16)
            .reshape(local_rows, kv_heads * HEAD_DIM)
        )
        tree_keys, tree_values = (
            lax.all_gather(key_low, "ctx", axis=0, tiled=True),
            lax.all_gather(value_reduced, "ctx", axis=0, tiled=True),
        )
        tree_keys = tree_keys.reshape(tree_len, kv_heads, HEAD_DIM)
        tree_values = tree_values.reshape(tree_len, kv_heads, HEAD_DIM)

        def masked_scores():
            raw_scores = jnp.einsum(
                "qhjd,khd->hjqk", query_reduced, tree_keys, preferred_element_type=jnp.float32
            )
            return jnp.where(allowed[None, None], raw_scores * SCORE_SCALE, -1e30)

        scores = masked_scores()
        top_score = jnp.max(scores, axis=-1, keepdims=True)
        log_total = top_score + jnp.log(
            jnp.sum(jnp.exp(scores - top_score), axis=-1, keepdims=True)
        )
        probs_low = jnp.exp(scores - log_total).astype(jnp.bfloat16)
        head_out = jnp.einsum(
            "hjqk,khd->qhjd", probs_low, tree_values, preferred_element_type=jnp.float32
        )
        head_low = head_out.reshape(local_rows, q_heads * HEAD_DIM).astype(jnp.bfloat16)
        attn_part = jnp.dot(head_low, out_full, preferred_element_type=jnp.float32)
        attended = lax.psum(attn_part.astype(jnp.bfloat16), "tp").astype(jnp.float32)
        mixed = inputs + RESIDUAL_SCALE * attended
        scale_two = norm_scale(mixed)
        normed_two = (mixed * scale_two * gain_two).astype(jnp.bfloat16)
        logits = jnp.dot(normed_two, router_full, preferred_element_type=jnp.float32)
        chosen_ids = routes[batch_index, 0]
        picked = (chosen_ids[:, :, None] == expert_ids[None, None, :]).astype(jnp.float32)
        chosen = jnp.sum(picked * logits[:, None, :], axis=2)
        gates = jax.nn.softmax(chosen, axis=1)
        flat_ids = chosen_ids.reshape(-1)
        flat_hot = (flat_ids[:, None] == expert_ids[None, :]).astype(jnp.int32)
        slots = jnp.sum((jnp.cumsum(flat_hot, axis=0) - flat_hot) * flat_hot, axis=1)
        targets = flat_ids * capacity + slots
        sources = (
            jnp.zeros((experts * capacity,), jnp.int32)
            .at[targets]
            .set(jnp.arange(local_rows * top_count, dtype=jnp.int32) // top_count)
        )
        filled = jnp.zeros((experts * capacity, 1), jnp.bfloat16).at[targets].set(1)
        dispatched = (normed_two[sources] * filled).reshape(experts, capacity, model_width)
        grad_out = d_out[batch_index, 0].astype(jnp.float32)
        grad_moe = RESIDUAL_SCALE * grad_out
        entry_grad = (
            (gates[:, :, None] * grad_moe[:, None, :])
            .astype(jnp.bfloat16)
            .reshape(local_rows * top_count, model_width)
        )
        slot_grad = (
            jnp.zeros((experts * capacity, model_width), jnp.bfloat16)
            .at[targets]
            .set(entry_grad)
            .reshape(experts, capacity, model_width)
        )
        expert_out, slot_input_grad, grad_gate_up, grad_down = expert_work(
            dispatched, slot_grad, gate_up_full, down_full, down_form
        )
        entry_out = expert_out.reshape(experts * capacity, model_width)[targets].reshape(
            local_rows, top_count, model_width
        )
        moe_part = jnp.sum(gates[:, :, None] * entry_out, axis=1)
        moe_sum = lax.psum(moe_part.astype(jnp.bfloat16), "tp").astype(jnp.float32)
        outputs.append(mixed + RESIDUAL_SCALE * moe_sum)
        gate_grad_part = jnp.sum(grad_moe[:, None, :] * entry_out, axis=2)
        expert_input_grad = jnp.sum(
            slot_input_grad.reshape(experts * capacity, model_width)[targets].reshape(
                local_rows, top_count, model_width
            ),
            axis=1,
        )
        expert_input_grad, gate_grads = (
            lax.psum(expert_input_grad.astype(jnp.bfloat16), "tp").astype(jnp.float32),
            lax.psum(gate_grad_part.astype(jnp.bfloat16), "tp").astype(jnp.float32),
        )
        chosen_grad = gates * (gate_grads - jnp.sum(gates * gate_grads, axis=1, keepdims=True))
        logit_grad = jnp.sum(picked * chosen_grad[:, :, None], axis=1).astype(jnp.bfloat16)
        normed_two_grad = expert_input_grad + jnp.einsum(
            "te,de->td", logit_grad, router_full, preferred_element_type=jnp.float32
        )
        grad_router = jnp.einsum(
            "td,te->de", normed_two, logit_grad, preferred_element_type=jnp.float32
        )
        unit_two = mixed * scale_two
        grad_gain_two = jnp.sum(normed_two_grad * unit_two, axis=0)
        scaled_two = normed_two_grad * gain_two
        mixed_grad = grad_out + scale_two * (
            scaled_two - unit_two * jnp.mean(scaled_two * unit_two, axis=-1, keepdims=True)
        )
        attn_grad = (RESIDUAL_SCALE * mixed_grad).astype(jnp.bfloat16)
        grad_out_proj = jnp.einsum(
            "tc,td->cd", head_low, attn_grad, preferred_element_type=jnp.float32
        )
        head_grad = (
            jnp.einsum("td,cd->tc", attn_grad, out_full, preferred_element_type=jnp.float32)
            .astype(jnp.bfloat16)
            .reshape(local_rows, kv_heads, group_size, HEAD_DIM)
        )
        scores = masked_scores()
        probs = jnp.exp(scores - log_total)
        probs_low = probs.astype(jnp.bfloat16)
        prob_grad = jnp.einsum(
            "qhjd,khd->hjqk", head_grad, tree_values, preferred_element_type=jnp.float32
        )
        value_grad = jnp.einsum(
            "hjqk,qhjd->khd", probs_low, head_grad, preferred_element_type=jnp.float32
        )
        score_grad = (
            SCORE_SCALE * probs * (prob_grad - jnp.sum(probs * prob_grad, axis=-1, keepdims=True))
        ).astype(jnp.bfloat16)
        query_grad = jnp.einsum(
            "hjqk,khd->qhjd", score_grad, tree_keys, preferred_element_type=jnp.float32
        ).reshape(local_rows, q_heads, HEAD_DIM)
        key_grad = jnp.einsum(
            "hjqk,qhjd->khd", score_grad, query_reduced, preferred_element_type=jnp.float32
        )
        key_grad, value_grad = (
            lax.psum_scatter(
                key_grad.reshape(tree_len, kv_heads * HEAD_DIM).astype(jnp.bfloat16),
                "ctx",
                scatter_dimension=0,
                tiled=True,
            ).astype(jnp.float32),
            lax.psum_scatter(
                value_grad.reshape(tree_len, kv_heads * HEAD_DIM).astype(jnp.bfloat16),
                "ctx",
                scatter_dimension=0,
                tiled=True,
            ).astype(jnp.float32),
        )
        query_pre_grad = (
            apply_rotary(query_grad, cosine_table, -sine_values)
            .astype(jnp.bfloat16)
            .reshape(local_rows, q_heads * HEAD_DIM)
        )
        key_pre_grad = (
            apply_rotary(
                key_grad.reshape(local_rows, kv_heads, HEAD_DIM), cosine_table, -sine_values
            )
            .astype(jnp.bfloat16)
            .reshape(local_rows, kv_heads * HEAD_DIM)
        )
        value_pre_grad = value_grad.astype(jnp.bfloat16)
        normed_one_grad = jnp.einsum(
            "tc,dc->td", query_pre_grad, query_full, preferred_element_type=jnp.float32
        )
        normed_one_grad = normed_one_grad + jnp.einsum(
            "tc,dc->td", key_pre_grad, key_full, preferred_element_type=jnp.float32
        )
        normed_one_grad = normed_one_grad + jnp.einsum(
            "tc,dc->td", value_pre_grad, value_full, preferred_element_type=jnp.float32
        )
        grad_query = jnp.einsum(
            "td,tc->dc", first_normed, query_pre_grad, preferred_element_type=jnp.float32
        )
        grad_key = jnp.einsum(
            "td,tc->dc", first_normed, key_pre_grad, preferred_element_type=jnp.float32
        )
        grad_value = jnp.einsum(
            "td,tc->dc", first_normed, value_pre_grad, preferred_element_type=jnp.float32
        )
        normed_one_grad = lax.psum(normed_one_grad.astype(jnp.bfloat16), "tp").astype(jnp.float32)
        unit_one = inputs * scale_one
        grad_gain_one = jnp.sum(normed_one_grad * unit_one, axis=0)
        scaled_one = normed_one_grad * gain_one
        input_grads.append(
            mixed_grad
            + scale_one
            * (scaled_one - unit_one * jnp.mean(scaled_one * unit_one, axis=-1, keepdims=True))
        )
        piece = (
            grad_gain_one,
            grad_query,
            grad_key,
            grad_value,
            grad_out_proj,
            grad_gain_two,
            grad_router,
            grad_gate_up,
            grad_down,
        )
        totals = piece if batch_index == 0 else add_tuples(totals, piece)
    summed = (
        lax.psum_scatter(totals[0], ("fsdp", "ctx"), scatter_dimension=0, tiled=True),
        lax.psum_scatter(totals[1], ("fsdp", "ctx"), scatter_dimension=0, tiled=True),
        lax.psum_scatter(totals[2], ("fsdp", "ctx"), scatter_dimension=0, tiled=True),
        lax.psum_scatter(totals[3], ("fsdp", "ctx"), scatter_dimension=0, tiled=True),
        lax.psum_scatter(totals[4], ("fsdp", "ctx"), scatter_dimension=1, tiled=True),
        lax.psum_scatter(totals[5], ("fsdp", "ctx"), scatter_dimension=0, tiled=True),
        lax.psum_scatter(totals[6], ("fsdp", "ctx"), scatter_dimension=0, tiled=True),
        lax.psum_scatter(totals[7], ("fsdp", "ctx"), scatter_dimension=1, tiled=True),
        lax.psum_scatter(totals[8], ("fsdp", "ctx"), scatter_dimension=2, tiled=True),
    )
    shares = (
        lax.all_gather(summed[0].astype(jnp.bfloat16), "ctx", axis=0, tiled=True).astype(
            jnp.float32
        ),
        lax.all_gather(summed[1].astype(jnp.bfloat16), "ctx", axis=0, tiled=True).astype(
            jnp.float32
        ),
        lax.all_gather(summed[2].astype(jnp.bfloat16), "ctx", axis=0, tiled=True).astype(
            jnp.float32
        ),
        lax.all_gather(summed[3].astype(jnp.bfloat16), "ctx", axis=0, tiled=True).astype(
            jnp.float32
        ),
        lax.all_gather(summed[4].astype(jnp.bfloat16), "ctx", axis=1, tiled=True).astype(
            jnp.float32
        ),
        lax.all_gather(summed[5].astype(jnp.bfloat16), "ctx", axis=0, tiled=True).astype(
            jnp.float32
        ),
        lax.all_gather(summed[6].astype(jnp.bfloat16), "ctx", axis=0, tiled=True).astype(
            jnp.float32
        ),
        lax.all_gather(summed[7].astype(jnp.bfloat16), "ctx", axis=1, tiled=True).astype(
            jnp.float32
        ),
        lax.all_gather(summed[8].astype(jnp.bfloat16), "ctx", axis=2, tiled=True).astype(
            jnp.float32
        ),
    )
    layer_out = jnp.stack(outputs, axis=0)[:, None]
    d_hidden = jnp.stack(input_grads, axis=0)[:, None]
    return (
        layer_out,
        d_hidden,
        shares[0],
        shares[1],
        shares[2],
        shares[3],
        shares[4],
        shares[5],
        shares[6],
        shares[7],
        shares[8],
    )


def dot(left, right, left_dim=1, right_dim=0):
    return lax.dot_general(
        left, right, (((left_dim,), (right_dim,)), ((), ())), preferred_element_type=jnp.float32
    )


def kernel_params(count=0):
    return pltpu.CompilerParams(
        dimension_semantics=("arbitrary",) * count if count else None,
        vmem_limit_bytes=60 * 1024 * 1024,
    )


def single(kernel, name, out_shape, scratch, scalars, *arrays):
    smem = pl.BlockSpec(memory_space=pltpu.SMEM)
    vmem = pl.BlockSpec(memory_space=pltpu.VMEM)
    return pl.pallas_call(
        kernel,
        out_shape=tuple(jax.ShapeDtypeStruct(shape, kind) for shape, kind in out_shape),
        in_specs=[smem] * len(scalars) + [vmem] * len(arrays),
        out_specs=(vmem,) * len(out_shape),
        scratch_shapes=[pltpu.VMEM(shape, kind) for shape, kind in scratch],
        compiler_params=kernel_params(),
        name=name,
    )(*scalars, *arrays)


def tree_path(parents_ref, m, start):
    path = [start]
    for _ in range(3):
        path.append(parents_ref[m, path[-1]])
    return path


def own_then_other(x_pos, array):
    half = array.shape[-1] // 2
    first, second = array[..., :half], array[..., half:]
    return jnp.where(x_pos == 0, first, second), jnp.where(x_pos == 0, second, first)


def row_scale(near, far):
    total = jnp.sum(near * near, axis=1, keepdims=True) + jnp.sum(far * far, axis=1, keepdims=True)
    return lax.rsqrt(total / (2 * near.shape[1]) + EPSILON)


def turn_heads(values):
    half_dim = HEAD_DIM // 2
    lane = lax.broadcasted_iota(jnp.int32, values.shape, 1) % HEAD_DIM
    width = values.shape[1]
    return jnp.where(
        lane < half_dim,
        -pltpu.roll(values, width - half_dim, 1),
        pltpu.roll(values, half_dim, 1),
    )


def split_kernel(base_ref, both_ref, down_ref, out_ref, wide_buf):
    wide_buf[...] = both_ref[0].astype(jnp.float32)
    half = both_ref.shape[1] // 2
    out_ref[0, :half, :] = wide_buf[pl.ds(0, half, stride=2), :].astype(jnp.bfloat16)
    out_ref[0, half : 2 * half, :] = wide_buf[pl.ds(1, half, stride=2), :].astype(jnp.bfloat16)
    if down_ref is not None:
        width = down_ref.shape[1]
        for j in range(half // 128):
            out_ref[0, 2 * half + j * width : 2 * half + (j + 1) * width, :] = down_ref[
                0, :, j * 128 : (j + 1) * 128
            ]


def split_plain_kernel(base_ref, both_ref, out_ref, wide_buf):
    split_kernel(base_ref, both_ref, None, out_ref, wide_buf)


def split_weights(base, count, gate_up, down):
    _, rows, width = gate_up.shape
    packed = rows if down is None else rows + rows // 2
    in_specs = [pl.BlockSpec((1, rows, width), lambda i, base: (base[0] + i, 0, 0))]
    operands = [base, gate_up]
    if down is not None:
        in_specs.append(
            pl.BlockSpec((1, *down.shape[1:]), lambda i, base: (base[0] + i, 0, 0))
        )
        operands.append(down)
    return pl.pallas_call(
        split_plain_kernel if down is None else split_kernel,
        out_shape=jax.ShapeDtypeStruct((count, packed, width), jnp.bfloat16),
        grid_spec=pltpu.PrefetchScalarGridSpec(
            num_scalar_prefetch=1,
            grid=(count,),
            in_specs=in_specs,
            out_specs=pl.BlockSpec((1, packed, width), lambda i, base: (i, 0, 0)),
            scratch_shapes=[pltpu.VMEM((rows, width), jnp.float32)],
        ),
        compiler_params=kernel_params(1),
        name="split_weights",
    )(*operands)


def before_kernel(
    place_ref,
    parents_ref,
    hidden_ref,
    small_ref,
    sent_ref,
    next_ref,
    cosine_ref,
    sine_ref,
    normed_ref,
    query_ref,
    key_value_ref,
    far_ref,
    gains_ref,
    turn_ref,
):
    x_pos, c_pos = place_ref[0], place_ref[1]
    first_core = c_pos % 2 == 0
    half = small_ref.shape[1]
    part = half // 2
    q_cols = query_ref.shape[1]
    kv_cols = key_value_ref.shape[1]
    cols = q_cols + kv_cols
    turned_cols = q_cols + kv_cols // 2
    own_rows = small_ref[: 2 * part, :]
    sent, beside = sent_ref[:part, :], next_ref[:part, :]
    top = jnp.where(first_core, sent, beside)
    low_rows = jnp.where(first_core, beside, sent)
    far_ref[:part, :] = top
    far_ref[part:, :] = low_rows
    own_gain = small_ref[2 * part : 2 * part + 16, :].astype(jnp.float32)
    far_gain = sent_ref[part : part + 16, :].astype(jnp.float32)
    gains_ref[:, :half] = own_gain
    gains_ref[:, half:] = far_gain
    near, far = own_then_other(x_pos, hidden_ref[...].astype(jnp.float32))
    scale = row_scale(near, far)
    near_low = (near * scale * own_gain[:1]).astype(jnp.bfloat16)
    far_low = (far * scale * far_gain[:1]).astype(jnp.bfloat16)
    normed_ref[:, :half] = near_low
    normed_ref[:, half:] = far_low
    made = (
        dot(near_low, own_rows[:, :cols])
        + dot(far_low[:, :part], top[:, :cols])
        + dot(far_low[:, part:], low_rows[:, :cols])
    )
    micro = parents_ref.shape[0]
    rows = hidden_ref.shape[0] // micro
    turns = []
    for m in range(micro):
        path = tree_path(parents_ref, m, c_pos)
        depth = sum((path[i + 1] != path[i]).astype(jnp.int32) for i in range(3))
        span = pl.ds(depth * rows, rows)
        turns.append((cosine_ref[span, :], sine_ref[span, :]))
    cosines = jnp.concatenate([pair[0] for pair in turns], axis=0)
    sines = jnp.concatenate([pair[1] for pair in turns], axis=0)
    turn_ref[0] = cosines
    turn_ref[1] = sines
    count = turned_cols // 128
    values = made[:, :turned_cols]
    rotated = (
        values * jnp.concatenate([cosines] * count, axis=1)
        + turn_heads(values) * jnp.concatenate([sines] * count, axis=1)
    ).astype(jnp.bfloat16)
    query_ref[...] = rotated[:, :q_cols]
    key_value_ref[:, : kv_cols // 2] = rotated[:, q_cols:]
    key_value_ref[:, kv_cols // 2 :] = made[:, turned_cols:].astype(jnp.bfloat16)


def give_pieces(whole_ref, z_pos, piece_refs):
    count = len(piece_refs)
    part = whole_ref.shape[0] // count
    for s in range(count):
        start = pl.multiple_of(((z_pos + s) % count) * part, part)
        piece_refs[s][...] = whole_ref[pl.ds(start, part), :].astype(piece_refs[s].dtype)


def take_pieces(piece_refs, z_pos, whole_ref):
    count = len(piece_refs)
    part = whole_ref.shape[0] // count
    for s in range(count):
        start = pl.multiple_of(((z_pos + s) % count) * part, part)
        whole_ref[pl.ds(start, part), :] = piece_refs[s][...].astype(whole_ref.dtype)


def stack_heads(source, first, group):
    return jnp.concatenate(
        [source[:, (first + h) * HEAD_DIM : (first + h + 1) * HEAD_DIM] for h in range(group)],
        axis=0,
    )


def attend_kernel(
    place_ref,
    parents_ref,
    query_ref,
    kv0,
    kv1,
    kv2,
    kv3,
    out_near_ref,
    out_sent_ref,
    out_next_ref,
    head_ref,
    probs_ref,
    out_far_ref,
    attn_ref,
):
    c_pos = place_ref[1]
    blocks = (kv0, kv1, kv2, kv3)
    micro = parents_ref.shape[0]
    rows = query_ref.shape[0] // micro
    kv_heads = kv0.shape[1] // (2 * HEAD_DIM)
    group = query_ref.shape[1] // HEAD_DIM // kv_heads
    shape = (group * rows, rows)
    causal = (
        lax.broadcasted_iota(jnp.int32, shape, 1)
        <= lax.broadcasted_iota(jnp.int32, shape, 0) % rows
    )
    for m in range(micro):
        span = pl.ds(m * rows, rows)
        whole = query_ref[span, :]
        path = tree_path(parents_ref, m, c_pos)
        pieces = []
        for g in range(kv_heads):
            query = stack_heads(whole, g * group, group)
            parts = []
            for r in range(4):
                keys = blocks[r][span, :][:, g * HEAD_DIM : (g + 1) * HEAD_DIM]
                part = dot(query, keys, 1, 1) * SCORE_SCALE
                if r == 0:
                    part = jnp.where(causal, part, -1e30)
                else:
                    seen = (path[1] == c_pos ^ r) | (path[2] == c_pos ^ r) | (path[3] == c_pos ^ r)
                    part = jnp.where(seen, part, -1e30)
                parts.append(part)
            scores = jnp.concatenate(parts, axis=1)
            powers = jnp.exp(scores - jnp.max(scores, axis=1, keepdims=True))
            probs = powers * (1.0 / jnp.sum(powers, axis=1, keepdims=True))
            probs_ref[m * kv_heads + g] = probs
            low = probs.astype(jnp.bfloat16)
            values = jnp.concatenate(
                [
                    blocks[r][span, :][:, (kv_heads + g) * HEAD_DIM : (kv_heads + g + 1) * HEAD_DIM]
                    for r in range(4)
                ],
                axis=0,
            )
            mixed = dot(low, values)
            pieces += [mixed[h * rows : (h + 1) * rows] for h in range(group)]
        head_ref[span, :] = jnp.concatenate(pieces, axis=1).astype(jnp.bfloat16)
    first_core = c_pos % 2 == 0
    sent, beside = out_sent_ref[...], out_next_ref[...]
    part = sent.shape[0]
    out_far_ref[:part, :] = jnp.where(first_core, sent, beside)
    out_far_ref[part:, :] = jnp.where(first_core, beside, sent)
    half = sent.shape[1]
    attn_ref[:, :half] = dot(head_ref[...], out_near_ref[...]).astype(jnp.bfloat16)
    attn_ref[:, half:] = dot(head_ref[...], out_far_ref[...]).astype(jnp.bfloat16)


def after_kernel(
    place_ref,
    hidden_ref,
    gains_ref,
    small_ref,
    far_ref,
    routes_ref,
    attended_ref,
    mixed_ref,
    rows_ref,
    gates_ref,
):
    half = small_ref.shape[1]
    near, far = own_then_other(place_ref[0], hidden_ref[...].astype(jnp.float32))
    near = near + RESIDUAL_SCALE * attended_ref[:, :half].astype(jnp.float32)
    far = far + RESIDUAL_SCALE * attended_ref[:, half:].astype(jnp.float32)
    mixed_ref[:, :half] = near
    mixed_ref[:, half:] = far
    scale = row_scale(near, far)
    near_low = (near * scale * gains_ref[1:2, :half]).astype(jnp.bfloat16)
    far_low = (far * scale * gains_ref[1:2, half:]).astype(jnp.bfloat16)
    rows_ref[:, :half] = near_low
    rows_ref[:, half : 2 * half] = far_low
    logits = dot(near_low, small_ref[:half, half - 128 :]) + dot(far_low, far_ref[:, half - 128 :])
    lane = lax.broadcasted_iota(jnp.int32, logits.shape, 1)
    named = lane == routes_ref[:, 0:1]
    for k in range(1, routes_ref.shape[1]):
        named = named | (lane == routes_ref[:, k : k + 1])
    logits = jnp.where(named, logits, -1e30)
    powers = jnp.where(named, jnp.exp(logits - jnp.max(logits, axis=1, keepdims=True)), 0.0)
    gates = powers / jnp.sum(powers, axis=1, keepdims=True)
    gates_ref[...] = gates
    high = gates.astype(jnp.bfloat16)
    rest_part = gates - high.astype(jnp.float32)
    rows_ref[:, 2 * half :] = jnp.where(
        lane < 64, high.astype(jnp.float32), pltpu.roll(rest_part, 64, 1)
    ).astype(jnp.bfloat16)


def expert_kernel(
    place_ref,
    near_ref,
    far_ref,
    near_out_ref,
    far_out_ref,
    rank_ref,
    gate_up_ref,
    down_ref,
    *rest,
    first,
    last,
    each,
    split,
):
    count = 4 if split else 1
    other_refs, rest = rest[:count], rest[count:]
    held = rest[:4] if last else ()
    slots_ref, *sums = rest[len(held) : -8]
    rows_buf, grads_buf, moe_buf, back_buf, hot_buf, gate_buf, out_ref, grad_ref = rest[-8:]
    half = down_ref.shape[-1]
    full = 2 * half
    width = down_ref.shape[-2]
    step = pl.program_id(0)
    quarter = [place_ref[1] ^ r for r in range(4)]
    expert = [(place_ref[0] * 4 + quarter[r]) * each + first + step for r in range(4)]
    iota = lax.broadcasted_iota(jnp.int32, (CAP, 128), 0)
    lane = lax.broadcasted_iota(jnp.int32, (CAP, 128), 1)

    @pl.when(step == 0)
    def _():
        if last:
            out_ref[...] = held[0][...].astype(jnp.float32) + held[2][...].astype(jnp.float32)
            grad_ref[...] = held[1][...].astype(jnp.float32) + held[3][...].astype(jnp.float32)
        else:
            out_ref[...] = jnp.zeros_like(out_ref)
            grad_ref[...] = jnp.zeros_like(grad_ref)

    marks = [((lane == expert[r]) | (lane == expert[r] + 64)) for r in range(4)]
    mark = jnp.concatenate(marks, axis=0)
    for b in range(4):
        low = jnp.concatenate(
            [
                jnp.where(iota == rank_ref[quarter[r], 0, pl.ds(b, 1), :], 1.0, 0.0)
                for r in range(4)
            ],
            axis=0,
        ).astype(jnp.bfloat16)
        hot_buf[b] = low
        span = pl.ds((b % 2) * 128, 128)
        source = near_ref if b < 2 else far_ref
        picked = jnp.where(mark, dot(low, source[span, pl.ds(full, 128)]), 0.0)
        gate_buf[b] = jnp.broadcast_to(jnp.sum(picked, axis=1, keepdims=True), (4 * CAP, 128))
        for part in range(2):
            keep = pl.ds(part * half, half)
            if b < 2:
                rows, grads = near_ref[span, keep], near_out_ref[span, keep]
            else:
                swap = pl.ds((1 - part) * half, half)
                rows, grads = far_ref[span, swap], far_out_ref[span, swap]
            rows_buf[b, :, keep] = dot(low, rows).astype(jnp.bfloat16)
            grads_buf[b, :, keep] = dot(low, grads).astype(jnp.bfloat16)
    for r in range(4):
        q = quarter[r]
        slot = slice(r * CAP, (r + 1) * CAP)
        rows = jnp.concatenate([rows_buf[b, slot, :] for b in range(4)], axis=0)
        grads = jnp.concatenate([grads_buf[b, slot, :] for b in range(4)], axis=0)
        gate = jnp.concatenate([gate_buf[b, slot, :] for b in range(4)], axis=0)
        near_w = jnp.concatenate(
            [gate_up_ref[q, 0, :half, :], gate_up_ref[q, 0, half:, :]], axis=1
        )
        def other(start, size):
            if split:
                return other_refs[r][0, start : start + size, :]
            return other_refs[0][q, 0, start : start + size, :]

        far_w = jnp.concatenate([other(0, half), other(half, half)], axis=1)
        near_down = down_ref[0, q, 0]
        far_down = jnp.concatenate(
            [other(2 * half + j * width, width) for j in range(half // 128)],
            axis=1,
        )
        gate_up = dot(rows[:, :half], near_w) + dot(rows[:, half:], far_w)
        gate_pre = gate_up[:, :width]
        up_pre = gate_up[:, width:]
        sigmoid = 1.0 / (1.0 + jnp.exp(-gate_pre))
        activ = (gate_pre * sigmoid * up_pre).astype(jnp.bfloat16)
        pulled = RESIDUAL_SCALE * (
            dot(grads[:, :half], near_down, 1, 1) + dot(grads[:, half:], far_down, 1, 1)
        )
        activ_wide = activ.astype(jnp.float32)
        gate_grad = jnp.sum(activ_wide * pulled, axis=1, keepdims=True)
        activ_grad = pulled * gate
        gate_pre_grad = activ_grad * up_pre * sigmoid * (1.0 + gate_pre * (1.0 - sigmoid))
        up_pre_grad = activ_grad * gate_pre * sigmoid
        both = jnp.concatenate([gate_pre_grad, up_pre_grad], axis=1).astype(jnp.bfloat16)
        slots_ref[q, 0, :, : 2 * width] = both
        slots_ref[q, 0, :, 2 * width :] = (activ_wide * gate * RESIDUAL_SCALE).astype(jnp.bfloat16)
        for part, (wide, low_w) in enumerate(((near_w, near_down), (far_w, far_down))):
            keep = pl.ds(part * half, half)
            made = dot(activ, low_w)
            back = dot(both, wide, 1, 1)
            for b in range(4):
                piece = slice(b * CAP, (b + 1) * CAP)
                scale = jnp.concatenate([gate[piece]] * (half // 128), axis=1)
                moe_buf[b, slot, keep] = (made[piece] * scale).astype(jnp.bfloat16)
                back_buf[b, slot, keep] = back[piece].astype(jnp.bfloat16)
        spot = lane == expert[r]
        for b in range(4):
            back_buf[b, slot, pl.ds(full, 128)] = jnp.where(
                spot, gate_grad[b * CAP : (b + 1) * CAP], 0.0
            ).astype(jnp.bfloat16)
    for b in range(4):
        span = pl.ds(b * 128, 128)
        out_ref[span, :] += dot(hot_buf[b], moe_buf[b], 0, 0)
        grad_ref[span, :] += dot(hot_buf[b], back_buf[b], 0, 0)

    @pl.when(step == pl.num_programs(0) - 1)
    def _():
        if not last:
            sums[0][...] = out_ref[...].astype(jnp.bfloat16)
            sums[1][...] = grad_ref[...].astype(jnp.bfloat16)
            return
        moe_ref, back_ref, moe_far_ref, back_far_ref = sums
        count = moe_ref.shape[0]
        span = pl.ds(count, count)
        moe_ref[...] = out_ref[:count, :]
        back_ref[...] = grad_ref[:count, :]
        for part in range(2):
            keep, swap = pl.ds(part * half, half), pl.ds((1 - part) * half, half)
            moe_far_ref[:, keep] = out_ref[span, swap].astype(jnp.bfloat16)
            back_far_ref[:, keep] = grad_ref[span, swap].astype(jnp.bfloat16)
        back_far_ref[:, pl.ds(full, 128)] = grad_ref[span, pl.ds(full, 128)].astype(jnp.bfloat16)


def run_experts(place, near, far, near_out, far_out, rank, gate_up, down, other, held, first, each):
    split = isinstance(other, list)
    others = other if split else [other]
    steps, packed, lanes = others[0].shape[-3:]
    quarters, _, rows, width = gate_up.shape
    half = rows // 2
    full = 2 * half
    tokens = 2 * near.shape[0]
    last = first + steps == each

    def fixed(shape):
        return pl.BlockSpec(shape, lambda j, sp: (0,) * len(shape))

    in_specs = [
        fixed(near.shape),
        fixed(far.shape),
        fixed((tokens // 2, full)),
        fixed((tokens // 2, full)),
        pl.BlockSpec((quarters, 1, 4, 128), lambda j, sp: (0, first + j, 0, 0)),
        pl.BlockSpec((quarters, 1, rows, width), lambda j, sp: (0, first + j, 0, 0)),
        pl.BlockSpec((1, quarters, 1, width, half), lambda j, sp: (sp[0], 0, first + j, 0, 0)),
    ]
    if split:
        in_specs += [pl.BlockSpec((1, packed, lanes), lambda j, sp: (j, 0, 0))] * 4
    else:
        in_specs.append(pl.BlockSpec((quarters, 1, packed, lanes), lambda j, sp: (0, j, 0, 0)))
    operands = [place, near, far, near_out, far_out, rank, gate_up, down, *others]
    if last:
        in_specs += [fixed(array.shape) for array in held]
        operands += list(held)
    out_shape = [jax.ShapeDtypeStruct((quarters, steps, 4 * CAP, 3 * width), jnp.bfloat16)]
    out_specs = [pl.BlockSpec((quarters, 1, 4 * CAP, 3 * width), lambda j, sp: (0, j, 0, 0))]
    count = tokens // 2 if last else tokens
    kinds = (jnp.float32, jnp.bfloat16) if last else (jnp.bfloat16,)
    for kind in kinds:
        for lanes_out in (full, full + 128):
            out_shape.append(jax.ShapeDtypeStruct((count, lanes_out), kind))
            out_specs.append(fixed((count, lanes_out)))
    return pl.pallas_call(
        functools.partial(expert_kernel, first=first, last=last, each=each, split=split),
        out_shape=tuple(out_shape),
        grid_spec=pltpu.PrefetchScalarGridSpec(
            num_scalar_prefetch=1,
            grid=(steps,),
            in_specs=in_specs,
            out_specs=tuple(out_specs),
            scratch_shapes=[pltpu.VMEM((4, 4 * CAP, full), jnp.bfloat16)] * 3
            + [
                pltpu.VMEM((4, 4 * CAP, full + 128), jnp.bfloat16),
                pltpu.VMEM((4, 4 * CAP, 128), jnp.bfloat16),
                pltpu.VMEM((4, 4 * CAP, 128), jnp.float32),
                pltpu.VMEM((tokens, full), jnp.float32),
                pltpu.VMEM((tokens, full + 128), jnp.float32),
            ],
        ),
        compiler_params=kernel_params(1),
        name="experts",
    )(*operands)


def join_kernel(place_ref, total_ref, got_ref, *rest):
    piece_refs, whole_buf = rest[:-1], rest[-1]
    count = got_ref.shape[0]
    whole_buf[...] = total_ref[:count, :] + got_ref[...].astype(jnp.float32)
    give_pieces(whole_buf, place_ref[2], piece_refs)


def back_kernel(
    place_ref,
    mixed_ref,
    gates_ref,
    gains_ref,
    small_ref,
    far_ref,
    out_grad_ref,
    out_near_ref,
    out_far_ref,
    query_ref,
    turn_ref,
    kv0,
    kv1,
    kv2,
    kv3,
    probs_ref,
    *rest,
):
    (
        mixed_grad_ref,
        attn_grad_ref,
        logit_grad_ref,
        gain_grad_ref,
        query_grad_ref,
        kept_ref,
        given_ref,
        whole_buf,
        head_buf,
    ) = rest[-9:]
    take_pieces(rest[:-9], place_ref[2], whole_buf)
    half = small_ref.shape[1]
    full = 2 * half
    gates = gates_ref[...]
    gate_grads = whole_buf[:, full:]
    inner = jnp.sum(gates * gate_grads, axis=1, keepdims=True)
    logit_grad = (gates * (gate_grads - inner)).astype(jnp.bfloat16)
    logit_grad_ref[...] = logit_grad
    near, far = mixed_ref[:, :half], mixed_ref[:, half:]
    scale = row_scale(near, far)
    near_unit, far_unit = near * scale, far * scale
    near_grad = whole_buf[:, :half] + dot(logit_grad, small_ref[:half, half - 128 :], 1, 1)
    far_grad = whole_buf[:, half:full] + dot(logit_grad, far_ref[:, half - 128 :], 1, 1)
    gain_grad_ref[:, :half] = jnp.broadcast_to(
        jnp.sum(near_grad * near_unit, axis=0, keepdims=True), (8, half)
    )
    gain_grad_ref[:, half:] = jnp.broadcast_to(
        jnp.sum(far_grad * far_unit, axis=0, keepdims=True), (8, half)
    )
    near_scaled = near_grad * gains_ref[1:2, :half]
    far_scaled = far_grad * gains_ref[1:2, half:]
    mean = (
        jnp.sum(near_scaled * near_unit, axis=1, keepdims=True)
        + jnp.sum(far_scaled * far_unit, axis=1, keepdims=True)
    ) / full
    near_mixed = out_grad_ref[:, :half].astype(jnp.float32) + scale * (
        near_scaled - near_unit * mean
    )
    far_mixed = out_grad_ref[:, half:full].astype(jnp.float32) + scale * (
        far_scaled - far_unit * mean
    )
    mixed_grad_ref[:, :half] = near_mixed
    mixed_grad_ref[:, half:] = far_mixed
    near_attn = (RESIDUAL_SCALE * near_mixed).astype(jnp.bfloat16)
    far_attn = (RESIDUAL_SCALE * far_mixed).astype(jnp.bfloat16)
    attn_grad_ref[:, :half] = near_attn
    attn_grad_ref[:, half:] = far_attn
    head_buf[...] = (
        dot(near_attn, out_near_ref[...], 1, 1) + dot(far_attn, out_far_ref[...], 1, 1)
    ).astype(jnp.bfloat16)
    blocks = (kv0, kv1, kv2, kv3)
    kv_heads = kv0.shape[1] // (2 * HEAD_DIM)
    micro = probs_ref.shape[0] // kv_heads
    rows = query_ref.shape[0] // micro
    group = query_ref.shape[1] // HEAD_DIM // kv_heads
    count = query_ref.shape[1] // 128
    for m in range(micro):
        span = pl.ds(m * rows, rows)
        whole = query_ref[span, :]
        whole_grad = head_buf[span, :]
        pieces = []
        key_grads = []
        value_grads = []
        for g in range(kv_heads):
            query = stack_heads(whole, g * group, group)
            head_grad = stack_heads(whole_grad, g * group, group)
            keys = jnp.concatenate(
                [blocks[r][span, :][:, g * HEAD_DIM : (g + 1) * HEAD_DIM] for r in range(4)], axis=0
            )
            values = jnp.concatenate(
                [
                    blocks[r][span, :][:, (kv_heads + g) * HEAD_DIM : (kv_heads + g + 1) * HEAD_DIM]
                    for r in range(4)
                ],
                axis=0,
            )
            probs = probs_ref[m * kv_heads + g]
            prob_grad = dot(head_grad, values, 1, 1)
            inner = jnp.sum(probs * prob_grad, axis=1, keepdims=True)
            score_grad = (SCORE_SCALE * probs * (prob_grad - inner)).astype(jnp.bfloat16)
            value_grads.append(dot(probs.astype(jnp.bfloat16), head_grad, 0, 0))
            key_grads.append(dot(score_grad, query, 0, 0))
            query_grad = dot(score_grad, keys)
            pieces += [query_grad[h * rows : (h + 1) * rows] for h in range(group)]
        query_grad = jnp.concatenate(pieces, axis=1)
        query_grad_ref[span, :] = (
            query_grad * jnp.concatenate([turn_ref[0, span, :]] * count, axis=1)
            - turn_heads(query_grad) * jnp.concatenate([turn_ref[1, span, :]] * count, axis=1)
        ).astype(jnp.bfloat16)
        joined = jnp.concatenate(key_grads + value_grads, axis=1)
        kept_ref[0, span, :] = joined[:rows]
        kept_ref[1, span, :] = joined[2 * rows : 3 * rows]
        given_ref[0, span, :] = joined[rows : 2 * rows].astype(jnp.bfloat16)
        given_ref[1, span, :] = joined[3 * rows :].astype(jnp.bfloat16)


def last_kernel(
    place_ref,
    query_grad_ref,
    kept_ref,
    near_ref,
    along_ref,
    turn_ref,
    small_ref,
    far_ref,
    grads_ref,
    *rest,
):
    piece_refs, whole_buf = rest[:-1], rest[-1]
    q_cols = query_grad_ref.shape[1]
    k_cols = turn_ref.shape[2]
    cols = q_cols + 2 * k_cols
    half = small_ref.shape[1]
    total = (
        kept_ref[0] + near_ref[0].astype(jnp.float32) + along_ref[...].astype(jnp.float32)
    )
    keys = total[:, :k_cols]
    grads_ref[:, :q_cols] = query_grad_ref[...]
    grads_ref[:, q_cols : q_cols + k_cols] = (
        keys * turn_ref[0] - turn_heads(keys) * turn_ref[1]
    ).astype(jnp.bfloat16)
    grads_ref[:, q_cols + k_cols :] = total[:, k_cols:].astype(jnp.bfloat16)
    grads = grads_ref[...]
    near_part = dot(grads, small_ref[:half, :cols], 1, 1)
    far_part = dot(grads, far_ref[:, :cols], 1, 1)
    whole_buf[:, :half] = near_part
    whole_buf[:, half:] = far_part
    give_pieces(whole_buf, place_ref[2], piece_refs)


def output_kernel(place_ref, mixed_ref, *rest):
    out_ref, whole_buf = rest[-2:]
    take_pieces(rest[:-2], place_ref[2], whole_buf)
    half = out_ref.shape[1] // 2
    total = mixed_ref[...] + RESIDUAL_SCALE * whole_buf[...]
    first, second = own_then_other(place_ref[0], total)
    out_ref[:, :half] = first
    out_ref[:, half:] = second


def hidden_kernel(place_ref, hidden_ref, gains_ref, mixed_grad_ref, mark_ref, *rest):
    out_ref, gain_ref, whole_buf = rest[-3:]
    take_pieces(rest[:-3], place_ref[2], whole_buf)
    half = out_ref.shape[1] // 2
    near, far = own_then_other(place_ref[0], hidden_ref[...].astype(jnp.float32))
    scale = row_scale(near, far)
    near, far = near * scale, far * scale
    gain_ref[:, :half] = jnp.broadcast_to(
        jnp.sum(whole_buf[:, :half] * near, axis=0, keepdims=True), (8, half)
    )
    gain_ref[:, half:] = jnp.broadcast_to(
        jnp.sum(whole_buf[:, half:] * far, axis=0, keepdims=True), (8, half)
    )
    near_scaled = whole_buf[:, :half] * gains_ref[0:1, :half]
    far_scaled = whole_buf[:, half:] * gains_ref[0:1, half:]
    mean = (
        jnp.sum(near_scaled * near, axis=1, keepdims=True)
        + jnp.sum(far_scaled * far, axis=1, keepdims=True)
    ) / (2 * half)
    near_out = mixed_grad_ref[:, :half] + scale * (near_scaled - near * mean)
    far_out = mixed_grad_ref[:, half:] + scale * (far_scaled - far * mean)
    out_ref[:, :half] = jnp.where(place_ref[0] == 0, near_out, far_out)
    out_ref[:, half:] = jnp.where(place_ref[0] == 0, far_out, near_out)


def weight_grad_kernel(
    place_ref, rows_ref, grads0, grads1, grads2, grads3, slots_ref, rank_ref, *refs, first, steps
):
    gate_up_ref, down_ref, mark_ref, rows_buf, grads_buf = refs[-5:]
    half = down_ref.shape[-1]
    width = down_ref.shape[-2]
    iota = lax.broadcasted_iota(jnp.int32, (CAP, 128), 0)
    grads_in = (grads0, grads1, grads2, grads3)
    ctx = [place_ref[1] ^ r for r in range(4)]
    step, side = pl.program_id(0), pl.program_id(1)
    mark_ref[...] = jnp.zeros_like(mark_ref)

    @pl.when((step == 0) & (side == 0))
    def _():
        for k in range(4):
            for b in range(4):
                span = pl.ds(b * 128, 128)
                for a in range(2):
                    hot = jnp.concatenate(
                        [
                            jnp.where(iota == rank_ref[a, q, first + j, pl.ds(4 * k + b, 1), :], 1.0, 0.0)
                            for j in range(steps)
                            for q in range(4)
                        ],
                        axis=0,
                    ).astype(jnp.bfloat16)
                    spot = 4 * k + (b ^ (2 * a))
                    rows = dot(hot, rows_ref[ctx[k], span, :]).astype(jnp.bfloat16)
                    grads = dot(hot, grads_in[k][span, :]).astype(jnp.bfloat16)
                    for j in range(steps):
                        piece = slice(j * 4 * CAP, (j + 1) * 4 * CAP)
                        rows_buf[j * 2 + a, spot] = rows[piece]
                        grads_buf[j * 2 + a, spot] = grads[piece]

    place = step * 2 + side
    for q in range(4):
        slot = slice(q * CAP, (q + 1) * CAP)
        rows = jnp.concatenate([rows_buf[place, n, slot, :] for n in range(16)], axis=0)
        grads = jnp.concatenate([grads_buf[place, n, slot, :] for n in range(16)], axis=0)
        taken = jnp.concatenate([slots_ref[0, ctx[k], q, 0] for k in range(4)], axis=0)
        made = dot(rows, taken[:, : 2 * width], 0, 0)
        gate_up_ref[0, q, 0, pl.ds(0, half, stride=2), :] = made[:, :width]
        gate_up_ref[0, q, 0, pl.ds(1, half, stride=2), :] = made[:, width:]
        down_ref[0, q, 0] = dot(taken[:, 2 * width :], grads, 0, 0)


def run_weight_grads(place, plane, early, slots, rank, held, each, first, mark):
    sides, _, quarters, steps, slot_count, lanes = slots.shape
    width = lanes // 3
    half = plane.shape[-1]
    tokens = plane.shape[1]

    def place_of(j, a, sp):
        return (sp[0] ^ a, 0, first + j, 0, 0)

    in_specs = [
        pl.BlockSpec((4, tokens, half), lambda j, a, sp: (0, 0, 0)),
        *[pl.BlockSpec((tokens, half), lambda j, a, sp: (0, 0))] * 4,
        pl.BlockSpec(
            (1, 4, quarters, 1, slot_count, lanes),
            lambda j, a, sp: (sp[0] ^ a, 0, 0, j, 0, 0),
        ),
        pl.BlockSpec(rank.shape, lambda j, a, sp: (0, 0, 0, 0, 0)),
        pl.BlockSpec(memory_space=pl.ANY),
    ]
    operands = [place, plane, *early, slots, rank, mark]
    aliases = {}
    if held is not None:
        in_specs += [pl.BlockSpec(memory_space=pl.ANY)] * 2
        aliases = {len(operands): 0, len(operands) + 1: 1}
        operands += list(held[:2])
    return pl.pallas_call(
        functools.partial(weight_grad_kernel, first=first, steps=steps),
        out_shape=(
            jax.ShapeDtypeStruct((sides, quarters, each, 2 * half, width), jnp.float32),
            jax.ShapeDtypeStruct((sides, quarters, each, width, half), jnp.float32),
            jax.ShapeDtypeStruct((8, 128), jnp.float32),
        ),
        grid_spec=pltpu.PrefetchScalarGridSpec(
            num_scalar_prefetch=1,
            grid=(steps, sides),
            in_specs=in_specs,
            out_specs=(
                pl.BlockSpec((1, quarters, 1, 2 * half, width), place_of),
                pl.BlockSpec((1, quarters, 1, width, half), place_of),
                pl.BlockSpec((8, 128), lambda j, a, sp: (0, 0)),
            ),
            scratch_shapes=[pltpu.VMEM((2 * steps, 16, 4 * CAP, half), jnp.bfloat16)] * 2,
        ),
        input_output_aliases=aliases,
        compiler_params=kernel_params(2),
        name="weight_grads",
    )(*operands)


def swap_halves(values):
    half = values.shape[-1] // 2
    return jnp.concatenate([values[..., half:], values[..., :half]], axis=-1)


def fast_body(
    hidden_in,
    parents,
    routes,
    attn_gain,
    w_query,
    key_projection,
    value_projection,
    w_out,
    moe_gain,
    w_router,
    w_gate_up,
    w_down,
    d_out,
):
    low, wide = jnp.bfloat16, jnp.float32
    x_pos = lax.axis_index("fsdp")
    c_pos = lax.axis_index("ctx")
    z_pos = lax.axis_index("tp")
    tp_size = lax.axis_size("tp")
    place = jnp.stack([x_pos, c_pos, z_pos]).astype(jnp.int32)
    micro, _, rows, model = hidden_in.shape
    half = model // 2
    tokens = micro * rows
    experts = w_gate_up.shape[0]
    mine = experts // 2
    each = mine // 4
    width = w_down.shape[1]
    q_cols = w_query.shape[1]
    k_cols = key_projection.shape[1]
    qkv_cols = q_cols + 2 * k_cols
    kv_heads = k_cols // HEAD_DIM
    group = q_cols // k_cols
    top = routes.shape[-1]
    chunks = ((0, 2), (2, 2), (4, 1))
    tie = lax.optimization_barrier

    def across(value):
        return lax.ppermute(value, "fsdp", [(0, 1), (1, 0)])

    def beside(value):
        return lax.ppermute(value, "ctx", [(i, i ^ 1) for i in range(4)])

    def along(value):
        return lax.ppermute(value, "ctx", [(i, i ^ 2) for i in range(4)])

    def from_tp(value, step):
        return lax.ppermute(value, "tp", [((i + step) % tp_size, i) for i in range(tp_size)])

    def all_ctx(value):
        nearby = beside(value)
        distant = along(value)
        return [value, nearby, distant, beside(distant)]

    def own_first(value):
        return jnp.where(x_pos == 0, value, swap_halves(value))

    def reduce_pieces(pieces):
        total = pieces[0].astype(wide)
        for step in range(1, tp_size):
            total = total + from_tp(pieces[tp_size - step], step).astype(wide)
        return total.astype(low)

    def spread_pieces(total):
        return [total] + [from_tp(total, step) for step in range(1, tp_size)]

    piece_shapes = [((tokens // tp_size, model), low)] * tp_size
    hidden = hidden_in.reshape(tokens, model)
    flat_routes = routes.reshape(tokens, top)

    core = c_pos % 2
    part = half // 2
    weights = jnp.concatenate(
        [
            w_query,
            key_projection,
            value_projection,
            jnp.pad(w_router, ((0, 0), (0, half - qkv_cols - experts))),
        ],
        axis=1,
    )
    gain_rows = jnp.pad(jnp.stack([attn_gain, moe_gain]), ((0, 14), (0, 0)))
    small = jnp.concatenate([weights, gain_rows], axis=0)
    sent = across(
        jnp.concatenate([lax.dynamic_slice_in_dim(weights, core * part, part, 0), gain_rows], axis=0)
    )

    both_view = w_gate_up.reshape(experts, 2 * half, width)
    base = (x_pos * mine).astype(jnp.int32)[None]
    away = ((1 - x_pos) * mine + c_pos * each).astype(jnp.int32)[None]
    packs = [split_weights(away + first, count, both_view, w_down) for first, count in chunks]
    down_all = w_down.reshape(2, 4, each, width, half)
    routes_low = jnp.pad(flat_routes.astype(low), ((0, 0), (0, 128 - top)))
    near_out = jnp.concatenate([own_first(d_out.reshape(tokens, model)), routes_low], axis=1)

    half_dim = HEAD_DIM // 2
    inverse = ROPE_BASE ** (-jnp.arange(half_dim, dtype=wide) * 2.0 / HEAD_DIM)
    angles = jnp.arange(4 * rows, dtype=wide)[:, None] * inverse[None, :]
    cosines = jnp.tile(jnp.cos(angles), (1, 4))
    sines = jnp.tile(jnp.sin(angles), (1, 4))
    sent, packs[0], out_start, small, cosines, sines, place = tie(
        (sent, packs[0], core * (q_cols // 2), small, cosines, sines, place)
    )
    out_sent = across(lax.dynamic_slice_in_dim(w_out, out_start, q_cols // 2, 0))

    normed_one, query, key_value, small_far, gains, turns = single(
        before_kernel,
        "before",
        [
            ((tokens, model), low),
            ((tokens, q_cols), low),
            ((tokens, 2 * k_cols), low),
            ((half, half), low),
            ((16, model), wide),
            ((2, tokens, 128), wide),
        ],
        [],
        [place, parents.reshape(micro, 4)],
        hidden,
        small,
        sent,
        beside(sent),
        cosines,
        sines,
    )
    key_value, packs[0], near_out, out_sent = tie((key_value, packs[0], near_out, out_sent))
    blocks = all_ctx(key_value)
    far_out = across(near_out)
    far_zero = across(packs[0])
    head_low, probs, out_far, attn_part = single(
        attend_kernel,
        "attend",
        [
            ((tokens, q_cols), low),
            ((micro * kv_heads, group * rows, 4 * rows), wide),
            ((q_cols, half), low),
            ((tokens, model), low),
        ],
        [],
        [place, parents.reshape(micro, 4)],
        query,
        *blocks,
        w_out,
        out_sent,
        beside(out_sent),
    )
    attn_part, base = tie((attn_part, base))
    gate_up_mine = split_weights(base, mine, both_view, None).reshape(4, each, 2 * half, width)
    attended = lax.psum(attn_part, "tp")
    far_zero, packs[1] = tie((far_zero, packs[1]))
    far_one = across(packs[1])
    attended, far_out, gate_up_mine = tie((attended, far_out, gate_up_mine))
    zero_along = along(far_zero)
    early = jnp.concatenate(
        [
            jnp.concatenate([near_out[:, :half], routes_low], axis=1),
            far_out[:, half:],
        ],
        axis=0,
    )
    early_along = along(early)
    early_near = beside(early)
    mixed, near, gates = single(
        after_kernel,
        "after",
        [((tokens, model), wide), ((tokens, model + 128), low), ((tokens, 128), wide)],
        [],
        [place],
        hidden,
        gains,
        small,
        small_far,
        flat_routes,
        attended,
    )
    upper = (
        lax.broadcasted_iota(jnp.int32, (rows, rows), 0)
        < lax.broadcasted_iota(jnp.int32, (rows, rows), 1)
    ).astype(low)

    def ranks(route_table, ids):
        flat = route_table.astype(jnp.int32).T
        hit = jnp.zeros((ids.shape[0], flat.shape[1]), jnp.bool_)
        for k in range(top):
            hit = hit | (flat[k][None, :] == ids[:, None])
        hot = hit.astype(low).reshape(-1, rows)
        found = jnp.where(hot > 0, dot(hot, upper), -1.0).astype(jnp.int32)
        return found.reshape(ids.shape[0], -1, rows)

    expert_ids = (jnp.arange(experts, dtype=jnp.int32) + x_pos * mine) % experts
    pair_routes = jnp.concatenate([routes_low, far_out[:, model:]], axis=0)[:, :top]
    rank_pair = ranks(pair_routes, expert_ids[:mine]).reshape(4, each, 4, rows)

    near, packs[2] = tie((near, packs[2]))
    far = across(near)
    one_along = along(far_one)
    far, packs[2], zero_along, gate_up_mine, early_along, early_near, rank_pair = tie(
        (far, packs[2], zero_along, gate_up_mine, early_along, early_near, rank_pair)
    )
    early = [early, early_near, early_along, beside(early_along)]
    far_two = across(packs[2])
    plane_in = jnp.concatenate([near[:, :half], far[:, half:model]], axis=0)
    def all_four(got, distant):
        return [got, beside(got), distant, beside(distant)]

    def gather_slots(part):
        return lax.all_gather(part, ("fsdp", "ctx")).reshape(2, 4, *part.shape)

    held = []
    slots = []
    for number, (first, count) in enumerate(chunks):
        if number == 0:
            other = all_four(far_zero, zero_along)
        if number == 1:
            slots[0], far_two, one_along, plane_in = tie(
                (slots[0], far_two, one_along, plane_in)
            )
            two_along = along(far_two)
            plane = lax.all_gather(plane_in, "ctx")
            other = all_four(far_one, one_along)
        if number == 2:
            slots[1], two_along = tie((slots[1], two_along))
            other = all_four(far_two, two_along)
        made = run_experts(
            place,
            near,
            far,
            near_out,
            far_out,
            rank_pair,
            gate_up_mine,
            down_all,
            other,
            held,
            first,
            each,
        )
        slots.append(made[0])
        held += made[1:]
    moe_all, back_all, moe_far, back_far = made[1:]

    all_routes = jnp.concatenate([part[:, half : half + top] for part in early], axis=0)
    rank_all = ranks(all_routes, expert_ids).reshape(2, 4, each, 16, rows)

    back_far, plane, slots[0] = tie((back_far, plane, slots[0]))
    back_got = across(back_far)
    pair_zero = gather_slots(slots[0])
    back_got, moe_far, rank_all = tie((back_got, moe_far, rank_all))

    def grads_of(number, pair, held, mark):
        first, count = chunks[number]
        return run_weight_grads(
            place,
            plane,
            early,
            pair,
            rank_all,
            held,
            each,
            first,
            mark,
        )

    pieces = single(
        join_kernel,
        "join",
        [((tokens // tp_size, model + 128), low)] * tp_size,
        [((tokens, model + 128), wide)],
        [place],
        back_all,
        back_got,
    )
    total = reduce_pieces(pieces)
    total, moe_far = tie((total, moe_far))
    moe_got = across(moe_far)
    found = spread_pieces(total)
    grads = grads_of(0, pair_zero, None, jnp.zeros((8, 128), wide))
    *found, moe_got, mark, slots[1] = tie((*found, moe_got, grads[2], slots[1]))
    pair_one = gather_slots(slots[1])
    moe_pieces = single(
        join_kernel, "join", piece_shapes, [((tokens, model), wide)], [place], moe_all, moe_got
    )
    moe_total = reduce_pieces(moe_pieces)
    (
        mixed_grad,
        attn_grad,
        logit_grad,
        gain_two_part,
        query_grad,
        kept,
        given,
    ) = single(
        back_kernel,
        "back",
        [
            ((tokens, model), wide),
            ((tokens, model), low),
            ((tokens, 128), low),
            ((8, model), wide),
            ((tokens, q_cols), low),
            ((2, tokens, 2 * k_cols), wide),
            ((2, tokens, 2 * k_cols), low),
        ],
        [((tokens, model + 128), wide), ((tokens, q_cols), low)],
        [place],
        mixed,
        gates,
        gains,
        small,
        small_far,
        near_out,
        w_out,
        out_far,
        query,
        turns,
        *blocks,
        probs,
        *found,
    )

    given, moe_total = tie((given, moe_total))
    near_pair = beside(given)
    moe_found = spread_pieces(moe_total)
    distant = along((kept[1] + near_pair[1].astype(wide)).astype(low))
    qkv_grad, *pieces = single(
        last_kernel,
        "last",
        [((tokens, qkv_cols), low)] + piece_shapes,
        [((tokens, model), wide)],
        [place],
        query_grad,
        kept,
        near_pair,
        distant,
        turns,
        small,
        small_far,
    )

    def hop_beside(value):
        share = value.shape[1] // 2
        kept = lax.dynamic_slice_in_dim(value, core * share, share, 1)
        given = lax.dynamic_slice_in_dim(value, (1 - core) * share, share, 1)
        return kept + beside(given.astype(low)).astype(wide)

    def hop_across(kept):
        return kept[0] + across(kept[1].astype(low)).astype(wide)

    def hop_along(total):
        return (total + along(total.astype(low)).astype(wide)).astype(low)

    def hop_join(total):
        other = beside(total)
        return jnp.where(
            core == 0,
            jnp.concatenate([total, other], axis=0),
            jnp.concatenate([other, total], axis=0),
        ).astype(wide)

    def both(left, right):
        return jnp.stack([dot(left, right[:, :half], 0, 0), dot(left, right[:, half:], 0, 0)])

    side = hop_beside(
        jnp.concatenate(
            [
                both(head_low, attn_grad),
                both(logit_grad[:, :experts], near[:, :model]),
                jnp.stack([gain_two_part[:, :half], gain_two_part[:, half:]]),
                jnp.zeros((2, 16, half), wide),
            ],
            axis=1,
        )
    )
    tied = tie((*pieces, *moe_found, mark, side, qkv_grad, pair_one, slots[2]))
    pieces, moe_found = tied[:tp_size], tied[tp_size : 2 * tp_size]
    mark, side, qkv_grad, pair_one, slots[2] = tied[2 * tp_size :]
    pair_two = gather_slots(slots[2])
    (layer_out,) = single(
        output_kernel,
        "output",
        [((tokens, model), wide)],
        [((tokens, model), wide)],
        [place],
        mixed,
        *moe_found,
    )
    total = reduce_pieces(pieces)
    grads = grads_of(1, pair_one, grads, mark)
    side = hop_across(side)
    d_qkv = hop_beside(dot(normed_one, qkv_grad, 0, 0).reshape(2, half, qkv_cols))
    total, mark, side, d_qkv = tie((total, grads[2], side, d_qkv))
    found = spread_pieces(total)
    grads = grads_of(2, pair_two, grads, mark)
    side = hop_along(side)
    d_qkv = hop_across(d_qkv)
    *found, mark, side, d_qkv = tie((*found, grads[2], side, d_qkv))
    d_hidden, gain_one = single(
        hidden_kernel,
        "hidden",
        [((tokens, model), wide), ((8, model), wide)],
        [((tokens, model), wide)],
        [place],
        hidden,
        gains,
        mixed_grad,
        mark,
        *found,
    )
    gain_one = gain_one[0]
    d_gate_up = grads[0].reshape(experts, half, 2, width)
    d_down = grads[1].reshape(experts, width, half)
    side_grads = hop_join(side)
    d_qkv = hop_join(hop_along(d_qkv))
    gain_one = gain_one + beside(gain_one)
    gain_one = gain_one + along(gain_one)
    gain_one = gain_one[:half] + across(gain_one[half:])
    return (
        layer_out.reshape(micro, 1, rows, model),
        d_hidden.reshape(micro, 1, rows, model),
        gain_one,
        d_qkv[:, :q_cols],
        d_qkv[:, q_cols : q_cols + k_cols],
        d_qkv[:, q_cols + k_cols :],
        side_grads[:q_cols],
        side_grads[q_cols + experts],
        side_grads[q_cols : q_cols + experts].T,
        d_gate_up,
        d_down,
    )


def solution(mesh):
    placed = (
        P(None, "fsdp", "ctx", None),
        P(None, "fsdp", None),
        P(None, "fsdp", "ctx", None),
        P("fsdp"),
        P("fsdp", "tp"),
        P("fsdp", "tp"),
        P("fsdp", "tp"),
        P("tp", "fsdp"),
        P("fsdp"),
        P("fsdp", None),
        P(None, "fsdp", None, "tp"),
        P(None, "tp", "fsdp"),
        P(None, "fsdp", "ctx", None),
    )
    fits = mesh.shape["fsdp"] == 2 and mesh.shape["ctx"] == 4
    return jax.shard_map(
        fast_body if fits else body,
        mesh=mesh,
        in_specs=placed,
        out_specs=(
            P(None, "fsdp", "ctx", None),
            P(None, "fsdp", "ctx", None),
            P("fsdp"),
            P("fsdp", "tp"),
            P("fsdp", "tp"),
            P("fsdp", "tp"),
            P("tp", "fsdp"),
            P("fsdp"),
            P("fsdp", None),
            P(None, "fsdp", None, "tp"),
            P(None, "tp", "fsdp"),
        ),
        check_vma=False,
    )
```

```python
import functools

import jax
import jax.numpy as jnp
from jax import lax
from jax.experimental import pallas as pl
from jax.experimental.pallas import tpu as pltpu
from jax.sharding import PartitionSpec as P

HEAD_DIM = 64
CAP = 32


EPSILON = 1e-06
RESIDUAL_SCALE = 0.22
SCORE_SCALE = 1.0 / 64.0
ROPE_BASE = 10000.0
TOP_PRECISION = lax.Precision.HIGHEST


def tree_tables(parent_row, tree_len):
    seg_total = parent_row.shape[0]
    seg_len = tree_len // seg_total
    seg_ids = jnp.arange(seg_total, dtype=jnp.int32)
    parent_links = (parent_row[:, None] == seg_ids[None, :]).astype(jnp.float32)
    reach_table = jnp.maximum(parent_links, jnp.eye(seg_total, dtype=jnp.float32))
    for squaring in range(max(seg_total - 1, 1).bit_length()):
        reach_table = jnp.minimum(jnp.dot(reach_table, reach_table, precision=TOP_PRECISION), 1.0)
    seg_depth = jnp.sum(reach_table, axis=1) - 1.0
    token_ids = jnp.arange(tree_len, dtype=jnp.int32)
    tok_owner = ((token_ids // seg_len)[:, None] == seg_ids[None, :]).astype(jnp.float32)
    tok_offset = (token_ids % seg_len).astype(jnp.float32)
    places = jnp.dot(tok_owner, seg_depth, precision=TOP_PRECISION) * seg_len + tok_offset
    return (places, jnp.dot(tok_owner, reach_table, precision=TOP_PRECISION), tok_owner)


def rope_tables(places):
    half_dim = HEAD_DIM // 2
    inverse = ROPE_BASE ** (-jnp.arange(half_dim, dtype=jnp.float32) * 2.0 / HEAD_DIM)
    angles = places[:, None] * inverse[None, :]
    cosine_table = jnp.concatenate([jnp.cos(angles), jnp.cos(angles)], axis=1)
    sine_values = jnp.concatenate([jnp.sin(angles), jnp.sin(angles)], axis=1)
    return (cosine_table, sine_values)


def apply_rotary(values, cosine_table, sine_values):
    half_dim = values.shape[-1] // 2
    turned = jnp.concatenate([-values[..., half_dim:], values[..., :half_dim]], axis=-1)
    return values * cosine_table[:, None, :] + turned * sine_values[:, None, :]


def norm_scale(values):
    return lax.rsqrt(jnp.mean(values * values, axis=-1, keepdims=True) + EPSILON)


def add_tuples(first_tuple, second_tuple):
    return tuple(
        (left_part + right_part for left_part, right_part in zip(first_tuple, second_tuple))
    )


def expert_work(rows, row_grads, gate_up_w, down_w, down_form):
    gate_up = jnp.einsum("ecd,edsf->ecsf", rows, gate_up_w, preferred_element_type=jnp.float32)
    gate_pre = gate_up[:, :, 0]
    up_pre = gate_up[:, :, 1]
    sigmoid = jax.nn.sigmoid(gate_pre)
    activ_low = (gate_pre * sigmoid * up_pre).astype(jnp.bfloat16)
    expert_out = jnp.einsum(
        "ecf," + down_form + "->ecd", activ_low, down_w, preferred_element_type=jnp.float32
    )
    activ_grad = jnp.einsum(
        "ecd," + down_form + "->ecf", row_grads, down_w, preferred_element_type=jnp.float32
    )
    gate_grad = activ_grad * up_pre * sigmoid * (1.0 + gate_pre * (1.0 - sigmoid))
    up_grad = activ_grad * gate_pre * sigmoid
    gate_up_grad = jnp.stack([gate_grad, up_grad], axis=2).astype(jnp.bfloat16)
    row_input_grad = jnp.einsum(
        "ecsf,edsf->ecd", gate_up_grad, gate_up_w, preferred_element_type=jnp.float32
    )
    grad_gate_up = jnp.einsum(
        "ecd,ecsf->edsf", rows, gate_up_grad, preferred_element_type=jnp.float32
    )
    grad_down = jnp.einsum(
        "ecf,ecd->" + down_form, activ_low, row_grads, preferred_element_type=jnp.float32
    )
    return (expert_out, row_input_grad, grad_gate_up, grad_down)


def body(
    hidden_in,
    parents,
    routes,
    attn_gain,
    w_query,
    key_projection,
    value_projection,
    w_out,
    moe_gain,
    w_router,
    w_gate_up,
    w_down,
    d_out,
):
    experts = w_gate_up.shape[0]
    gathered = (
        lax.all_gather(attn_gain, "fsdp", axis=0, tiled=True),
        lax.all_gather(w_query, "fsdp", axis=0, tiled=True),
        lax.all_gather(key_projection, "fsdp", axis=0, tiled=True),
        lax.all_gather(value_projection, "fsdp", axis=0, tiled=True),
        lax.all_gather(w_out, "fsdp", axis=1, tiled=True),
        lax.all_gather(moe_gain, "fsdp", axis=0, tiled=True),
        lax.all_gather(w_router, "fsdp", axis=0, tiled=True),
        lax.all_gather(w_gate_up, "fsdp", axis=1, tiled=True),
        lax.all_gather(w_down, "fsdp", axis=2, tiled=True),
    )
    gate_up_full = gathered[7]
    down_full = gathered[8]
    down_form = "efd"
    gain_one = gathered[0].astype(jnp.float32)
    query_full = gathered[1]
    key_full = gathered[2]
    value_full = gathered[3]
    out_full = gathered[4]
    gain_two = gathered[5].astype(jnp.float32)
    router_full = gathered[6]
    micro_count = hidden_in.shape[0]
    local_rows = hidden_in.shape[2]
    model_width = hidden_in.shape[3]
    top_count = routes.shape[3]
    kv_heads = key_projection.shape[1] // HEAD_DIM
    q_heads = w_query.shape[1] // HEAD_DIM
    group_size = q_heads // kv_heads
    tree_len = local_rows * lax.axis_size("ctx")
    row_start = lax.axis_index("ctx") * local_rows
    capacity = CAP
    expert_ids = jnp.arange(experts, dtype=jnp.int32)
    outputs = []
    input_grads = []
    totals = None
    for batch_index in range(micro_count):
        tree_places, reach_rows, tok_owner = tree_tables(parents[batch_index, 0], tree_len)
        local_places = lax.dynamic_slice_in_dim(tree_places, row_start, local_rows, 0)
        local_reach = lax.dynamic_slice_in_dim(reach_rows, row_start, local_rows, 0)
        allowed = (jnp.dot(local_reach, tok_owner.T, precision=TOP_PRECISION) > 0.5) & (
            tree_places[None, :] <= local_places[:, None]
        )
        cosine_table, sine_values = rope_tables(local_places)
        inputs = hidden_in[batch_index, 0].astype(jnp.float32)
        scale_one = norm_scale(inputs)
        first_normed = (inputs * scale_one * gain_one).astype(jnp.bfloat16)
        query_unrotated = jnp.dot(
            first_normed, query_full, preferred_element_type=jnp.float32
        ).reshape(local_rows, q_heads, HEAD_DIM)
        key_unrotated = jnp.dot(first_normed, key_full, preferred_element_type=jnp.float32).reshape(
            local_rows, kv_heads, HEAD_DIM
        )
        value_reduced = jnp.dot(
            first_normed, value_full, preferred_element_type=jnp.float32
        ).astype(jnp.bfloat16)
        query_reduced = (
            apply_rotary(query_unrotated, cosine_table, sine_values)
            .astype(jnp.bfloat16)
            .reshape(local_rows, kv_heads, group_size, HEAD_DIM)
        )
        key_low = (
            apply_rotary(key_unrotated, cosine_table, sine_values)
            .astype(jnp.bfloat16)
            .reshape(local_rows, kv_heads * HEAD_DIM)
        )
        tree_keys, tree_values = (
            lax.all_gather(key_low, "ctx", axis=0, tiled=True),
            lax.all_gather(value_reduced, "ctx", axis=0, tiled=True),
        )
        tree_keys = tree_keys.reshape(tree_len, kv_heads, HEAD_DIM)
        tree_values = tree_values.reshape(tree_len, kv_heads, HEAD_DIM)

        def masked_scores():
            raw_scores = jnp.einsum(
                "qhjd,khd->hjqk", query_reduced, tree_keys, preferred_element_type=jnp.float32
            )
            return jnp.where(allowed[None, None], raw_scores * SCORE_SCALE, -1e30)

        scores = masked_scores()
        top_score = jnp.max(scores, axis=-1, keepdims=True)
        log_total = top_score + jnp.log(
            jnp.sum(jnp.exp(scores - top_score), axis=-1, keepdims=True)
        )
        probs_low = jnp.exp(scores - log_total).astype(jnp.bfloat16)
        head_out = jnp.einsum(
            "hjqk,khd->qhjd", probs_low, tree_values, preferred_element_type=jnp.float32
        )
        head_low = head_out.reshape(local_rows, q_heads * HEAD_DIM).astype(jnp.bfloat16)
        attn_part = jnp.dot(head_low, out_full, preferred_element_type=jnp.float32)
        attended = lax.psum(attn_part.astype(jnp.bfloat16), "tp").astype(jnp.float32)
        mixed = inputs + RESIDUAL_SCALE * attended
        scale_two = norm_scale(mixed)
        normed_two = (mixed * scale_two * gain_two).astype(jnp.bfloat16)
        logits = jnp.dot(normed_two, router_full, preferred_element_type=jnp.float32)
        chosen_ids = routes[batch_index, 0]
        picked = (chosen_ids[:, :, None] == expert_ids[None, None, :]).astype(jnp.float32)
        chosen = jnp.sum(picked * logits[:, None, :], axis=2)
        gates = jax.nn.softmax(chosen, axis=1)
        flat_ids = chosen_ids.reshape(-1)
        flat_hot = (flat_ids[:, None] == expert_ids[None, :]).astype(jnp.int32)
        slots = jnp.sum((jnp.cumsum(flat_hot, axis=0) - flat_hot) * flat_hot, axis=1)
        targets = flat_ids * capacity + slots
        sources = (
            jnp.zeros((experts * capacity,), jnp.int32)
            .at[targets]
            .set(jnp.arange(local_rows * top_count, dtype=jnp.int32) // top_count)
        )
        filled = jnp.zeros((experts * capacity, 1), jnp.bfloat16).at[targets].set(1)
        dispatched = (normed_two[sources] * filled).reshape(experts, capacity, model_width)
        grad_out = d_out[batch_index, 0].astype(jnp.float32)
        grad_moe = RESIDUAL_SCALE * grad_out
        entry_grad = (
            (gates[:, :, None] * grad_moe[:, None, :])
            .astype(jnp.bfloat16)
            .reshape(local_rows * top_count, model_width)
        )
        slot_grad = (
            jnp.zeros((experts * capacity, model_width), jnp.bfloat16)
            .at[targets]
            .set(entry_grad)
            .reshape(experts, capacity, model_width)
        )
        expert_out, slot_input_grad, grad_gate_up, grad_down = expert_work(
            dispatched, slot_grad, gate_up_full, down_full, down_form
        )
        entry_out = expert_out.reshape(experts * capacity, model_width)[targets].reshape(
            local_rows, top_count, model_width
        )
        moe_part = jnp.sum(gates[:, :, None] * entry_out, axis=1)
        moe_sum = lax.psum(moe_part.astype(jnp.bfloat16), "tp").astype(jnp.float32)
        outputs.append(mixed + RESIDUAL_SCALE * moe_sum)
        gate_grad_part = jnp.sum(grad_moe[:, None, :] * entry_out, axis=2)
        expert_input_grad = jnp.sum(
            slot_input_grad.reshape(experts * capacity, model_width)[targets].reshape(
                local_rows, top_count, model_width
            ),
            axis=1,
        )
        expert_input_grad, gate_grads = (
            lax.psum(expert_input_grad.astype(jnp.bfloat16), "tp").astype(jnp.float32),
            lax.psum(gate_grad_part.astype(jnp.bfloat16), "tp").astype(jnp.float32),
        )
        chosen_grad = gates * (gate_grads - jnp.sum(gates * gate_grads, axis=1, keepdims=True))
        logit_grad = jnp.sum(picked * chosen_grad[:, :, None], axis=1).astype(jnp.bfloat16)
        normed_two_grad = expert_input_grad + jnp.einsum(
            "te,de->td", logit_grad, router_full, preferred_element_type=jnp.float32
        )
        grad_router = jnp.einsum(
            "td,te->de", normed_two, logit_grad, preferred_element_type=jnp.float32
        )
        unit_two = mixed * scale_two
        grad_gain_two = jnp.sum(normed_two_grad * unit_two, axis=0)
        scaled_two = normed_two_grad * gain_two
        mixed_grad = grad_out + scale_two * (
            scaled_two - unit_two * jnp.mean(scaled_two * unit_two, axis=-1, keepdims=True)
        )
        attn_grad = (RESIDUAL_SCALE * mixed_grad).astype(jnp.bfloat16)
        grad_out_proj = jnp.einsum(
            "tc,td->cd", head_low, attn_grad, preferred_element_type=jnp.float32
        )
        head_grad = (
            jnp.einsum("td,cd->tc", attn_grad, out_full, preferred_element_type=jnp.float32)
            .astype(jnp.bfloat16)
            .reshape(local_rows, kv_heads, group_size, HEAD_DIM)
        )
        scores = masked_scores()
        probs = jnp.exp(scores - log_total)
        probs_low = probs.astype(jnp.bfloat16)
        prob_grad = jnp.einsum(
            "qhjd,khd->hjqk", head_grad, tree_values, preferred_element_type=jnp.float32
        )
        value_grad = jnp.einsum(
            "hjqk,qhjd->khd", probs_low, head_grad, preferred_element_type=jnp.float32
        )
        score_grad = (
            SCORE_SCALE * probs * (prob_grad - jnp.sum(probs * prob_grad, axis=-1, keepdims=True))
        ).astype(jnp.bfloat16)
        query_grad = jnp.einsum(
            "hjqk,khd->qhjd", score_grad, tree_keys, preferred_element_type=jnp.float32
        ).reshape(local_rows, q_heads, HEAD_DIM)
        key_grad = jnp.einsum(
            "hjqk,qhjd->khd", score_grad, query_reduced, preferred_element_type=jnp.float32
        )
        key_grad, value_grad = (
            lax.psum_scatter(
                key_grad.reshape(tree_len, kv_heads * HEAD_DIM).astype(jnp.bfloat16),
                "ctx",
                scatter_dimension=0,
                tiled=True,
            ).astype(jnp.float32),
            lax.psum_scatter(
                value_grad.reshape(tree_len, kv_heads * HEAD_DIM).astype(jnp.bfloat16),
                "ctx",
                scatter_dimension=0,
                tiled=True,
            ).astype(jnp.float32),
        )
        query_pre_grad = (
            apply_rotary(query_grad, cosine_table, -sine_values)
            .astype(jnp.bfloat16)
            .reshape(local_rows, q_heads * HEAD_DIM)
        )
        key_pre_grad = (
            apply_rotary(
                key_grad.reshape(local_rows, kv_heads, HEAD_DIM), cosine_table, -sine_values
            )
            .astype(jnp.bfloat16)
            .reshape(local_rows, kv_heads * HEAD_DIM)
        )
        value_pre_grad = value_grad.astype(jnp.bfloat16)
        normed_one_grad = jnp.einsum(
            "tc,dc->td", query_pre_grad, query_full, preferred_element_type=jnp.float32
        )
        normed_one_grad = normed_one_grad + jnp.einsum(
            "tc,dc->td", key_pre_grad, key_full, preferred_element_type=jnp.float32
        )
        normed_one_grad = normed_one_grad + jnp.einsum(
            "tc,dc->td", value_pre_grad, value_full, preferred_element_type=jnp.float32
        )
        grad_query = jnp.einsum(
            "td,tc->dc", first_normed, query_pre_grad, preferred_element_type=jnp.float32
        )
        grad_key = jnp.einsum(
            "td,tc->dc", first_normed, key_pre_grad, preferred_element_type=jnp.float32
        )
        grad_value = jnp.einsum(
            "td,tc->dc", first_normed, value_pre_grad, preferred_element_type=jnp.float32
        )
        normed_one_grad = lax.psum(normed_one_grad.astype(jnp.bfloat16), "tp").astype(jnp.float32)
        unit_one = inputs * scale_one
        grad_gain_one = jnp.sum(normed_one_grad * unit_one, axis=0)
        scaled_one = normed_one_grad * gain_one
        input_grads.append(
            mixed_grad
            + scale_one
            * (scaled_one - unit_one * jnp.mean(scaled_one * unit_one, axis=-1, keepdims=True))
        )
        piece = (
            grad_gain_one,
            grad_query,
            grad_key,
            grad_value,
            grad_out_proj,
            grad_gain_two,
            grad_router,
            grad_gate_up,
            grad_down,
        )
        totals = piece if batch_index == 0 else add_tuples(totals, piece)
    summed = (
        lax.psum_scatter(totals[0], ("fsdp", "ctx"), scatter_dimension=0, tiled=True),
        lax.psum_scatter(totals[1], ("fsdp", "ctx"), scatter_dimension=0, tiled=True),
        lax.psum_scatter(totals[2], ("fsdp", "ctx"), scatter_dimension=0, tiled=True),
        lax.psum_scatter(totals[3], ("fsdp", "ctx"), scatter_dimension=0, tiled=True),
        lax.psum_scatter(totals[4], ("fsdp", "ctx"), scatter_dimension=1, tiled=True),
        lax.psum_scatter(totals[5], ("fsdp", "ctx"), scatter_dimension=0, tiled=True),
        lax.psum_scatter(totals[6], ("fsdp", "ctx"), scatter_dimension=0, tiled=True),
        lax.psum_scatter(totals[7], ("fsdp", "ctx"), scatter_dimension=1, tiled=True),
        lax.psum_scatter(totals[8], ("fsdp", "ctx"), scatter_dimension=2, tiled=True),
    )
    shares = (
        lax.all_gather(summed[0].astype(jnp.bfloat16), "ctx", axis=0, tiled=True).astype(
            jnp.float32
        ),
        lax.all_gather(summed[1].astype(jnp.bfloat16), "ctx", axis=0, tiled=True).astype(
            jnp.float32
        ),
        lax.all_gather(summed[2].astype(jnp.bfloat16), "ctx", axis=0, tiled=True).astype(
            jnp.float32
        ),
        lax.all_gather(summed[3].astype(jnp.bfloat16), "ctx", axis=0, tiled=True).astype(
            jnp.float32
        ),
        lax.all_gather(summed[4].astype(jnp.bfloat16), "ctx", axis=1, tiled=True).astype(
            jnp.float32
        ),
        lax.all_gather(summed[5].astype(jnp.bfloat16), "ctx", axis=0, tiled=True).astype(
            jnp.float32
        ),
        lax.all_gather(summed[6].astype(jnp.bfloat16), "ctx", axis=0, tiled=True).astype(
            jnp.float32
        ),
        lax.all_gather(summed[7].astype(jnp.bfloat16), "ctx", axis=1, tiled=True).astype(
            jnp.float32
        ),
        lax.all_gather(summed[8].astype(jnp.bfloat16), "ctx", axis=2, tiled=True).astype(
            jnp.float32
        ),
    )
    layer_out = jnp.stack(outputs, axis=0)[:, None]
    d_hidden = jnp.stack(input_grads, axis=0)[:, None]
    return (
        layer_out,
        d_hidden,
        shares[0],
        shares[1],
        shares[2],
        shares[3],
        shares[4],
        shares[5],
        shares[6],
        shares[7],
        shares[8],
    )


def dot(left, right, left_dim=1, right_dim=0):
    return lax.dot_general(
        left, right, (((left_dim,), (right_dim,)), ((), ())), preferred_element_type=jnp.float32
    )


def pick(hot, rows):
    return dot(hot, rows).astype(jnp.bfloat16)


def kernel_params(count=0):
    return pltpu.CompilerParams(
        dimension_semantics=("arbitrary",) * count if count else None,
        vmem_limit_bytes=60 * 1024 * 1024,
    )


def single(kernel, name, out_shape, scratch, scalars, *arrays):
    smem = pl.BlockSpec(memory_space=pltpu.SMEM)
    vmem = pl.BlockSpec(memory_space=pltpu.VMEM)
    return pl.pallas_call(
        kernel,
        out_shape=tuple(jax.ShapeDtypeStruct(shape, kind) for shape, kind in out_shape),
        in_specs=[smem] * len(scalars) + [vmem] * len(arrays),
        out_specs=(vmem,) * len(out_shape),
        scratch_shapes=[pltpu.VMEM(shape, kind) for shape, kind in scratch],
        compiler_params=kernel_params(),
        name=name,
    )(*scalars, *arrays)


def tree_path(parents_ref, m, start):
    path = [start]
    for _ in range(3):
        path.append(parents_ref[m, path[-1]])
    return path


def own_then_other(x_pos, array):
    half = array.shape[-1] // 2
    first, second = array[..., :half], array[..., half:]
    return jnp.where(x_pos == 0, first, second), jnp.where(x_pos == 0, second, first)


def row_scale(near, far):
    total = jnp.sum(near * near, axis=1, keepdims=True) + jnp.sum(far * far, axis=1, keepdims=True)
    return lax.rsqrt(total / (2 * near.shape[1]) + EPSILON)


def turn_heads(values):
    half_dim = HEAD_DIM // 2
    lane = lax.broadcasted_iota(jnp.int32, values.shape, 1) % HEAD_DIM
    width = values.shape[1]
    return jnp.where(
        lane < half_dim,
        -pltpu.roll(values, width - half_dim, 1),
        pltpu.roll(values, half_dim, 1),
    )


def split_kernel(base_ref, both_ref, down_ref, out_ref, wide_buf):
    wide_buf[...] = both_ref[0].astype(jnp.float32)
    half = both_ref.shape[1] // 2
    out_ref[0, :half, :] = wide_buf[pl.ds(0, half, stride=2), :].astype(jnp.bfloat16)
    out_ref[0, half : 2 * half, :] = wide_buf[pl.ds(1, half, stride=2), :].astype(jnp.bfloat16)
    if down_ref is not None:
        width = down_ref.shape[1]
        for j in range(half // 128):
            out_ref[0, 2 * half + j * width : 2 * half + (j + 1) * width, :] = down_ref[
                0, :, j * 128 : (j + 1) * 128
            ]


def split_plain_kernel(base_ref, both_ref, out_ref, wide_buf):
    split_kernel(base_ref, both_ref, None, out_ref, wide_buf)


def split_weights(base, count, gate_up, down):
    _, rows, width = gate_up.shape
    packed = rows if down is None else rows + rows // 2
    in_specs = [pl.BlockSpec((1, rows, width), lambda i, base: (base[0] + i, 0, 0))]
    operands = [base, gate_up]
    if down is not None:
        in_specs.append(
            pl.BlockSpec((1, *down.shape[1:]), lambda i, base: (base[0] + i, 0, 0))
        )
        operands.append(down)
    return pl.pallas_call(
        split_plain_kernel if down is None else split_kernel,
        out_shape=jax.ShapeDtypeStruct((count, packed, width), jnp.bfloat16),
        grid_spec=pltpu.PrefetchScalarGridSpec(
            num_scalar_prefetch=1,
            grid=(count,),
            in_specs=in_specs,
            out_specs=pl.BlockSpec((1, packed, width), lambda i, base: (i, 0, 0)),
            scratch_shapes=[pltpu.VMEM((rows, width), jnp.float32)],
        ),
        compiler_params=kernel_params(1),
        name="split_weights",
    )(*operands)


def before_kernel(
    place_ref,
    parents_ref,
    hidden_ref,
    small_ref,
    sent_ref,
    next_ref,
    cosine_ref,
    sine_ref,
    normed_ref,
    query_ref,
    key_value_ref,
    far_ref,
    gains_ref,
    turn_ref,
):
    x_pos, c_pos = place_ref[0], place_ref[1]
    first_core = c_pos % 2 == 0
    half = small_ref.shape[1]
    part = half // 2
    q_cols = query_ref.shape[1]
    kv_cols = key_value_ref.shape[1]
    cols = q_cols + kv_cols
    turned_cols = q_cols + kv_cols // 2
    own_rows = small_ref[: 2 * part, :]
    sent, beside = sent_ref[:part, :], next_ref[:part, :]
    top = jnp.where(first_core, sent, beside)
    low_rows = jnp.where(first_core, beside, sent)
    far_ref[:part, :] = top
    far_ref[part:, :] = low_rows
    own_gain = small_ref[2 * part : 2 * part + 16, :].astype(jnp.float32)
    far_gain = sent_ref[part : part + 16, :].astype(jnp.float32)
    gains_ref[:, :half] = own_gain
    gains_ref[:, half:] = far_gain
    near, far = own_then_other(x_pos, hidden_ref[...].astype(jnp.float32))
    scale = row_scale(near, far)
    near_low = (near * scale * own_gain[:1]).astype(jnp.bfloat16)
    far_low = (far * scale * far_gain[:1]).astype(jnp.bfloat16)
    normed_ref[:, :half] = near_low
    normed_ref[:, half:] = far_low
    made = (
        dot(near_low, own_rows[:, :cols])
        + dot(far_low[:, :part], top[:, :cols])
        + dot(far_low[:, part:], low_rows[:, :cols])
    )
    micro = parents_ref.shape[0]
    rows = hidden_ref.shape[0] // micro
    turns = []
    for m in range(micro):
        path = tree_path(parents_ref, m, c_pos)
        depth = sum((path[i + 1] != path[i]).astype(jnp.int32) for i in range(3))
        span = pl.ds(depth * rows, rows)
        turns.append((cosine_ref[span, :], sine_ref[span, :]))
    cosines = jnp.concatenate([pair[0] for pair in turns], axis=0)
    sines = jnp.concatenate([pair[1] for pair in turns], axis=0)
    turn_ref[0] = cosines
    turn_ref[1] = sines
    count = turned_cols // 128
    values = made[:, :turned_cols]
    rotated = (
        values * jnp.concatenate([cosines] * count, axis=1)
        + turn_heads(values) * jnp.concatenate([sines] * count, axis=1)
    ).astype(jnp.bfloat16)
    query_ref[...] = rotated[:, :q_cols]
    key_value_ref[:, : kv_cols // 2] = rotated[:, q_cols:]
    key_value_ref[:, kv_cols // 2 :] = made[:, turned_cols:].astype(jnp.bfloat16)


def give_pieces(whole_ref, z_pos, piece_refs):
    count = len(piece_refs)
    part = whole_ref.shape[0] // count
    for s in range(count):
        start = pl.multiple_of(((z_pos + s) % count) * part, part)
        piece_refs[s][...] = whole_ref[pl.ds(start, part), :].astype(piece_refs[s].dtype)


def take_pieces(piece_refs, z_pos, whole_ref):
    count = len(piece_refs)
    part = whole_ref.shape[0] // count
    for s in range(count):
        start = pl.multiple_of(((z_pos + s) % count) * part, part)
        whole_ref[pl.ds(start, part), :] = piece_refs[s][...].astype(whole_ref.dtype)


def stack_heads(source, first, group):
    return jnp.concatenate(
        [source[:, (first + h) * HEAD_DIM : (first + h + 1) * HEAD_DIM] for h in range(group)],
        axis=0,
    )


def attend_kernel(
    place_ref,
    parents_ref,
    query_ref,
    kv0,
    kv1,
    kv2,
    kv3,
    out_near_ref,
    out_sent_ref,
    out_next_ref,
    head_ref,
    probs_ref,
    out_far_ref,
    attn_ref,
):
    c_pos = place_ref[1]
    blocks = (kv0, kv1, kv2, kv3)
    micro = parents_ref.shape[0]
    rows = query_ref.shape[0] // micro
    kv_heads = kv0.shape[1] // (2 * HEAD_DIM)
    group = query_ref.shape[1] // HEAD_DIM // kv_heads
    shape = (group * rows, rows)
    causal = (
        lax.broadcasted_iota(jnp.int32, shape, 1)
        <= lax.broadcasted_iota(jnp.int32, shape, 0) % rows
    )
    for m in range(micro):
        span = pl.ds(m * rows, rows)
        whole = query_ref[span, :]
        path = tree_path(parents_ref, m, c_pos)
        pieces = []
        for g in range(kv_heads):
            query = stack_heads(whole, g * group, group)
            parts = []
            for r in range(4):
                keys = blocks[r][span, :][:, g * HEAD_DIM : (g + 1) * HEAD_DIM]
                part = dot(query, keys, 1, 1) * SCORE_SCALE
                if r == 0:
                    part = jnp.where(causal, part, -1e30)
                else:
                    seen = (path[1] == c_pos ^ r) | (path[2] == c_pos ^ r) | (path[3] == c_pos ^ r)
                    part = jnp.where(seen, part, -1e30)
                parts.append(part)
            scores = jnp.concatenate(parts, axis=1)
            powers = jnp.exp(scores - jnp.max(scores, axis=1, keepdims=True))
            probs = powers * (1.0 / jnp.sum(powers, axis=1, keepdims=True))
            probs_ref[m * kv_heads + g] = probs
            low = probs.astype(jnp.bfloat16)
            values = jnp.concatenate(
                [
                    blocks[r][span, :][:, (kv_heads + g) * HEAD_DIM : (kv_heads + g + 1) * HEAD_DIM]
                    for r in range(4)
                ],
                axis=0,
            )
            mixed = dot(low, values)
            pieces += [mixed[h * rows : (h + 1) * rows] for h in range(group)]
        head_ref[span, :] = jnp.concatenate(pieces, axis=1).astype(jnp.bfloat16)
    first_core = c_pos % 2 == 0
    sent, beside = out_sent_ref[...], out_next_ref[...]
    part = sent.shape[0]
    out_far_ref[:part, :] = jnp.where(first_core, sent, beside)
    out_far_ref[part:, :] = jnp.where(first_core, beside, sent)
    half = sent.shape[1]
    attn_ref[:, :half] = dot(head_ref[...], out_near_ref[...]).astype(jnp.bfloat16)
    attn_ref[:, half:] = dot(head_ref[...], out_far_ref[...]).astype(jnp.bfloat16)


def after_kernel(
    place_ref,
    hidden_ref,
    gains_ref,
    small_ref,
    far_ref,
    routes_ref,
    attended_ref,
    mixed_ref,
    rows_ref,
    gates_ref,
):
    half = small_ref.shape[1]
    near, far = own_then_other(place_ref[0], hidden_ref[...].astype(jnp.float32))
    near = near + RESIDUAL_SCALE * attended_ref[:, :half].astype(jnp.float32)
    far = far + RESIDUAL_SCALE * attended_ref[:, half:].astype(jnp.float32)
    mixed_ref[:, :half] = near
    mixed_ref[:, half:] = far
    scale = row_scale(near, far)
    near_low = (near * scale * gains_ref[1:2, :half]).astype(jnp.bfloat16)
    far_low = (far * scale * gains_ref[1:2, half:]).astype(jnp.bfloat16)
    rows_ref[:, :half] = near_low
    rows_ref[:, half : 2 * half] = far_low
    logits = dot(near_low, small_ref[:half, half - 128 :]) + dot(far_low, far_ref[:, half - 128 :])
    lane = lax.broadcasted_iota(jnp.int32, logits.shape, 1)
    named = lane == routes_ref[:, 0:1]
    for k in range(1, routes_ref.shape[1]):
        named = named | (lane == routes_ref[:, k : k + 1])
    logits = jnp.where(named, logits, -1e30)
    powers = jnp.where(named, jnp.exp(logits - jnp.max(logits, axis=1, keepdims=True)), 0.0)
    gates = powers / jnp.sum(powers, axis=1, keepdims=True)
    gates_ref[...] = gates
    high = gates.astype(jnp.bfloat16)
    rest_part = gates - high.astype(jnp.float32)
    rows_ref[:, 2 * half :] = jnp.where(
        lane < 64, high.astype(jnp.float32), pltpu.roll(rest_part, 64, 1)
    ).astype(jnp.bfloat16)


def expert_kernel(
    place_ref,
    near_ref,
    far_ref,
    near_out_ref,
    far_out_ref,
    rank_ref,
    gate_up_ref,
    down_ref,
    *rest,
    first,
    last,
    each,
    split,
):
    count = 4 if split else 1
    other_refs, rest = rest[:count], rest[count:]
    held = rest[:4] if last else ()
    slots_ref, *sums = rest[len(held) : -8]
    rows_buf, grads_buf, moe_buf, back_buf, hot_buf, gate_buf, out_ref, grad_ref = rest[-8:]
    half = down_ref.shape[-1]
    full = 2 * half
    width = down_ref.shape[-2]
    step = pl.program_id(0)
    quarter = [place_ref[1] ^ r for r in range(4)]
    expert = [(place_ref[0] * 4 + quarter[r]) * each + first + step for r in range(4)]
    iota = lax.broadcasted_iota(jnp.int32, (CAP, 128), 0)
    lane = lax.broadcasted_iota(jnp.int32, (CAP, 128), 1)

    @pl.when(step == 0)
    def _():
        if last:
            out_ref[...] = held[0][...].astype(jnp.float32) + held[2][...].astype(jnp.float32)
            grad_ref[...] = held[1][...].astype(jnp.float32) + held[3][...].astype(jnp.float32)
        else:
            out_ref[...] = jnp.zeros_like(out_ref)
            grad_ref[...] = jnp.zeros_like(grad_ref)

    marks = [((lane == expert[r]) | (lane == expert[r] + 64)) for r in range(4)]
    mark = jnp.concatenate(marks, axis=0)
    for b in range(4):
        low = jnp.concatenate(
            [
                jnp.where(iota == rank_ref[quarter[r], 0, pl.ds(b, 1), :], 1.0, 0.0)
                for r in range(4)
            ],
            axis=0,
        ).astype(jnp.bfloat16)
        hot_buf[b] = low
        span = pl.ds((b % 2) * 128, 128)
        source = near_ref if b < 2 else far_ref
        picked = jnp.where(mark, dot(low, source[span, pl.ds(full, 128)]), 0.0)
        gate_buf[b] = jnp.broadcast_to(jnp.sum(picked, axis=1, keepdims=True), (4 * CAP, 128))
        for part in range(2):
            keep = pl.ds(part * half, half)
            if b < 2:
                rows, grads = near_ref[span, keep], near_out_ref[span, keep]
            else:
                swap = pl.ds((1 - part) * half, half)
                rows, grads = far_ref[span, swap], far_out_ref[span, swap]
            rows_buf[b, :, keep] = pick(low, rows)
            grads_buf[b, :, keep] = pick(low, grads)
    for r in range(4):
        q = quarter[r]
        slot = slice(r * CAP, (r + 1) * CAP)
        rows = jnp.concatenate([rows_buf[b, slot, :] for b in range(4)], axis=0)
        grads = jnp.concatenate([grads_buf[b, slot, :] for b in range(4)], axis=0)
        gate = jnp.concatenate([gate_buf[b, slot, :] for b in range(4)], axis=0)
        near_w = jnp.concatenate(
            [gate_up_ref[q, 0, :half, :], gate_up_ref[q, 0, half:, :]], axis=1
        )
        def other(start, size):
            if split:
                return other_refs[r][0, start : start + size, :]
            return other_refs[0][q, 0, start : start + size, :]

        far_w = jnp.concatenate([other(0, half), other(half, half)], axis=1)
        near_down = down_ref[0, q, 0]
        far_down = jnp.concatenate(
            [other(2 * half + j * width, width) for j in range(half // 128)],
            axis=1,
        )
        gate_up = dot(rows[:, :half], near_w) + dot(rows[:, half:], far_w)
        gate_pre = gate_up[:, :width]
        up_pre = gate_up[:, width:]
        sigmoid = 1.0 / (1.0 + jnp.exp(-gate_pre))
        activ = (gate_pre * sigmoid * up_pre).astype(jnp.bfloat16)
        pulled = RESIDUAL_SCALE * (
            dot(grads[:, :half], near_down, 1, 1) + dot(grads[:, half:], far_down, 1, 1)
        )
        activ_wide = activ.astype(jnp.float32)
        gate_grad = jnp.sum(activ_wide * pulled, axis=1, keepdims=True)
        activ_grad = pulled * gate
        gate_pre_grad = activ_grad * up_pre * sigmoid * (1.0 + gate_pre * (1.0 - sigmoid))
        up_pre_grad = activ_grad * gate_pre * sigmoid
        both = jnp.concatenate([gate_pre_grad, up_pre_grad], axis=1).astype(jnp.bfloat16)
        slots_ref[q, 0, :, : 2 * width] = both
        slots_ref[q, 0, :, 2 * width :] = (activ_wide * gate * RESIDUAL_SCALE).astype(jnp.bfloat16)
        for part, (wide, low_w) in enumerate(((near_w, near_down), (far_w, far_down))):
            keep = pl.ds(part * half, half)
            made = dot(activ, low_w)
            back = dot(both, wide, 1, 1)
            for b in range(4):
                piece = slice(b * CAP, (b + 1) * CAP)
                scale = jnp.concatenate([gate[piece]] * (half // 128), axis=1)
                moe_buf[b, slot, keep] = (made[piece] * scale).astype(jnp.bfloat16)
                back_buf[b, slot, keep] = back[piece].astype(jnp.bfloat16)
        spot = lane == expert[r]
        for b in range(4):
            back_buf[b, slot, pl.ds(full, 128)] = jnp.where(
                spot, gate_grad[b * CAP : (b + 1) * CAP], 0.0
            ).astype(jnp.bfloat16)
    for b in range(4):
        span = pl.ds(b * 128, 128)
        out_ref[span, :] += dot(hot_buf[b], moe_buf[b], 0, 0)
        grad_ref[span, :] += dot(hot_buf[b], back_buf[b], 0, 0)

    @pl.when(step == pl.num_programs(0) - 1)
    def _():
        if not last:
            sums[0][...] = out_ref[...].astype(jnp.bfloat16)
            sums[1][...] = grad_ref[...].astype(jnp.bfloat16)
            return
        moe_ref, back_ref, moe_far_ref, back_far_ref = sums
        count = moe_ref.shape[0]
        span = pl.ds(count, count)
        moe_ref[...] = out_ref[:count, :]
        back_ref[...] = grad_ref[:count, :]
        for part in range(2):
            keep, swap = pl.ds(part * half, half), pl.ds((1 - part) * half, half)
            moe_far_ref[:, keep] = out_ref[span, swap].astype(jnp.bfloat16)
            back_far_ref[:, keep] = grad_ref[span, swap].astype(jnp.bfloat16)
        back_far_ref[:, pl.ds(full, 128)] = grad_ref[span, pl.ds(full, 128)].astype(jnp.bfloat16)


def run_experts(place, near, far, near_out, far_out, rank, gate_up, down, other, held, first, each):
    split = isinstance(other, list)
    others = other if split else [other]
    steps, packed, lanes = others[0].shape[-3:]
    quarters, _, rows, width = gate_up.shape
    half = rows // 2
    full = 2 * half
    tokens = 2 * near.shape[0]
    last = first + steps == each

    def fixed(shape):
        return pl.BlockSpec(shape, lambda j, sp: (0,) * len(shape))

    in_specs = [
        fixed(near.shape),
        fixed(far.shape),
        fixed((tokens // 2, full)),
        fixed((tokens // 2, full)),
        pl.BlockSpec((quarters, 1, 4, 128), lambda j, sp: (0, first + j, 0, 0)),
        pl.BlockSpec((quarters, 1, rows, width), lambda j, sp: (0, first + j, 0, 0)),
        pl.BlockSpec((1, quarters, 1, width, half), lambda j, sp: (sp[0], 0, first + j, 0, 0)),
    ]
    if split:
        in_specs += [pl.BlockSpec((1, packed, lanes), lambda j, sp: (j, 0, 0))] * 4
    else:
        in_specs.append(pl.BlockSpec((quarters, 1, packed, lanes), lambda j, sp: (0, j, 0, 0)))
    operands = [place, near, far, near_out, far_out, rank, gate_up, down, *others]
    if last:
        in_specs += [fixed(array.shape) for array in held]
        operands += list(held)
    out_shape = [jax.ShapeDtypeStruct((quarters, steps, 4 * CAP, 3 * width), jnp.bfloat16)]
    out_specs = [pl.BlockSpec((quarters, 1, 4 * CAP, 3 * width), lambda j, sp: (0, j, 0, 0))]
    count = tokens // 2 if last else tokens
    kinds = (jnp.float32, jnp.bfloat16) if last else (jnp.bfloat16,)
    for kind in kinds:
        for lanes_out in (full, full + 128):
            out_shape.append(jax.ShapeDtypeStruct((count, lanes_out), kind))
            out_specs.append(fixed((count, lanes_out)))
    return pl.pallas_call(
        functools.partial(expert_kernel, first=first, last=last, each=each, split=split),
        out_shape=tuple(out_shape),
        grid_spec=pltpu.PrefetchScalarGridSpec(
            num_scalar_prefetch=1,
            grid=(steps,),
            in_specs=in_specs,
            out_specs=tuple(out_specs),
            scratch_shapes=[pltpu.VMEM((4, 4 * CAP, full), jnp.bfloat16)] * 3
            + [
                pltpu.VMEM((4, 4 * CAP, full + 128), jnp.bfloat16),
                pltpu.VMEM((4, 4 * CAP, 128), jnp.bfloat16),
                pltpu.VMEM((4, 4 * CAP, 128), jnp.float32),
                pltpu.VMEM((tokens, full), jnp.float32),
                pltpu.VMEM((tokens, full + 128), jnp.float32),
            ],
        ),
        compiler_params=kernel_params(1),
        name="experts",
    )(*operands)


def join_kernel(place_ref, total_ref, got_ref, *rest):
    piece_refs, whole_buf = rest[:-1], rest[-1]
    count = got_ref.shape[0]
    whole_buf[...] = total_ref[:count, :] + got_ref[...].astype(jnp.float32)
    give_pieces(whole_buf, place_ref[2], piece_refs)


def back_kernel(
    place_ref,
    mixed_ref,
    gates_ref,
    gains_ref,
    small_ref,
    far_ref,
    out_grad_ref,
    out_near_ref,
    out_far_ref,
    query_ref,
    turn_ref,
    kv0,
    kv1,
    kv2,
    kv3,
    probs_ref,
    *rest,
):
    (
        mixed_grad_ref,
        attn_grad_ref,
        logit_grad_ref,
        gain_grad_ref,
        query_grad_ref,
        kept_ref,
        given_ref,
        whole_buf,
        head_buf,
    ) = rest[-9:]
    take_pieces(rest[:-9], place_ref[2], whole_buf)
    half = small_ref.shape[1]
    full = 2 * half
    gates = gates_ref[...]
    gate_grads = whole_buf[:, full:]
    inner = jnp.sum(gates * gate_grads, axis=1, keepdims=True)
    logit_grad = (gates * (gate_grads - inner)).astype(jnp.bfloat16)
    logit_grad_ref[...] = logit_grad
    near, far = mixed_ref[:, :half], mixed_ref[:, half:]
    scale = row_scale(near, far)
    near_unit, far_unit = near * scale, far * scale
    near_grad = whole_buf[:, :half] + dot(logit_grad, small_ref[:half, half - 128 :], 1, 1)
    far_grad = whole_buf[:, half:full] + dot(logit_grad, far_ref[:, half - 128 :], 1, 1)
    gain_grad_ref[:, :half] = jnp.broadcast_to(
        jnp.sum(near_grad * near_unit, axis=0, keepdims=True), (8, half)
    )
    gain_grad_ref[:, half:] = jnp.broadcast_to(
        jnp.sum(far_grad * far_unit, axis=0, keepdims=True), (8, half)
    )
    near_scaled = near_grad * gains_ref[1:2, :half]
    far_scaled = far_grad * gains_ref[1:2, half:]
    mean = (
        jnp.sum(near_scaled * near_unit, axis=1, keepdims=True)
        + jnp.sum(far_scaled * far_unit, axis=1, keepdims=True)
    ) / full
    near_mixed = out_grad_ref[:, :half].astype(jnp.float32) + scale * (
        near_scaled - near_unit * mean
    )
    far_mixed = out_grad_ref[:, half:full].astype(jnp.float32) + scale * (
        far_scaled - far_unit * mean
    )
    mixed_grad_ref[:, :half] = near_mixed
    mixed_grad_ref[:, half:] = far_mixed
    near_attn = (RESIDUAL_SCALE * near_mixed).astype(jnp.bfloat16)
    far_attn = (RESIDUAL_SCALE * far_mixed).astype(jnp.bfloat16)
    attn_grad_ref[:, :half] = near_attn
    attn_grad_ref[:, half:] = far_attn
    head_buf[...] = (
        dot(near_attn, out_near_ref[...], 1, 1) + dot(far_attn, out_far_ref[...], 1, 1)
    ).astype(jnp.bfloat16)
    blocks = (kv0, kv1, kv2, kv3)
    kv_heads = kv0.shape[1] // (2 * HEAD_DIM)
    micro = probs_ref.shape[0] // kv_heads
    rows = query_ref.shape[0] // micro
    group = query_ref.shape[1] // HEAD_DIM // kv_heads
    count = query_ref.shape[1] // 128
    for m in range(micro):
        span = pl.ds(m * rows, rows)
        whole = query_ref[span, :]
        whole_grad = head_buf[span, :]
        pieces = []
        key_grads = []
        value_grads = []
        for g in range(kv_heads):
            query = stack_heads(whole, g * group, group)
            head_grad = stack_heads(whole_grad, g * group, group)
            keys = jnp.concatenate(
                [blocks[r][span, :][:, g * HEAD_DIM : (g + 1) * HEAD_DIM] for r in range(4)], axis=0
            )
            values = jnp.concatenate(
                [
                    blocks[r][span, :][:, (kv_heads + g) * HEAD_DIM : (kv_heads + g + 1) * HEAD_DIM]
                    for r in range(4)
                ],
                axis=0,
            )
            probs = probs_ref[m * kv_heads + g]
            prob_grad = dot(head_grad, values, 1, 1)
            inner = jnp.sum(probs * prob_grad, axis=1, keepdims=True)
            score_grad = (SCORE_SCALE * probs * (prob_grad - inner)).astype(jnp.bfloat16)
            value_grads.append(dot(probs.astype(jnp.bfloat16), head_grad, 0, 0))
            key_grads.append(dot(score_grad, query, 0, 0))
            query_grad = dot(score_grad, keys)
            pieces += [query_grad[h * rows : (h + 1) * rows] for h in range(group)]
        query_grad = jnp.concatenate(pieces, axis=1)
        query_grad_ref[span, :] = (
            query_grad * jnp.concatenate([turn_ref[0, span, :]] * count, axis=1)
            - turn_heads(query_grad) * jnp.concatenate([turn_ref[1, span, :]] * count, axis=1)
        ).astype(jnp.bfloat16)
        joined = jnp.concatenate(key_grads + value_grads, axis=1)
        kept_ref[0, span, :] = joined[:rows]
        kept_ref[1, span, :] = joined[2 * rows : 3 * rows]
        given_ref[0, span, :] = joined[rows : 2 * rows].astype(jnp.bfloat16)
        given_ref[1, span, :] = joined[3 * rows :].astype(jnp.bfloat16)


def last_kernel(
    place_ref,
    query_grad_ref,
    kept_ref,
    near_ref,
    along_ref,
    turn_ref,
    small_ref,
    far_ref,
    grads_ref,
    *rest,
):
    piece_refs, whole_buf = rest[:-1], rest[-1]
    q_cols = query_grad_ref.shape[1]
    k_cols = turn_ref.shape[2]
    cols = q_cols + 2 * k_cols
    half = small_ref.shape[1]
    total = (
        kept_ref[0] + near_ref[0].astype(jnp.float32) + along_ref[...].astype(jnp.float32)
    )
    keys = total[:, :k_cols]
    grads_ref[:, :q_cols] = query_grad_ref[...]
    grads_ref[:, q_cols : q_cols + k_cols] = (
        keys * turn_ref[0] - turn_heads(keys) * turn_ref[1]
    ).astype(jnp.bfloat16)
    grads_ref[:, q_cols + k_cols :] = total[:, k_cols:].astype(jnp.bfloat16)
    grads = grads_ref[...]
    near_part = dot(grads, small_ref[:half, :cols], 1, 1)
    far_part = dot(grads, far_ref[:, :cols], 1, 1)
    whole_buf[:, :half] = near_part
    whole_buf[:, half:] = far_part
    give_pieces(whole_buf, place_ref[2], piece_refs)


def output_kernel(place_ref, mixed_ref, *rest):
    out_ref, whole_buf = rest[-2:]
    take_pieces(rest[:-2], place_ref[2] // 2, whole_buf)
    half = out_ref.shape[1] // 2
    total = mixed_ref[...] + RESIDUAL_SCALE * whole_buf[...]
    first, second = own_then_other(place_ref[0], total)
    out_ref[:, :half] = first
    out_ref[:, half:] = second


def hidden_kernel(place_ref, hidden_ref, gains_ref, mixed_grad_ref, mark_ref, *rest):
    out_ref, gain_ref, whole_buf = rest[-3:]
    take_pieces(rest[:-3], place_ref[2], whole_buf)
    half = out_ref.shape[1] // 2
    near, far = own_then_other(place_ref[0], hidden_ref[...].astype(jnp.float32))
    scale = row_scale(near, far)
    near, far = near * scale, far * scale
    gain_ref[:, :half] = jnp.broadcast_to(
        jnp.sum(whole_buf[:, :half] * near, axis=0, keepdims=True), (8, half)
    )
    gain_ref[:, half:] = jnp.broadcast_to(
        jnp.sum(whole_buf[:, half:] * far, axis=0, keepdims=True), (8, half)
    )
    near_scaled = whole_buf[:, :half] * gains_ref[0:1, :half]
    far_scaled = whole_buf[:, half:] * gains_ref[0:1, half:]
    mean = (
        jnp.sum(near_scaled * near, axis=1, keepdims=True)
        + jnp.sum(far_scaled * far, axis=1, keepdims=True)
    ) / (2 * half)
    near_out = mixed_grad_ref[:, :half] + scale * (near_scaled - near * mean)
    far_out = mixed_grad_ref[:, half:] + scale * (far_scaled - far * mean)
    out_ref[:, :half] = jnp.where(place_ref[0] == 0, near_out, far_out)
    out_ref[:, half:] = jnp.where(place_ref[0] == 0, far_out, near_out)


def weight_grad_kernel(
    place_ref, rows_ref, grads0, grads1, grads2, grads3, slots_ref, rank_ref, *refs, first, steps
):
    gate_up_ref, down_ref, mark_ref, rows_buf, grads_buf = refs[-5:]
    half = down_ref.shape[-1]
    width = down_ref.shape[-2]
    iota = lax.broadcasted_iota(jnp.int32, (CAP, 128), 0)
    grads_in = (grads0, grads1, grads2, grads3)
    ctx = [place_ref[1] ^ r for r in range(4)]
    step, side = pl.program_id(0), pl.program_id(1)
    mark_ref[...] = jnp.zeros_like(mark_ref)

    @pl.when((step == 0) & (side == 0))
    def _():
        for k in range(4):
            for b in range(4):
                span = pl.ds(b * 128, 128)
                hot = jnp.concatenate(
                    [
                        jnp.where(
                            iota == rank_ref[a, q, first + j, pl.ds(4 * k + b, 1), :], 1.0, 0.0
                        )
                        for a in range(2)
                        for j in range(steps)
                        for q in range(4)
                    ],
                    axis=0,
                ).astype(jnp.bfloat16)
                rows = pick(hot, rows_ref[ctx[k], span, :])
                grads = pick(hot, grads_in[k][span, :])
                for a in range(2):
                    spot = 4 * k + (b ^ (2 * a))
                    for j in range(steps):
                        start = (a * steps + j) * 4 * CAP
                        piece = slice(start, start + 4 * CAP)
                        rows_buf[j * 2 + a, spot] = rows[piece]
                        grads_buf[j * 2 + a, spot] = grads[piece]

    place = step * 2 + side
    for q in range(4):
        slot = slice(q * CAP, (q + 1) * CAP)
        rows = jnp.concatenate([rows_buf[place, n, slot, :] for n in range(16)], axis=0)
        grads = jnp.concatenate([grads_buf[place, n, slot, :] for n in range(16)], axis=0)
        taken = jnp.concatenate([slots_ref[0, ctx[k], q, 0] for k in range(4)], axis=0)
        made = dot(rows, taken[:, : 2 * width], 0, 0)
        gate_up_ref[0, q, 0, pl.ds(0, half, stride=2), :] = made[:, :width]
        gate_up_ref[0, q, 0, pl.ds(1, half, stride=2), :] = made[:, width:]
        down_ref[0, q, 0] = dot(taken[:, 2 * width :], grads, 0, 0)


def run_weight_grads(place, plane, early, slots, rank, held, each, first, mark):
    sides, _, quarters, steps, slot_count, lanes = slots.shape
    width = lanes // 3
    half = plane.shape[-1]
    tokens = plane.shape[1]

    def place_of(j, a, sp):
        return (sp[0] ^ a, 0, first + j, 0, 0)

    in_specs = [
        pl.BlockSpec((4, tokens, half), lambda j, a, sp: (0, 0, 0)),
        *[pl.BlockSpec((tokens, half), lambda j, a, sp: (0, 0))] * 4,
        pl.BlockSpec(
            (1, 4, quarters, 1, slot_count, lanes),
            lambda j, a, sp: (sp[0] ^ a, 0, 0, j, 0, 0),
        ),
        pl.BlockSpec(rank.shape, lambda j, a, sp: (0, 0, 0, 0, 0)),
        pl.BlockSpec(memory_space=pl.ANY),
    ]
    operands = [place, plane, *early, slots, rank, mark]
    aliases = {}
    if held is not None:
        in_specs += [pl.BlockSpec(memory_space=pl.ANY)] * 2
        aliases = {len(operands): 0, len(operands) + 1: 1}
        operands += list(held[:2])
    return pl.pallas_call(
        functools.partial(weight_grad_kernel, first=first, steps=steps),
        out_shape=(
            jax.ShapeDtypeStruct((sides, quarters, each, 2 * half, width), jnp.float32),
            jax.ShapeDtypeStruct((sides, quarters, each, width, half), jnp.float32),
            jax.ShapeDtypeStruct((8, 128), jnp.float32),
        ),
        grid_spec=pltpu.PrefetchScalarGridSpec(
            num_scalar_prefetch=1,
            grid=(steps, sides),
            in_specs=in_specs,
            out_specs=(
                pl.BlockSpec((1, quarters, 1, 2 * half, width), place_of),
                pl.BlockSpec((1, quarters, 1, width, half), place_of),
                pl.BlockSpec((8, 128), lambda j, a, sp: (0, 0)),
            ),
            scratch_shapes=[pltpu.VMEM((2 * steps, 16, 4 * CAP, half), jnp.bfloat16)] * 2,
        ),
        input_output_aliases=aliases,
        compiler_params=kernel_params(2),
        name="weight_grads",
    )(*operands)


def swap_halves(values):
    half = values.shape[-1] // 2
    return jnp.concatenate([values[..., half:], values[..., :half]], axis=-1)


def fast_body(
    hidden_in,
    parents,
    routes,
    attn_gain,
    w_query,
    key_projection,
    value_projection,
    w_out,
    moe_gain,
    w_router,
    w_gate_up,
    w_down,
    d_out,
):
    low, wide = jnp.bfloat16, jnp.float32
    x_pos = lax.axis_index("fsdp")
    c_pos = lax.axis_index("ctx")
    z_pos = lax.axis_index("tp")
    tp_size = lax.axis_size("tp")
    place = jnp.stack([x_pos, c_pos, z_pos]).astype(jnp.int32)
    micro, _, rows, model = hidden_in.shape
    half = model // 2
    tokens = micro * rows
    experts = w_gate_up.shape[0]
    mine = experts // 2
    each = mine // 4
    width = w_down.shape[1]
    q_cols = w_query.shape[1]
    k_cols = key_projection.shape[1]
    qkv_cols = q_cols + 2 * k_cols
    kv_heads = k_cols // HEAD_DIM
    group = q_cols // k_cols
    top = routes.shape[-1]
    chunks = ((0, 2), (2, 2), (4, 1))
    tie = lax.optimization_barrier

    def across(value):
        return lax.ppermute(value, "fsdp", [(0, 1), (1, 0)])

    def beside(value):
        return lax.ppermute(value, "ctx", [(i, i ^ 1) for i in range(4)])

    def along(value):
        return lax.ppermute(value, "ctx", [(i, i ^ 2) for i in range(4)])

    def from_tp(value, step):
        return lax.ppermute(value, "tp", [((i + step) % tp_size, i) for i in range(tp_size)])

    def all_ctx(value):
        nearby = beside(value)
        distant = along(value)
        return [value, nearby, distant, beside(distant)]

    def own_first(value):
        return jnp.where(x_pos == 0, value, swap_halves(value))

    def reduce_pieces(pieces):
        total = pieces[0].astype(wide)
        for step in range(1, tp_size):
            total = total + from_tp(pieces[tp_size - step], step).astype(wide)
        return total.astype(low)

    def spread_pieces(total):
        return [total] + [from_tp(total, step) for step in range(1, tp_size)]

    piece_shapes = [((tokens // tp_size, model), low)] * tp_size
    hidden = hidden_in.reshape(tokens, model)
    flat_routes = routes.reshape(tokens, top)

    core = c_pos % 2
    part = half // 2
    weights = jnp.concatenate(
        [
            w_query,
            key_projection,
            value_projection,
            jnp.pad(w_router, ((0, 0), (0, half - qkv_cols - experts))),
        ],
        axis=1,
    )
    gain_rows = jnp.pad(jnp.stack([attn_gain, moe_gain]), ((0, 14), (0, 0)))
    small = jnp.concatenate([weights, gain_rows], axis=0)
    sent = across(
        jnp.concatenate([lax.dynamic_slice_in_dim(weights, core * part, part, 0), gain_rows], axis=0)
    )

    both_view = w_gate_up.reshape(experts, 2 * half, width)
    base = (x_pos * mine).astype(jnp.int32)[None]
    away = ((1 - x_pos) * mine + c_pos * each).astype(jnp.int32)[None]
    packs = [split_weights(away + first, count, both_view, w_down) for first, count in chunks]
    down_all = w_down.reshape(2, 4, each, width, half)
    routes_low = jnp.pad(flat_routes.astype(low), ((0, 0), (0, 128 - top)))
    near_out = jnp.concatenate([own_first(d_out.reshape(tokens, model)), routes_low], axis=1)

    half_dim = HEAD_DIM // 2
    inverse = ROPE_BASE ** (-jnp.arange(half_dim, dtype=wide) * 2.0 / HEAD_DIM)
    angles = jnp.arange(4 * rows, dtype=wide)[:, None] * inverse[None, :]
    cosines = jnp.tile(jnp.cos(angles), (1, 4))
    sines = jnp.tile(jnp.sin(angles), (1, 4))
    sent, packs[0], out_start, small, cosines, sines, place = tie(
        (sent, packs[0], core * (q_cols // 2), small, cosines, sines, place)
    )
    out_sent = across(lax.dynamic_slice_in_dim(w_out, out_start, q_cols // 2, 0))

    normed_one, query, key_value, small_far, gains, turns = single(
        before_kernel,
        "before",
        [
            ((tokens, model), low),
            ((tokens, q_cols), low),
            ((tokens, 2 * k_cols), low),
            ((half, half), low),
            ((16, model), wide),
            ((2, tokens, 128), wide),
        ],
        [],
        [place, parents.reshape(micro, 4)],
        hidden,
        small,
        sent,
        beside(sent),
        cosines,
        sines,
    )
    key_value, packs[0], near_out, out_sent = tie((key_value, packs[0], near_out, out_sent))
    blocks = all_ctx(key_value)
    far_out = across(near_out)
    far_zero = across(packs[0])
    head_low, probs, out_far, attn_part = single(
        attend_kernel,
        "attend",
        [
            ((tokens, q_cols), low),
            ((micro * kv_heads, group * rows, 4 * rows), wide),
            ((q_cols, half), low),
            ((tokens, model), low),
        ],
        [],
        [place, parents.reshape(micro, 4)],
        query,
        *blocks,
        w_out,
        out_sent,
        beside(out_sent),
    )
    attn_part, base = tie((attn_part, base))
    gate_up_mine = split_weights(base, mine, both_view, None).reshape(4, each, 2 * half, width)
    attended = lax.psum(attn_part, "tp")
    far_zero, packs[1] = tie((far_zero, packs[1]))
    far_one = across(packs[1])
    attended, far_out, gate_up_mine = tie((attended, far_out, gate_up_mine))
    zero_along = along(far_zero)
    early = jnp.concatenate(
        [
            jnp.concatenate([near_out[:, :half], routes_low], axis=1),
            far_out[:, half:],
        ],
        axis=0,
    )
    early_along = along(early)
    early_near = beside(early)
    mixed, near, gates = single(
        after_kernel,
        "after",
        [((tokens, model), wide), ((tokens, model + 128), low), ((tokens, 128), wide)],
        [],
        [place],
        hidden,
        gains,
        small,
        small_far,
        flat_routes,
        attended,
    )
    upper = (
        lax.broadcasted_iota(jnp.int32, (rows, rows), 0)
        < lax.broadcasted_iota(jnp.int32, (rows, rows), 1)
    ).astype(low)

    def ranks(route_table, ids):
        flat = route_table.astype(jnp.int32).T
        hit = jnp.zeros((ids.shape[0], flat.shape[1]), jnp.bool_)
        for k in range(top):
            hit = hit | (flat[k][None, :] == ids[:, None])
        hot = hit.astype(low).reshape(-1, rows)
        found = jnp.where(hot > 0, dot(hot, upper), -1.0).astype(jnp.int32)
        return found.reshape(ids.shape[0], -1, rows)

    expert_ids = (jnp.arange(experts, dtype=jnp.int32) + x_pos * mine) % experts
    pair_routes = jnp.concatenate([routes_low, far_out[:, model:]], axis=0)[:, :top]
    rank_pair = ranks(pair_routes, expert_ids[:mine]).reshape(4, each, 4, rows)

    near, packs[2] = tie((near, packs[2]))
    far = across(near)
    one_along = along(far_one)
    far, packs[2], zero_along, gate_up_mine, early_along, early_near, rank_pair = tie(
        (far, packs[2], zero_along, gate_up_mine, early_along, early_near, rank_pair)
    )
    early = [early, early_near, early_along, beside(early_along)]
    far_two = across(packs[2])
    plane_in = jnp.concatenate([near[:, :half], far[:, half:model]], axis=0)
    def all_four(got, distant):
        return [got, beside(got), distant, beside(distant)]

    def gather_slots(part):
        return lax.all_gather(part, ("fsdp", "ctx")).reshape(2, 4, *part.shape)

    held = []
    slots = []
    for number, (first, count) in enumerate(chunks):
        if number == 0:
            other = all_four(far_zero, zero_along)
        if number == 1:
            slots[0], far_two, one_along, plane_in = tie(
                (slots[0], far_two, one_along, plane_in)
            )
            two_along = along(far_two)
            plane = lax.all_gather(plane_in, "ctx")
            other = all_four(far_one, one_along)
        if number == 2:
            slots[1], two_along = tie((slots[1], two_along))
            other = all_four(far_two, two_along)
        made = run_experts(
            place,
            near,
            far,
            near_out,
            far_out,
            rank_pair,
            gate_up_mine,
            down_all,
            other,
            held,
            first,
            each,
        )
        slots.append(made[0])
        held += made[1:]
    moe_all, back_all, moe_far, back_far = made[1:]

    all_routes = jnp.concatenate([part[:, half : half + top] for part in early], axis=0)
    rank_all = ranks(all_routes, expert_ids).reshape(2, 4, each, 16, rows)

    back_far, plane, slots[0] = tie((back_far, plane, slots[0]))
    back_got = across(back_far)
    pair_zero = gather_slots(slots[0])
    back_got, moe_far, rank_all = tie((back_got, moe_far, rank_all))

    def grads_of(number, pair, held, mark):
        first, count = chunks[number]
        return run_weight_grads(
            place,
            plane,
            early,
            pair,
            rank_all,
            held,
            each,
            first,
            mark,
        )

    pieces = single(
        join_kernel,
        "join",
        [((tokens // tp_size, model + 128), low)] * tp_size,
        [((tokens, model + 128), wide)],
        [place],
        back_all,
        back_got,
    )
    total = reduce_pieces(pieces)
    total, moe_far, pair_zero, slots[1] = tie((total, moe_far, pair_zero, slots[1]))
    moe_got = across(moe_far)
    pair_one = gather_slots(slots[1])
    found = spread_pieces(total)
    grads = grads_of(0, pair_zero, None, jnp.zeros((8, 128), wide))
    *found, moe_got, mark = tie((*found, moe_got, grads[2]))
    moe_pieces = single(
        join_kernel, "join", piece_shapes, [((tokens, model), wide)], [place], moe_all, moe_got
    )
    moe_total = reduce_pieces(moe_pieces)
    (
        mixed_grad,
        attn_grad,
        logit_grad,
        gain_two_part,
        query_grad,
        kept,
        given,
    ) = single(
        back_kernel,
        "back",
        [
            ((tokens, model), wide),
            ((tokens, model), low),
            ((tokens, 128), low),
            ((8, model), wide),
            ((tokens, q_cols), low),
            ((2, tokens, 2 * k_cols), wide),
            ((2, tokens, 2 * k_cols), low),
        ],
        [((tokens, model + 128), wide), ((tokens, q_cols), low)],
        [place],
        mixed,
        gates,
        gains,
        small,
        small_far,
        near_out,
        w_out,
        out_far,
        query,
        turns,
        *blocks,
        probs,
        *found,
    )

    given, moe_total = tie((given, moe_total))
    near_pair = beside(given)
    near_pair, attn_grad = tie((near_pair, attn_grad))
    moe_next = lax.ppermute(moe_total, "tp", [(i, i ^ 1) for i in range(tp_size)])
    distant = along((kept[1] + near_pair[1].astype(wide)).astype(low))
    qkv_grad, *pieces = single(
        last_kernel,
        "last",
        [((tokens, qkv_cols), low)] + piece_shapes,
        [((tokens, model), wide)],
        [place],
        query_grad,
        kept,
        near_pair,
        distant,
        turns,
        small,
        small_far,
    )

    def hop_beside(value):
        share = value.shape[1] // 2
        kept = lax.dynamic_slice_in_dim(value, core * share, share, 1)
        given = lax.dynamic_slice_in_dim(value, (1 - core) * share, share, 1)
        return kept + beside(given.astype(low)).astype(wide)

    def hop_across(kept):
        return kept[0] + across(kept[1].astype(low)).astype(wide)

    def hop_along(total):
        return (total + along(total.astype(low)).astype(wide)).astype(low)

    def hop_join(total):
        other = beside(total)
        return jnp.where(
            core == 0,
            jnp.concatenate([total, other], axis=0),
            jnp.concatenate([other, total], axis=0),
        ).astype(wide)

    def both(left, right):
        return jnp.stack([dot(left, right[:, :half], 0, 0), dot(left, right[:, half:], 0, 0)])

    side = hop_beside(
        jnp.concatenate(
            [
                both(head_low, attn_grad),
                both(logit_grad[:, :experts], near[:, :model]),
                jnp.stack([gain_two_part[:, :half], gain_two_part[:, half:]]),
                jnp.zeros((2, 16, half), wide),
            ],
            axis=1,
        )
    )
    side_got = across(side[1].astype(low))
    *pieces, mark, side_got, qkv_grad, pair_one, slots[2], moe_next = tie(
        (*pieces, mark, side_got, qkv_grad, pair_one, slots[2], moe_next)
    )
    side = side[0] + side_got.astype(wide)
    pair_two = gather_slots(slots[2])
    moe_pair = jnp.where(
        z_pos % 2 == 0,
        jnp.concatenate([moe_total, moe_next], axis=0),
        jnp.concatenate([moe_next, moe_total], axis=0),
    )
    moe_rest = lax.ppermute(moe_pair, "tp", [(i, i ^ 2) for i in range(tp_size)])
    total = reduce_pieces(pieces)
    grads = grads_of(1, pair_one, grads, mark)
    d_qkv = hop_beside(dot(normed_one, qkv_grad, 0, 0).reshape(2, half, qkv_cols))
    total, mark, side, d_qkv, moe_rest = tie((total, grads[2], side, d_qkv, moe_rest))
    (layer_out,) = single(
        output_kernel,
        "output",
        [((tokens, model), wide)],
        [((tokens, model), wide)],
        [place],
        mixed,
        moe_pair,
        moe_rest,
    )
    found = spread_pieces(total)
    grads = grads_of(2, pair_two, grads, mark)
    side_got = along(side.astype(low))
    qkv_got = across(d_qkv[1].astype(low))
    *found, mark, side_got, qkv_got = tie((*found, grads[2], side_got, qkv_got))
    side = (side + side_got.astype(wide)).astype(low)
    d_qkv = d_qkv[0] + qkv_got.astype(wide)
    d_hidden, gain_one = single(
        hidden_kernel,
        "hidden",
        [((tokens, model), wide), ((8, model), wide)],
        [((tokens, model), wide)],
        [place],
        hidden,
        gains,
        mixed_grad,
        mark,
        *found,
    )
    gain_one = gain_one[0]
    d_gate_up = grads[0].reshape(experts, half, 2, width)
    d_down = grads[1].reshape(experts, width, half)
    side_grads = hop_join(side)
    d_qkv = hop_join(hop_along(d_qkv))
    gain_one = gain_one + beside(gain_one)
    gain_one = gain_one + along(gain_one)
    gain_one = gain_one[:half] + across(gain_one[half:])
    return (
        layer_out.reshape(micro, 1, rows, model),
        d_hidden.reshape(micro, 1, rows, model),
        gain_one,
        d_qkv[:, :q_cols],
        d_qkv[:, q_cols : q_cols + k_cols],
        d_qkv[:, q_cols + k_cols :],
        side_grads[:q_cols],
        side_grads[q_cols + experts],
        side_grads[q_cols : q_cols + experts].T,
        d_gate_up,
        d_down,
    )


def solution(mesh):
    placed = (
        P(None, "fsdp", "ctx", None),
        P(None, "fsdp", None),
        P(None, "fsdp", "ctx", None),
        P("fsdp"),
        P("fsdp", "tp"),
        P("fsdp", "tp"),
        P("fsdp", "tp"),
        P("tp", "fsdp"),
        P("fsdp"),
        P("fsdp", None),
        P(None, "fsdp", None, "tp"),
        P(None, "tp", "fsdp"),
        P(None, "fsdp", "ctx", None),
    )
    fits = mesh.shape["fsdp"] == 2 and mesh.shape["ctx"] == 4 and mesh.shape["tp"] == 4
    return jax.shard_map(
        fast_body if fits else body,
        mesh=mesh,
        in_specs=placed,
        out_specs=(
            P(None, "fsdp", "ctx", None),
            P(None, "fsdp", "ctx", None),
            P("fsdp"),
            P("fsdp", "tp"),
            P("fsdp", "tp"),
            P("fsdp", "tp"),
            P("tp", "fsdp"),
            P("fsdp"),
            P("fsdp", None),
            P(None, "fsdp", None, "tp"),
            P(None, "tp", "fsdp"),
        ),
        check_vma=False,
    )
```

```python
import functools

import jax
import jax.numpy as jnp
from jax import lax
from jax.experimental import pallas as pl
from jax.experimental.pallas import tpu as pltpu
from jax.sharding import PartitionSpec as P

HEAD_DIM = 64
CAP = 32


EPSILON = 1e-06
RESIDUAL_SCALE = 0.22
SCORE_SCALE = 1.0 / 64.0
ROPE_BASE = 10000.0
TOP_PRECISION = lax.Precision.HIGHEST


def tree_tables(parent_row, tree_len):
    seg_total = parent_row.shape[0]
    seg_len = tree_len // seg_total
    seg_ids = jnp.arange(seg_total, dtype=jnp.int32)
    parent_links = (parent_row[:, None] == seg_ids[None, :]).astype(jnp.float32)
    reach_table = jnp.maximum(parent_links, jnp.eye(seg_total, dtype=jnp.float32))
    for squaring in range(max(seg_total - 1, 1).bit_length()):
        reach_table = jnp.minimum(jnp.dot(reach_table, reach_table, precision=TOP_PRECISION), 1.0)
    seg_depth = jnp.sum(reach_table, axis=1) - 1.0
    token_ids = jnp.arange(tree_len, dtype=jnp.int32)
    tok_owner = ((token_ids // seg_len)[:, None] == seg_ids[None, :]).astype(jnp.float32)
    tok_offset = (token_ids % seg_len).astype(jnp.float32)
    places = jnp.dot(tok_owner, seg_depth, precision=TOP_PRECISION) * seg_len + tok_offset
    return (places, jnp.dot(tok_owner, reach_table, precision=TOP_PRECISION), tok_owner)


def rope_tables(places):
    half_dim = HEAD_DIM // 2
    inverse = ROPE_BASE ** (-jnp.arange(half_dim, dtype=jnp.float32) * 2.0 / HEAD_DIM)
    angles = places[:, None] * inverse[None, :]
    cosine_table = jnp.concatenate([jnp.cos(angles), jnp.cos(angles)], axis=1)
    sine_values = jnp.concatenate([jnp.sin(angles), jnp.sin(angles)], axis=1)
    return (cosine_table, sine_values)


def apply_rotary(values, cosine_table, sine_values):
    half_dim = values.shape[-1] // 2
    turned = jnp.concatenate([-values[..., half_dim:], values[..., :half_dim]], axis=-1)
    return values * cosine_table[:, None, :] + turned * sine_values[:, None, :]


def norm_scale(values):
    return lax.rsqrt(jnp.mean(values * values, axis=-1, keepdims=True) + EPSILON)


def add_tuples(first_tuple, second_tuple):
    return tuple(
        (left_part + right_part for left_part, right_part in zip(first_tuple, second_tuple))
    )


def expert_work(rows, row_grads, gate_up_w, down_w, down_form):
    gate_up = jnp.einsum("ecd,edsf->ecsf", rows, gate_up_w, preferred_element_type=jnp.float32)
    gate_pre = gate_up[:, :, 0]
    up_pre = gate_up[:, :, 1]
    sigmoid = jax.nn.sigmoid(gate_pre)
    activ_low = (gate_pre * sigmoid * up_pre).astype(jnp.bfloat16)
    expert_out = jnp.einsum(
        "ecf," + down_form + "->ecd", activ_low, down_w, preferred_element_type=jnp.float32
    )
    activ_grad = jnp.einsum(
        "ecd," + down_form + "->ecf", row_grads, down_w, preferred_element_type=jnp.float32
    )
    gate_grad = activ_grad * up_pre * sigmoid * (1.0 + gate_pre * (1.0 - sigmoid))
    up_grad = activ_grad * gate_pre * sigmoid
    gate_up_grad = jnp.stack([gate_grad, up_grad], axis=2).astype(jnp.bfloat16)
    row_input_grad = jnp.einsum(
        "ecsf,edsf->ecd", gate_up_grad, gate_up_w, preferred_element_type=jnp.float32
    )
    grad_gate_up = jnp.einsum(
        "ecd,ecsf->edsf", rows, gate_up_grad, preferred_element_type=jnp.float32
    )
    grad_down = jnp.einsum(
        "ecf,ecd->" + down_form, activ_low, row_grads, preferred_element_type=jnp.float32
    )
    return (expert_out, row_input_grad, grad_gate_up, grad_down)


def body(
    hidden_in,
    parents,
    routes,
    attn_gain,
    w_query,
    key_projection,
    value_projection,
    w_out,
    moe_gain,
    w_router,
    w_gate_up,
    w_down,
    d_out,
):
    experts = w_gate_up.shape[0]
    gathered = (
        lax.all_gather(attn_gain, "fsdp", axis=0, tiled=True),
        lax.all_gather(w_query, "fsdp", axis=0, tiled=True),
        lax.all_gather(key_projection, "fsdp", axis=0, tiled=True),
        lax.all_gather(value_projection, "fsdp", axis=0, tiled=True),
        lax.all_gather(w_out, "fsdp", axis=1, tiled=True),
        lax.all_gather(moe_gain, "fsdp", axis=0, tiled=True),
        lax.all_gather(w_router, "fsdp", axis=0, tiled=True),
        lax.all_gather(w_gate_up, "fsdp", axis=1, tiled=True),
        lax.all_gather(w_down, "fsdp", axis=2, tiled=True),
    )
    gate_up_full = gathered[7]
    down_full = gathered[8]
    down_form = "efd"
    gain_one = gathered[0].astype(jnp.float32)
    query_full = gathered[1]
    key_full = gathered[2]
    value_full = gathered[3]
    out_full = gathered[4]
    gain_two = gathered[5].astype(jnp.float32)
    router_full = gathered[6]
    micro_count = hidden_in.shape[0]
    local_rows = hidden_in.shape[2]
    model_width = hidden_in.shape[3]
    top_count = routes.shape[3]
    kv_heads = key_projection.shape[1] // HEAD_DIM
    q_heads = w_query.shape[1] // HEAD_DIM
    group_size = q_heads // kv_heads
    tree_len = local_rows * lax.axis_size("ctx")
    row_start = lax.axis_index("ctx") * local_rows
    capacity = CAP
    expert_ids = jnp.arange(experts, dtype=jnp.int32)
    outputs = []
    input_grads = []
    totals = None
    for batch_index in range(micro_count):
        tree_places, reach_rows, tok_owner = tree_tables(parents[batch_index, 0], tree_len)
        local_places = lax.dynamic_slice_in_dim(tree_places, row_start, local_rows, 0)
        local_reach = lax.dynamic_slice_in_dim(reach_rows, row_start, local_rows, 0)
        allowed = (jnp.dot(local_reach, tok_owner.T, precision=TOP_PRECISION) > 0.5) & (
            tree_places[None, :] <= local_places[:, None]
        )
        cosine_table, sine_values = rope_tables(local_places)
        inputs = hidden_in[batch_index, 0].astype(jnp.float32)
        scale_one = norm_scale(inputs)
        first_normed = (inputs * scale_one * gain_one).astype(jnp.bfloat16)
        query_unrotated = jnp.dot(
            first_normed, query_full, preferred_element_type=jnp.float32
        ).reshape(local_rows, q_heads, HEAD_DIM)
        key_unrotated = jnp.dot(first_normed, key_full, preferred_element_type=jnp.float32).reshape(
            local_rows, kv_heads, HEAD_DIM
        )
        value_reduced = jnp.dot(
            first_normed, value_full, preferred_element_type=jnp.float32
        ).astype(jnp.bfloat16)
        query_reduced = (
            apply_rotary(query_unrotated, cosine_table, sine_values)
            .astype(jnp.bfloat16)
            .reshape(local_rows, kv_heads, group_size, HEAD_DIM)
        )
        key_low = (
            apply_rotary(key_unrotated, cosine_table, sine_values)
            .astype(jnp.bfloat16)
            .reshape(local_rows, kv_heads * HEAD_DIM)
        )
        tree_keys, tree_values = (
            lax.all_gather(key_low, "ctx", axis=0, tiled=True),
            lax.all_gather(value_reduced, "ctx", axis=0, tiled=True),
        )
        tree_keys = tree_keys.reshape(tree_len, kv_heads, HEAD_DIM)
        tree_values = tree_values.reshape(tree_len, kv_heads, HEAD_DIM)

        def masked_scores():
            raw_scores = jnp.einsum(
                "qhjd,khd->hjqk", query_reduced, tree_keys, preferred_element_type=jnp.float32
            )
            return jnp.where(allowed[None, None], raw_scores * SCORE_SCALE, -1e30)

        scores = masked_scores()
        top_score = jnp.max(scores, axis=-1, keepdims=True)
        log_total = top_score + jnp.log(
            jnp.sum(jnp.exp(scores - top_score), axis=-1, keepdims=True)
        )
        probs_low = jnp.exp(scores - log_total).astype(jnp.bfloat16)
        head_out = jnp.einsum(
            "hjqk,khd->qhjd", probs_low, tree_values, preferred_element_type=jnp.float32
        )
        head_low = head_out.reshape(local_rows, q_heads * HEAD_DIM).astype(jnp.bfloat16)
        attn_part = jnp.dot(head_low, out_full, preferred_element_type=jnp.float32)
        attended = lax.psum(attn_part.astype(jnp.bfloat16), "tp").astype(jnp.float32)
        mixed = inputs + RESIDUAL_SCALE * attended
        scale_two = norm_scale(mixed)
        normed_two = (mixed * scale_two * gain_two).astype(jnp.bfloat16)
        logits = jnp.dot(normed_two, router_full, preferred_element_type=jnp.float32)
        chosen_ids = routes[batch_index, 0]
        picked = (chosen_ids[:, :, None] == expert_ids[None, None, :]).astype(jnp.float32)
        chosen = jnp.sum(picked * logits[:, None, :], axis=2)
        gates = jax.nn.softmax(chosen, axis=1)
        flat_ids = chosen_ids.reshape(-1)
        flat_hot = (flat_ids[:, None] == expert_ids[None, :]).astype(jnp.int32)
        slots = jnp.sum((jnp.cumsum(flat_hot, axis=0) - flat_hot) * flat_hot, axis=1)
        targets = flat_ids * capacity + slots
        sources = (
            jnp.zeros((experts * capacity,), jnp.int32)
            .at[targets]
            .set(jnp.arange(local_rows * top_count, dtype=jnp.int32) // top_count)
        )
        filled = jnp.zeros((experts * capacity, 1), jnp.bfloat16).at[targets].set(1)
        dispatched = (normed_two[sources] * filled).reshape(experts, capacity, model_width)
        grad_out = d_out[batch_index, 0].astype(jnp.float32)
        grad_moe = RESIDUAL_SCALE * grad_out
        entry_grad = (
            (gates[:, :, None] * grad_moe[:, None, :])
            .astype(jnp.bfloat16)
            .reshape(local_rows * top_count, model_width)
        )
        slot_grad = (
            jnp.zeros((experts * capacity, model_width), jnp.bfloat16)
            .at[targets]
            .set(entry_grad)
            .reshape(experts, capacity, model_width)
        )
        expert_out, slot_input_grad, grad_gate_up, grad_down = expert_work(
            dispatched, slot_grad, gate_up_full, down_full, down_form
        )
        entry_out = expert_out.reshape(experts * capacity, model_width)[targets].reshape(
            local_rows, top_count, model_width
        )
        moe_part = jnp.sum(gates[:, :, None] * entry_out, axis=1)
        moe_sum = lax.psum(moe_part.astype(jnp.bfloat16), "tp").astype(jnp.float32)
        outputs.append(mixed + RESIDUAL_SCALE * moe_sum)
        gate_grad_part = jnp.sum(grad_moe[:, None, :] * entry_out, axis=2)
        expert_input_grad = jnp.sum(
            slot_input_grad.reshape(experts * capacity, model_width)[targets].reshape(
                local_rows, top_count, model_width
            ),
            axis=1,
        )
        expert_input_grad, gate_grads = (
            lax.psum(expert_input_grad.astype(jnp.bfloat16), "tp").astype(jnp.float32),
            lax.psum(gate_grad_part.astype(jnp.bfloat16), "tp").astype(jnp.float32),
        )
        chosen_grad = gates * (gate_grads - jnp.sum(gates * gate_grads, axis=1, keepdims=True))
        logit_grad = jnp.sum(picked * chosen_grad[:, :, None], axis=1).astype(jnp.bfloat16)
        normed_two_grad = expert_input_grad + jnp.einsum(
            "te,de->td", logit_grad, router_full, preferred_element_type=jnp.float32
        )
        grad_router = jnp.einsum(
            "td,te->de", normed_two, logit_grad, preferred_element_type=jnp.float32
        )
        unit_two = mixed * scale_two
        grad_gain_two = jnp.sum(normed_two_grad * unit_two, axis=0)
        scaled_two = normed_two_grad * gain_two
        mixed_grad = grad_out + scale_two * (
            scaled_two - unit_two * jnp.mean(scaled_two * unit_two, axis=-1, keepdims=True)
        )
        attn_grad = (RESIDUAL_SCALE * mixed_grad).astype(jnp.bfloat16)
        grad_out_proj = jnp.einsum(
            "tc,td->cd", head_low, attn_grad, preferred_element_type=jnp.float32
        )
        head_grad = (
            jnp.einsum("td,cd->tc", attn_grad, out_full, preferred_element_type=jnp.float32)
            .astype(jnp.bfloat16)
            .reshape(local_rows, kv_heads, group_size, HEAD_DIM)
        )
        scores = masked_scores()
        probs = jnp.exp(scores - log_total)
        probs_low = probs.astype(jnp.bfloat16)
        prob_grad = jnp.einsum(
            "qhjd,khd->hjqk", head_grad, tree_values, preferred_element_type=jnp.float32
        )
        value_grad = jnp.einsum(
            "hjqk,qhjd->khd", probs_low, head_grad, preferred_element_type=jnp.float32
        )
        score_grad = (
            SCORE_SCALE * probs * (prob_grad - jnp.sum(probs * prob_grad, axis=-1, keepdims=True))
        ).astype(jnp.bfloat16)
        query_grad = jnp.einsum(
            "hjqk,khd->qhjd", score_grad, tree_keys, preferred_element_type=jnp.float32
        ).reshape(local_rows, q_heads, HEAD_DIM)
        key_grad = jnp.einsum(
            "hjqk,qhjd->khd", score_grad, query_reduced, preferred_element_type=jnp.float32
        )
        key_grad, value_grad = (
            lax.psum_scatter(
                key_grad.reshape(tree_len, kv_heads * HEAD_DIM).astype(jnp.bfloat16),
                "ctx",
                scatter_dimension=0,
                tiled=True,
            ).astype(jnp.float32),
            lax.psum_scatter(
                value_grad.reshape(tree_len, kv_heads * HEAD_DIM).astype(jnp.bfloat16),
                "ctx",
                scatter_dimension=0,
                tiled=True,
            ).astype(jnp.float32),
        )
        query_pre_grad = (
            apply_rotary(query_grad, cosine_table, -sine_values)
            .astype(jnp.bfloat16)
            .reshape(local_rows, q_heads * HEAD_DIM)
        )
        key_pre_grad = (
            apply_rotary(
                key_grad.reshape(local_rows, kv_heads, HEAD_DIM), cosine_table, -sine_values
            )
            .astype(jnp.bfloat16)
            .reshape(local_rows, kv_heads * HEAD_DIM)
        )
        value_pre_grad = value_grad.astype(jnp.bfloat16)
        normed_one_grad = jnp.einsum(
            "tc,dc->td", query_pre_grad, query_full, preferred_element_type=jnp.float32
        )
        normed_one_grad = normed_one_grad + jnp.einsum(
            "tc,dc->td", key_pre_grad, key_full, preferred_element_type=jnp.float32
        )
        normed_one_grad = normed_one_grad + jnp.einsum(
            "tc,dc->td", value_pre_grad, value_full, preferred_element_type=jnp.float32
        )
        grad_query = jnp.einsum(
            "td,tc->dc", first_normed, query_pre_grad, preferred_element_type=jnp.float32
        )
        grad_key = jnp.einsum(
            "td,tc->dc", first_normed, key_pre_grad, preferred_element_type=jnp.float32
        )
        grad_value = jnp.einsum(
            "td,tc->dc", first_normed, value_pre_grad, preferred_element_type=jnp.float32
        )
        normed_one_grad = lax.psum(normed_one_grad.astype(jnp.bfloat16), "tp").astype(jnp.float32)
        unit_one = inputs * scale_one
        grad_gain_one = jnp.sum(normed_one_grad * unit_one, axis=0)
        scaled_one = normed_one_grad * gain_one
        input_grads.append(
            mixed_grad
            + scale_one
            * (scaled_one - unit_one * jnp.mean(scaled_one * unit_one, axis=-1, keepdims=True))
        )
        piece = (
            grad_gain_one,
            grad_query,
            grad_key,
            grad_value,
            grad_out_proj,
            grad_gain_two,
            grad_router,
            grad_gate_up,
            grad_down,
        )
        totals = piece if batch_index == 0 else add_tuples(totals, piece)
    summed = (
        lax.psum_scatter(totals[0], ("fsdp", "ctx"), scatter_dimension=0, tiled=True),
        lax.psum_scatter(totals[1], ("fsdp", "ctx"), scatter_dimension=0, tiled=True),
        lax.psum_scatter(totals[2], ("fsdp", "ctx"), scatter_dimension=0, tiled=True),
        lax.psum_scatter(totals[3], ("fsdp", "ctx"), scatter_dimension=0, tiled=True),
        lax.psum_scatter(totals[4], ("fsdp", "ctx"), scatter_dimension=1, tiled=True),
        lax.psum_scatter(totals[5], ("fsdp", "ctx"), scatter_dimension=0, tiled=True),
        lax.psum_scatter(totals[6], ("fsdp", "ctx"), scatter_dimension=0, tiled=True),
        lax.psum_scatter(totals[7], ("fsdp", "ctx"), scatter_dimension=1, tiled=True),
        lax.psum_scatter(totals[8], ("fsdp", "ctx"), scatter_dimension=2, tiled=True),
    )
    shares = (
        lax.all_gather(summed[0].astype(jnp.bfloat16), "ctx", axis=0, tiled=True).astype(
            jnp.float32
        ),
        lax.all_gather(summed[1].astype(jnp.bfloat16), "ctx", axis=0, tiled=True).astype(
            jnp.float32
        ),
        lax.all_gather(summed[2].astype(jnp.bfloat16), "ctx", axis=0, tiled=True).astype(
            jnp.float32
        ),
        lax.all_gather(summed[3].astype(jnp.bfloat16), "ctx", axis=0, tiled=True).astype(
            jnp.float32
        ),
        lax.all_gather(summed[4].astype(jnp.bfloat16), "ctx", axis=1, tiled=True).astype(
            jnp.float32
        ),
        lax.all_gather(summed[5].astype(jnp.bfloat16), "ctx", axis=0, tiled=True).astype(
            jnp.float32
        ),
        lax.all_gather(summed[6].astype(jnp.bfloat16), "ctx", axis=0, tiled=True).astype(
            jnp.float32
        ),
        lax.all_gather(summed[7].astype(jnp.bfloat16), "ctx", axis=1, tiled=True).astype(
            jnp.float32
        ),
        lax.all_gather(summed[8].astype(jnp.bfloat16), "ctx", axis=2, tiled=True).astype(
            jnp.float32
        ),
    )
    layer_out = jnp.stack(outputs, axis=0)[:, None]
    d_hidden = jnp.stack(input_grads, axis=0)[:, None]
    return (
        layer_out,
        d_hidden,
        shares[0],
        shares[1],
        shares[2],
        shares[3],
        shares[4],
        shares[5],
        shares[6],
        shares[7],
        shares[8],
    )


def dot(left, right, left_dim=1, right_dim=0):
    return lax.dot_general(
        left, right, (((left_dim,), (right_dim,)), ((), ())), preferred_element_type=jnp.float32
    )


def pick(hot, rows):
    return dot(hot, rows).astype(jnp.bfloat16)


def kernel_params(count=0):
    return pltpu.CompilerParams(
        dimension_semantics=("arbitrary",) * count if count else None,
        vmem_limit_bytes=60 * 1024 * 1024,
    )


def single(kernel, name, out_shape, scratch, scalars, *arrays):
    smem = pl.BlockSpec(memory_space=pltpu.SMEM)
    vmem = pl.BlockSpec(memory_space=pltpu.VMEM)
    return pl.pallas_call(
        kernel,
        out_shape=tuple(jax.ShapeDtypeStruct(shape, kind) for shape, kind in out_shape),
        in_specs=[smem] * len(scalars) + [vmem] * len(arrays),
        out_specs=(vmem,) * len(out_shape),
        scratch_shapes=[pltpu.VMEM(shape, kind) for shape, kind in scratch],
        compiler_params=kernel_params(),
        name=name,
    )(*scalars, *arrays)


def tree_path(parents_ref, m, start):
    path = [start]
    for _ in range(3):
        path.append(parents_ref[m, path[-1]])
    return path


def own_then_other(x_pos, array):
    half = array.shape[-1] // 2
    first, second = array[..., :half], array[..., half:]
    return jnp.where(x_pos == 0, first, second), jnp.where(x_pos == 0, second, first)


def row_scale(near, far):
    total = jnp.sum(near * near, axis=1, keepdims=True) + jnp.sum(far * far, axis=1, keepdims=True)
    return lax.rsqrt(total / (2 * near.shape[1]) + EPSILON)


def turn_heads(values):
    half_dim = HEAD_DIM // 2
    lane = lax.broadcasted_iota(jnp.int32, values.shape, 1) % HEAD_DIM
    width = values.shape[1]
    return jnp.where(
        lane < half_dim,
        -pltpu.roll(values, width - half_dim, 1),
        pltpu.roll(values, half_dim, 1),
    )


def split_kernel(base_ref, both_ref, down_ref, out_ref, wide_buf):
    wide_buf[...] = both_ref[0].astype(jnp.float32)
    half = both_ref.shape[1] // 2
    out_ref[0, :half, :] = wide_buf[pl.ds(0, half, stride=2), :].astype(jnp.bfloat16)
    out_ref[0, half : 2 * half, :] = wide_buf[pl.ds(1, half, stride=2), :].astype(jnp.bfloat16)
    if down_ref is not None:
        width = down_ref.shape[1]
        for j in range(half // 128):
            out_ref[0, 2 * half + j * width : 2 * half + (j + 1) * width, :] = down_ref[
                0, :, j * 128 : (j + 1) * 128
            ]


def split_plain_kernel(base_ref, both_ref, out_ref, wide_buf):
    split_kernel(base_ref, both_ref, None, out_ref, wide_buf)


def split_weights(base, count, gate_up, down):
    _, rows, width = gate_up.shape
    packed = rows if down is None else rows + rows // 2
    in_specs = [pl.BlockSpec((1, rows, width), lambda i, base: (base[0] + i, 0, 0))]
    operands = [base, gate_up]
    if down is not None:
        in_specs.append(
            pl.BlockSpec((1, *down.shape[1:]), lambda i, base: (base[0] + i, 0, 0))
        )
        operands.append(down)
    return pl.pallas_call(
        split_plain_kernel if down is None else split_kernel,
        out_shape=jax.ShapeDtypeStruct((count, packed, width), jnp.bfloat16),
        grid_spec=pltpu.PrefetchScalarGridSpec(
            num_scalar_prefetch=1,
            grid=(count,),
            in_specs=in_specs,
            out_specs=pl.BlockSpec((1, packed, width), lambda i, base: (i, 0, 0)),
            scratch_shapes=[pltpu.VMEM((rows, width), jnp.float32)],
        ),
        compiler_params=kernel_params(1),
        name="split_weights",
    )(*operands)


def before_kernel(
    place_ref,
    parents_ref,
    hidden_ref,
    small_ref,
    sent_ref,
    next_ref,
    cosine_ref,
    sine_ref,
    normed_ref,
    query_ref,
    key_value_ref,
    far_ref,
    gains_ref,
    turn_ref,
):
    x_pos, c_pos = place_ref[0], place_ref[1]
    first_core = c_pos % 2 == 0
    half = small_ref.shape[1]
    part = half // 2
    q_cols = query_ref.shape[1]
    kv_cols = key_value_ref.shape[1]
    cols = q_cols + kv_cols
    turned_cols = q_cols + kv_cols // 2
    own_rows = small_ref[: 2 * part, :]
    sent, beside = sent_ref[:part, :], next_ref[:part, :]
    top = jnp.where(first_core, sent, beside)
    low_rows = jnp.where(first_core, beside, sent)
    far_ref[:part, :] = top
    far_ref[part:, :] = low_rows
    own_gain = small_ref[2 * part : 2 * part + 16, :].astype(jnp.float32)
    far_gain = sent_ref[part : part + 16, :].astype(jnp.float32)
    gains_ref[:, :half] = own_gain
    gains_ref[:, half:] = far_gain
    near, far = own_then_other(x_pos, hidden_ref[...].astype(jnp.float32))
    scale = row_scale(near, far)
    near_low = (near * scale * own_gain[:1]).astype(jnp.bfloat16)
    far_low = (far * scale * far_gain[:1]).astype(jnp.bfloat16)
    normed_ref[:, :half] = near_low
    normed_ref[:, half:] = far_low
    made = (
        dot(near_low, own_rows[:, :cols])
        + dot(far_low[:, :part], top[:, :cols])
        + dot(far_low[:, part:], low_rows[:, :cols])
    )
    micro = parents_ref.shape[0]
    rows = hidden_ref.shape[0] // micro
    turns = []
    for m in range(micro):
        path = tree_path(parents_ref, m, c_pos)
        depth = sum((path[i + 1] != path[i]).astype(jnp.int32) for i in range(3))
        span = pl.ds(depth * rows, rows)
        turns.append((cosine_ref[span, :], sine_ref[span, :]))
    cosines = jnp.concatenate([pair[0] for pair in turns], axis=0)
    sines = jnp.concatenate([pair[1] for pair in turns], axis=0)
    turn_ref[0] = cosines
    turn_ref[1] = sines
    count = turned_cols // 128
    values = made[:, :turned_cols]
    rotated = (
        values * jnp.concatenate([cosines] * count, axis=1)
        + turn_heads(values) * jnp.concatenate([sines] * count, axis=1)
    ).astype(jnp.bfloat16)
    query_ref[...] = rotated[:, :q_cols]
    key_value_ref[:, : kv_cols // 2] = rotated[:, q_cols:]
    key_value_ref[:, kv_cols // 2 :] = made[:, turned_cols:].astype(jnp.bfloat16)


def give_pieces(whole_ref, z_pos, piece_refs):
    count = len(piece_refs)
    part = whole_ref.shape[0] // count
    for s in range(count):
        start = pl.multiple_of(((z_pos + s) % count) * part, part)
        piece_refs[s][...] = whole_ref[pl.ds(start, part), :].astype(piece_refs[s].dtype)


def take_pieces(piece_refs, z_pos, whole_ref):
    count = len(piece_refs)
    part = whole_ref.shape[0] // count
    for s in range(count):
        start = pl.multiple_of(((z_pos + s) % count) * part, part)
        whole_ref[pl.ds(start, part), :] = piece_refs[s][...].astype(whole_ref.dtype)


def stack_heads(source, first, group):
    return jnp.concatenate(
        [source[:, (first + h) * HEAD_DIM : (first + h + 1) * HEAD_DIM] for h in range(group)],
        axis=0,
    )


def attend_kernel(
    place_ref,
    parents_ref,
    query_ref,
    kv0,
    kv1,
    kv2,
    kv3,
    out_near_ref,
    out_sent_ref,
    out_next_ref,
    head_ref,
    probs_ref,
    out_far_ref,
    attn_ref,
):
    c_pos = place_ref[1]
    blocks = (kv0, kv1, kv2, kv3)
    micro = parents_ref.shape[0]
    rows = query_ref.shape[0] // micro
    kv_heads = kv0.shape[1] // (2 * HEAD_DIM)
    group = query_ref.shape[1] // HEAD_DIM // kv_heads
    shape = (group * rows, rows)
    causal = (
        lax.broadcasted_iota(jnp.int32, shape, 1)
        <= lax.broadcasted_iota(jnp.int32, shape, 0) % rows
    )
    for m in range(micro):
        span = pl.ds(m * rows, rows)
        whole = query_ref[span, :]
        path = tree_path(parents_ref, m, c_pos)
        pieces = []
        for g in range(kv_heads):
            query = stack_heads(whole, g * group, group)
            parts = []
            for r in range(4):
                keys = blocks[r][span, :][:, g * HEAD_DIM : (g + 1) * HEAD_DIM]
                part = dot(query, keys, 1, 1) * SCORE_SCALE
                if r == 0:
                    part = jnp.where(causal, part, -1e30)
                else:
                    seen = (path[1] == c_pos ^ r) | (path[2] == c_pos ^ r) | (path[3] == c_pos ^ r)
                    part = jnp.where(seen, part, -1e30)
                parts.append(part)
            scores = jnp.concatenate(parts, axis=1)
            powers = jnp.exp(scores - jnp.max(scores, axis=1, keepdims=True))
            probs = powers * (1.0 / jnp.sum(powers, axis=1, keepdims=True))
            probs_ref[m * kv_heads + g] = probs
            low = probs.astype(jnp.bfloat16)
            values = jnp.concatenate(
                [
                    blocks[r][span, :][:, (kv_heads + g) * HEAD_DIM : (kv_heads + g + 1) * HEAD_DIM]
                    for r in range(4)
                ],
                axis=0,
            )
            mixed = dot(low, values)
            pieces += [mixed[h * rows : (h + 1) * rows] for h in range(group)]
        head_ref[span, :] = jnp.concatenate(pieces, axis=1).astype(jnp.bfloat16)
    first_core = c_pos % 2 == 0
    sent, beside = out_sent_ref[...], out_next_ref[...]
    part = sent.shape[0]
    out_far_ref[:part, :] = jnp.where(first_core, sent, beside)
    out_far_ref[part:, :] = jnp.where(first_core, beside, sent)
    half = sent.shape[1]
    attn_ref[:, :half] = dot(head_ref[...], out_near_ref[...]).astype(jnp.bfloat16)
    attn_ref[:, half:] = dot(head_ref[...], out_far_ref[...]).astype(jnp.bfloat16)


def after_kernel(
    place_ref,
    hidden_ref,
    gains_ref,
    small_ref,
    far_ref,
    routes_ref,
    attended_ref,
    mixed_ref,
    rows_ref,
    gates_ref,
):
    half = small_ref.shape[1]
    near, far = own_then_other(place_ref[0], hidden_ref[...].astype(jnp.float32))
    near = near + RESIDUAL_SCALE * attended_ref[:, :half].astype(jnp.float32)
    far = far + RESIDUAL_SCALE * attended_ref[:, half:].astype(jnp.float32)
    mixed_ref[:, :half] = near
    mixed_ref[:, half:] = far
    scale = row_scale(near, far)
    near_low = (near * scale * gains_ref[1:2, :half]).astype(jnp.bfloat16)
    far_low = (far * scale * gains_ref[1:2, half:]).astype(jnp.bfloat16)
    rows_ref[:, :half] = near_low
    rows_ref[:, half : 2 * half] = far_low
    logits = dot(near_low, small_ref[:half, half - 128 :]) + dot(far_low, far_ref[:, half - 128 :])
    lane = lax.broadcasted_iota(jnp.int32, logits.shape, 1)
    named = lane == routes_ref[:, 0:1]
    for k in range(1, routes_ref.shape[1]):
        named = named | (lane == routes_ref[:, k : k + 1])
    logits = jnp.where(named, logits, -1e30)
    powers = jnp.where(named, jnp.exp(logits - jnp.max(logits, axis=1, keepdims=True)), 0.0)
    gates = powers / jnp.sum(powers, axis=1, keepdims=True)
    gates_ref[...] = gates
    high = gates.astype(jnp.bfloat16)
    rest_part = gates - high.astype(jnp.float32)
    rows_ref[:, 2 * half :] = jnp.where(
        lane < 64, high.astype(jnp.float32), pltpu.roll(rest_part, 64, 1)
    ).astype(jnp.bfloat16)


def expert_kernel(
    place_ref,
    near_ref,
    far_ref,
    near_out_ref,
    far_out_ref,
    rank_ref,
    gate_up_ref,
    down_ref,
    *rest,
    first,
    last,
    each,
    split,
):
    count = 4 if split else 1
    other_refs, rest = rest[:count], rest[count:]
    held = rest[:4] if last else ()
    slots_ref, *sums = rest[len(held) : -8]
    rows_buf, grads_buf, moe_buf, back_buf, hot_buf, gate_buf, out_ref, grad_ref = rest[-8:]
    half = down_ref.shape[-1]
    full = 2 * half
    width = down_ref.shape[-2]
    step = pl.program_id(0)
    quarter = [place_ref[1] ^ r for r in range(4)]
    expert = [(place_ref[0] * 4 + quarter[r]) * each + first + step for r in range(4)]
    iota = lax.broadcasted_iota(jnp.int32, (CAP, 128), 0)
    lane = lax.broadcasted_iota(jnp.int32, (CAP, 128), 1)

    @pl.when(step == 0)
    def _():
        if last:
            out_ref[...] = held[0][...].astype(jnp.float32) + held[2][...].astype(jnp.float32)
            grad_ref[...] = held[1][...].astype(jnp.float32) + held[3][...].astype(jnp.float32)
        else:
            out_ref[...] = jnp.zeros_like(out_ref)
            grad_ref[...] = jnp.zeros_like(grad_ref)

    marks = [((lane == expert[r]) | (lane == expert[r] + 64)) for r in range(4)]
    mark = jnp.concatenate(marks, axis=0)
    for b in range(4):
        low = jnp.concatenate(
            [
                jnp.where(iota == rank_ref[quarter[r], 0, pl.ds(b, 1), :], 1.0, 0.0)
                for r in range(4)
            ],
            axis=0,
        ).astype(jnp.bfloat16)
        hot_buf[b] = low
        span = pl.ds((b % 2) * 128, 128)
        source = near_ref if b < 2 else far_ref
        picked = jnp.where(mark, dot(low, source[span, pl.ds(full, 128)]), 0.0)
        gate_buf[b] = jnp.broadcast_to(jnp.sum(picked, axis=1, keepdims=True), (4 * CAP, 128))
        for part in range(2):
            keep = pl.ds(part * half, half)
            if b < 2:
                rows, grads = near_ref[span, keep], near_out_ref[span, keep]
            else:
                swap = pl.ds((1 - part) * half, half)
                rows, grads = far_ref[span, swap], far_out_ref[span, swap]
            rows_buf[b, :, keep] = pick(low, rows)
            grads_buf[b, :, keep] = pick(low, grads)
    for r in range(4):
        q = quarter[r]
        slot = slice(r * CAP, (r + 1) * CAP)
        rows = jnp.concatenate([rows_buf[b, slot, :] for b in range(4)], axis=0)
        grads = jnp.concatenate([grads_buf[b, slot, :] for b in range(4)], axis=0)
        gate = jnp.concatenate([gate_buf[b, slot, :] for b in range(4)], axis=0)
        near_w = jnp.concatenate(
            [gate_up_ref[q, 0, :half, :], gate_up_ref[q, 0, half:, :]], axis=1
        )
        def other(start, size):
            if split:
                return other_refs[r][0, start : start + size, :]
            return other_refs[0][q, 0, start : start + size, :]

        far_w = jnp.concatenate([other(0, half), other(half, half)], axis=1)
        near_down = down_ref[0, q, 0]
        far_down = jnp.concatenate(
            [other(2 * half + j * width, width) for j in range(half // 128)],
            axis=1,
        )
        gate_up = dot(rows[:, :half], near_w) + dot(rows[:, half:], far_w)
        gate_pre = gate_up[:, :width]
        up_pre = gate_up[:, width:]
        sigmoid = 1.0 / (1.0 + jnp.exp(-gate_pre))
        activ = (gate_pre * sigmoid * up_pre).astype(jnp.bfloat16)
        pulled = RESIDUAL_SCALE * (
            dot(grads[:, :half], near_down, 1, 1) + dot(grads[:, half:], far_down, 1, 1)
        )
        activ_wide = activ.astype(jnp.float32)
        gate_grad = jnp.sum(activ_wide * pulled, axis=1, keepdims=True)
        activ_grad = pulled * gate
        gate_pre_grad = activ_grad * up_pre * sigmoid * (1.0 + gate_pre * (1.0 - sigmoid))
        up_pre_grad = activ_grad * gate_pre * sigmoid
        both = jnp.concatenate([gate_pre_grad, up_pre_grad], axis=1).astype(jnp.bfloat16)
        slots_ref[q, 0, :, : 2 * width] = both
        slots_ref[q, 0, :, 2 * width :] = (activ_wide * gate * RESIDUAL_SCALE).astype(jnp.bfloat16)
        for part, (wide, low_w) in enumerate(((near_w, near_down), (far_w, far_down))):
            keep = pl.ds(part * half, half)
            made = dot(activ, low_w)
            back = dot(both, wide, 1, 1)
            for b in range(4):
                piece = slice(b * CAP, (b + 1) * CAP)
                scale = jnp.concatenate([gate[piece]] * (half // 128), axis=1)
                moe_buf[b, slot, keep] = (made[piece] * scale).astype(jnp.bfloat16)
                back_buf[b, slot, keep] = back[piece].astype(jnp.bfloat16)
        spot = lane == expert[r]
        for b in range(4):
            back_buf[b, slot, pl.ds(full, 128)] = jnp.where(
                spot, gate_grad[b * CAP : (b + 1) * CAP], 0.0
            ).astype(jnp.bfloat16)
    for b in range(4):
        span = pl.ds(b * 128, 128)
        out_ref[span, :] += dot(hot_buf[b], moe_buf[b], 0, 0)
        grad_ref[span, :] += dot(hot_buf[b], back_buf[b], 0, 0)

    @pl.when(step == pl.num_programs(0) - 1)
    def _():
        if not last:
            sums[0][...] = out_ref[...].astype(jnp.bfloat16)
            sums[1][...] = grad_ref[...].astype(jnp.bfloat16)
            return
        moe_ref, back_ref, moe_far_ref, back_far_ref = sums
        count = moe_ref.shape[0]
        span = pl.ds(count, count)
        moe_ref[...] = out_ref[:count, :]
        back_ref[...] = grad_ref[:count, :]
        for part in range(2):
            keep, swap = pl.ds(part * half, half), pl.ds((1 - part) * half, half)
            moe_far_ref[:, keep] = out_ref[span, swap].astype(jnp.bfloat16)
            back_far_ref[:, keep] = grad_ref[span, swap].astype(jnp.bfloat16)
        back_far_ref[:, pl.ds(full, 128)] = grad_ref[span, pl.ds(full, 128)].astype(jnp.bfloat16)


def run_experts(place, near, far, near_out, far_out, rank, gate_up, down, other, held, first, each):
    split = isinstance(other, list)
    others = other if split else [other]
    steps, packed, lanes = others[0].shape[-3:]
    quarters, _, rows, width = gate_up.shape
    half = rows // 2
    full = 2 * half
    tokens = 2 * near.shape[0]
    last = first + steps == each

    def fixed(shape):
        return pl.BlockSpec(shape, lambda j, sp: (0,) * len(shape))

    in_specs = [
        fixed(near.shape),
        fixed(far.shape),
        fixed((tokens // 2, full)),
        fixed((tokens // 2, full)),
        pl.BlockSpec((quarters, 1, 4, 128), lambda j, sp: (0, first + j, 0, 0)),
        pl.BlockSpec((quarters, 1, rows, width), lambda j, sp: (0, first + j, 0, 0)),
        pl.BlockSpec((1, quarters, 1, width, half), lambda j, sp: (sp[0], 0, first + j, 0, 0)),
    ]
    if split:
        in_specs += [pl.BlockSpec((1, packed, lanes), lambda j, sp: (j, 0, 0))] * 4
    else:
        in_specs.append(pl.BlockSpec((quarters, 1, packed, lanes), lambda j, sp: (0, j, 0, 0)))
    operands = [place, near, far, near_out, far_out, rank, gate_up, down, *others]
    if last:
        in_specs += [fixed(array.shape) for array in held]
        operands += list(held)
    out_shape = [jax.ShapeDtypeStruct((quarters, steps, 4 * CAP, 3 * width), jnp.bfloat16)]
    out_specs = [pl.BlockSpec((quarters, 1, 4 * CAP, 3 * width), lambda j, sp: (0, j, 0, 0))]
    count = tokens // 2 if last else tokens
    kinds = (jnp.float32, jnp.bfloat16) if last else (jnp.bfloat16,)
    for kind in kinds:
        for lanes_out in (full, full + 128):
            out_shape.append(jax.ShapeDtypeStruct((count, lanes_out), kind))
            out_specs.append(fixed((count, lanes_out)))
    return pl.pallas_call(
        functools.partial(expert_kernel, first=first, last=last, each=each, split=split),
        out_shape=tuple(out_shape),
        grid_spec=pltpu.PrefetchScalarGridSpec(
            num_scalar_prefetch=1,
            grid=(steps,),
            in_specs=in_specs,
            out_specs=tuple(out_specs),
            scratch_shapes=[pltpu.VMEM((4, 4 * CAP, full), jnp.bfloat16)] * 3
            + [
                pltpu.VMEM((4, 4 * CAP, full + 128), jnp.bfloat16),
                pltpu.VMEM((4, 4 * CAP, 128), jnp.bfloat16),
                pltpu.VMEM((4, 4 * CAP, 128), jnp.float32),
                pltpu.VMEM((tokens, full), jnp.float32),
                pltpu.VMEM((tokens, full + 128), jnp.float32),
            ],
        ),
        compiler_params=kernel_params(1),
        name="experts",
    )(*operands)


def join_kernel(place_ref, total_ref, got_ref, *rest):
    piece_refs, whole_buf = rest[:-1], rest[-1]
    count = got_ref.shape[0]
    whole_buf[...] = total_ref[:count, :] + got_ref[...].astype(jnp.float32)
    give_pieces(whole_buf, place_ref[2], piece_refs)


def back_kernel(
    place_ref,
    mixed_ref,
    gates_ref,
    gains_ref,
    small_ref,
    far_ref,
    out_grad_ref,
    out_near_ref,
    out_far_ref,
    query_ref,
    turn_ref,
    kv0,
    kv1,
    kv2,
    kv3,
    probs_ref,
    *rest,
):
    (
        mixed_grad_ref,
        attn_grad_ref,
        logit_grad_ref,
        gain_grad_ref,
        query_grad_ref,
        kept_ref,
        given_ref,
        whole_buf,
        head_buf,
    ) = rest[-9:]
    take_pieces(rest[:-9], place_ref[2], whole_buf)
    half = small_ref.shape[1]
    full = 2 * half
    gates = gates_ref[...]
    gate_grads = whole_buf[:, full:]
    inner = jnp.sum(gates * gate_grads, axis=1, keepdims=True)
    logit_grad = (gates * (gate_grads - inner)).astype(jnp.bfloat16)
    logit_grad_ref[...] = logit_grad
    near, far = mixed_ref[:, :half], mixed_ref[:, half:]
    scale = row_scale(near, far)
    near_unit, far_unit = near * scale, far * scale
    near_grad = whole_buf[:, :half] + dot(logit_grad, small_ref[:half, half - 128 :], 1, 1)
    far_grad = whole_buf[:, half:full] + dot(logit_grad, far_ref[:, half - 128 :], 1, 1)
    gain_grad_ref[:, :half] = jnp.broadcast_to(
        jnp.sum(near_grad * near_unit, axis=0, keepdims=True), (8, half)
    )
    gain_grad_ref[:, half:] = jnp.broadcast_to(
        jnp.sum(far_grad * far_unit, axis=0, keepdims=True), (8, half)
    )
    near_scaled = near_grad * gains_ref[1:2, :half]
    far_scaled = far_grad * gains_ref[1:2, half:]
    mean = (
        jnp.sum(near_scaled * near_unit, axis=1, keepdims=True)
        + jnp.sum(far_scaled * far_unit, axis=1, keepdims=True)
    ) / full
    near_mixed = out_grad_ref[:, :half].astype(jnp.float32) + scale * (
        near_scaled - near_unit * mean
    )
    far_mixed = out_grad_ref[:, half:full].astype(jnp.float32) + scale * (
        far_scaled - far_unit * mean
    )
    mixed_grad_ref[:, :half] = near_mixed
    mixed_grad_ref[:, half:] = far_mixed
    near_attn = (RESIDUAL_SCALE * near_mixed).astype(jnp.bfloat16)
    far_attn = (RESIDUAL_SCALE * far_mixed).astype(jnp.bfloat16)
    attn_grad_ref[:, :half] = near_attn
    attn_grad_ref[:, half:] = far_attn
    head_buf[...] = (
        dot(near_attn, out_near_ref[...], 1, 1) + dot(far_attn, out_far_ref[...], 1, 1)
    ).astype(jnp.bfloat16)
    blocks = (kv0, kv1, kv2, kv3)
    kv_heads = kv0.shape[1] // (2 * HEAD_DIM)
    micro = probs_ref.shape[0] // kv_heads
    rows = query_ref.shape[0] // micro
    group = query_ref.shape[1] // HEAD_DIM // kv_heads
    count = query_ref.shape[1] // 128
    for m in range(micro):
        span = pl.ds(m * rows, rows)
        whole = query_ref[span, :]
        whole_grad = head_buf[span, :]
        pieces = []
        key_grads = []
        value_grads = []
        for g in range(kv_heads):
            query = stack_heads(whole, g * group, group)
            head_grad = stack_heads(whole_grad, g * group, group)
            keys = jnp.concatenate(
                [blocks[r][span, :][:, g * HEAD_DIM : (g + 1) * HEAD_DIM] for r in range(4)], axis=0
            )
            values = jnp.concatenate(
                [
                    blocks[r][span, :][:, (kv_heads + g) * HEAD_DIM : (kv_heads + g + 1) * HEAD_DIM]
                    for r in range(4)
                ],
                axis=0,
            )
            probs = probs_ref[m * kv_heads + g]
            prob_grad = dot(head_grad, values, 1, 1)
            inner = jnp.sum(probs * prob_grad, axis=1, keepdims=True)
            score_grad = (SCORE_SCALE * probs * (prob_grad - inner)).astype(jnp.bfloat16)
            value_grads.append(dot(probs.astype(jnp.bfloat16), head_grad, 0, 0))
            key_grads.append(dot(score_grad, query, 0, 0))
            query_grad = dot(score_grad, keys)
            pieces += [query_grad[h * rows : (h + 1) * rows] for h in range(group)]
        query_grad = jnp.concatenate(pieces, axis=1)
        query_grad_ref[span, :] = (
            query_grad * jnp.concatenate([turn_ref[0, span, :]] * count, axis=1)
            - turn_heads(query_grad) * jnp.concatenate([turn_ref[1, span, :]] * count, axis=1)
        ).astype(jnp.bfloat16)
        joined = jnp.concatenate(key_grads + value_grads, axis=1)
        kept_ref[0, span, :] = joined[:rows]
        kept_ref[1, span, :] = joined[2 * rows : 3 * rows]
        given_ref[0, span, :] = joined[rows : 2 * rows].astype(jnp.bfloat16)
        given_ref[1, span, :] = joined[3 * rows :].astype(jnp.bfloat16)


def last_kernel(
    place_ref,
    query_grad_ref,
    kept_ref,
    near_ref,
    along_ref,
    turn_ref,
    small_ref,
    far_ref,
    grads_ref,
    *rest,
):
    piece_refs, whole_buf = rest[:-1], rest[-1]
    q_cols = query_grad_ref.shape[1]
    k_cols = turn_ref.shape[2]
    cols = q_cols + 2 * k_cols
    half = small_ref.shape[1]
    total = (
        kept_ref[0] + near_ref[0].astype(jnp.float32) + along_ref[...].astype(jnp.float32)
    )
    keys = total[:, :k_cols]
    grads_ref[:, :q_cols] = query_grad_ref[...]
    grads_ref[:, q_cols : q_cols + k_cols] = (
        keys * turn_ref[0] - turn_heads(keys) * turn_ref[1]
    ).astype(jnp.bfloat16)
    grads_ref[:, q_cols + k_cols :] = total[:, k_cols:].astype(jnp.bfloat16)
    grads = grads_ref[...]
    near_part = dot(grads, small_ref[:half, :cols], 1, 1)
    far_part = dot(grads, far_ref[:, :cols], 1, 1)
    whole_buf[:, :half] = near_part
    whole_buf[:, half:] = far_part
    give_pieces(whole_buf, place_ref[2], piece_refs)


def output_kernel(place_ref, mixed_ref, *rest):
    out_ref, whole_buf = rest[-2:]
    take_pieces(rest[:-2], place_ref[2] // 2, whole_buf)
    half = out_ref.shape[1] // 2
    total = mixed_ref[...] + RESIDUAL_SCALE * whole_buf[...]
    first, second = own_then_other(place_ref[0], total)
    out_ref[:, :half] = first
    out_ref[:, half:] = second


def hidden_kernel(place_ref, hidden_ref, gains_ref, mixed_grad_ref, mark_ref, *rest):
    out_ref, gain_ref, whole_buf = rest[-3:]
    take_pieces(rest[:-3], place_ref[2], whole_buf)
    half = out_ref.shape[1] // 2
    near, far = own_then_other(place_ref[0], hidden_ref[...].astype(jnp.float32))
    scale = row_scale(near, far)
    near, far = near * scale, far * scale
    gain_ref[:, :half] = jnp.broadcast_to(
        jnp.sum(whole_buf[:, :half] * near, axis=0, keepdims=True), (8, half)
    )
    gain_ref[:, half:] = jnp.broadcast_to(
        jnp.sum(whole_buf[:, half:] * far, axis=0, keepdims=True), (8, half)
    )
    near_scaled = whole_buf[:, :half] * gains_ref[0:1, :half]
    far_scaled = whole_buf[:, half:] * gains_ref[0:1, half:]
    mean = (
        jnp.sum(near_scaled * near, axis=1, keepdims=True)
        + jnp.sum(far_scaled * far, axis=1, keepdims=True)
    ) / (2 * half)
    near_out = mixed_grad_ref[:, :half] + scale * (near_scaled - near * mean)
    far_out = mixed_grad_ref[:, half:] + scale * (far_scaled - far * mean)
    out_ref[:, :half] = jnp.where(place_ref[0] == 0, near_out, far_out)
    out_ref[:, half:] = jnp.where(place_ref[0] == 0, far_out, near_out)


def weight_grad_kernel(
    place_ref, rows_ref, grads0, grads1, grads2, grads3, slots_ref, rank_ref, *refs, first, steps
):
    gate_up_ref, down_ref, mark_ref, rows_buf, grads_buf = refs[-5:]
    half = down_ref.shape[-1]
    width = down_ref.shape[-2]
    iota = lax.broadcasted_iota(jnp.int32, (CAP, 128), 0)
    grads_in = (grads0, grads1, grads2, grads3)
    ctx = [place_ref[1] ^ r for r in range(4)]
    step, side = pl.program_id(0), pl.program_id(1)
    mark_ref[...] = jnp.zeros_like(mark_ref)

    @pl.when((step == 0) & (side == 0))
    def _():
        @pl.loop(0, 4)
        def _(b):
            span = pl.ds(pl.multiple_of(b * 128, 128), 128)
            for k in range(4):
                hot = jnp.concatenate(
                    [
                        jnp.where(
                            iota == rank_ref[a, q, first + j, pl.ds(4 * k + b, 1), :], 1.0, 0.0
                        )
                        for a in range(2)
                        for j in range(steps)
                        for q in range(4)
                    ],
                    axis=0,
                ).astype(jnp.bfloat16)
                rows = pick(hot, rows_ref[ctx[k], span, :])
                grads = pick(hot, grads_in[k][span, :])
                for a in range(2):
                    spot = 4 * k + (b ^ (2 * a))
                    for j in range(steps):
                        start = (a * steps + j) * 4 * CAP
                        piece = slice(start, start + 4 * CAP)
                        rows_buf[j * 2 + a, spot] = rows[piece]
                        grads_buf[j * 2 + a, spot] = grads[piece]

    place = step * 2 + side
    for q in range(4):
        slot = slice(q * CAP, (q + 1) * CAP)
        rows = jnp.concatenate([rows_buf[place, n, slot, :] for n in range(16)], axis=0)
        grads = jnp.concatenate([grads_buf[place, n, slot, :] for n in range(16)], axis=0)
        taken = jnp.concatenate([slots_ref[0, ctx[k], q, 0] for k in range(4)], axis=0)
        made = dot(rows, taken[:, : 2 * width], 0, 0)
        gate_up_ref[0, q, 0, pl.ds(0, half, stride=2), :] = made[:, :width]
        gate_up_ref[0, q, 0, pl.ds(1, half, stride=2), :] = made[:, width:]
        down_ref[0, q, 0] = dot(taken[:, 2 * width :], grads, 0, 0)


def run_weight_grads(place, plane, early, slots, rank, held, each, first, mark):
    sides, _, quarters, steps, slot_count, lanes = slots.shape
    width = lanes // 3
    half = plane.shape[-1]
    tokens = plane.shape[1]

    def place_of(j, a, sp):
        return (sp[0] ^ a, 0, first + j, 0, 0)

    in_specs = [
        pl.BlockSpec((4, tokens, half), lambda j, a, sp: (0, 0, 0)),
        *[pl.BlockSpec((tokens, half), lambda j, a, sp: (0, 0))] * 4,
        pl.BlockSpec(
            (1, 4, quarters, 1, slot_count, lanes),
            lambda j, a, sp: (sp[0] ^ a, 0, 0, j, 0, 0),
        ),
        pl.BlockSpec(rank.shape, lambda j, a, sp: (0, 0, 0, 0, 0)),
        pl.BlockSpec(memory_space=pl.ANY),
    ]
    operands = [place, plane, *early, slots, rank, mark]
    aliases = {}
    if held is not None:
        in_specs += [pl.BlockSpec(memory_space=pl.ANY)] * 2
        aliases = {len(operands): 0, len(operands) + 1: 1}
        operands += list(held[:2])
    return pl.pallas_call(
        functools.partial(weight_grad_kernel, first=first, steps=steps),
        out_shape=(
            jax.ShapeDtypeStruct((sides, quarters, each, 2 * half, width), jnp.float32),
            jax.ShapeDtypeStruct((sides, quarters, each, width, half), jnp.float32),
            jax.ShapeDtypeStruct((8, 128), jnp.float32),
        ),
        grid_spec=pltpu.PrefetchScalarGridSpec(
            num_scalar_prefetch=1,
            grid=(steps, sides),
            in_specs=in_specs,
            out_specs=(
                pl.BlockSpec((1, quarters, 1, 2 * half, width), place_of),
                pl.BlockSpec((1, quarters, 1, width, half), place_of),
                pl.BlockSpec((8, 128), lambda j, a, sp: (0, 0)),
            ),
            scratch_shapes=[pltpu.VMEM((2 * steps, 16, 4 * CAP, half), jnp.bfloat16)] * 2,
        ),
        input_output_aliases=aliases,
        compiler_params=kernel_params(2),
        name="weight_grads",
    )(*operands)


def swap_halves(values):
    half = values.shape[-1] // 2
    return jnp.concatenate([values[..., half:], values[..., :half]], axis=-1)


def fast_body(
    hidden_in,
    parents,
    routes,
    attn_gain,
    w_query,
    key_projection,
    value_projection,
    w_out,
    moe_gain,
    w_router,
    w_gate_up,
    w_down,
    d_out,
):
    low, wide = jnp.bfloat16, jnp.float32
    x_pos = lax.axis_index("fsdp")
    c_pos = lax.axis_index("ctx")
    z_pos = lax.axis_index("tp")
    tp_size = lax.axis_size("tp")
    place = jnp.stack([x_pos, c_pos, z_pos]).astype(jnp.int32)
    micro, _, rows, model = hidden_in.shape
    half = model // 2
    tokens = micro * rows
    experts = w_gate_up.shape[0]
    mine = experts // 2
    each = mine // 4
    width = w_down.shape[1]
    q_cols = w_query.shape[1]
    k_cols = key_projection.shape[1]
    qkv_cols = q_cols + 2 * k_cols
    kv_heads = k_cols // HEAD_DIM
    group = q_cols // k_cols
    top = routes.shape[-1]
    chunks = ((0, 2), (2, 2), (4, 1))
    tie = lax.optimization_barrier

    def across(value):
        return lax.ppermute(value, "fsdp", [(0, 1), (1, 0)])

    def beside(value):
        return lax.ppermute(value, "ctx", [(i, i ^ 1) for i in range(4)])

    def along(value):
        return lax.ppermute(value, "ctx", [(i, i ^ 2) for i in range(4)])

    def from_tp(value, step):
        return lax.ppermute(value, "tp", [((i + step) % tp_size, i) for i in range(tp_size)])

    def all_ctx(value):
        nearby = beside(value)
        distant = along(value)
        return [value, nearby, distant, beside(distant)]

    def own_first(value):
        return jnp.where(x_pos == 0, value, swap_halves(value))

    def reduce_pieces(pieces):
        total = pieces[0].astype(wide)
        for step in range(1, tp_size):
            total = total + from_tp(pieces[tp_size - step], step).astype(wide)
        return total.astype(low)

    def spread_pieces(total):
        return [total] + [from_tp(total, step) for step in range(1, tp_size)]

    piece_shapes = [((tokens // tp_size, model), low)] * tp_size
    hidden = hidden_in.reshape(tokens, model)
    flat_routes = routes.reshape(tokens, top)

    core = c_pos % 2
    part = half // 2
    weights = jnp.concatenate(
        [
            w_query,
            key_projection,
            value_projection,
            jnp.pad(w_router, ((0, 0), (0, half - qkv_cols - experts))),
        ],
        axis=1,
    )
    gain_rows = jnp.pad(jnp.stack([attn_gain, moe_gain]), ((0, 14), (0, 0)))
    small = jnp.concatenate([weights, gain_rows], axis=0)
    sent = across(
        jnp.concatenate([lax.dynamic_slice_in_dim(weights, core * part, part, 0), gain_rows], axis=0)
    )

    both_view = w_gate_up.reshape(experts, 2 * half, width)
    base = (x_pos * mine).astype(jnp.int32)[None]
    away = ((1 - x_pos) * mine + c_pos * each).astype(jnp.int32)[None]
    packs = [split_weights(away + first, count, both_view, w_down) for first, count in chunks]
    down_all = w_down.reshape(2, 4, each, width, half)
    routes_low = jnp.pad(flat_routes.astype(low), ((0, 0), (0, 128 - top)))
    near_out = jnp.concatenate([own_first(d_out.reshape(tokens, model)), routes_low], axis=1)

    half_dim = HEAD_DIM // 2
    inverse = ROPE_BASE ** (-jnp.arange(half_dim, dtype=wide) * 2.0 / HEAD_DIM)
    angles = jnp.arange(4 * rows, dtype=wide)[:, None] * inverse[None, :]
    cosines = jnp.tile(jnp.cos(angles), (1, 4))
    sines = jnp.tile(jnp.sin(angles), (1, 4))
    sent, packs[0], out_start, small, cosines, sines, place = tie(
        (sent, packs[0], core * (q_cols // 2), small, cosines, sines, place)
    )
    out_sent = across(lax.dynamic_slice_in_dim(w_out, out_start, q_cols // 2, 0))

    normed_one, query, key_value, small_far, gains, turns = single(
        before_kernel,
        "before",
        [
            ((tokens, model), low),
            ((tokens, q_cols), low),
            ((tokens, 2 * k_cols), low),
            ((half, half), low),
            ((16, model), wide),
            ((2, tokens, 128), wide),
        ],
        [],
        [place, parents.reshape(micro, 4)],
        hidden,
        small,
        sent,
        beside(sent),
        cosines,
        sines,
    )
    key_value, packs[0], near_out, out_sent = tie((key_value, packs[0], near_out, out_sent))
    blocks = all_ctx(key_value)
    far_out = across(near_out)
    far_zero = across(packs[0])
    head_low, probs, out_far, attn_part = single(
        attend_kernel,
        "attend",
        [
            ((tokens, q_cols), low),
            ((micro * kv_heads, group * rows, 4 * rows), wide),
            ((q_cols, half), low),
            ((tokens, model), low),
        ],
        [],
        [place, parents.reshape(micro, 4)],
        query,
        *blocks,
        w_out,
        out_sent,
        beside(out_sent),
    )
    attn_part, base = tie((attn_part, base))
    gate_up_mine = split_weights(base, mine, both_view, None).reshape(4, each, 2 * half, width)
    attended = lax.psum(attn_part, "tp")
    far_zero, packs[1] = tie((far_zero, packs[1]))
    far_one = across(packs[1])
    attended, far_out, gate_up_mine, packs[2] = tie(
        (attended, far_out, gate_up_mine, packs[2])
    )
    zero_along = along(far_zero)
    early = jnp.concatenate(
        [
            jnp.concatenate([near_out[:, :half], routes_low], axis=1),
            far_out[:, half:],
        ],
        axis=0,
    )
    early_along = along(early)
    early_near = beside(early)
    mixed, near, gates = single(
        after_kernel,
        "after",
        [((tokens, model), wide), ((tokens, model + 128), low), ((tokens, 128), wide)],
        [],
        [place],
        hidden,
        gains,
        small,
        small_far,
        flat_routes,
        attended,
    )
    upper = (
        lax.broadcasted_iota(jnp.int32, (rows, rows), 0)
        < lax.broadcasted_iota(jnp.int32, (rows, rows), 1)
    ).astype(low)

    def ranks(route_table, ids):
        flat = route_table.astype(jnp.int32).T
        hit = jnp.zeros((ids.shape[0], flat.shape[1]), jnp.bool_)
        for k in range(top):
            hit = hit | (flat[k][None, :] == ids[:, None])
        hot = hit.astype(low).reshape(-1, rows)
        found = jnp.where(hot > 0, dot(hot, upper), -1.0).astype(jnp.int32)
        return found.reshape(ids.shape[0], -1, rows)

    expert_ids = (jnp.arange(experts, dtype=jnp.int32) + x_pos * mine) % experts
    pair_routes = jnp.concatenate([routes_low, far_out[:, model:]], axis=0)[:, :top]
    rank_pair = ranks(pair_routes, expert_ids[:mine]).reshape(4, each, 4, rows)

    near, packs[2] = tie((near, packs[2]))
    far = across(near)
    one_along = along(far_one)
    far, packs[2], zero_along, gate_up_mine, early_along, early_near, rank_pair = tie(
        (far, packs[2], zero_along, gate_up_mine, early_along, early_near, rank_pair)
    )
    early = [early, early_near, early_along, beside(early_along)]
    far_two = across(packs[2])
    plane_in = jnp.concatenate([near[:, :half], far[:, half:model]], axis=0)
    def all_four(got, distant):
        return [got, beside(got), distant, beside(distant)]

    def gather_slots(part):
        return lax.all_gather(part, ("fsdp", "ctx")).reshape(2, 4, *part.shape)

    held = []
    slots = []
    for number, (first, count) in enumerate(chunks):
        if number == 0:
            other = all_four(far_zero, zero_along)
        if number == 1:
            slots[0], far_two, one_along, plane_in = tie(
                (slots[0], far_two, one_along, plane_in)
            )
            two_along = along(far_two)
            plane = lax.all_gather(plane_in, "ctx")
            other = all_four(far_one, one_along)
        if number == 2:
            slots[1], two_along = tie((slots[1], two_along))
            other = all_four(far_two, two_along)
        made = run_experts(
            place,
            near,
            far,
            near_out,
            far_out,
            rank_pair,
            gate_up_mine,
            down_all,
            other,
            held,
            first,
            each,
        )
        slots.append(made[0])
        held += made[1:]
    moe_all, back_all, moe_far, back_far = made[1:]

    all_routes = jnp.concatenate([part[:, half : half + top] for part in early], axis=0)
    rank_all = ranks(all_routes, expert_ids).reshape(2, 4, each, 16, rows)

    back_far, plane, slots[0] = tie((back_far, plane, slots[0]))
    back_got = across(back_far)
    pair_zero = gather_slots(slots[0])
    back_got, moe_far, rank_all = tie((back_got, moe_far, rank_all))

    def grads_of(number, pair, held, mark):
        first, count = chunks[number]
        return run_weight_grads(
            place,
            plane,
            early,
            pair,
            rank_all,
            held,
            each,
            first,
            mark,
        )

    pieces = single(
        join_kernel,
        "join",
        [((tokens // tp_size, model + 128), low)] * tp_size,
        [((tokens, model + 128), wide)],
        [place],
        back_all,
        back_got,
    )
    total = reduce_pieces(pieces)
    total, moe_far, pair_zero, slots[1] = tie((total, moe_far, pair_zero, slots[1]))
    moe_got = across(moe_far)
    pair_one = gather_slots(slots[1])
    found = spread_pieces(total)
    grads = grads_of(0, pair_zero, None, jnp.zeros((8, 128), wide))
    *found, moe_got, mark = tie((*found, moe_got, grads[2]))
    moe_pieces = single(
        join_kernel, "join", piece_shapes, [((tokens, model), wide)], [place], moe_all, moe_got
    )
    moe_total = reduce_pieces(moe_pieces)
    (
        mixed_grad,
        attn_grad,
        logit_grad,
        gain_two_part,
        query_grad,
        kept,
        given,
    ) = single(
        back_kernel,
        "back",
        [
            ((tokens, model), wide),
            ((tokens, model), low),
            ((tokens, 128), low),
            ((8, model), wide),
            ((tokens, q_cols), low),
            ((2, tokens, 2 * k_cols), wide),
            ((2, tokens, 2 * k_cols), low),
        ],
        [((tokens, model + 128), wide), ((tokens, q_cols), low)],
        [place],
        mixed,
        gates,
        gains,
        small,
        small_far,
        near_out,
        w_out,
        out_far,
        query,
        turns,
        *blocks,
        probs,
        *found,
    )

    given, moe_total = tie((given, moe_total))
    near_pair = beside(given)
    near_pair, attn_grad = tie((near_pair, attn_grad))
    moe_next = lax.ppermute(moe_total, "tp", [(i, i ^ 1) for i in range(tp_size)])
    distant = along((kept[1] + near_pair[1].astype(wide)).astype(low))
    qkv_grad, *pieces = single(
        last_kernel,
        "last",
        [((tokens, qkv_cols), low)] + piece_shapes,
        [((tokens, model), wide)],
        [place],
        query_grad,
        kept,
        near_pair,
        distant,
        turns,
        small,
        small_far,
    )

    def hop_beside(value):
        share = value.shape[1] // 2
        kept = lax.dynamic_slice_in_dim(value, core * share, share, 1)
        given = lax.dynamic_slice_in_dim(value, (1 - core) * share, share, 1)
        return kept + beside(given.astype(low)).astype(wide)

    def hop_across(kept):
        return kept[0] + across(kept[1].astype(low)).astype(wide)

    def hop_along(total):
        return (total + along(total.astype(low)).astype(wide)).astype(low)

    def hop_join(total):
        other = beside(total)
        return jnp.where(
            core == 0,
            jnp.concatenate([total, other], axis=0),
            jnp.concatenate([other, total], axis=0),
        ).astype(wide)

    def both(left, right):
        return jnp.stack([dot(left, right[:, :half], 0, 0), dot(left, right[:, half:], 0, 0)])

    side = hop_beside(
        jnp.concatenate(
            [
                both(head_low, attn_grad),
                both(logit_grad[:, :experts], near[:, :model]),
                jnp.stack([gain_two_part[:, :half], gain_two_part[:, half:]]),
                jnp.zeros((2, 16, half), wide),
            ],
            axis=1,
        )
    )
    side_got = across(side[1].astype(low))
    *pieces, mark, side_got, qkv_grad, pair_one, slots[2], moe_next = tie(
        (*pieces, mark, side_got, qkv_grad, pair_one, slots[2], moe_next)
    )
    side = side[0] + side_got.astype(wide)
    pair_two = gather_slots(slots[2])
    moe_pair = jnp.where(
        z_pos % 2 == 0,
        jnp.concatenate([moe_total, moe_next], axis=0),
        jnp.concatenate([moe_next, moe_total], axis=0),
    )
    moe_rest = lax.ppermute(moe_pair, "tp", [(i, i ^ 2) for i in range(tp_size)])
    total = reduce_pieces(pieces)
    grads = grads_of(1, pair_one, grads, mark)
    d_qkv = hop_beside(dot(normed_one, qkv_grad, 0, 0).reshape(2, half, qkv_cols))
    total, mark, side, d_qkv, moe_rest = tie((total, grads[2], side, d_qkv, moe_rest))
    (layer_out,) = single(
        output_kernel,
        "output",
        [((tokens, model), wide)],
        [((tokens, model), wide)],
        [place],
        mixed,
        moe_pair,
        moe_rest,
    )
    found = spread_pieces(total)
    grads = grads_of(2, pair_two, grads, mark)
    side_got = along(side.astype(low))
    qkv_got = across(d_qkv[1].astype(low))
    *found, mark, side_got, qkv_got = tie((*found, grads[2], side_got, qkv_got))
    side = (side + side_got.astype(wide)).astype(low)
    d_qkv = d_qkv[0] + qkv_got.astype(wide)
    d_hidden, gain_one = single(
        hidden_kernel,
        "hidden",
        [((tokens, model), wide), ((8, model), wide)],
        [((tokens, model), wide)],
        [place],
        hidden,
        gains,
        mixed_grad,
        mark,
        *found,
    )
    gain_one = gain_one[0]
    d_gate_up = grads[0].reshape(experts, half, 2, width)
    d_down = grads[1].reshape(experts, width, half)
    side_grads = hop_join(side)
    d_qkv = hop_join(hop_along(d_qkv))
    gain_one = gain_one + beside(gain_one)
    gain_one = gain_one + along(gain_one)
    gain_one = gain_one[:half] + across(gain_one[half:])
    return (
        layer_out.reshape(micro, 1, rows, model),
        d_hidden.reshape(micro, 1, rows, model),
        gain_one,
        d_qkv[:, :q_cols],
        d_qkv[:, q_cols : q_cols + k_cols],
        d_qkv[:, q_cols + k_cols :],
        side_grads[:q_cols],
        side_grads[q_cols + experts],
        side_grads[q_cols : q_cols + experts].T,
        d_gate_up,
        d_down,
    )


def solution(mesh):
    placed = (
        P(None, "fsdp", "ctx", None),
        P(None, "fsdp", None),
        P(None, "fsdp", "ctx", None),
        P("fsdp"),
        P("fsdp", "tp"),
        P("fsdp", "tp"),
        P("fsdp", "tp"),
        P("tp", "fsdp"),
        P("fsdp"),
        P("fsdp", None),
        P(None, "fsdp", None, "tp"),
        P(None, "tp", "fsdp"),
        P(None, "fsdp", "ctx", None),
    )
    fits = mesh.shape["fsdp"] == 2 and mesh.shape["ctx"] == 4 and mesh.shape["tp"] == 4
    return jax.shard_map(
        fast_body if fits else body,
        mesh=mesh,
        in_specs=placed,
        out_specs=(
            P(None, "fsdp", "ctx", None),
            P(None, "fsdp", "ctx", None),
            P("fsdp"),
            P("fsdp", "tp"),
            P("fsdp", "tp"),
            P("fsdp", "tp"),
            P("tp", "fsdp"),
            P("fsdp"),
            P("fsdp", None),
            P(None, "fsdp", None, "tp"),
            P(None, "tp", "fsdp"),
        ),
        check_vma=False,
    )
```

```python
import functools

import jax
import jax.numpy as jnp
from jax import lax
from jax.experimental import pallas as pl
from jax.experimental.pallas import tpu as pltpu
from jax.sharding import PartitionSpec as P

HEAD_DIM = 64
CAP = 32


EPSILON = 1e-06
RESIDUAL_SCALE = 0.22
SCORE_SCALE = 1.0 / 64.0
ROPE_BASE = 10000.0
TOP_PRECISION = lax.Precision.HIGHEST


def tree_tables(parent_row, tree_len):
    seg_total = parent_row.shape[0]
    seg_len = tree_len // seg_total
    seg_ids = jnp.arange(seg_total, dtype=jnp.int32)
    parent_links = (parent_row[:, None] == seg_ids[None, :]).astype(jnp.float32)
    reach_table = jnp.maximum(parent_links, jnp.eye(seg_total, dtype=jnp.float32))
    for squaring in range(max(seg_total - 1, 1).bit_length()):
        reach_table = jnp.minimum(jnp.dot(reach_table, reach_table, precision=TOP_PRECISION), 1.0)
    seg_depth = jnp.sum(reach_table, axis=1) - 1.0
    token_ids = jnp.arange(tree_len, dtype=jnp.int32)
    tok_owner = ((token_ids // seg_len)[:, None] == seg_ids[None, :]).astype(jnp.float32)
    tok_offset = (token_ids % seg_len).astype(jnp.float32)
    places = jnp.dot(tok_owner, seg_depth, precision=TOP_PRECISION) * seg_len + tok_offset
    return (places, jnp.dot(tok_owner, reach_table, precision=TOP_PRECISION), tok_owner)


def rope_tables(places):
    half_dim = HEAD_DIM // 2
    inverse = ROPE_BASE ** (-jnp.arange(half_dim, dtype=jnp.float32) * 2.0 / HEAD_DIM)
    angles = places[:, None] * inverse[None, :]
    cosine_table = jnp.concatenate([jnp.cos(angles), jnp.cos(angles)], axis=1)
    sine_values = jnp.concatenate([jnp.sin(angles), jnp.sin(angles)], axis=1)
    return (cosine_table, sine_values)


def apply_rotary(values, cosine_table, sine_values):
    half_dim = values.shape[-1] // 2
    turned = jnp.concatenate([-values[..., half_dim:], values[..., :half_dim]], axis=-1)
    return values * cosine_table[:, None, :] + turned * sine_values[:, None, :]


def norm_scale(values):
    return lax.rsqrt(jnp.mean(values * values, axis=-1, keepdims=True) + EPSILON)


def add_tuples(first_tuple, second_tuple):
    return tuple(
        (left_part + right_part for left_part, right_part in zip(first_tuple, second_tuple))
    )


def expert_work(rows, row_grads, gate_up_w, down_w, down_form):
    gate_up = jnp.einsum("ecd,edsf->ecsf", rows, gate_up_w, preferred_element_type=jnp.float32)
    gate_pre = gate_up[:, :, 0]
    up_pre = gate_up[:, :, 1]
    sigmoid = jax.nn.sigmoid(gate_pre)
    activ_low = (gate_pre * sigmoid * up_pre).astype(jnp.bfloat16)
    expert_out = jnp.einsum(
        "ecf," + down_form + "->ecd", activ_low, down_w, preferred_element_type=jnp.float32
    )
    activ_grad = jnp.einsum(
        "ecd," + down_form + "->ecf", row_grads, down_w, preferred_element_type=jnp.float32
    )
    gate_grad = activ_grad * up_pre * sigmoid * (1.0 + gate_pre * (1.0 - sigmoid))
    up_grad = activ_grad * gate_pre * sigmoid
    gate_up_grad = jnp.stack([gate_grad, up_grad], axis=2).astype(jnp.bfloat16)
    row_input_grad = jnp.einsum(
        "ecsf,edsf->ecd", gate_up_grad, gate_up_w, preferred_element_type=jnp.float32
    )
    grad_gate_up = jnp.einsum(
        "ecd,ecsf->edsf", rows, gate_up_grad, preferred_element_type=jnp.float32
    )
    grad_down = jnp.einsum(
        "ecf,ecd->" + down_form, activ_low, row_grads, preferred_element_type=jnp.float32
    )
    return (expert_out, row_input_grad, grad_gate_up, grad_down)


def body(
    hidden_in,
    parents,
    routes,
    attn_gain,
    w_query,
    key_projection,
    value_projection,
    w_out,
    moe_gain,
    w_router,
    w_gate_up,
    w_down,
    d_out,
):
    experts = w_gate_up.shape[0]
    gathered = (
        lax.all_gather(attn_gain, "fsdp", axis=0, tiled=True),
        lax.all_gather(w_query, "fsdp", axis=0, tiled=True),
        lax.all_gather(key_projection, "fsdp", axis=0, tiled=True),
        lax.all_gather(value_projection, "fsdp", axis=0, tiled=True),
        lax.all_gather(w_out, "fsdp", axis=1, tiled=True),
        lax.all_gather(moe_gain, "fsdp", axis=0, tiled=True),
        lax.all_gather(w_router, "fsdp", axis=0, tiled=True),
        lax.all_gather(w_gate_up, "fsdp", axis=1, tiled=True),
        lax.all_gather(w_down, "fsdp", axis=2, tiled=True),
    )
    gate_up_full = gathered[7]
    down_full = gathered[8]
    down_form = "efd"
    gain_one = gathered[0].astype(jnp.float32)
    query_full = gathered[1]
    key_full = gathered[2]
    value_full = gathered[3]
    out_full = gathered[4]
    gain_two = gathered[5].astype(jnp.float32)
    router_full = gathered[6]
    micro_count = hidden_in.shape[0]
    local_rows = hidden_in.shape[2]
    model_width = hidden_in.shape[3]
    top_count = routes.shape[3]
    kv_heads = key_projection.shape[1] // HEAD_DIM
    q_heads = w_query.shape[1] // HEAD_DIM
    group_size = q_heads // kv_heads
    tree_len = local_rows * lax.axis_size("ctx")
    row_start = lax.axis_index("ctx") * local_rows
    capacity = CAP
    expert_ids = jnp.arange(experts, dtype=jnp.int32)
    outputs = []
    input_grads = []
    totals = None
    for batch_index in range(micro_count):
        tree_places, reach_rows, tok_owner = tree_tables(parents[batch_index, 0], tree_len)
        local_places = lax.dynamic_slice_in_dim(tree_places, row_start, local_rows, 0)
        local_reach = lax.dynamic_slice_in_dim(reach_rows, row_start, local_rows, 0)
        allowed = (jnp.dot(local_reach, tok_owner.T, precision=TOP_PRECISION) > 0.5) & (
            tree_places[None, :] <= local_places[:, None]
        )
        cosine_table, sine_values = rope_tables(local_places)
        inputs = hidden_in[batch_index, 0].astype(jnp.float32)
        scale_one = norm_scale(inputs)
        first_normed = (inputs * scale_one * gain_one).astype(jnp.bfloat16)
        query_unrotated = jnp.dot(
            first_normed, query_full, preferred_element_type=jnp.float32
        ).reshape(local_rows, q_heads, HEAD_DIM)
        key_unrotated = jnp.dot(first_normed, key_full, preferred_element_type=jnp.float32).reshape(
            local_rows, kv_heads, HEAD_DIM
        )
        value_reduced = jnp.dot(
            first_normed, value_full, preferred_element_type=jnp.float32
        ).astype(jnp.bfloat16)
        query_reduced = (
            apply_rotary(query_unrotated, cosine_table, sine_values)
            .astype(jnp.bfloat16)
            .reshape(local_rows, kv_heads, group_size, HEAD_DIM)
        )
        key_low = (
            apply_rotary(key_unrotated, cosine_table, sine_values)
            .astype(jnp.bfloat16)
            .reshape(local_rows, kv_heads * HEAD_DIM)
        )
        tree_keys, tree_values = (
            lax.all_gather(key_low, "ctx", axis=0, tiled=True),
            lax.all_gather(value_reduced, "ctx", axis=0, tiled=True),
        )
        tree_keys = tree_keys.reshape(tree_len, kv_heads, HEAD_DIM)
        tree_values = tree_values.reshape(tree_len, kv_heads, HEAD_DIM)

        def masked_scores():
            raw_scores = jnp.einsum(
                "qhjd,khd->hjqk", query_reduced, tree_keys, preferred_element_type=jnp.float32
            )
            return jnp.where(allowed[None, None], raw_scores * SCORE_SCALE, -1e30)

        scores = masked_scores()
        top_score = jnp.max(scores, axis=-1, keepdims=True)
        log_total = top_score + jnp.log(
            jnp.sum(jnp.exp(scores - top_score), axis=-1, keepdims=True)
        )
        probs_low = jnp.exp(scores - log_total).astype(jnp.bfloat16)
        head_out = jnp.einsum(
            "hjqk,khd->qhjd", probs_low, tree_values, preferred_element_type=jnp.float32
        )
        head_low = head_out.reshape(local_rows, q_heads * HEAD_DIM).astype(jnp.bfloat16)
        attn_part = jnp.dot(head_low, out_full, preferred_element_type=jnp.float32)
        attended = lax.psum(attn_part.astype(jnp.bfloat16), "tp").astype(jnp.float32)
        mixed = inputs + RESIDUAL_SCALE * attended
        scale_two = norm_scale(mixed)
        normed_two = (mixed * scale_two * gain_two).astype(jnp.bfloat16)
        logits = jnp.dot(normed_two, router_full, preferred_element_type=jnp.float32)
        chosen_ids = routes[batch_index, 0]
        picked = (chosen_ids[:, :, None] == expert_ids[None, None, :]).astype(jnp.float32)
        chosen = jnp.sum(picked * logits[:, None, :], axis=2)
        gates = jax.nn.softmax(chosen, axis=1)
        flat_ids = chosen_ids.reshape(-1)
        flat_hot = (flat_ids[:, None] == expert_ids[None, :]).astype(jnp.int32)
        slots = jnp.sum((jnp.cumsum(flat_hot, axis=0) - flat_hot) * flat_hot, axis=1)
        targets = flat_ids * capacity + slots
        sources = (
            jnp.zeros((experts * capacity,), jnp.int32)
            .at[targets]
            .set(jnp.arange(local_rows * top_count, dtype=jnp.int32) // top_count)
        )
        filled = jnp.zeros((experts * capacity, 1), jnp.bfloat16).at[targets].set(1)
        dispatched = (normed_two[sources] * filled).reshape(experts, capacity, model_width)
        grad_out = d_out[batch_index, 0].astype(jnp.float32)
        grad_moe = RESIDUAL_SCALE * grad_out
        entry_grad = (
            (gates[:, :, None] * grad_moe[:, None, :])
            .astype(jnp.bfloat16)
            .reshape(local_rows * top_count, model_width)
        )
        slot_grad = (
            jnp.zeros((experts * capacity, model_width), jnp.bfloat16)
            .at[targets]
            .set(entry_grad)
            .reshape(experts, capacity, model_width)
        )
        expert_out, slot_input_grad, grad_gate_up, grad_down = expert_work(
            dispatched, slot_grad, gate_up_full, down_full, down_form
        )
        entry_out = expert_out.reshape(experts * capacity, model_width)[targets].reshape(
            local_rows, top_count, model_width
        )
        moe_part = jnp.sum(gates[:, :, None] * entry_out, axis=1)
        moe_sum = lax.psum(moe_part.astype(jnp.bfloat16), "tp").astype(jnp.float32)
        outputs.append(mixed + RESIDUAL_SCALE * moe_sum)
        gate_grad_part = jnp.sum(grad_moe[:, None, :] * entry_out, axis=2)
        expert_input_grad = jnp.sum(
            slot_input_grad.reshape(experts * capacity, model_width)[targets].reshape(
                local_rows, top_count, model_width
            ),
            axis=1,
        )
        expert_input_grad, gate_grads = (
            lax.psum(expert_input_grad.astype(jnp.bfloat16), "tp").astype(jnp.float32),
            lax.psum(gate_grad_part.astype(jnp.bfloat16), "tp").astype(jnp.float32),
        )
        chosen_grad = gates * (gate_grads - jnp.sum(gates * gate_grads, axis=1, keepdims=True))
        logit_grad = jnp.sum(picked * chosen_grad[:, :, None], axis=1).astype(jnp.bfloat16)
        normed_two_grad = expert_input_grad + jnp.einsum(
            "te,de->td", logit_grad, router_full, preferred_element_type=jnp.float32
        )
        grad_router = jnp.einsum(
            "td,te->de", normed_two, logit_grad, preferred_element_type=jnp.float32
        )
        unit_two = mixed * scale_two
        grad_gain_two = jnp.sum(normed_two_grad * unit_two, axis=0)
        scaled_two = normed_two_grad * gain_two
        mixed_grad = grad_out + scale_two * (
            scaled_two - unit_two * jnp.mean(scaled_two * unit_two, axis=-1, keepdims=True)
        )
        attn_grad = (RESIDUAL_SCALE * mixed_grad).astype(jnp.bfloat16)
        grad_out_proj = jnp.einsum(
            "tc,td->cd", head_low, attn_grad, preferred_element_type=jnp.float32
        )
        head_grad = (
            jnp.einsum("td,cd->tc", attn_grad, out_full, preferred_element_type=jnp.float32)
            .astype(jnp.bfloat16)
            .reshape(local_rows, kv_heads, group_size, HEAD_DIM)
        )
        scores = masked_scores()
        probs = jnp.exp(scores - log_total)
        probs_low = probs.astype(jnp.bfloat16)
        prob_grad = jnp.einsum(
            "qhjd,khd->hjqk", head_grad, tree_values, preferred_element_type=jnp.float32
        )
        value_grad = jnp.einsum(
            "hjqk,qhjd->khd", probs_low, head_grad, preferred_element_type=jnp.float32
        )
        score_grad = (
            SCORE_SCALE * probs * (prob_grad - jnp.sum(probs * prob_grad, axis=-1, keepdims=True))
        ).astype(jnp.bfloat16)
        query_grad = jnp.einsum(
            "hjqk,khd->qhjd", score_grad, tree_keys, preferred_element_type=jnp.float32
        ).reshape(local_rows, q_heads, HEAD_DIM)
        key_grad = jnp.einsum(
            "hjqk,qhjd->khd", score_grad, query_reduced, preferred_element_type=jnp.float32
        )
        key_grad, value_grad = (
            lax.psum_scatter(
                key_grad.reshape(tree_len, kv_heads * HEAD_DIM).astype(jnp.bfloat16),
                "ctx",
                scatter_dimension=0,
                tiled=True,
            ).astype(jnp.float32),
            lax.psum_scatter(
                value_grad.reshape(tree_len, kv_heads * HEAD_DIM).astype(jnp.bfloat16),
                "ctx",
                scatter_dimension=0,
                tiled=True,
            ).astype(jnp.float32),
        )
        query_pre_grad = (
            apply_rotary(query_grad, cosine_table, -sine_values)
            .astype(jnp.bfloat16)
            .reshape(local_rows, q_heads * HEAD_DIM)
        )
        key_pre_grad = (
            apply_rotary(
                key_grad.reshape(local_rows, kv_heads, HEAD_DIM), cosine_table, -sine_values
            )
            .astype(jnp.bfloat16)
            .reshape(local_rows, kv_heads * HEAD_DIM)
        )
        value_pre_grad = value_grad.astype(jnp.bfloat16)
        normed_one_grad = jnp.einsum(
            "tc,dc->td", query_pre_grad, query_full, preferred_element_type=jnp.float32
        )
        normed_one_grad = normed_one_grad + jnp.einsum(
            "tc,dc->td", key_pre_grad, key_full, preferred_element_type=jnp.float32
        )
        normed_one_grad = normed_one_grad + jnp.einsum(
            "tc,dc->td", value_pre_grad, value_full, preferred_element_type=jnp.float32
        )
        grad_query = jnp.einsum(
            "td,tc->dc", first_normed, query_pre_grad, preferred_element_type=jnp.float32
        )
        grad_key = jnp.einsum(
            "td,tc->dc", first_normed, key_pre_grad, preferred_element_type=jnp.float32
        )
        grad_value = jnp.einsum(
            "td,tc->dc", first_normed, value_pre_grad, preferred_element_type=jnp.float32
        )
        normed_one_grad = lax.psum(normed_one_grad.astype(jnp.bfloat16), "tp").astype(jnp.float32)
        unit_one = inputs * scale_one
        grad_gain_one = jnp.sum(normed_one_grad * unit_one, axis=0)
        scaled_one = normed_one_grad * gain_one
        input_grads.append(
            mixed_grad
            + scale_one
            * (scaled_one - unit_one * jnp.mean(scaled_one * unit_one, axis=-1, keepdims=True))
        )
        piece = (
            grad_gain_one,
            grad_query,
            grad_key,
            grad_value,
            grad_out_proj,
            grad_gain_two,
            grad_router,
            grad_gate_up,
            grad_down,
        )
        totals = piece if batch_index == 0 else add_tuples(totals, piece)
    summed = (
        lax.psum_scatter(totals[0], ("fsdp", "ctx"), scatter_dimension=0, tiled=True),
        lax.psum_scatter(totals[1], ("fsdp", "ctx"), scatter_dimension=0, tiled=True),
        lax.psum_scatter(totals[2], ("fsdp", "ctx"), scatter_dimension=0, tiled=True),
        lax.psum_scatter(totals[3], ("fsdp", "ctx"), scatter_dimension=0, tiled=True),
        lax.psum_scatter(totals[4], ("fsdp", "ctx"), scatter_dimension=1, tiled=True),
        lax.psum_scatter(totals[5], ("fsdp", "ctx"), scatter_dimension=0, tiled=True),
        lax.psum_scatter(totals[6], ("fsdp", "ctx"), scatter_dimension=0, tiled=True),
        lax.psum_scatter(totals[7], ("fsdp", "ctx"), scatter_dimension=1, tiled=True),
        lax.psum_scatter(totals[8], ("fsdp", "ctx"), scatter_dimension=2, tiled=True),
    )
    shares = (
        lax.all_gather(summed[0].astype(jnp.bfloat16), "ctx", axis=0, tiled=True).astype(
            jnp.float32
        ),
        lax.all_gather(summed[1].astype(jnp.bfloat16), "ctx", axis=0, tiled=True).astype(
            jnp.float32
        ),
        lax.all_gather(summed[2].astype(jnp.bfloat16), "ctx", axis=0, tiled=True).astype(
            jnp.float32
        ),
        lax.all_gather(summed[3].astype(jnp.bfloat16), "ctx", axis=0, tiled=True).astype(
            jnp.float32
        ),
        lax.all_gather(summed[4].astype(jnp.bfloat16), "ctx", axis=1, tiled=True).astype(
            jnp.float32
        ),
        lax.all_gather(summed[5].astype(jnp.bfloat16), "ctx", axis=0, tiled=True).astype(
            jnp.float32
        ),
        lax.all_gather(summed[6].astype(jnp.bfloat16), "ctx", axis=0, tiled=True).astype(
            jnp.float32
        ),
        lax.all_gather(summed[7].astype(jnp.bfloat16), "ctx", axis=1, tiled=True).astype(
            jnp.float32
        ),
        lax.all_gather(summed[8].astype(jnp.bfloat16), "ctx", axis=2, tiled=True).astype(
            jnp.float32
        ),
    )
    layer_out = jnp.stack(outputs, axis=0)[:, None]
    d_hidden = jnp.stack(input_grads, axis=0)[:, None]
    return (
        layer_out,
        d_hidden,
        shares[0],
        shares[1],
        shares[2],
        shares[3],
        shares[4],
        shares[5],
        shares[6],
        shares[7],
        shares[8],
    )


def dot(left, right, left_dim=1, right_dim=0):
    return lax.dot_general(
        left, right, (((left_dim,), (right_dim,)), ((), ())), preferred_element_type=jnp.float32
    )


def pick(hot, rows):
    return dot(hot, rows).astype(jnp.bfloat16)


def kernel_params(count=0):
    return pltpu.CompilerParams(
        dimension_semantics=("arbitrary",) * count if count else None,
        vmem_limit_bytes=60 * 1024 * 1024,
    )


def single(kernel, name, out_shape, scratch, scalars, *arrays):
    smem = pl.BlockSpec(memory_space=pltpu.SMEM)
    vmem = pl.BlockSpec(memory_space=pltpu.VMEM)
    return pl.pallas_call(
        kernel,
        out_shape=tuple(jax.ShapeDtypeStruct(shape, kind) for shape, kind in out_shape),
        in_specs=[smem] * len(scalars) + [vmem] * len(arrays),
        out_specs=(vmem,) * len(out_shape),
        scratch_shapes=[pltpu.VMEM(shape, kind) for shape, kind in scratch],
        compiler_params=kernel_params(),
        name=name,
    )(*scalars, *arrays)


def tree_path(parents_ref, m, start):
    path = [start]
    for _ in range(3):
        path.append(parents_ref[m, path[-1]])
    return path


def own_then_other(x_pos, array):
    half = array.shape[-1] // 2
    first, second = array[..., :half], array[..., half:]
    return jnp.where(x_pos == 0, first, second), jnp.where(x_pos == 0, second, first)


def row_scale(near, far):
    total = jnp.sum(near * near, axis=1, keepdims=True) + jnp.sum(far * far, axis=1, keepdims=True)
    return lax.rsqrt(total / (2 * near.shape[1]) + EPSILON)


def turn_heads(values):
    half_dim = HEAD_DIM // 2
    lane = lax.broadcasted_iota(jnp.int32, values.shape, 1) % HEAD_DIM
    width = values.shape[1]
    return jnp.where(
        lane < half_dim,
        -pltpu.roll(values, width - half_dim, 1),
        pltpu.roll(values, half_dim, 1),
    )


def split_kernel(base_ref, both_ref, down_ref, out_ref, wide_buf):
    wide_buf[...] = both_ref[0].astype(jnp.float32)
    half = both_ref.shape[1] // 2
    out_ref[0, :half, :] = wide_buf[pl.ds(0, half, stride=2), :].astype(jnp.bfloat16)
    out_ref[0, half : 2 * half, :] = wide_buf[pl.ds(1, half, stride=2), :].astype(jnp.bfloat16)
    if down_ref is not None:
        width = down_ref.shape[1]
        for j in range(half // 128):
            out_ref[0, 2 * half + j * width : 2 * half + (j + 1) * width, :] = down_ref[
                0, :, j * 128 : (j + 1) * 128
            ]


def split_plain_kernel(base_ref, both_ref, out_ref, wide_buf):
    split_kernel(base_ref, both_ref, None, out_ref, wide_buf)


def split_weights(base, count, gate_up, down):
    _, rows, width = gate_up.shape
    packed = rows if down is None else rows + rows // 2
    in_specs = [pl.BlockSpec((1, rows, width), lambda i, base: (base[0] + i, 0, 0))]
    operands = [base, gate_up]
    if down is not None:
        in_specs.append(
            pl.BlockSpec((1, *down.shape[1:]), lambda i, base: (base[0] + i, 0, 0))
        )
        operands.append(down)
    return pl.pallas_call(
        split_plain_kernel if down is None else split_kernel,
        out_shape=jax.ShapeDtypeStruct((count, packed, width), jnp.bfloat16),
        grid_spec=pltpu.PrefetchScalarGridSpec(
            num_scalar_prefetch=1,
            grid=(count,),
            in_specs=in_specs,
            out_specs=pl.BlockSpec((1, packed, width), lambda i, base: (i, 0, 0)),
            scratch_shapes=[pltpu.VMEM((rows, width), jnp.float32)],
        ),
        compiler_params=kernel_params(1),
        name="split_weights",
    )(*operands)


def before_kernel(
    place_ref,
    parents_ref,
    hidden_ref,
    small_ref,
    sent_ref,
    next_ref,
    cosine_ref,
    sine_ref,
    normed_ref,
    query_ref,
    key_value_ref,
    far_ref,
    gains_ref,
    turn_ref,
):
    x_pos, c_pos = place_ref[0], place_ref[1]
    first_core = c_pos % 2 == 0
    half = small_ref.shape[1]
    part = half // 2
    q_cols = query_ref.shape[1]
    kv_cols = key_value_ref.shape[1]
    cols = q_cols + kv_cols
    turned_cols = q_cols + kv_cols // 2
    own_rows = small_ref[: 2 * part, :]
    sent, beside = sent_ref[:part, :], next_ref[:part, :]
    top = jnp.where(first_core, sent, beside)
    low_rows = jnp.where(first_core, beside, sent)
    far_ref[:part, :] = top
    far_ref[part:, :] = low_rows
    own_gain = small_ref[2 * part : 2 * part + 16, :].astype(jnp.float32)
    far_gain = sent_ref[part : part + 16, :].astype(jnp.float32)
    gains_ref[:, :half] = own_gain
    gains_ref[:, half:] = far_gain
    near, far = own_then_other(x_pos, hidden_ref[...].astype(jnp.float32))
    scale = row_scale(near, far)
    near_low = (near * scale * own_gain[:1]).astype(jnp.bfloat16)
    far_low = (far * scale * far_gain[:1]).astype(jnp.bfloat16)
    normed_ref[:, :half] = near_low
    normed_ref[:, half:] = far_low
    made = (
        dot(near_low, own_rows[:, :cols])
        + dot(far_low[:, :part], top[:, :cols])
        + dot(far_low[:, part:], low_rows[:, :cols])
    )
    micro = parents_ref.shape[0]
    rows = hidden_ref.shape[0] // micro
    turns = []
    for m in range(micro):
        path = tree_path(parents_ref, m, c_pos)
        depth = sum((path[i + 1] != path[i]).astype(jnp.int32) for i in range(3))
        span = pl.ds(depth * rows, rows)
        turns.append((cosine_ref[span, :], sine_ref[span, :]))
    cosines = jnp.concatenate([pair[0] for pair in turns], axis=0)
    sines = jnp.concatenate([pair[1] for pair in turns], axis=0)
    turn_ref[0] = cosines
    turn_ref[1] = sines
    count = turned_cols // 128
    values = made[:, :turned_cols]
    rotated = (
        values * jnp.concatenate([cosines] * count, axis=1)
        + turn_heads(values) * jnp.concatenate([sines] * count, axis=1)
    ).astype(jnp.bfloat16)
    query_ref[...] = rotated[:, :q_cols]
    key_value_ref[:, : kv_cols // 2] = rotated[:, q_cols:]
    key_value_ref[:, kv_cols // 2 :] = made[:, turned_cols:].astype(jnp.bfloat16)


def give_pieces(whole_ref, z_pos, piece_refs):
    count = len(piece_refs)
    part = whole_ref.shape[0] // count
    for s in range(count):
        start = pl.multiple_of(((z_pos + s) % count) * part, part)
        piece_refs[s][...] = whole_ref[pl.ds(start, part), :].astype(piece_refs[s].dtype)


def take_pieces(piece_refs, z_pos, whole_ref):
    count = len(piece_refs)
    part = whole_ref.shape[0] // count
    for s in range(count):
        start = pl.multiple_of(((z_pos + s) % count) * part, part)
        whole_ref[pl.ds(start, part), :] = piece_refs[s][...].astype(whole_ref.dtype)


def stack_heads(source, first, group):
    return jnp.concatenate(
        [source[:, (first + h) * HEAD_DIM : (first + h + 1) * HEAD_DIM] for h in range(group)],
        axis=0,
    )


def attend_kernel(
    place_ref,
    parents_ref,
    query_ref,
    kv0,
    kv1,
    kv2,
    kv3,
    out_near_ref,
    out_sent_ref,
    out_next_ref,
    head_ref,
    probs_ref,
    out_far_ref,
    attn_ref,
):
    c_pos = place_ref[1]
    blocks = (kv0, kv1, kv2, kv3)
    micro = parents_ref.shape[0]
    rows = query_ref.shape[0] // micro
    kv_heads = kv0.shape[1] // (2 * HEAD_DIM)
    group = query_ref.shape[1] // HEAD_DIM // kv_heads
    shape = (group * rows, rows)
    causal = (
        lax.broadcasted_iota(jnp.int32, shape, 1)
        <= lax.broadcasted_iota(jnp.int32, shape, 0) % rows
    )
    for m in range(micro):
        span = pl.ds(m * rows, rows)
        whole = query_ref[span, :]
        path = tree_path(parents_ref, m, c_pos)
        pieces = []
        for g in range(kv_heads):
            query = stack_heads(whole, g * group, group)
            parts = []
            for r in range(4):
                keys = blocks[r][span, :][:, g * HEAD_DIM : (g + 1) * HEAD_DIM]
                part = dot(query, keys, 1, 1) * SCORE_SCALE
                if r == 0:
                    part = jnp.where(causal, part, -1e30)
                else:
                    seen = (path[1] == c_pos ^ r) | (path[2] == c_pos ^ r) | (path[3] == c_pos ^ r)
                    part = jnp.where(seen, part, -1e30)
                parts.append(part)
            scores = jnp.concatenate(parts, axis=1)
            powers = jnp.exp(scores - jnp.max(scores, axis=1, keepdims=True))
            probs = powers * (1.0 / jnp.sum(powers, axis=1, keepdims=True))
            probs_ref[m * kv_heads + g] = probs
            low = probs.astype(jnp.bfloat16)
            values = jnp.concatenate(
                [
                    blocks[r][span, :][:, (kv_heads + g) * HEAD_DIM : (kv_heads + g + 1) * HEAD_DIM]
                    for r in range(4)
                ],
                axis=0,
            )
            mixed = dot(low, values)
            pieces += [mixed[h * rows : (h + 1) * rows] for h in range(group)]
        head_ref[span, :] = jnp.concatenate(pieces, axis=1).astype(jnp.bfloat16)
    first_core = c_pos % 2 == 0
    sent, beside = out_sent_ref[...], out_next_ref[...]
    part = sent.shape[0]
    out_far_ref[:part, :] = jnp.where(first_core, sent, beside)
    out_far_ref[part:, :] = jnp.where(first_core, beside, sent)
    half = sent.shape[1]
    attn_ref[:, :half] = dot(head_ref[...], out_near_ref[...]).astype(jnp.bfloat16)
    attn_ref[:, half:] = dot(head_ref[...], out_far_ref[...]).astype(jnp.bfloat16)


def after_kernel(
    place_ref,
    hidden_ref,
    gains_ref,
    small_ref,
    far_ref,
    routes_ref,
    attended_ref,
    mixed_ref,
    rows_ref,
    gates_ref,
):
    half = small_ref.shape[1]
    near, far = own_then_other(place_ref[0], hidden_ref[...].astype(jnp.float32))
    near = near + RESIDUAL_SCALE * attended_ref[:, :half].astype(jnp.float32)
    far = far + RESIDUAL_SCALE * attended_ref[:, half:].astype(jnp.float32)
    mixed_ref[:, :half] = near
    mixed_ref[:, half:] = far
    scale = row_scale(near, far)
    near_low = (near * scale * gains_ref[1:2, :half]).astype(jnp.bfloat16)
    far_low = (far * scale * gains_ref[1:2, half:]).astype(jnp.bfloat16)
    rows_ref[:, :half] = near_low
    rows_ref[:, half : 2 * half] = far_low
    logits = dot(near_low, small_ref[:half, half - 128 :]) + dot(far_low, far_ref[:, half - 128 :])
    lane = lax.broadcasted_iota(jnp.int32, logits.shape, 1)
    named = lane == routes_ref[:, 0:1]
    for k in range(1, routes_ref.shape[1]):
        named = named | (lane == routes_ref[:, k : k + 1])
    logits = jnp.where(named, logits, -1e30)
    powers = jnp.where(named, jnp.exp(logits - jnp.max(logits, axis=1, keepdims=True)), 0.0)
    gates = powers / jnp.sum(powers, axis=1, keepdims=True)
    gates_ref[...] = gates
    high = gates.astype(jnp.bfloat16)
    rest_part = gates - high.astype(jnp.float32)
    rows_ref[:, 2 * half :] = jnp.where(
        lane < 64, high.astype(jnp.float32), pltpu.roll(rest_part, 64, 1)
    ).astype(jnp.bfloat16)


def expert_kernel(
    place_ref,
    near_ref,
    far_ref,
    near_out_ref,
    far_out_ref,
    rank_ref,
    gate_up_ref,
    down_ref,
    *rest,
    first,
    last,
    each,
    split,
):
    count = 4 if split else 1
    other_refs, rest = rest[:count], rest[count:]
    held = rest[:4] if last else ()
    slots_ref, *sums = rest[len(held) : -8]
    rows_buf, grads_buf, moe_buf, back_buf, hot_buf, gate_buf, out_ref, grad_ref = rest[-8:]
    half = down_ref.shape[-1]
    full = 2 * half
    width = down_ref.shape[-2]
    step = pl.program_id(0)
    quarter = [place_ref[1] ^ r for r in range(4)]
    expert = [(place_ref[0] * 4 + quarter[r]) * each + first + step for r in range(4)]
    iota = lax.broadcasted_iota(jnp.int32, (CAP, 128), 0)
    lane = lax.broadcasted_iota(jnp.int32, (CAP, 128), 1)

    @pl.when(step == 0)
    def _():
        if last:
            out_ref[...] = held[0][...].astype(jnp.float32) + held[2][...].astype(jnp.float32)
            grad_ref[...] = held[1][...].astype(jnp.float32) + held[3][...].astype(jnp.float32)
        else:
            out_ref[...] = jnp.zeros_like(out_ref)
            grad_ref[...] = jnp.zeros_like(grad_ref)

    marks = [((lane == expert[r]) | (lane == expert[r] + 64)) for r in range(4)]
    mark = jnp.concatenate(marks, axis=0)
    for b in range(4):
        low = jnp.concatenate(
            [
                jnp.where(iota == rank_ref[quarter[r], 0, pl.ds(b, 1), :], 1.0, 0.0)
                for r in range(4)
            ],
            axis=0,
        ).astype(jnp.bfloat16)
        hot_buf[b] = low
        span = pl.ds((b % 2) * 128, 128)
        source = near_ref if b < 2 else far_ref
        picked = jnp.where(mark, dot(low, source[span, pl.ds(full, 128)]), 0.0)
        gate_buf[b] = jnp.broadcast_to(jnp.sum(picked, axis=1, keepdims=True), (4 * CAP, 128))
        for part in range(2):
            keep = pl.ds(part * half, half)
            if b < 2:
                rows, grads = near_ref[span, keep], near_out_ref[span, keep]
            else:
                swap = pl.ds((1 - part) * half, half)
                rows, grads = far_ref[span, swap], far_out_ref[span, swap]
            rows_buf[b, :, keep] = pick(low, rows)
            grads_buf[b, :, keep] = pick(low, grads)
    for r in range(4):
        q = quarter[r]
        slot = slice(r * CAP, (r + 1) * CAP)
        rows = jnp.concatenate([rows_buf[b, slot, :] for b in range(4)], axis=0)
        grads = jnp.concatenate([grads_buf[b, slot, :] for b in range(4)], axis=0)
        gate = jnp.concatenate([gate_buf[b, slot, :] for b in range(4)], axis=0)
        near_w = jnp.concatenate(
            [gate_up_ref[q, 0, :half, :], gate_up_ref[q, 0, half:, :]], axis=1
        )
        def other(start, size):
            if split:
                return other_refs[r][0, start : start + size, :]
            return other_refs[0][q, 0, start : start + size, :]

        far_w = jnp.concatenate([other(0, half), other(half, half)], axis=1)
        near_down = down_ref[0, q, 0]
        far_down = jnp.concatenate(
            [other(2 * half + j * width, width) for j in range(half // 128)],
            axis=1,
        )
        gate_up = dot(rows[:, :half], near_w) + dot(rows[:, half:], far_w)
        gate_pre = gate_up[:, :width]
        up_pre = gate_up[:, width:]
        sigmoid = 1.0 / (1.0 + jnp.exp(-gate_pre))
        activ = (gate_pre * sigmoid * up_pre).astype(jnp.bfloat16)
        pulled = RESIDUAL_SCALE * (
            dot(grads[:, :half], near_down, 1, 1) + dot(grads[:, half:], far_down, 1, 1)
        )
        activ_wide = activ.astype(jnp.float32)
        gate_grad = jnp.sum(activ_wide * pulled, axis=1, keepdims=True)
        activ_grad = pulled * gate
        gate_pre_grad = activ_grad * up_pre * sigmoid * (1.0 + gate_pre * (1.0 - sigmoid))
        up_pre_grad = activ_grad * gate_pre * sigmoid
        both = jnp.concatenate([gate_pre_grad, up_pre_grad], axis=1).astype(jnp.bfloat16)
        slots_ref[q, 0, :, : 2 * width] = both
        slots_ref[q, 0, :, 2 * width :] = (activ_wide * gate * RESIDUAL_SCALE).astype(jnp.bfloat16)
        for part, (wide, low_w) in enumerate(((near_w, near_down), (far_w, far_down))):
            keep = pl.ds(part * half, half)
            made = dot(activ, low_w)
            back = dot(both, wide, 1, 1)
            for b in range(4):
                piece = slice(b * CAP, (b + 1) * CAP)
                scale = jnp.concatenate([gate[piece]] * (half // 128), axis=1)
                moe_buf[b, slot, keep] = (made[piece] * scale).astype(jnp.bfloat16)
                back_buf[b, slot, keep] = back[piece].astype(jnp.bfloat16)
        spot = lane == expert[r]
        for b in range(4):
            back_buf[b, slot, pl.ds(full, 128)] = jnp.where(
                spot, gate_grad[b * CAP : (b + 1) * CAP], 0.0
            ).astype(jnp.bfloat16)
    for b in range(4):
        span = pl.ds(b * 128, 128)
        out_ref[span, :] += dot(hot_buf[b], moe_buf[b], 0, 0)
        grad_ref[span, :] += dot(hot_buf[b], back_buf[b], 0, 0)

    @pl.when(step == pl.num_programs(0) - 1)
    def _():
        if not last:
            sums[0][...] = out_ref[...].astype(jnp.bfloat16)
            sums[1][...] = grad_ref[...].astype(jnp.bfloat16)
            return
        moe_ref, back_ref, moe_far_ref, back_far_ref = sums
        count = moe_ref.shape[0]
        span = pl.ds(count, count)
        moe_ref[...] = out_ref[:count, :]
        back_ref[...] = grad_ref[:count, :]
        for part in range(2):
            keep, swap = pl.ds(part * half, half), pl.ds((1 - part) * half, half)
            moe_far_ref[:, keep] = out_ref[span, swap].astype(jnp.bfloat16)
            back_far_ref[:, keep] = grad_ref[span, swap].astype(jnp.bfloat16)
        back_far_ref[:, pl.ds(full, 128)] = grad_ref[span, pl.ds(full, 128)].astype(jnp.bfloat16)


def run_experts(place, near, far, near_out, far_out, rank, gate_up, down, other, held, first, each):
    split = isinstance(other, list)
    others = other if split else [other]
    steps, packed, lanes = others[0].shape[-3:]
    quarters, _, rows, width = gate_up.shape
    half = rows // 2
    full = 2 * half
    tokens = 2 * near.shape[0]
    last = first + steps == each

    def fixed(shape):
        return pl.BlockSpec(shape, lambda j, sp: (0,) * len(shape))

    in_specs = [
        fixed(near.shape),
        fixed(far.shape),
        fixed((tokens // 2, full)),
        fixed((tokens // 2, full)),
        pl.BlockSpec((quarters, 1, 4, 128), lambda j, sp: (0, first + j, 0, 0)),
        pl.BlockSpec((quarters, 1, rows, width), lambda j, sp: (0, first + j, 0, 0)),
        pl.BlockSpec((1, quarters, 1, width, half), lambda j, sp: (sp[0], 0, first + j, 0, 0)),
    ]
    if split:
        in_specs += [pl.BlockSpec((1, packed, lanes), lambda j, sp: (j, 0, 0))] * 4
    else:
        in_specs.append(pl.BlockSpec((quarters, 1, packed, lanes), lambda j, sp: (0, j, 0, 0)))
    operands = [place, near, far, near_out, far_out, rank, gate_up, down, *others]
    if last:
        in_specs += [fixed(array.shape) for array in held]
        operands += list(held)
    out_shape = [jax.ShapeDtypeStruct((quarters, steps, 4 * CAP, 3 * width), jnp.bfloat16)]
    out_specs = [pl.BlockSpec((quarters, 1, 4 * CAP, 3 * width), lambda j, sp: (0, j, 0, 0))]
    count = tokens // 2 if last else tokens
    kinds = (jnp.float32, jnp.bfloat16) if last else (jnp.bfloat16,)
    for kind in kinds:
        for lanes_out in (full, full + 128):
            out_shape.append(jax.ShapeDtypeStruct((count, lanes_out), kind))
            out_specs.append(fixed((count, lanes_out)))
    return pl.pallas_call(
        functools.partial(expert_kernel, first=first, last=last, each=each, split=split),
        out_shape=tuple(out_shape),
        grid_spec=pltpu.PrefetchScalarGridSpec(
            num_scalar_prefetch=1,
            grid=(steps,),
            in_specs=in_specs,
            out_specs=tuple(out_specs),
            scratch_shapes=[pltpu.VMEM((4, 4 * CAP, full), jnp.bfloat16)] * 3
            + [
                pltpu.VMEM((4, 4 * CAP, full + 128), jnp.bfloat16),
                pltpu.VMEM((4, 4 * CAP, 128), jnp.bfloat16),
                pltpu.VMEM((4, 4 * CAP, 128), jnp.float32),
                pltpu.VMEM((tokens, full), jnp.float32),
                pltpu.VMEM((tokens, full + 128), jnp.float32),
            ],
        ),
        compiler_params=kernel_params(1),
        name="experts",
    )(*operands)


def join_kernel(place_ref, total_ref, got_ref, *rest):
    piece_refs, whole_buf = rest[:-1], rest[-1]
    count = got_ref.shape[0]
    whole_buf[...] = total_ref[:count, :] + got_ref[...].astype(jnp.float32)
    give_pieces(whole_buf, place_ref[2], piece_refs)


def back_kernel(
    place_ref,
    mixed_ref,
    gates_ref,
    gains_ref,
    small_ref,
    far_ref,
    out_grad_ref,
    out_near_ref,
    out_far_ref,
    query_ref,
    turn_ref,
    kv0,
    kv1,
    kv2,
    kv3,
    probs_ref,
    *rest,
):
    (
        mixed_grad_ref,
        attn_grad_ref,
        logit_grad_ref,
        gain_grad_ref,
        query_grad_ref,
        kept_ref,
        given_ref,
        whole_buf,
        head_buf,
    ) = rest[-9:]
    take_pieces(rest[:-9], place_ref[2], whole_buf)
    half = small_ref.shape[1]
    full = 2 * half
    gates = gates_ref[...]
    gate_grads = whole_buf[:, full:]
    inner = jnp.sum(gates * gate_grads, axis=1, keepdims=True)
    logit_grad = (gates * (gate_grads - inner)).astype(jnp.bfloat16)
    logit_grad_ref[...] = logit_grad
    near, far = mixed_ref[:, :half], mixed_ref[:, half:]
    scale = row_scale(near, far)
    near_unit, far_unit = near * scale, far * scale
    near_grad = whole_buf[:, :half] + dot(logit_grad, small_ref[:half, half - 128 :], 1, 1)
    far_grad = whole_buf[:, half:full] + dot(logit_grad, far_ref[:, half - 128 :], 1, 1)
    gain_grad_ref[:, :half] = jnp.broadcast_to(
        jnp.sum(near_grad * near_unit, axis=0, keepdims=True), (8, half)
    )
    gain_grad_ref[:, half:] = jnp.broadcast_to(
        jnp.sum(far_grad * far_unit, axis=0, keepdims=True), (8, half)
    )
    near_scaled = near_grad * gains_ref[1:2, :half]
    far_scaled = far_grad * gains_ref[1:2, half:]
    mean = (
        jnp.sum(near_scaled * near_unit, axis=1, keepdims=True)
        + jnp.sum(far_scaled * far_unit, axis=1, keepdims=True)
    ) / full
    near_mixed = out_grad_ref[:, :half].astype(jnp.float32) + scale * (
        near_scaled - near_unit * mean
    )
    far_mixed = out_grad_ref[:, half:full].astype(jnp.float32) + scale * (
        far_scaled - far_unit * mean
    )
    mixed_grad_ref[:, :half] = near_mixed
    mixed_grad_ref[:, half:] = far_mixed
    near_attn = (RESIDUAL_SCALE * near_mixed).astype(jnp.bfloat16)
    far_attn = (RESIDUAL_SCALE * far_mixed).astype(jnp.bfloat16)
    attn_grad_ref[:, :half] = near_attn
    attn_grad_ref[:, half:] = far_attn
    head_buf[...] = (
        dot(near_attn, out_near_ref[...], 1, 1) + dot(far_attn, out_far_ref[...], 1, 1)
    ).astype(jnp.bfloat16)
    blocks = (kv0, kv1, kv2, kv3)
    kv_heads = kv0.shape[1] // (2 * HEAD_DIM)
    micro = probs_ref.shape[0] // kv_heads
    rows = query_ref.shape[0] // micro
    group = query_ref.shape[1] // HEAD_DIM // kv_heads
    count = query_ref.shape[1] // 128
    for m in range(micro):
        span = pl.ds(m * rows, rows)
        whole = query_ref[span, :]
        whole_grad = head_buf[span, :]
        pieces = []
        key_grads = []
        value_grads = []
        for g in range(kv_heads):
            query = stack_heads(whole, g * group, group)
            head_grad = stack_heads(whole_grad, g * group, group)
            keys = jnp.concatenate(
                [blocks[r][span, :][:, g * HEAD_DIM : (g + 1) * HEAD_DIM] for r in range(4)], axis=0
            )
            values = jnp.concatenate(
                [
                    blocks[r][span, :][:, (kv_heads + g) * HEAD_DIM : (kv_heads + g + 1) * HEAD_DIM]
                    for r in range(4)
                ],
                axis=0,
            )
            probs = probs_ref[m * kv_heads + g]
            prob_grad = dot(head_grad, values, 1, 1)
            inner = jnp.sum(probs * prob_grad, axis=1, keepdims=True)
            score_grad = (SCORE_SCALE * probs * (prob_grad - inner)).astype(jnp.bfloat16)
            value_grads.append(dot(probs.astype(jnp.bfloat16), head_grad, 0, 0))
            key_grads.append(dot(score_grad, query, 0, 0))
            query_grad = dot(score_grad, keys)
            pieces += [query_grad[h * rows : (h + 1) * rows] for h in range(group)]
        query_grad = jnp.concatenate(pieces, axis=1)
        query_grad_ref[span, :] = (
            query_grad * jnp.concatenate([turn_ref[0, span, :]] * count, axis=1)
            - turn_heads(query_grad) * jnp.concatenate([turn_ref[1, span, :]] * count, axis=1)
        ).astype(jnp.bfloat16)
        joined = jnp.concatenate(key_grads + value_grads, axis=1)
        kept_ref[0, span, :] = joined[:rows]
        kept_ref[1, span, :] = joined[2 * rows : 3 * rows]
        given_ref[0, span, :] = joined[rows : 2 * rows].astype(jnp.bfloat16)
        given_ref[1, span, :] = joined[3 * rows :].astype(jnp.bfloat16)


def last_kernel(
    place_ref,
    query_grad_ref,
    kept_ref,
    near_ref,
    along_ref,
    turn_ref,
    small_ref,
    far_ref,
    grads_ref,
    *rest,
):
    piece_refs, whole_buf = rest[:-1], rest[-1]
    q_cols = query_grad_ref.shape[1]
    k_cols = turn_ref.shape[2]
    cols = q_cols + 2 * k_cols
    half = small_ref.shape[1]
    total = (
        kept_ref[0] + near_ref[0].astype(jnp.float32) + along_ref[...].astype(jnp.float32)
    )
    keys = total[:, :k_cols]
    grads_ref[:, :q_cols] = query_grad_ref[...]
    grads_ref[:, q_cols : q_cols + k_cols] = (
        keys * turn_ref[0] - turn_heads(keys) * turn_ref[1]
    ).astype(jnp.bfloat16)
    grads_ref[:, q_cols + k_cols :] = total[:, k_cols:].astype(jnp.bfloat16)
    grads = grads_ref[...]
    near_part = dot(grads, small_ref[:half, :cols], 1, 1)
    far_part = dot(grads, far_ref[:, :cols], 1, 1)
    whole_buf[:, :half] = near_part
    whole_buf[:, half:] = far_part
    give_pieces(whole_buf, place_ref[2], piece_refs)


def output_kernel(place_ref, mixed_ref, *rest):
    out_ref, whole_buf = rest[-2:]
    take_pieces(rest[:-2], place_ref[2] // 2, whole_buf)
    half = out_ref.shape[1] // 2
    total = mixed_ref[...] + RESIDUAL_SCALE * whole_buf[...]
    first, second = own_then_other(place_ref[0], total)
    out_ref[:, :half] = first
    out_ref[:, half:] = second


def hidden_kernel(place_ref, hidden_ref, gains_ref, mixed_grad_ref, mark_ref, *rest):
    out_ref, gain_ref, whole_buf = rest[-3:]
    take_pieces(rest[:-3], place_ref[2], whole_buf)
    half = out_ref.shape[1] // 2
    near, far = own_then_other(place_ref[0], hidden_ref[...].astype(jnp.float32))
    scale = row_scale(near, far)
    near, far = near * scale, far * scale
    gain_ref[:, :half] = jnp.broadcast_to(
        jnp.sum(whole_buf[:, :half] * near, axis=0, keepdims=True), (8, half)
    )
    gain_ref[:, half:] = jnp.broadcast_to(
        jnp.sum(whole_buf[:, half:] * far, axis=0, keepdims=True), (8, half)
    )
    near_scaled = whole_buf[:, :half] * gains_ref[0:1, :half]
    far_scaled = whole_buf[:, half:] * gains_ref[0:1, half:]
    mean = (
        jnp.sum(near_scaled * near, axis=1, keepdims=True)
        + jnp.sum(far_scaled * far, axis=1, keepdims=True)
    ) / (2 * half)
    near_out = mixed_grad_ref[:, :half] + scale * (near_scaled - near * mean)
    far_out = mixed_grad_ref[:, half:] + scale * (far_scaled - far * mean)
    out_ref[:, :half] = jnp.where(place_ref[0] == 0, near_out, far_out)
    out_ref[:, half:] = jnp.where(place_ref[0] == 0, far_out, near_out)


def weight_grad_kernel(
    place_ref, rows_ref, grads0, grads1, grads2, grads3, slots_ref, rank_ref, *refs, first, steps
):
    gate_up_ref, down_ref, mark_ref, rows_buf, grads_buf = refs[-5:]
    half = down_ref.shape[-1]
    width = down_ref.shape[-2]
    iota = lax.broadcasted_iota(jnp.int32, (CAP, 128), 0)
    grads_in = (grads0, grads1, grads2, grads3)
    ctx = [place_ref[1] ^ r for r in range(4)]
    step, side = pl.program_id(0), pl.program_id(1)
    mark_ref[...] = jnp.zeros_like(mark_ref)

    @pl.when((step == 0) & (side == 0))
    def _():
        @pl.loop(0, 4)
        def _(b):
            span = pl.ds(pl.multiple_of(b * 128, 128), 128)
            for k in range(4):
                hot = jnp.concatenate(
                    [
                        jnp.where(
                            iota == rank_ref[a, q, first + j, pl.ds(4 * k + b, 1), :], 1.0, 0.0
                        )
                        for a in range(2)
                        for j in range(steps)
                        for q in range(4)
                    ],
                    axis=0,
                ).astype(jnp.bfloat16)
                rows = pick(hot, rows_ref[ctx[k], span, :])
                grads = pick(hot, grads_in[k][span, :])
                for a in range(2):
                    spot = 4 * k + (b ^ (2 * a))
                    for j in range(steps):
                        start = (a * steps + j) * 4 * CAP
                        piece = slice(start, start + 4 * CAP)
                        rows_buf[j * 2 + a, spot] = rows[piece]
                        grads_buf[j * 2 + a, spot] = grads[piece]

    place = step * 2 + side
    for q in range(4):
        slot = slice(q * CAP, (q + 1) * CAP)
        rows = jnp.concatenate([rows_buf[place, n, slot, :] for n in range(16)], axis=0)
        grads = jnp.concatenate([grads_buf[place, n, slot, :] for n in range(16)], axis=0)
        taken = jnp.concatenate([slots_ref[0, ctx[k], q, 0] for k in range(4)], axis=0)
        made = dot(rows, taken[:, : 2 * width], 0, 0)
        gate_up_ref[0, q, 0, pl.ds(0, half, stride=2), :] = made[:, :width]
        gate_up_ref[0, q, 0, pl.ds(1, half, stride=2), :] = made[:, width:]
        down_ref[0, q, 0] = dot(taken[:, 2 * width :], grads, 0, 0)


def run_weight_grads(place, plane, early, slots, rank, held, each, first, mark):
    sides, _, quarters, steps, slot_count, lanes = slots.shape
    width = lanes // 3
    half = plane.shape[-1]
    tokens = plane.shape[1]

    def place_of(j, a, sp):
        return (sp[0] ^ a, 0, first + j, 0, 0)

    in_specs = [
        pl.BlockSpec((4, tokens, half), lambda j, a, sp: (0, 0, 0)),
        *[pl.BlockSpec((tokens, half), lambda j, a, sp: (0, 0))] * 4,
        pl.BlockSpec(
            (1, 4, quarters, 1, slot_count, lanes),
            lambda j, a, sp: (sp[0] ^ a, 0, 0, j, 0, 0),
        ),
        pl.BlockSpec(rank.shape, lambda j, a, sp: (0, 0, 0, 0, 0)),
        pl.BlockSpec(memory_space=pl.ANY),
    ]
    operands = [place, plane, *early, slots, rank, mark]
    aliases = {}
    if held is not None:
        in_specs += [pl.BlockSpec(memory_space=pl.ANY)] * 2
        aliases = {len(operands): 0, len(operands) + 1: 1}
        operands += list(held[:2])
    return pl.pallas_call(
        functools.partial(weight_grad_kernel, first=first, steps=steps),
        out_shape=(
            jax.ShapeDtypeStruct((sides, quarters, each, 2 * half, width), jnp.float32),
            jax.ShapeDtypeStruct((sides, quarters, each, width, half), jnp.float32),
            jax.ShapeDtypeStruct((8, 128), jnp.float32),
        ),
        grid_spec=pltpu.PrefetchScalarGridSpec(
            num_scalar_prefetch=1,
            grid=(steps, sides),
            in_specs=in_specs,
            out_specs=(
                pl.BlockSpec((1, quarters, 1, 2 * half, width), place_of),
                pl.BlockSpec((1, quarters, 1, width, half), place_of),
                pl.BlockSpec((8, 128), lambda j, a, sp: (0, 0)),
            ),
            scratch_shapes=[pltpu.VMEM((2 * steps, 16, 4 * CAP, half), jnp.bfloat16)] * 2,
        ),
        input_output_aliases=aliases,
        compiler_params=kernel_params(2),
        name="weight_grads",
    )(*operands)


def swap_halves(values):
    half = values.shape[-1] // 2
    return jnp.concatenate([values[..., half:], values[..., :half]], axis=-1)


def fast_body(
    hidden_in,
    parents,
    routes,
    attn_gain,
    w_query,
    key_projection,
    value_projection,
    w_out,
    moe_gain,
    w_router,
    w_gate_up,
    w_down,
    d_out,
):
    low, wide = jnp.bfloat16, jnp.float32
    x_pos = lax.axis_index("fsdp")
    c_pos = lax.axis_index("ctx")
    z_pos = lax.axis_index("tp")
    tp_size = lax.axis_size("tp")
    place = jnp.stack([x_pos, c_pos, z_pos]).astype(jnp.int32)
    micro, _, rows, model = hidden_in.shape
    half = model // 2
    tokens = micro * rows
    experts = w_gate_up.shape[0]
    mine = experts // 2
    each = mine // 4
    width = w_down.shape[1]
    q_cols = w_query.shape[1]
    k_cols = key_projection.shape[1]
    qkv_cols = q_cols + 2 * k_cols
    kv_heads = k_cols // HEAD_DIM
    group = q_cols // k_cols
    top = routes.shape[-1]
    chunks = ((0, 1), (1, 2), (3, 2))
    tie = lax.optimization_barrier

    def across(value):
        return lax.ppermute(value, "fsdp", [(0, 1), (1, 0)])

    def beside(value):
        return lax.ppermute(value, "ctx", [(i, i ^ 1) for i in range(4)])

    def along(value):
        return lax.ppermute(value, "ctx", [(i, i ^ 2) for i in range(4)])

    def from_tp(value, step):
        return lax.ppermute(value, "tp", [((i + step) % tp_size, i) for i in range(tp_size)])

    def all_ctx(value):
        nearby = beside(value)
        distant = along(value)
        return [value, nearby, distant, beside(distant)]

    def own_first(value):
        return jnp.where(x_pos == 0, value, swap_halves(value))

    def reduce_pieces(pieces):
        total = pieces[0].astype(wide)
        for step in range(1, tp_size):
            total = total + from_tp(pieces[tp_size - step], step).astype(wide)
        return total.astype(low)

    def spread_pieces(total):
        return [total] + [from_tp(total, step) for step in range(1, tp_size)]

    piece_shapes = [((tokens // tp_size, model), low)] * tp_size
    hidden = hidden_in.reshape(tokens, model)
    flat_routes = routes.reshape(tokens, top)

    core = c_pos % 2
    part = half // 2
    weights = jnp.concatenate(
        [
            w_query,
            key_projection,
            value_projection,
            jnp.pad(w_router, ((0, 0), (0, half - qkv_cols - experts))),
        ],
        axis=1,
    )
    gain_rows = jnp.pad(jnp.stack([attn_gain, moe_gain]), ((0, 14), (0, 0)))
    small = jnp.concatenate([weights, gain_rows], axis=0)
    sent = across(
        jnp.concatenate([lax.dynamic_slice_in_dim(weights, core * part, part, 0), gain_rows], axis=0)
    )

    both_view = w_gate_up.reshape(experts, 2 * half, width)
    base = (x_pos * mine).astype(jnp.int32)[None]
    away = ((1 - x_pos) * mine + c_pos * each).astype(jnp.int32)[None]
    packs = [split_weights(away + first, count, both_view, w_down) for first, count in chunks]
    down_all = w_down.reshape(2, 4, each, width, half)
    routes_low = jnp.pad(flat_routes.astype(low), ((0, 0), (0, 128 - top)))
    near_out = jnp.concatenate([own_first(d_out.reshape(tokens, model)), routes_low], axis=1)

    half_dim = HEAD_DIM // 2
    inverse = ROPE_BASE ** (-jnp.arange(half_dim, dtype=wide) * 2.0 / HEAD_DIM)
    angles = jnp.arange(4 * rows, dtype=wide)[:, None] * inverse[None, :]
    cosines = jnp.tile(jnp.cos(angles), (1, 4))
    sines = jnp.tile(jnp.sin(angles), (1, 4))
    sent, packs[0], out_start, small, cosines, sines, place = tie(
        (sent, packs[0], core * (q_cols // 2), small, cosines, sines, place)
    )
    out_sent = across(lax.dynamic_slice_in_dim(w_out, out_start, q_cols // 2, 0))

    normed_one, query, key_value, small_far, gains, turns = single(
        before_kernel,
        "before",
        [
            ((tokens, model), low),
            ((tokens, q_cols), low),
            ((tokens, 2 * k_cols), low),
            ((half, half), low),
            ((16, model), wide),
            ((2, tokens, 128), wide),
        ],
        [],
        [place, parents.reshape(micro, 4)],
        hidden,
        small,
        sent,
        beside(sent),
        cosines,
        sines,
    )
    key_value, packs[0], near_out, out_sent = tie((key_value, packs[0], near_out, out_sent))
    blocks = all_ctx(key_value)
    far_out = across(near_out)
    far_zero = across(packs[0])
    head_low, probs, out_far, attn_part = single(
        attend_kernel,
        "attend",
        [
            ((tokens, q_cols), low),
            ((micro * kv_heads, group * rows, 4 * rows), wide),
            ((q_cols, half), low),
            ((tokens, model), low),
        ],
        [],
        [place, parents.reshape(micro, 4)],
        query,
        *blocks,
        w_out,
        out_sent,
        beside(out_sent),
    )
    attn_part, base = tie((attn_part, base))
    gate_up_mine = split_weights(base, mine, both_view, None).reshape(4, each, 2 * half, width)
    attended = lax.psum(attn_part, "tp")
    far_zero, packs[1] = tie((far_zero, packs[1]))
    far_one = across(packs[1])
    attended, far_out, gate_up_mine, packs[2] = tie(
        (attended, far_out, gate_up_mine, packs[2])
    )
    zero_along = along(far_zero)
    early = jnp.concatenate(
        [
            jnp.concatenate([near_out[:, :half], routes_low], axis=1),
            far_out[:, half:],
        ],
        axis=0,
    )
    early_along = along(early)
    early_near = beside(early)
    mixed, near, gates = single(
        after_kernel,
        "after",
        [((tokens, model), wide), ((tokens, model + 128), low), ((tokens, 128), wide)],
        [],
        [place],
        hidden,
        gains,
        small,
        small_far,
        flat_routes,
        attended,
    )
    upper = (
        lax.broadcasted_iota(jnp.int32, (rows, rows), 0)
        < lax.broadcasted_iota(jnp.int32, (rows, rows), 1)
    ).astype(low)

    def ranks(route_table, ids):
        flat = route_table.astype(jnp.int32).T
        hit = jnp.zeros((ids.shape[0], flat.shape[1]), jnp.bool_)
        for k in range(top):
            hit = hit | (flat[k][None, :] == ids[:, None])
        hot = hit.astype(low).reshape(-1, rows)
        found = jnp.where(hot > 0, dot(hot, upper), -1.0).astype(jnp.int32)
        return found.reshape(ids.shape[0], -1, rows)

    expert_ids = (jnp.arange(experts, dtype=jnp.int32) + x_pos * mine) % experts
    pair_routes = jnp.concatenate([routes_low, far_out[:, model:]], axis=0)[:, :top]
    rank_pair = ranks(pair_routes, expert_ids[:mine]).reshape(4, each, 4, rows)

    near, packs[2] = tie((near, packs[2]))
    far = across(near)
    one_along = along(far_one)
    far, packs[2], zero_along, gate_up_mine, early_along, early_near, rank_pair = tie(
        (far, packs[2], zero_along, gate_up_mine, early_along, early_near, rank_pair)
    )
    early = [early, early_near, early_along, beside(early_along)]
    far_two = across(packs[2])
    plane_in = jnp.concatenate([near[:, :half], far[:, half:model]], axis=0)
    def all_four(got, distant):
        return [got, beside(got), distant, beside(distant)]

    def gather_slots(part):
        return lax.all_gather(part, ("fsdp", "ctx")).reshape(2, 4, *part.shape)

    held = []
    slots = []
    for number, (first, count) in enumerate(chunks):
        if number == 0:
            other = all_four(far_zero, zero_along)
        if number == 1:
            slots[0], far_two, one_along, plane_in = tie(
                (slots[0], far_two, one_along, plane_in)
            )
            two_along = along(far_two)
            plane = lax.all_gather(plane_in, "ctx")
            other = all_four(far_one, one_along)
        if number == 2:
            slots[1], two_along = tie((slots[1], two_along))
            other = all_four(far_two, two_along)
        made = run_experts(
            place,
            near,
            far,
            near_out,
            far_out,
            rank_pair,
            gate_up_mine,
            down_all,
            other,
            held,
            first,
            each,
        )
        slots.append(made[0])
        held += made[1:]
    moe_all, back_all, moe_far, back_far = made[1:]

    all_routes = jnp.concatenate([part[:, half : half + top] for part in early], axis=0)
    rank_all = ranks(all_routes, expert_ids).reshape(2, 4, each, 16, rows)

    back_far, plane, slots[0] = tie((back_far, plane, slots[0]))
    back_got = across(back_far)
    pair_zero = gather_slots(slots[0])
    back_got, moe_far, rank_all = tie((back_got, moe_far, rank_all))

    def grads_of(number, pair, held, mark):
        first, count = chunks[number]
        return run_weight_grads(
            place,
            plane,
            early,
            pair,
            rank_all,
            held,
            each,
            first,
            mark,
        )

    pieces = single(
        join_kernel,
        "join",
        [((tokens // tp_size, model + 128), low)] * tp_size,
        [((tokens, model + 128), wide)],
        [place],
        back_all,
        back_got,
    )
    total = reduce_pieces(pieces)
    total, moe_far, pair_zero, slots[1] = tie((total, moe_far, pair_zero, slots[1]))
    moe_got = across(moe_far)
    pair_one = gather_slots(slots[1])
    found = spread_pieces(total)
    grads = grads_of(0, pair_zero, None, jnp.zeros((8, 128), wide))
    *found, moe_got, mark = tie((*found, moe_got, grads[2]))
    moe_pieces = single(
        join_kernel, "join", piece_shapes, [((tokens, model), wide)], [place], moe_all, moe_got
    )
    moe_total = reduce_pieces(moe_pieces)
    (
        mixed_grad,
        attn_grad,
        logit_grad,
        gain_two_part,
        query_grad,
        kept,
        given,
    ) = single(
        back_kernel,
        "back",
        [
            ((tokens, model), wide),
            ((tokens, model), low),
            ((tokens, 128), low),
            ((8, model), wide),
            ((tokens, q_cols), low),
            ((2, tokens, 2 * k_cols), wide),
            ((2, tokens, 2 * k_cols), low),
        ],
        [((tokens, model + 128), wide), ((tokens, q_cols), low)],
        [place],
        mixed,
        gates,
        gains,
        small,
        small_far,
        near_out,
        w_out,
        out_far,
        query,
        turns,
        *blocks,
        probs,
        *found,
    )

    given, moe_total = tie((given, moe_total))
    near_pair = beside(given)
    near_pair, attn_grad = tie((near_pair, attn_grad))
    moe_next = lax.ppermute(moe_total, "tp", [(i, i ^ 1) for i in range(tp_size)])
    distant = along((kept[1] + near_pair[1].astype(wide)).astype(low))
    qkv_grad, *pieces = single(
        last_kernel,
        "last",
        [((tokens, qkv_cols), low)] + piece_shapes,
        [((tokens, model), wide)],
        [place],
        query_grad,
        kept,
        near_pair,
        distant,
        turns,
        small,
        small_far,
    )

    def hop_beside(value):
        share = value.shape[1] // 2
        kept = lax.dynamic_slice_in_dim(value, core * share, share, 1)
        given = lax.dynamic_slice_in_dim(value, (1 - core) * share, share, 1)
        return kept + beside(given.astype(low)).astype(wide)

    def hop_across(kept):
        return kept[0] + across(kept[1].astype(low)).astype(wide)

    def hop_along(total):
        return (total + along(total.astype(low)).astype(wide)).astype(low)

    def hop_join(total):
        other = beside(total)
        return jnp.where(
            core == 0,
            jnp.concatenate([total, other], axis=0),
            jnp.concatenate([other, total], axis=0),
        ).astype(wide)

    def both(left, right):
        return jnp.stack([dot(left, right[:, :half], 0, 0), dot(left, right[:, half:], 0, 0)])

    side = hop_beside(
        jnp.concatenate(
            [
                both(head_low, attn_grad),
                both(logit_grad[:, :experts], near[:, :model]),
                jnp.stack([gain_two_part[:, :half], gain_two_part[:, half:]]),
                jnp.zeros((2, 16, half), wide),
            ],
            axis=1,
        )
    )
    side_got = across(side[1].astype(low))
    *pieces, mark, side_got, qkv_grad, pair_one, slots[2], moe_next = tie(
        (*pieces, mark, side_got, qkv_grad, pair_one, slots[2], moe_next)
    )
    side = side[0] + side_got.astype(wide)
    pair_two = gather_slots(slots[2])
    moe_pair = jnp.where(
        z_pos % 2 == 0,
        jnp.concatenate([moe_total, moe_next], axis=0),
        jnp.concatenate([moe_next, moe_total], axis=0),
    )
    moe_rest = lax.ppermute(moe_pair, "tp", [(i, i ^ 2) for i in range(tp_size)])
    total = reduce_pieces(pieces)
    grads = grads_of(1, pair_one, grads, mark)
    d_qkv = hop_beside(dot(normed_one, qkv_grad, 0, 0).reshape(2, half, qkv_cols))
    total, mark, side, d_qkv, moe_rest = tie((total, grads[2], side, d_qkv, moe_rest))
    (layer_out,) = single(
        output_kernel,
        "output",
        [((tokens, model), wide)],
        [((tokens, model), wide)],
        [place],
        mixed,
        moe_pair,
        moe_rest,
    )
    found = spread_pieces(total)
    grads = grads_of(2, pair_two, grads, mark)
    side_got = along(side.astype(low))
    qkv_got = across(d_qkv[1].astype(low))
    *found, mark, side_got, qkv_got = tie((*found, grads[2], side_got, qkv_got))
    side = (side + side_got.astype(wide)).astype(low)
    d_qkv = d_qkv[0] + qkv_got.astype(wide)
    d_hidden, gain_one = single(
        hidden_kernel,
        "hidden",
        [((tokens, model), wide), ((8, model), wide)],
        [((tokens, model), wide)],
        [place],
        hidden,
        gains,
        mixed_grad,
        mark,
        *found,
    )
    gain_one = gain_one[0]
    d_gate_up = grads[0].reshape(experts, half, 2, width)
    d_down = grads[1].reshape(experts, width, half)
    side_grads = hop_join(side)
    d_qkv = hop_join(hop_along(d_qkv))
    gain_one = gain_one + beside(gain_one)
    gain_one = gain_one + along(gain_one)
    gain_one = gain_one[:half] + across(gain_one[half:])
    return (
        layer_out.reshape(micro, 1, rows, model),
        d_hidden.reshape(micro, 1, rows, model),
        gain_one,
        d_qkv[:, :q_cols],
        d_qkv[:, q_cols : q_cols + k_cols],
        d_qkv[:, q_cols + k_cols :],
        side_grads[:q_cols],
        side_grads[q_cols + experts],
        side_grads[q_cols : q_cols + experts].T,
        d_gate_up,
        d_down,
    )


def solution(mesh):
    placed = (
        P(None, "fsdp", "ctx", None),
        P(None, "fsdp", None),
        P(None, "fsdp", "ctx", None),
        P("fsdp"),
        P("fsdp", "tp"),
        P("fsdp", "tp"),
        P("fsdp", "tp"),
        P("tp", "fsdp"),
        P("fsdp"),
        P("fsdp", None),
        P(None, "fsdp", None, "tp"),
        P(None, "tp", "fsdp"),
        P(None, "fsdp", "ctx", None),
    )
    fits = mesh.shape["fsdp"] == 2 and mesh.shape["ctx"] == 4 and mesh.shape["tp"] == 4
    return jax.shard_map(
        fast_body if fits else body,
        mesh=mesh,
        in_specs=placed,
        out_specs=(
            P(None, "fsdp", "ctx", None),
            P(None, "fsdp", "ctx", None),
            P("fsdp"),
            P("fsdp", "tp"),
            P("fsdp", "tp"),
            P("fsdp", "tp"),
            P("tp", "fsdp"),
            P("fsdp"),
            P("fsdp", None),
            P(None, "fsdp", None, "tp"),
            P(None, "tp", "fsdp"),
        ),
        check_vma=False,
    )
```
